32 devices in a mesh: dp: 8 (over z, y), seq: 4 (over x, core).
Axes of the slice: x: 2, y: 2, z: 4, core: 2. Of those that a mesh axis runs over, the one named last changes fastest.
Arguments:
- layer_input: bfloat16 [8, 1024, 2048], P('dp', 'seq'), may hold values from -6 to 6
- pic_starts: int32 [8, 2], P('dp'), may hold values from 0 to 768, as said below
- skip_mask: int32 [8, 1024], P('dp', 'seq'), may hold values 0 or 1
- gain_attn: float32 [2048], P(('dp', 'seq')), may hold values from 0.1 to 1.9
- w_query: bfloat16 [2048, 2048], P(('dp', 'seq')), may hold values from -0.125 to 0.125
- w_key: bfloat16 [2048, 512], P(('dp', 'seq')), may hold values from -0.125 to 0.125
- w_value: bfloat16 [2048, 512], P(('dp', 'seq')), may hold values from -0.125 to 0.125
- w_out: bfloat16 [2048, 2048], P(None, ('dp', 'seq')), may hold values from -1 to 1
- gain_ffn: float32 [2048], P(('dp', 'seq')), may hold values from 0.1 to 1.9
- w_gate: bfloat16 [2048, 5632], P(('dp', 'seq')), may hold values from -0.125 to 0.125
- w_up: bfloat16 [2048, 5632], P(('dp', 'seq')), may hold values from -0.125 to 0.125
- w_down: bfloat16 [5632, 2048], P(None, ('dp', 'seq')), may hold values from -0.078125 to 0.078125
- cotangent: bfloat16 [8, 1024, 2048], P('dp', 'seq'), may hold values from -6 to 6
Outputs:
- out_hidden: bfloat16 [8, 1024, 2048], P('dp', 'seq')
- grad_input: float32 [8, 1024, 2048], P('dp', 'seq')
- grad_gain_attn: float32 [2048], P(('dp', 'seq'))
- grad_w_query: float32 [2048, 2048], P(('dp', 'seq'))
- grad_w_key: float32 [2048, 512], P(('dp', 'seq'))
- grad_w_value: float32 [2048, 512], P(('dp', 'seq'))
- grad_w_out: float32 [2048, 2048], P(None, ('dp', 'seq'))
- grad_gain_ffn: float32 [2048], P(('dp', 'seq'))
- grad_w_gate: float32 [2048, 5632], P(('dp', 'seq'))
- grad_w_up: float32 [2048, 5632], P(('dp', 'seq'))
- grad_w_down: float32 [5632, 2048], P(None, ('dp', 'seq'))
The draws below stay inside these ranges and needn't reach their ends.
Inputs may be any that keep to these rules, and one draw needn't show every extreme that they name: `pic_starts`: piece j of a sequence starts between j * 512 and (j + 1) * 512 - 256, so pieces of one sequence never intersect.
All inputs are finite; a program needn't handle non-finite values. No bound on the sum of `skip_mask` on one device may be relied on, other than what follows from the above.
Results may differ from the reference program's by a relative error of at most 0.039.
Values may be sent and summed in bfloat16 or wider, within the bound.
A program may use at most 640 MiB of HBM per device.

```python
import jax
import jax.numpy as jnp
from jax import lax

D = 2048
H = 16
KV = 4
DH = 128
FF = 5632
PIC = 256
NPIC = 2
SEQ_LEN = 1024
SEQS = 8


def draw_pic_starts(key, part):
    region = SEQ_LEN // NPIC
    offsets = jax.random.randint(key, (SEQS, NPIC), 0, region - PIC + 1, dtype=jnp.int32)
    return (offsets + jnp.arange(NPIC, dtype=jnp.int32)[None, :] * region).astype(jnp.int32)


def place_ends(values, key, low, largest):
    spot = [jax.random.randint(jax.random.fold_in(key, axis), (), 0, length) for axis, length in enumerate(values.shape)]
    longest = values.shape.index(max(values.shape))
    beside = spot[:longest] + [(spot[longest] + 1) % values.shape[longest]] + spot[longest + 1:]
    return values.at[tuple(spot)].set(low).at[tuple(beside)].set(largest)


def block_scale(own_key, dims, pieces, low, top_value):
    def one(axis_at, shards_of):
        heights = jax.random.uniform(jax.random.fold_in(jax.random.fold_in(own_key, 6), axis_at), (shards_of,), jnp.float32, low / len(pieces), top_value / len(pieces))
        return jnp.repeat(jnp.exp(heights), dims[axis_at] // shards_of).reshape((-1,) + (1,) * (len(dims) - axis_at - 1))

    gain = one(*pieces[0])
    for cut in pieces[1:]:
        gain = gain * one(*cut)
    return gain


def bell_draw(rng, extent, deviation, reach, shards=(), kind=jnp.bfloat16):
    values = deviation * jax.random.normal(rng, extent, jnp.float32)
    if shards:
        values = values * block_scale(rng, extent, shards, -0.22, 0.18)
    return jnp.clip(values, -reach, reach).astype(kind)


def setup_inputs(seed: int = 0) -> dict:
    splits = jax.random.split(jax.random.key(seed), 14)
    return {
        "layer_input": bell_draw(splits[0], (SEQS, SEQ_LEN, D), 1.0, 6.0, ((0, 8), (1, 4))),
        "pic_starts": draw_pic_starts(jax.random.fold_in(splits[13], 71), 0),
        "skip_mask": place_ends((jax.random.randint(splits[2], (SEQS, SEQ_LEN), 0, 4) < 1).astype(jnp.int32), jax.random.fold_in(splits[2], 1), 0, 1),
        "gain_attn": jnp.clip(1.0 + 0.18 * jax.random.normal(splits[3], (D,), jnp.float32), 0.1, 1.9),
        "w_query": bell_draw(splits[4], (D, H * DH), D ** -0.5, 0.125, ((0, 32),)),
        "w_key": bell_draw(splits[5], (D, KV * DH), D ** -0.5, 0.125, ((0, 32),)),
        "w_value": bell_draw(splits[6], (D, KV * DH), D ** -0.5, 0.125, ((0, 32),)),
        "w_out": bell_draw(splits[7], (H * DH, D), (H * DH // 64) ** -0.5, 1.0, ((1, 32),)),
        "gain_ffn": jnp.clip(1.0 + 0.18 * jax.random.normal(splits[8], (D,), jnp.float32), 0.1, 1.9),
        "w_gate": bell_draw(splits[9], (D, FF), D ** -0.5, 0.125, ((0, 32),)),
        "w_up": bell_draw(splits[10], (D, FF), D ** -0.5, 0.125, ((0, 32),)),
        "w_down": bell_draw(splits[11], (FF, D), FF ** -0.5, 0.078125, ((1, 32),)),
        "cotangent": bell_draw(splits[12], (SEQS, SEQ_LEN, D), 1.0, 6.0, ((0, 8), (1, 4))),
    }


@jax.custom_vjp
def low(v):
    return lax.optimization_barrier(v.astype(jnp.bfloat16)).astype(jnp.float32)

@jax.custom_vjp
def low_back(v):
    return v

def low_keep(v):
    return (low(v), None)

def low_pass(kept, grad):
    return (grad,)

def back_keep(v):
    return (v, None)

def back_low(kept, grad):
    return (low(grad),)
low.defvjp(low_keep, low_pass)
low_back.defvjp(back_keep, back_low)
EPS = 1e-05
HIGHEST = lax.Precision.HIGHEST

def matmul(left, right):
    return jnp.dot(left, right, precision=HIGHEST, preferred_element_type=jnp.float32)

def rotary_tables(positions, head_dim):
    half_dim = head_dim // 2
    inverse = 10000.0 ** (-(jnp.arange(half_dim, dtype=jnp.float32) * 2.0 / head_dim))
    angles = positions.astype(jnp.float32)[:, None] * inverse[None, :]
    return (jnp.cos(angles), jnp.sin(angles))

def rotate(values, cos_table, sin_table):
    half_dim = values.shape[-1] // 2
    table_shape = (cos_table.shape[0],) + (1,) * (values.ndim - 3) + (half_dim,)
    cos_part = cos_table.reshape(table_shape)
    sin_part = sin_table.reshape(table_shape)
    first_half = values[..., :half_dim]
    second = values[..., half_dim:]
    return jnp.concatenate([first_half * cos_part - second * sin_part, second * cos_part + first_half * sin_part], axis=-1)

def picture_ids(positions, starts):
    inside = (positions[None, None, :] >= starts[:, :, None]) & (positions[None, None, :] < starts[:, :, None] + PIC)
    labels = jnp.arange(1, NPIC + 1, dtype=jnp.int32)
    return lax.optimization_barrier(jnp.sum(jnp.where(inside, labels[None, :, None], 0), axis=1))

def visible(query_pos, key_pos, starts):
    query_ids = picture_ids(query_pos, starts)
    key_ids = picture_ids(key_pos, starts)
    causal = key_pos[None, None, :] <= query_pos[None, :, None]
    same_piece = (query_ids[:, :, None] == key_ids[:, None, :]) & (query_ids[:, :, None] > 0)
    return causal | same_piece

def rms_scale(rows_in):
    return lax.rsqrt(lax.optimization_barrier(jnp.mean(rows_in * rows_in, axis=-1, keepdims=True)) + EPS)

def attend_one(packed):
    queries, keys_all, values_all, starts = packed
    positions = jnp.arange(SEQ_LEN, dtype=jnp.int32)
    allowed = visible(positions, positions, starts[None, :])[0]
    scores = jnp.einsum('qngd,knd->ngqk', queries, keys_all, precision=HIGHEST) * DH ** (-0.5)
    scores = low_back(scores)
    scores = jnp.where(allowed[None, None], scores, -jnp.inf)
    probs = low(jax.nn.softmax(scores, axis=-1))
    return jnp.einsum('ngqk,knd->qngd', probs, values_all, precision=HIGHEST)

def reference(layer_input, pic_starts, skip_mask, gain_attn, w_query, w_key, w_value, w_out, gain_ffn, w_gate, w_up, w_down, cotangent):
    groups = H // KV
    tok_rows = SEQS * SEQ_LEN
    keep = (1 - skip_mask).astype(jnp.float32).reshape(tok_rows, 1)
    cos_table, sin_table = rotary_tables(jnp.arange(SEQ_LEN, dtype=jnp.int32), DH)

    def forward(inputs, first_gain, query_weight, key_weight, value_weight, output_weight, second_gain, gate_weight, up_weight, down_weight):
        tokens = inputs.reshape(tok_rows, D)
        normed = low(tokens * rms_scale(tokens) * first_gain)
        query_pre = low_back(matmul(normed, query_weight)).reshape(SEQS, SEQ_LEN, KV, groups, DH)
        key_pre = low_back(matmul(normed, key_weight)).reshape(SEQS, SEQ_LEN, KV, DH)
        value_rows = low(low_back(matmul(normed, value_weight))).reshape(SEQS, SEQ_LEN, KV, DH)
        queries = low(rotate(query_pre, cos_table, sin_table))
        keys_rot = low(rotate(key_pre, cos_table, sin_table))
        mixed = lax.map(jax.checkpoint(attend_one), (queries, keys_rot, value_rows, pic_starts))
        mixed = low(low_back(mixed)).reshape(tok_rows, H * DH)
        branch = low_back(matmul(mixed, output_weight))
        hidden = tokens + keep * branch
        second_low = low(hidden * rms_scale(hidden) * second_gain)
        gate = low_back(matmul(second_low, gate_weight))
        upward = low_back(matmul(second_low, up_weight))
        inner = low(jax.nn.silu(gate) * upward)
        result = hidden + keep * low_back(matmul(inner, down_weight))
        return result.reshape(SEQS, SEQ_LEN, D)
    output, pullback = jax.vjp(forward, layer_input.astype(jnp.float32), gain_attn.astype(jnp.float32), w_query.astype(jnp.float32), w_key.astype(jnp.float32), w_value.astype(jnp.float32), w_out.astype(jnp.float32), gain_ffn.astype(jnp.float32), w_gate.astype(jnp.float32), w_up.astype(jnp.float32), w_down.astype(jnp.float32))
    gradients = pullback(cotangent.astype(jnp.float32))
    return (output.astype(jnp.bfloat16), gradients[0], gradients[1], gradients[2], gradients[3], gradients[4], gradients[5], gradients[6], gradients[7], gradients[8], gradients[9])
```

```python
import jax
import jax.numpy as jnp
from jax import lax
from jax.sharding import Mesh
from jax.sharding import PartitionSpec as P

H = 16
KV = 4
DH = 128
PIC = 256
NPIC = 2
EPS = 1e-05
TP = 2
BF = jnp.bfloat16
F32 = jnp.float32


def rotary_tables(positions, head_dim):
    half_dim = head_dim // 2
    inverse = 10000.0 ** (-(jnp.arange(half_dim, dtype=F32) * 2.0 / head_dim))
    angles = positions.astype(F32)[:, None] * inverse[None, :]
    return (jnp.cos(angles), jnp.sin(angles))


def rotate(values, cos_table, sin_table):
    half = values.shape[-1] // 2
    shape = (cos_table.shape[0],) + (1,) * (values.ndim - 2) + (half,)
    cos_part = cos_table.reshape(shape)
    sin_part = sin_table.reshape(shape)
    first = values[..., :half]
    second = values[..., half:]
    return jnp.concatenate(
        [first * cos_part - second * sin_part, second * cos_part + first * sin_part], axis=-1
    )


def picture_ids(positions, starts):
    inside = (positions[None, :] >= starts[:, None]) & (positions[None, :] < starts[:, None] + PIC)
    labels = jnp.arange(1, NPIC + 1, dtype=jnp.int32)
    return jnp.sum(jnp.where(inside, labels[:, None], 0), axis=0)


def visible(positions, starts):
    ids = picture_ids(positions, starts)
    causal = positions[None, :] <= positions[:, None]
    same_piece = (ids[:, None] == ids[None, :]) & (ids[:, None] > 0)
    return causal | same_piece


def rms_scale(rows):
    return lax.rsqrt(jnp.mean(rows * rows, axis=-1, keepdims=True) + EPS)


def dot(left, right, contract):
    return lax.dot_general(
        left, right, ((contract[:1], contract[1:]), ((), ())), preferred_element_type=F32
    )


def nn(left, right):
    return dot(left, right, (1, 0))


def nt(left, right):
    return dot(left, right, (1, 1))


def tn(left, right):
    return dot(left, right, (0, 0))


def columns(matrix, parts):
    rows, cols = matrix.shape
    return jnp.transpose(matrix.reshape(rows, parts, cols // parts), (1, 0, 2))


def uncolumns(blocks):
    parts, rows, cols = blocks.shape
    return jnp.transpose(blocks, (1, 0, 2)).reshape(rows, parts * cols)


def per_device(
    layer_input,
    pic_starts,
    skip_mask,
    gain_attn,
    w_query,
    w_key,
    w_value,
    w_out,
    gain_ffn,
    w_gate,
    w_up,
    w_down,
    cotangent,
):
    _, local_len, width = layer_input.shape
    seq = lax.axis_size("seq")
    plane = lax.axis_size("tp") * seq
    total_len = local_len * seq
    heads = H // seq
    kv_heads = KV // seq
    groups = H // KV
    ff = w_gate.shape[1]
    ff_part = ff // plane
    q_part = heads * DH
    k_part = kv_heads * DH
    scale = DH ** (-0.5)
    in_plane = ("tp", "seq")

    gain1 = gain_attn[:, None]
    gain2 = gain_ffn[:, None]
    wq32, wk32, wv32 = w_query.astype(F32), w_key.astype(F32), w_value.astype(F32)
    wg32, wu32 = w_gate.astype(F32), w_up.astype(F32)
    attn_pack = jnp.concatenate(
        [
            columns((wq32 * gain1).astype(BF), seq),
            columns((wk32 * gain1).astype(BF), seq),
            columns((wv32 * gain1).astype(BF), seq),
            columns(w_out.T, seq),
        ],
        axis=2,
    )
    attn_rows = lax.all_to_all(attn_pack, "seq", 0, 0, tiled=True)
    attn_rows = attn_rows.reshape(-1, attn_rows.shape[2])
    attn_weight = lax.all_gather(attn_rows, ("rep", "tp"), axis=0, tiled=True)
    qkv_weight = attn_weight[:, : q_part + 2 * k_part]
    out_weight = attn_weight[:, q_part + 2 * k_part :]

    ffn_pack = jnp.concatenate(
        [
            columns((wg32 * gain2).astype(BF), plane),
            columns((wu32 * gain2).astype(BF), plane),
            columns(w_down.T, plane),
        ],
        axis=2,
    )
    ffn_rows = lax.all_to_all(ffn_pack, in_plane, 0, 0, tiled=True)
    ffn_rows = ffn_rows.reshape(-1, ffn_rows.shape[2])
    gu_weight = lax.all_gather(ffn_rows[:, : 2 * ff_part], "rep", axis=0, tiled=True)
    down_weight = lax.all_gather(ffn_rows[:, 2 * ff_part :], "rep", axis=0, tiled=True)

    tokens = layer_input.reshape(local_len, width).astype(F32)
    keep = (1 - skip_mask).astype(F32).reshape(local_len, 1)
    upstream = cotangent.reshape(local_len, width).astype(F32)
    scale1 = rms_scale(tokens)
    norm1 = tokens * scale1
    norm1_all = lax.all_gather(norm1.astype(BF), "seq", axis=0, tiled=True)
    ffn_grad = lax.all_gather((keep * upstream).astype(BF), in_plane, axis=0, tiled=True)

    positions = jnp.arange(total_len, dtype=jnp.int32)
    cos_table, sin_table = rotary_tables(positions, DH)
    allowed = visible(positions, pic_starts[0])[None, None]

    projected = nn(norm1_all, qkv_weight)
    queries = rotate(
        projected[:, :q_part].reshape(total_len, kv_heads, groups, DH), cos_table, sin_table
    ).astype(BF)
    keys = rotate(
        projected[:, q_part : q_part + k_part].reshape(total_len, kv_heads, DH),
        cos_table,
        sin_table,
    ).astype(BF)
    values = projected[:, q_part + k_part :].reshape(total_len, kv_heads, DH).astype(BF)

    def raw_scores():
        scores = jnp.einsum("qngd,knd->ngqk", queries, keys, preferred_element_type=F32) * scale
        return jnp.where(allowed, scores, -jnp.inf)

    scores = raw_scores()
    peak = jnp.max(scores, axis=-1, keepdims=True)
    log_total = peak + jnp.log(jnp.sum(jnp.exp(scores - peak), axis=-1, keepdims=True))
    probs = jnp.exp(scores - log_total)
    probs_low = probs.astype(BF)
    mixed = jnp.einsum("ngqk,knd->qngd", probs_low, values, preferred_element_type=F32)
    mixed = mixed.astype(BF).reshape(total_len, q_part)
    branch = lax.psum_scatter(
        nt(mixed, out_weight).astype(BF), "seq", scatter_dimension=0, tiled=True
    )
    hidden = tokens + keep * branch.astype(F32)

    scale2 = rms_scale(hidden)
    norm2 = hidden * scale2
    norm2_all = lax.all_gather(norm2.astype(BF), in_plane, axis=0, tiled=True)
    inner_grad = nn(ffn_grad, down_weight)
    gate_up = nn(norm2_all, gu_weight)
    gate, upward = gate_up[:, :ff_part], gate_up[:, ff_part:]
    sigmoid_gate = jax.nn.sigmoid(gate)
    silu_gate = gate * sigmoid_gate
    inner = (silu_gate * upward).astype(BF)
    slope = sigmoid_gate * (1.0 + gate * (1.0 - sigmoid_gate))
    gate_up_grad = jnp.concatenate(
        [(inner_grad * upward * slope).astype(BF), (inner_grad * silu_gate).astype(BF)], axis=1
    )
    scaled2 = lax.psum_scatter(
        nt(gate_up_grad, gu_weight).astype(BF), in_plane, scatter_dimension=0, tiled=True
    ).astype(F32)
    ffn_out = lax.psum_scatter(
        nt(inner, down_weight).astype(BF), in_plane, scatter_dimension=0, tiled=True
    )
    out_hidden = (hidden + keep * ffn_out.astype(F32)).astype(BF)
    hidden_grad = upstream + scale2 * (
        scaled2 - norm2 * jnp.mean(scaled2 * norm2, axis=-1, keepdims=True)
    )
    ffn_partial = jnp.concatenate(
        [tn(norm2_all, gate_up_grad).astype(BF), tn(ffn_grad, inner).astype(BF)], axis=1
    )
    ffn_sums = lax.psum_scatter(ffn_partial, "rep", scatter_dimension=0, tiled=True)

    branch_grad = lax.all_gather((keep * hidden_grad).astype(BF), "seq", axis=0, tiled=True)
    mixed_grad = nn(branch_grad, out_weight).astype(BF).reshape(total_len, kv_heads, groups, DH)
    values_grad = jnp.einsum(
        "ngqk,qngd->knd", probs_low, mixed_grad, preferred_element_type=F32
    ).astype(BF)
    prob_grad = jnp.einsum("qngd,knd->ngqk", mixed_grad, values, preferred_element_type=F32)
    score_grad = (
        probs * (prob_grad - jnp.sum(probs * prob_grad, axis=-1, keepdims=True))
    ).astype(BF)
    queries_grad = (
        jnp.einsum("ngqk,knd->qngd", score_grad, keys, preferred_element_type=F32) * scale
    )
    keys_grad = (
        jnp.einsum("ngqk,qngd->knd", score_grad, queries, preferred_element_type=F32) * scale
    )
    qkv_grad = jnp.concatenate(
        [
            rotate(queries_grad, cos_table, -sin_table).astype(BF).reshape(total_len, q_part),
            rotate(keys_grad, cos_table, -sin_table).astype(BF).reshape(total_len, k_part),
            values_grad.reshape(total_len, k_part),
        ],
        axis=1,
    )
    scaled1 = lax.psum_scatter(
        nt(qkv_grad, qkv_weight).astype(BF), "seq", scatter_dimension=0, tiled=True
    ).astype(F32)
    input_grad = hidden_grad + scale1 * (
        scaled1 - norm1 * jnp.mean(scaled1 * norm1, axis=-1, keepdims=True)
    )
    attn_partial = jnp.concatenate(
        [tn(norm1_all, qkv_grad).astype(BF), tn(branch_grad, mixed).astype(BF)], axis=1
    )
    attn_sums = lax.psum_scatter(attn_partial, ("rep", "tp"), scatter_dimension=0, tiled=True)

    ffn_own = lax.all_to_all(
        ffn_sums.reshape(plane, -1, ffn_sums.shape[1]), in_plane, 0, 0, tiled=True
    ).astype(F32)
    gate_own = uncolumns(ffn_own[:, :, :ff_part])
    up_own = uncolumns(ffn_own[:, :, ff_part : 2 * ff_part])
    down_own = uncolumns(ffn_own[:, :, 2 * ff_part :])
    gain_ffn_grad = jnp.sum(gate_own * wg32, axis=1) + jnp.sum(up_own * wu32, axis=1)

    attn_own = lax.all_to_all(
        attn_sums.reshape(seq, -1, attn_sums.shape[1]), "seq", 0, 0, tiled=True
    ).astype(F32)
    query_own = uncolumns(attn_own[:, :, :q_part])
    key_own = uncolumns(attn_own[:, :, q_part : q_part + k_part])
    value_own = uncolumns(attn_own[:, :, q_part + k_part : q_part + 2 * k_part])
    out_own = uncolumns(attn_own[:, :, q_part + 2 * k_part :])
    gain_attn_grad = (
        jnp.sum(query_own * wq32, axis=1)
        + jnp.sum(key_own * wk32, axis=1)
        + jnp.sum(value_own * wv32, axis=1)
    )
    return (
        out_hidden[None],
        input_grad[None],
        gain_attn_grad,
        query_own * gain1,
        key_own * gain1,
        value_own * gain1,
        out_own.T,
        gain_ffn_grad,
        gate_own * gain2,
        up_own * gain2,
        down_own.T,
    )


def solution(mesh):
    devices = mesh.devices
    dp, seq = devices.shape
    inner = Mesh(devices.reshape(dp // TP, TP, seq), ("rep", "tp", "seq"))
    dps = ("rep", "tp")
    every = ("rep", "tp", "seq")
    token = P(dps, "seq", None)
    row = P(every, None)
    col = P(None, every)
    return jax.shard_map(
        per_device,
        mesh=inner,
        in_specs=(
            token,
            P(dps, None),
            P(dps, "seq"),
            P(every),
            row,
            row,
            row,
            col,
            P(every),
            row,
            row,
            col,
            token,
        ),
        out_specs=(token, token, P(every), row, row, row, col, P(every), row, row, col),
        check_vma=False,
    )
```

```python
import jax
import jax.numpy as jnp
from jax import lax
from jax.experimental import pallas as pl
from jax.experimental.pallas import tpu as pltpu
from jax.sharding import Mesh
from jax.sharding import PartitionSpec as P

H = 16
KV = 4
DH = 128
PIC = 256
NPIC = 2
EPS = 1e-05
TP = 2
BF = jnp.bfloat16
F32 = jnp.float32


def rotary_tables(positions, head_dim):
    half_dim = head_dim // 2
    inverse = 10000.0 ** (-(jnp.arange(half_dim, dtype=F32) * 2.0 / head_dim))
    angles = positions.astype(F32)[:, None] * inverse[None, :]
    return (jnp.cos(angles), jnp.sin(angles))


def rotate(values, cos_table, sin_table):
    half = values.shape[-1] // 2
    shape = (cos_table.shape[0],) + (1,) * (values.ndim - 2) + (half,)
    cos_part = cos_table.reshape(shape)
    sin_part = sin_table.reshape(shape)
    first = values[..., :half]
    second = values[..., half:]
    return jnp.concatenate(
        [first * cos_part - second * sin_part, second * cos_part + first * sin_part], axis=-1
    )


def picture_ids(positions, starts):
    inside = (positions[None, :] >= starts[:, None]) & (positions[None, :] < starts[:, None] + PIC)
    labels = jnp.arange(1, NPIC + 1, dtype=jnp.int32)
    return jnp.sum(jnp.where(inside, labels[:, None], 0), axis=0)


def visible(positions, starts):
    ids = picture_ids(positions, starts)
    causal = positions[None, :] <= positions[:, None]
    same_piece = (ids[:, None] == ids[None, :]) & (ids[:, None] > 0)
    return causal | same_piece


def rms_scale(rows):
    return lax.rsqrt(jnp.mean(rows * rows, axis=-1, keepdims=True) + EPS)


def dot(left, right, contract):
    return lax.dot_general(
        left, right, ((contract[:1], contract[1:]), ((), ())), preferred_element_type=F32
    )


def nn(left, right):
    return dot(left, right, (1, 0))


def nt(left, right):
    return dot(left, right, (1, 1))


def tn(left, right):
    return dot(left, right, (0, 0))


MESH_ID = pl.DeviceIdType.MESH
SUB = 32


def plane_place():
    tp_at = lax.axis_index("tp")
    seq_at = lax.axis_index("seq")
    seq = lax.axis_size("seq")
    half = seq // 2
    far = lax.rem(seq_at + half, seq)
    mate = seq_at + 1 - 2 * lax.rem(seq_at, 2)
    far_mate = far + 1 - 2 * lax.rem(far, 2)
    return tp_at, seq_at, far, mate, far_mate


def at_device(tp_at, seq_at):
    return (lax.axis_index("rep"), tp_at, seq_at)


def enter(devices):
    barrier = pltpu.get_barrier_semaphore()
    for device in devices:
        pl.semaphore_signal(barrier, inc=1, device_id=device, device_id_type=MESH_ID)
    pl.semaphore_wait(barrier, len(devices))


def remote(src, dst, send, recv, device):
    return pltpu.make_async_remote_copy(
        src_ref=src,
        dst_ref=dst,
        send_sem=send,
        recv_sem=recv,
        device_id=device,
        device_id_type=MESH_ID,
    )


def gather_kernel(own_ref, all_ref, sends, recvs, local):
    tp_at, seq_at, far, mate, _ = plane_place()
    seq = lax.axis_size("seq")
    other = 1 - tp_at
    to_x = at_device(tp_at, far)
    to_y = at_device(other, seq_at)
    to_c = at_device(tp_at, mate)
    rows = own_ref.shape[0]
    part = rows // 2
    enter((to_x, to_y, to_c))

    def piece(t, s, h):
        return all_ref.at[t * seq + s, pl.ds(h * part, part)]

    def pass_on(i, t, s, h, device):
        copy = remote(piece(t, s, h), piece(t, s, h), sends.at[i], recvs.at[i], device)
        copy.start()
        return copy

    def own(i, h, device):
        copy = remote(
            own_ref.at[pl.ds(h * part, part)],
            piece(tp_at, seq_at, h),
            sends.at[i],
            recvs.at[i],
            device,
        )
        copy.start()
        return copy

    x0 = own(0, 0, to_x)
    y0 = own(1, 0, to_y)
    c0 = own(2, 0, to_c)
    x1 = own(3, 1, to_x)
    y1 = own(4, 1, to_y)
    c1 = own(5, 1, to_c)
    mine = pltpu.make_async_copy(own_ref, all_ref.at[tp_at * seq + seq_at], local)
    mine.start()
    x0.wait_recv()
    diag0 = pass_on(6, tp_at, far, 0, to_y)
    rx0 = pass_on(8, tp_at, far, 0, to_c)
    y0.wait_recv()
    ry0 = pass_on(9, other, seq_at, 0, to_c)
    y1.wait_recv()
    diag1 = pass_on(7, other, seq_at, 1, to_x)
    ry1 = pass_on(10, other, seq_at, 1, to_c)
    x1.wait_recv()
    rx1 = pass_on(11, tp_at, far, 1, to_c)
    diag0.wait_recv()
    rd0 = pass_on(12, other, far, 0, to_c)
    diag1.wait_recv()
    rd1 = pass_on(13, other, far, 1, to_c)
    for copy in (c0, c1, rx0, ry0, ry1, rx1, rd0, rd1):
        copy.wait_recv()
    for copy in (x0, y0, c0, x1, y1, c1, diag0, diag1, rx0, ry0, ry1, rx1, rd0, rd1):
        copy.wait_send()
    mine.wait()


def gather_plane(block, ident):
    rows, width = block.shape
    plane = lax.axis_size("tp") * lax.axis_size("seq")
    size = rows * width * 2
    gathered = pl.pallas_call(
        gather_kernel,
        out_shape=jax.ShapeDtypeStruct((plane, rows, width), block.dtype),
        in_specs=[pl.BlockSpec(memory_space=pltpu.VMEM)],
        out_specs=pl.BlockSpec(memory_space=pltpu.HBM),
        scratch_shapes=[
            pltpu.SemaphoreType.DMA((14,)),
            pltpu.SemaphoreType.DMA((14,)),
            pltpu.SemaphoreType.DMA,
        ],
        cost_estimate=pl.CostEstimate(
            flops=0, transcendentals=0, bytes_accessed=plane * size * 12
        ),
        compiler_params=pltpu.CompilerParams(collective_id=ident, has_side_effects=True),
        name="gather_plane",
    )(block)
    return gathered.reshape(plane * rows, width)


def add_rows(target, sources, start, count, kind):
    step = min(SUB, count)

    def body(i, carry):
        at = pl.ds(start + i * step, step)
        total = sources[0][at, :].astype(F32)
        for source in sources[1:]:
            total = total + source[at, :].astype(F32)
        target[at, :] = total.astype(kind)
        return carry

    lax.fori_loop(0, count // step, body, 0)


def scatter_kernel(part_ref, sum_ref, held, chip_in, far_in, near_in, loads, sends, recvs):
    tp_at, seq_at, far, mate, far_mate = plane_place()
    seq = lax.axis_size("seq")
    other = 1 - tp_at
    to_x = at_device(tp_at, far)
    to_y = at_device(other, seq_at)
    to_c = at_device(tp_at, mate)
    rows = sum_ref.shape[0]
    part = rows // 2
    top, low = pl.ds(0, part), pl.ds(part, part)
    enter((to_x, to_y, to_c))
    chips = ((other, far, far_mate), (tp_at, far, far_mate), (other, seq_at, mate), (tp_at, seq_at, mate))
    gives, takes = [], []
    for k, (t, s, m) in enumerate(chips):
        give = remote(
            part_ref.at[t * seq + m], chip_in.at[k], sends.at[k], recvs.at[k], to_c
        )
        give.start()
        take = pltpu.make_async_copy(part_ref.at[t * seq + s], held.at[k], loads.at[k])
        take.start()
        gives.append(give)
        takes.append(take)

    def chip_sum(k):
        takes[k].wait()
        gives[k].wait_recv()
        add_rows(held.at[k], (held.at[k], chip_in.at[k]), 0, rows, held.dtype)

    def send(i, src, dst, device):
        copy = remote(src, dst, sends.at[i], recvs.at[i], device)
        copy.start()
        return copy

    chip_sum(0)
    d0 = send(4, held.at[0, top], far_in.at[0, top], to_x)
    d1 = send(5, held.at[0, low], far_in.at[1, low], to_y)
    chip_sum(1)
    x0 = send(6, held.at[1, top], near_in.at[0, top], to_x)
    chip_sum(2)
    y1 = send(7, held.at[2, low], near_in.at[1, low], to_y)
    chip_sum(3)
    d0.wait_recv()
    add_rows(held.at[2], (held.at[2], far_in.at[0]), 0, part, held.dtype)
    y0 = send(8, held.at[2, top], near_in.at[1, top], to_y)
    d1.wait_recv()
    add_rows(held.at[1], (held.at[1], far_in.at[1]), part, part, held.dtype)
    x1 = send(9, held.at[1, low], near_in.at[0, low], to_x)
    x0.wait_recv()
    y0.wait_recv()
    add_rows(sum_ref, (held.at[3], near_in.at[0], near_in.at[1]), 0, part, sum_ref.dtype)
    y1.wait_recv()
    x1.wait_recv()
    add_rows(sum_ref, (held.at[3], near_in.at[0], near_in.at[1]), part, part, sum_ref.dtype)
    for copy in gives + [d0, d1, x0, y1, y0, x1]:
        copy.wait_send()


def scatter_plane(partial, ident):
    plane = lax.axis_size("tp") * lax.axis_size("seq")
    rows, width = partial.shape[0] // plane, partial.shape[1]
    kind = partial.dtype
    size = rows * width * 2
    return pl.pallas_call(
        scatter_kernel,
        out_shape=jax.ShapeDtypeStruct((rows, width), F32),
        in_specs=[pl.BlockSpec(memory_space=pltpu.HBM)],
        out_specs=pl.BlockSpec(memory_space=pltpu.VMEM),
        scratch_shapes=[
            pltpu.VMEM((4, rows, width), kind),
            pltpu.VMEM((4, rows, width), kind),
            pltpu.VMEM((2, rows, width), kind),
            pltpu.VMEM((2, rows, width), kind),
            pltpu.SemaphoreType.DMA((4,)),
            pltpu.SemaphoreType.DMA((10,)),
            pltpu.SemaphoreType.DMA((10,)),
        ],
        cost_estimate=pl.CostEstimate(
            flops=0, transcendentals=0, bytes_accessed=plane * size * 14
        ),
        compiler_params=pltpu.CompilerParams(
            collective_id=ident, has_side_effects=True, vmem_limit_bytes=32 << 20
        ),
        name="scatter_plane",
    )(partial.reshape(plane, rows, width))


def exchange_kernel(in_ref, out_ref, stage, local, sends, recvs):
    tp_at, seq_at, _, _, _ = plane_place()
    seq = lax.axis_size("seq")
    plane = lax.axis_size("tp") * seq
    me = tp_at * seq + seq_at
    peers = [lax.rem(me + k, plane) for k in range(1, plane)]
    devices = [at_device(peer // seq, lax.rem(peer, seq)) for peer in peers]
    enter(devices)
    copies = []
    for k, (peer, device) in enumerate(zip(peers, devices)):
        copy = remote(in_ref.at[peer], out_ref.at[me], sends.at[k], recvs.at[k], device)
        copy.start()
        copies.append(copy)
    take = pltpu.make_async_copy(in_ref.at[me], stage, local.at[0])
    take.start()
    take.wait()
    put = pltpu.make_async_copy(stage, out_ref.at[me], local.at[1])
    put.start()
    for copy in copies:
        copy.wait()
    put.wait()


def exchange_plane(blocks, ident):
    plane, rows, width = blocks.shape
    size = plane * rows * width * 2
    return pl.pallas_call(
        exchange_kernel,
        out_shape=jax.ShapeDtypeStruct(blocks.shape, blocks.dtype),
        in_specs=[pl.BlockSpec(memory_space=pltpu.HBM)],
        out_specs=pl.BlockSpec(memory_space=pltpu.HBM),
        scratch_shapes=[
            pltpu.VMEM((rows, width), blocks.dtype),
            pltpu.SemaphoreType.DMA((2,)),
            pltpu.SemaphoreType.DMA((plane - 1,)),
            pltpu.SemaphoreType.DMA((plane - 1,)),
        ],
        cost_estimate=pl.CostEstimate(flops=0, transcendentals=0, bytes_accessed=size * 20),
        compiler_params=pltpu.CompilerParams(collective_id=ident, has_side_effects=True),
        name="exchange_plane",
    )(blocks)


def columns(matrix, parts):
    rows, cols = matrix.shape
    return jnp.transpose(matrix.reshape(rows, parts, cols // parts), (1, 0, 2))


def uncolumns(blocks):
    parts, rows, cols = blocks.shape
    return jnp.transpose(blocks, (1, 0, 2)).reshape(rows, parts * cols)


def after(value, *earlier):
    return lax.optimization_barrier((value,) + earlier)[0]


def per_device(
    layer_input,
    pic_starts,
    skip_mask,
    gain_attn,
    w_query,
    w_key,
    w_value,
    w_out,
    gain_ffn,
    w_gate,
    w_up,
    w_down,
    cotangent,
):
    _, local_len, width = layer_input.shape
    seq = lax.axis_size("seq")
    plane = lax.axis_size("tp") * seq
    total_len = local_len * seq
    heads = H // plane
    share = plane // KV
    ff_part = w_gate.shape[1] // plane
    q_part = heads * DH
    scale = DH ** (-0.5)

    gain1 = gain_attn[:, None]
    gain2 = gain_ffn[:, None]
    wq32, wk32, wv32 = w_query.astype(F32), w_key.astype(F32), w_value.astype(F32)
    wg32, wu32 = w_gate.astype(F32), w_up.astype(F32)
    attn_pack = jnp.concatenate(
        [
            columns((wq32 * gain1).astype(BF), plane),
            jnp.repeat(columns((wk32 * gain1).astype(BF), KV), share, axis=0),
            jnp.repeat(columns((wv32 * gain1).astype(BF), KV), share, axis=0),
            columns(w_out.T, plane),
        ],
        axis=2,
    )
    attn_rows = exchange_plane(attn_pack, 0)
    attn_rows = attn_rows.reshape(-1, attn_rows.shape[2])
    attn_weight = lax.all_gather(attn_rows, "rep", axis=0, tiled=True)
    qkv_weight = attn_weight[:, : q_part + 2 * DH]
    out_weight = attn_weight[:, q_part + 2 * DH :]

    tokens = layer_input.reshape(local_len, width).astype(F32)
    keep = (1 - skip_mask).astype(F32).reshape(local_len, 1)
    upstream = cotangent.reshape(local_len, width).astype(F32)
    scale1 = rms_scale(tokens)
    norm1 = tokens * scale1
    norm1_all = gather_plane(after(norm1.astype(BF), attn_rows), 1)

    ffn_pack = jnp.concatenate(
        [
            columns((wg32 * gain2).astype(BF), plane),
            columns((wu32 * gain2).astype(BF), plane),
            columns(w_down.T, plane),
        ],
        axis=2,
    )
    ffn_rows = exchange_plane(after(ffn_pack, norm1_all), 2)
    ffn_rows = ffn_rows.reshape(-1, ffn_rows.shape[2])
    down_weight = lax.all_gather(ffn_rows[:, 2 * ff_part :], "rep", axis=0, tiled=True)
    gu_weight = lax.all_gather(ffn_rows[:, : 2 * ff_part], "rep", axis=0, tiled=True)
    ffn_grad = gather_plane(after((keep * upstream).astype(BF), ffn_rows), 3)

    other_starts = lax.ppermute(pic_starts, "tp", [(0, 1), (1, 0)])
    starts = jnp.where(
        lax.axis_index("tp") == 0,
        jnp.concatenate([pic_starts, other_starts], axis=0),
        jnp.concatenate([other_starts, pic_starts], axis=0),
    )
    positions = jnp.arange(total_len, dtype=jnp.int32)
    cos_table, sin_table = rotary_tables(positions, DH)
    allowed = jax.vmap(visible, (None, 0))(positions, starts)[:, None]
    turn = jax.vmap(rotate, (0, None, None))

    projected = nn(norm1_all, qkv_weight).reshape(TP, total_len, q_part + 2 * DH)
    queries = turn(
        projected[..., :q_part].reshape(TP, total_len, heads, DH), cos_table, sin_table
    ).astype(BF)
    keys = turn(projected[..., q_part : q_part + DH], cos_table, sin_table).astype(BF)
    values = projected[..., q_part + DH :].astype(BF)
    scores = jnp.einsum("tqhd,tkd->thqk", queries, keys, preferred_element_type=F32) * scale
    scores = jnp.where(allowed, scores, -jnp.inf)
    peak = jnp.max(scores, axis=-1, keepdims=True)
    log_total = peak + jnp.log(jnp.sum(jnp.exp(scores - peak), axis=-1, keepdims=True))
    probs = jnp.exp(scores - log_total)
    probs_low = probs.astype(BF)
    mixed = jnp.einsum("thqk,tkd->tqhd", probs_low, values, preferred_element_type=F32)
    mixed = mixed.astype(BF).reshape(TP * total_len, q_part)
    branch = scatter_plane(nt(mixed, out_weight).astype(BF), 4)
    hidden = tokens + keep * branch

    scale2 = rms_scale(hidden)
    norm2 = hidden * scale2
    norm2_all = gather_plane(norm2.astype(BF), 5)
    inner_grad = nn(ffn_grad, down_weight)
    gate_up = nn(norm2_all, gu_weight)
    gate, upward = gate_up[:, :ff_part], gate_up[:, ff_part:]
    sigmoid_gate = jax.nn.sigmoid(gate)
    silu_gate = gate * sigmoid_gate
    inner = (silu_gate * upward).astype(BF)
    slope = sigmoid_gate * (1.0 + gate * (1.0 - sigmoid_gate))
    gate_up_grad = jnp.concatenate(
        [(inner_grad * upward * slope).astype(BF), (inner_grad * silu_gate).astype(BF)], axis=1
    )
    scaled2_partial = nt(gate_up_grad, gu_weight).astype(BF)
    down_partial = tn(ffn_grad, inner).astype(BF)
    gu_partial = tn(norm2_all, gate_up_grad).astype(BF)
    down_sums = lax.psum_scatter(down_partial, "rep", scatter_dimension=0, tiled=True)
    gu_sums = lax.psum_scatter(gu_partial, "rep", scatter_dimension=0, tiled=True)
    scaled2 = scatter_plane(after(scaled2_partial, down_partial, gu_partial), 6)
    hidden_grad = upstream + scale2 * (
        scaled2 - norm2 * jnp.mean(scaled2 * norm2, axis=-1, keepdims=True)
    )

    branch_grad = gather_plane((keep * hidden_grad).astype(BF), 7)
    mixed_grad = nn(branch_grad, out_weight).astype(BF).reshape(TP, total_len, heads, DH)
    values_grad = jnp.einsum(
        "thqk,tqhd->tkd", probs_low, mixed_grad, preferred_element_type=F32
    ).astype(BF)
    prob_grad = jnp.einsum("tqhd,tkd->thqk", mixed_grad, values, preferred_element_type=F32)
    score_grad = (
        probs * (prob_grad - jnp.sum(probs * prob_grad, axis=-1, keepdims=True))
    ).astype(BF)
    queries_grad = (
        jnp.einsum("thqk,tkd->tqhd", score_grad, keys, preferred_element_type=F32) * scale
    )
    keys_grad = (
        jnp.einsum("thqk,tqhd->tkd", score_grad, queries, preferred_element_type=F32) * scale
    )
    qkv_grad = jnp.concatenate(
        [
            turn(queries_grad, cos_table, -sin_table).astype(BF).reshape(-1, q_part),
            turn(keys_grad, cos_table, -sin_table).astype(BF).reshape(-1, DH),
            values_grad.reshape(-1, DH),
        ],
        axis=1,
    )
    attn_partial = jnp.concatenate(
        [tn(norm1_all, qkv_grad).astype(BF), tn(branch_grad, mixed).astype(BF)], axis=1
    )
    attn_sums = lax.psum_scatter(attn_partial, "rep", scatter_dimension=0, tiled=True)
    scaled1 = scatter_plane(after(nt(qkv_grad, qkv_weight).astype(BF), attn_partial), 8)
    input_grad = hidden_grad + scale1 * (
        scaled1 - norm1 * jnp.mean(scaled1 * norm1, axis=-1, keepdims=True)
    )
    ffn_out = scatter_plane(after(nt(inner, down_weight).astype(BF), scaled1), 9)
    out_hidden = (hidden + keep * ffn_out).astype(BF)

    ffn_sums = jnp.concatenate([gu_sums, down_sums], axis=1)
    ffn_sums = after(ffn_sums.reshape(plane, -1, ffn_sums.shape[1]), ffn_out)
    ffn_own = exchange_plane(ffn_sums, 10).astype(F32)
    gate_own = uncolumns(ffn_own[:, :, :ff_part])
    up_own = uncolumns(ffn_own[:, :, ff_part : 2 * ff_part])
    down_own = uncolumns(ffn_own[:, :, 2 * ff_part :])
    gain_ffn_grad = jnp.sum(gate_own * wg32, axis=1) + jnp.sum(up_own * wu32, axis=1)

    attn_own = exchange_plane(attn_sums.reshape(plane, -1, attn_sums.shape[1]), 11).astype(F32)
    query_own = uncolumns(attn_own[:, :, :q_part])
    kv_own = attn_own[:, :, q_part : q_part + 2 * DH]
    kv_own = jnp.sum(kv_own.reshape(KV, share, -1, 2 * DH), axis=1)
    key_own = uncolumns(kv_own[:, :, :DH])
    value_own = uncolumns(kv_own[:, :, DH:])
    out_own = uncolumns(attn_own[:, :, q_part + 2 * DH :])
    gain_attn_grad = (
        jnp.sum(query_own * wq32, axis=1)
        + jnp.sum(key_own * wk32, axis=1)
        + jnp.sum(value_own * wv32, axis=1)
    )
    return (
        out_hidden[None],
        input_grad[None],
        gain_attn_grad,
        query_own * gain1,
        key_own * gain1,
        value_own * gain1,
        out_own.T,
        gain_ffn_grad,
        gate_own * gain2,
        up_own * gain2,
        down_own.T,
    )


def solution(mesh):
    devices = mesh.devices
    dp, seq = devices.shape
    inner = Mesh(devices.reshape(dp // TP, TP, seq), ("rep", "tp", "seq"))
    dps = ("rep", "tp")
    every = ("rep", "tp", "seq")
    token = P(dps, "seq", None)
    row = P(every, None)
    col = P(None, every)
    return jax.shard_map(
        per_device,
        mesh=inner,
        in_specs=(
            token,
            P(dps, None),
            P(dps, "seq"),
            P(every),
            row,
            row,
            row,
            col,
            P(every),
            row,
            row,
            col,
            token,
        ),
        out_specs=(token, token, P(every), row, row, row, col, P(every), row, row, col),
        check_vma=False,
    )
```

```python
import jax
import jax.numpy as jnp
from jax import lax
from jax.experimental import pallas as pl
from jax.experimental.pallas import tpu as pltpu
from jax.sharding import Mesh
from jax.sharding import PartitionSpec as P

H = 16
KV = 4
DH = 128
PIC = 256
NPIC = 2
EPS = 1e-05
TP = 2
BF = jnp.bfloat16
F32 = jnp.float32


def rotary_tables(positions, head_dim):
    half_dim = head_dim // 2
    inverse = 10000.0 ** (-(jnp.arange(half_dim, dtype=F32) * 2.0 / head_dim))
    angles = positions.astype(F32)[:, None] * inverse[None, :]
    return (jnp.cos(angles), jnp.sin(angles))


def rotate(values, cos_table, sin_table):
    half = values.shape[-1] // 2
    shape = (cos_table.shape[0],) + (1,) * (values.ndim - 2) + (half,)
    cos_part = cos_table.reshape(shape)
    sin_part = sin_table.reshape(shape)
    first = values[..., :half]
    second = values[..., half:]
    return jnp.concatenate(
        [first * cos_part - second * sin_part, second * cos_part + first * sin_part], axis=-1
    )


def picture_ids(positions, starts):
    inside = (positions[None, :] >= starts[:, None]) & (positions[None, :] < starts[:, None] + PIC)
    labels = jnp.arange(1, NPIC + 1, dtype=jnp.int32)
    return jnp.sum(jnp.where(inside, labels[:, None], 0), axis=0)


def visible(positions, starts):
    ids = picture_ids(positions, starts)
    causal = positions[None, :] <= positions[:, None]
    same_piece = (ids[:, None] == ids[None, :]) & (ids[:, None] > 0)
    return causal | same_piece


def rms_scale(rows):
    return lax.rsqrt(jnp.mean(rows * rows, axis=-1, keepdims=True) + EPS)


def dot(left, right, contract):
    return lax.dot_general(
        left, right, ((contract[:1], contract[1:]), ((), ())), preferred_element_type=F32
    )


def nn(left, right):
    return dot(left, right, (1, 0))


def nt(left, right):
    return dot(left, right, (1, 1))


def tn(left, right):
    return dot(left, right, (0, 0))


MESH_ID = pl.DeviceIdType.MESH
SUB = 32


def plane_place():
    tp_at = lax.axis_index("tp")
    seq_at = lax.axis_index("seq")
    seq = lax.axis_size("seq")
    half = seq // 2
    far = lax.rem(seq_at + half, seq)
    mate = seq_at + 1 - 2 * lax.rem(seq_at, 2)
    far_mate = far + 1 - 2 * lax.rem(far, 2)
    return tp_at, seq_at, far, mate, far_mate


def at_device(tp_at, seq_at):
    return (lax.axis_index("rep"), tp_at, seq_at)


def enter(devices):
    barrier = pltpu.get_barrier_semaphore()
    for device in devices:
        pl.semaphore_signal(barrier, inc=1, device_id=device, device_id_type=MESH_ID)
    pl.semaphore_wait(barrier, len(devices))


def remote(src, dst, send, recv, device):
    return pltpu.make_async_remote_copy(
        src_ref=src,
        dst_ref=dst,
        send_sem=send,
        recv_sem=recv,
        device_id=device,
        device_id_type=MESH_ID,
    )


def gather_kernel(own_ref, all_ref, sends, recvs, local):
    tp_at, seq_at, far, mate, _ = plane_place()
    seq = lax.axis_size("seq")
    other = 1 - tp_at
    to_x = at_device(tp_at, far)
    to_y = at_device(other, seq_at)
    to_c = at_device(tp_at, mate)
    rows = own_ref.shape[0]
    part = rows // 2
    enter((to_x, to_y, to_c))

    def piece(t, s, h):
        return all_ref.at[t * seq + s, pl.ds(h * part, part)]

    def pass_on(i, t, s, h, device):
        copy = remote(piece(t, s, h), piece(t, s, h), sends.at[i], recvs.at[i], device)
        copy.start()
        return copy

    def own(i, h, device):
        copy = remote(
            own_ref.at[pl.ds(h * part, part)],
            piece(tp_at, seq_at, h),
            sends.at[i],
            recvs.at[i],
            device,
        )
        copy.start()
        return copy

    x0 = own(0, 0, to_x)
    y0 = own(1, 0, to_y)
    c0 = own(2, 0, to_c)
    x1 = own(3, 1, to_x)
    y1 = own(4, 1, to_y)
    c1 = own(5, 1, to_c)
    mine = pltpu.make_async_copy(own_ref, all_ref.at[tp_at * seq + seq_at], local)
    mine.start()
    x0.wait_recv()
    diag0 = pass_on(6, tp_at, far, 0, to_y)
    rx0 = pass_on(8, tp_at, far, 0, to_c)
    y0.wait_recv()
    ry0 = pass_on(9, other, seq_at, 0, to_c)
    y1.wait_recv()
    diag1 = pass_on(7, other, seq_at, 1, to_x)
    ry1 = pass_on(10, other, seq_at, 1, to_c)
    x1.wait_recv()
    rx1 = pass_on(11, tp_at, far, 1, to_c)
    diag0.wait_recv()
    rd0 = pass_on(12, other, far, 0, to_c)
    diag1.wait_recv()
    rd1 = pass_on(13, other, far, 1, to_c)
    for copy in (c0, c1, rx0, ry0, ry1, rx1, rd0, rd1):
        copy.wait_recv()
    for copy in (x0, y0, c0, x1, y1, c1, diag0, diag1, rx0, ry0, ry1, rx1, rd0, rd1):
        copy.wait_send()
    mine.wait()


def gather_plane(block, ident):
    rows, width = block.shape
    plane = lax.axis_size("tp") * lax.axis_size("seq")
    size = rows * width * 2
    gathered = pl.pallas_call(
        gather_kernel,
        out_shape=jax.ShapeDtypeStruct((plane, rows, width), block.dtype),
        in_specs=[pl.BlockSpec(memory_space=pltpu.VMEM)],
        out_specs=pl.BlockSpec(memory_space=pltpu.HBM),
        scratch_shapes=[
            pltpu.SemaphoreType.DMA((14,)),
            pltpu.SemaphoreType.DMA((14,)),
            pltpu.SemaphoreType.DMA,
        ],
        cost_estimate=pl.CostEstimate(
            flops=0, transcendentals=0, bytes_accessed=plane * size * 12
        ),
        compiler_params=pltpu.CompilerParams(collective_id=ident, has_side_effects=True),
        name="gather_plane",
    )(block)
    return gathered.reshape(plane * rows, width)


def add_rows(target, sources, start, count, kind):
    step = min(SUB, count)

    def body(i, carry):
        at = pl.ds(start + i * step, step)
        total = sources[0][at, :].astype(F32)
        for source in sources[1:]:
            total = total + source[at, :].astype(F32)
        target[at, :] = total.astype(kind)
        return carry

    lax.fori_loop(0, count // step, body, 0)


def scatter_kernel(part_ref, sum_ref, held, chip_in, far_in, near_in, loads, sends, recvs):
    tp_at, seq_at, far, mate, far_mate = plane_place()
    seq = lax.axis_size("seq")
    other = 1 - tp_at
    to_x = at_device(tp_at, far)
    to_y = at_device(other, seq_at)
    to_c = at_device(tp_at, mate)
    rows = sum_ref.shape[0]
    part = rows // 2
    top, low = pl.ds(0, part), pl.ds(part, part)
    enter((to_x, to_y, to_c))
    chips = ((other, far, far_mate), (tp_at, far, far_mate), (other, seq_at, mate), (tp_at, seq_at, mate))
    gives, takes = [], []
    for k, (t, s, m) in enumerate(chips):
        give = remote(
            part_ref.at[t * seq + m], chip_in.at[k], sends.at[k], recvs.at[k], to_c
        )
        give.start()
        take = pltpu.make_async_copy(part_ref.at[t * seq + s], held.at[k], loads.at[k])
        take.start()
        gives.append(give)
        takes.append(take)

    def chip_sum(k):
        takes[k].wait()
        gives[k].wait_recv()
        add_rows(held.at[k], (held.at[k], chip_in.at[k]), 0, rows, held.dtype)

    def send(i, src, dst, device):
        copy = remote(src, dst, sends.at[i], recvs.at[i], device)
        copy.start()
        return copy

    chip_sum(0)
    d0 = send(4, held.at[0, top], far_in.at[0, top], to_x)
    d1 = send(5, held.at[0, low], far_in.at[1, low], to_y)
    chip_sum(1)
    x0 = send(6, held.at[1, top], near_in.at[0, top], to_x)
    chip_sum(2)
    y1 = send(7, held.at[2, low], near_in.at[1, low], to_y)
    chip_sum(3)
    d0.wait_recv()
    add_rows(held.at[2], (held.at[2], far_in.at[0]), 0, part, held.dtype)
    y0 = send(8, held.at[2, top], near_in.at[1, top], to_y)
    d1.wait_recv()
    add_rows(held.at[1], (held.at[1], far_in.at[1]), part, part, held.dtype)
    x1 = send(9, held.at[1, low], near_in.at[0, low], to_x)
    x0.wait_recv()
    y0.wait_recv()
    add_rows(sum_ref, (held.at[3], near_in.at[0], near_in.at[1]), 0, part, sum_ref.dtype)
    y1.wait_recv()
    x1.wait_recv()
    add_rows(sum_ref, (held.at[3], near_in.at[0], near_in.at[1]), part, part, sum_ref.dtype)
    for copy in gives + [d0, d1, x0, y1, y0, x1]:
        copy.wait_send()


def scatter_plane(partial, ident):
    plane = lax.axis_size("tp") * lax.axis_size("seq")
    rows, width = partial.shape[0] // plane, partial.shape[1]
    kind = partial.dtype
    size = rows * width * 2
    return pl.pallas_call(
        scatter_kernel,
        out_shape=jax.ShapeDtypeStruct((rows, width), F32),
        in_specs=[pl.BlockSpec(memory_space=pltpu.HBM)],
        out_specs=pl.BlockSpec(memory_space=pltpu.VMEM),
        scratch_shapes=[
            pltpu.VMEM((4, rows, width), kind),
            pltpu.VMEM((4, rows, width), kind),
            pltpu.VMEM((2, rows, width), kind),
            pltpu.VMEM((2, rows, width), kind),
            pltpu.SemaphoreType.DMA((4,)),
            pltpu.SemaphoreType.DMA((10,)),
            pltpu.SemaphoreType.DMA((10,)),
        ],
        cost_estimate=pl.CostEstimate(
            flops=0, transcendentals=0, bytes_accessed=plane * size * 14
        ),
        compiler_params=pltpu.CompilerParams(
            collective_id=ident, has_side_effects=True, vmem_limit_bytes=32 << 20
        ),
        name="scatter_plane",
    )(partial.reshape(plane, rows, width))


def exchange_kernel(in_ref, out_ref, stage, local, sends, recvs):
    tp_at, seq_at, _, _, _ = plane_place()
    seq = lax.axis_size("seq")
    plane = lax.axis_size("tp") * seq
    me = tp_at * seq + seq_at
    peers = [lax.rem(me + k, plane) for k in range(1, plane)]
    devices = [at_device(peer // seq, lax.rem(peer, seq)) for peer in peers]
    enter(devices)
    copies = []
    for k, (peer, device) in enumerate(zip(peers, devices)):
        copy = remote(in_ref.at[peer], out_ref.at[me], sends.at[k], recvs.at[k], device)
        copy.start()
        copies.append(copy)
    take = pltpu.make_async_copy(in_ref.at[me], stage, local.at[0])
    take.start()
    take.wait()
    put = pltpu.make_async_copy(stage, out_ref.at[me], local.at[1])
    put.start()
    for copy in copies:
        copy.wait()
    put.wait()


def exchange_plane(blocks, ident):
    plane, rows, width = blocks.shape
    size = plane * rows * width * 2
    return pl.pallas_call(
        exchange_kernel,
        out_shape=jax.ShapeDtypeStruct(blocks.shape, blocks.dtype),
        in_specs=[pl.BlockSpec(memory_space=pltpu.HBM)],
        out_specs=pl.BlockSpec(memory_space=pltpu.HBM),
        scratch_shapes=[
            pltpu.VMEM((rows, width), blocks.dtype),
            pltpu.SemaphoreType.DMA((2,)),
            pltpu.SemaphoreType.DMA((plane - 1,)),
            pltpu.SemaphoreType.DMA((plane - 1,)),
        ],
        cost_estimate=pl.CostEstimate(flops=0, transcendentals=0, bytes_accessed=size * 20),
        compiler_params=pltpu.CompilerParams(collective_id=ident, has_side_effects=True),
        name="exchange_plane",
    )(blocks)


def columns(matrix, parts):
    rows, cols = matrix.shape
    return jnp.transpose(matrix.reshape(rows, parts, cols // parts), (1, 0, 2))


def uncolumns(blocks):
    parts, rows, cols = blocks.shape
    return jnp.transpose(blocks, (1, 0, 2)).reshape(rows, parts * cols)


def after(value, *earlier):
    return lax.optimization_barrier((value,) + earlier)[0]


def per_device(
    layer_input,
    pic_starts,
    skip_mask,
    gain_attn,
    w_query,
    w_key,
    w_value,
    w_out,
    gain_ffn,
    w_gate,
    w_up,
    w_down,
    cotangent,
):
    _, local_len, width = layer_input.shape
    seq = lax.axis_size("seq")
    plane = lax.axis_size("tp") * seq
    total_len = local_len * seq
    heads = H // plane
    share = plane // KV
    ff_part = w_gate.shape[1] // plane
    q_part = heads * DH
    scale = DH ** (-0.5)

    gain1 = gain_attn[:, None]
    gain2 = gain_ffn[:, None]
    wq32, wk32, wv32 = w_query.astype(F32), w_key.astype(F32), w_value.astype(F32)
    wg32, wu32 = w_gate.astype(F32), w_up.astype(F32)
    attn_pack = jnp.concatenate(
        [
            columns((wq32 * gain1).astype(BF), plane),
            jnp.repeat(columns((wk32 * gain1).astype(BF), KV), share, axis=0),
            jnp.repeat(columns((wv32 * gain1).astype(BF), KV), share, axis=0),
            columns(w_out.T, plane),
        ],
        axis=2,
    )
    attn_rows = exchange_plane(attn_pack, 0)
    attn_rows = attn_rows.reshape(-1, attn_rows.shape[2])
    attn_weight = lax.all_gather(attn_rows, "rep", axis=0, tiled=True)
    qkv_weight = attn_weight[:, : q_part + 2 * DH]
    out_weight = attn_weight[:, q_part + 2 * DH :]

    tokens = layer_input.reshape(local_len, width).astype(F32)
    keep = (1 - skip_mask).astype(F32).reshape(local_len, 1)
    upstream = cotangent.reshape(local_len, width).astype(F32)
    scale1 = rms_scale(tokens)
    norm1 = tokens * scale1

    ffn_pack = jnp.concatenate(
        [
            columns((wg32 * gain2).astype(BF), plane),
            columns((wu32 * gain2).astype(BF), plane),
            columns(w_down.T, plane),
        ],
        axis=2,
    )
    ffn_rows = exchange_plane(after(ffn_pack, attn_rows), 2)
    ffn_rows = ffn_rows.reshape(-1, ffn_rows.shape[2])
    down_weight = lax.all_gather(ffn_rows[:, 2 * ff_part :], "rep", axis=0, tiled=True)
    gu_weight = lax.all_gather(ffn_rows[:, : 2 * ff_part], "rep", axis=0, tiled=True)
    norm1_all = gather_plane(after(norm1.astype(BF), ffn_rows), 1)
    ffn_grad = gather_plane(after((keep * upstream).astype(BF), norm1_all), 3)

    other_starts = lax.ppermute(pic_starts, "tp", [(0, 1), (1, 0)])
    starts = jnp.where(
        lax.axis_index("tp") == 0,
        jnp.concatenate([pic_starts, other_starts], axis=0),
        jnp.concatenate([other_starts, pic_starts], axis=0),
    )
    positions = jnp.arange(total_len, dtype=jnp.int32)
    cos_table, sin_table = rotary_tables(positions, DH)
    allowed = jax.vmap(visible, (None, 0))(positions, starts)[:, None]
    turn = jax.vmap(rotate, (0, None, None))

    projected = nn(norm1_all, qkv_weight).reshape(TP, total_len, q_part + 2 * DH)
    queries = turn(
        projected[..., :q_part].reshape(TP, total_len, heads, DH), cos_table, sin_table
    ).astype(BF)
    keys = turn(projected[..., q_part : q_part + DH], cos_table, sin_table).astype(BF)
    values = projected[..., q_part + DH :].astype(BF)
    scores = jnp.einsum("tqhd,tkd->thqk", queries, keys, preferred_element_type=F32) * scale
    scores = jnp.where(allowed, scores, -jnp.inf)
    peak = jnp.max(scores, axis=-1, keepdims=True)
    log_total = peak + jnp.log(jnp.sum(jnp.exp(scores - peak), axis=-1, keepdims=True))
    probs = jnp.exp(scores - log_total)
    probs_low = probs.astype(BF)
    mixed = jnp.einsum("thqk,tkd->tqhd", probs_low, values, preferred_element_type=F32)
    mixed = mixed.astype(BF).reshape(TP * total_len, q_part)
    branch = scatter_plane(nt(mixed, out_weight).astype(BF), 4)
    hidden = tokens + keep * branch

    scale2 = rms_scale(hidden)
    norm2 = hidden * scale2
    norm2_all = gather_plane(norm2.astype(BF), 5)
    inner_grad = nn(ffn_grad, down_weight)
    gate_up = nn(norm2_all, gu_weight)
    gate, upward = gate_up[:, :ff_part], gate_up[:, ff_part:]
    sigmoid_gate = jax.nn.sigmoid(gate)
    silu_gate = gate * sigmoid_gate
    inner = (silu_gate * upward).astype(BF)
    slope = sigmoid_gate * (1.0 + gate * (1.0 - sigmoid_gate))
    gate_up_grad = jnp.concatenate(
        [(inner_grad * upward * slope).astype(BF), (inner_grad * silu_gate).astype(BF)], axis=1
    )
    scaled2_partial = nt(gate_up_grad, gu_weight).astype(BF)
    down_partial = tn(ffn_grad, inner).astype(BF)
    gu_partial = tn(norm2_all, gate_up_grad).astype(BF)
    down_sums = lax.psum_scatter(down_partial, "rep", scatter_dimension=0, tiled=True)
    gu_sums = lax.psum_scatter(gu_partial, "rep", scatter_dimension=0, tiled=True)
    scaled2 = scatter_plane(after(scaled2_partial, down_partial, gu_partial), 6)
    hidden_grad = upstream + scale2 * (
        scaled2 - norm2 * jnp.mean(scaled2 * norm2, axis=-1, keepdims=True)
    )

    branch_grad = gather_plane((keep * hidden_grad).astype(BF), 7)
    mixed_grad = nn(branch_grad, out_weight).astype(BF).reshape(TP, total_len, heads, DH)
    values_grad = jnp.einsum(
        "thqk,tqhd->tkd", probs_low, mixed_grad, preferred_element_type=F32
    ).astype(BF)
    prob_grad = jnp.einsum("tqhd,tkd->thqk", mixed_grad, values, preferred_element_type=F32)
    score_grad = (
        probs * (prob_grad - jnp.sum(probs * prob_grad, axis=-1, keepdims=True))
    ).astype(BF)
    queries_grad = (
        jnp.einsum("thqk,tkd->tqhd", score_grad, keys, preferred_element_type=F32) * scale
    )
    keys_grad = (
        jnp.einsum("thqk,tqhd->tkd", score_grad, queries, preferred_element_type=F32) * scale
    )
    qkv_grad = jnp.concatenate(
        [
            turn(queries_grad, cos_table, -sin_table).astype(BF).reshape(-1, q_part),
            turn(keys_grad, cos_table, -sin_table).astype(BF).reshape(-1, DH),
            values_grad.reshape(-1, DH),
        ],
        axis=1,
    )
    attn_partial = jnp.concatenate(
        [tn(norm1_all, qkv_grad).astype(BF), tn(branch_grad, mixed).astype(BF)], axis=1
    )
    attn_partial = after(attn_partial, gu_sums, down_sums)
    attn_sums = lax.psum_scatter(attn_partial, "rep", scatter_dimension=0, tiled=True)
    scaled1 = scatter_plane(after(nt(qkv_grad, qkv_weight).astype(BF), attn_partial), 8)
    input_grad = hidden_grad + scale1 * (
        scaled1 - norm1 * jnp.mean(scaled1 * norm1, axis=-1, keepdims=True)
    )
    ffn_out = scatter_plane(after(nt(inner, down_weight).astype(BF), scaled1), 9)
    out_hidden = (hidden + keep * ffn_out).astype(BF)

    ffn_sums = jnp.concatenate([gu_sums, down_sums], axis=1)
    ffn_sums = after(ffn_sums.reshape(plane, -1, ffn_sums.shape[1]), ffn_out)
    ffn_own = exchange_plane(ffn_sums, 10).astype(F32)
    gate_own = uncolumns(ffn_own[:, :, :ff_part])
    up_own = uncolumns(ffn_own[:, :, ff_part : 2 * ff_part])
    down_own = uncolumns(ffn_own[:, :, 2 * ff_part :])
    gain_ffn_grad = jnp.sum(gate_own * wg32, axis=1) + jnp.sum(up_own * wu32, axis=1)

    attn_own = exchange_plane(attn_sums.reshape(plane, -1, attn_sums.shape[1]), 11).astype(F32)
    query_own = uncolumns(attn_own[:, :, :q_part])
    kv_own = attn_own[:, :, q_part : q_part + 2 * DH]
    kv_own = jnp.sum(kv_own.reshape(KV, share, -1, 2 * DH), axis=1)
    key_own = uncolumns(kv_own[:, :, :DH])
    value_own = uncolumns(kv_own[:, :, DH:])
    out_own = uncolumns(attn_own[:, :, q_part + 2 * DH :])
    gain_attn_grad = (
        jnp.sum(query_own * wq32, axis=1)
        + jnp.sum(key_own * wk32, axis=1)
        + jnp.sum(value_own * wv32, axis=1)
    )
    return (
        out_hidden[None],
        input_grad[None],
        gain_attn_grad,
        query_own * gain1,
        key_own * gain1,
        value_own * gain1,
        out_own.T,
        gain_ffn_grad,
        gate_own * gain2,
        up_own * gain2,
        down_own.T,
    )


def solution(mesh):
    devices = mesh.devices
    dp, seq = devices.shape
    inner = Mesh(devices.reshape(dp // TP, TP, seq), ("rep", "tp", "seq"))
    dps = ("rep", "tp")
    every = ("rep", "tp", "seq")
    token = P(dps, "seq", None)
    row = P(every, None)
    col = P(None, every)
    return jax.shard_map(
        per_device,
        mesh=inner,
        in_specs=(
            token,
            P(dps, None),
            P(dps, "seq"),
            P(every),
            row,
            row,
            row,
            col,
            P(every),
            row,
            row,
            col,
            token,
        ),
        out_specs=(token, token, P(every), row, row, row, col, P(every), row, row, col),
        check_vma=False,
    )
```

```python
import jax
import jax.numpy as jnp
from jax import lax
from jax.experimental import pallas as pl
from jax.experimental.pallas import tpu as pltpu
from jax.sharding import Mesh
from jax.sharding import PartitionSpec as P

H = 16
KV = 4
DH = 128
PIC = 256
NPIC = 2
EPS = 1e-05
TP = 2
BF = jnp.bfloat16
F32 = jnp.float32


def rotary_tables(positions, head_dim):
    half_dim = head_dim // 2
    inverse = 10000.0 ** (-(jnp.arange(half_dim, dtype=F32) * 2.0 / head_dim))
    angles = positions.astype(F32)[:, None] * inverse[None, :]
    return (jnp.cos(angles), jnp.sin(angles))


def rotate(values, cos_table, sin_table):
    half = values.shape[-1] // 2
    shape = (cos_table.shape[0],) + (1,) * (values.ndim - 2) + (half,)
    cos_part = cos_table.reshape(shape)
    sin_part = sin_table.reshape(shape)
    first = values[..., :half]
    second = values[..., half:]
    return jnp.concatenate(
        [first * cos_part - second * sin_part, second * cos_part + first * sin_part], axis=-1
    )


def picture_ids(positions, starts):
    inside = (positions[None, :] >= starts[:, None]) & (positions[None, :] < starts[:, None] + PIC)
    labels = jnp.arange(1, NPIC + 1, dtype=jnp.int32)
    return jnp.sum(jnp.where(inside, labels[:, None], 0), axis=0)


def visible(positions, starts):
    ids = picture_ids(positions, starts)
    causal = positions[None, :] <= positions[:, None]
    same_piece = (ids[:, None] == ids[None, :]) & (ids[:, None] > 0)
    return causal | same_piece


def rms_scale(rows):
    return lax.rsqrt(jnp.mean(rows * rows, axis=-1, keepdims=True) + EPS)


def dot(left, right, contract):
    return lax.dot_general(
        left, right, ((contract[:1], contract[1:]), ((), ())), preferred_element_type=F32
    )


def nn(left, right):
    return dot(left, right, (1, 0))


def nt(left, right):
    return dot(left, right, (1, 1))


def tn(left, right):
    return dot(left, right, (0, 0))


MESH_ID = pl.DeviceIdType.MESH
SUB = 32


def plane_place():
    tp_at = lax.axis_index("tp")
    seq_at = lax.axis_index("seq")
    seq = lax.axis_size("seq")
    half = seq // 2
    far = lax.rem(seq_at + half, seq)
    mate = seq_at + 1 - 2 * lax.rem(seq_at, 2)
    far_mate = far + 1 - 2 * lax.rem(far, 2)
    return tp_at, seq_at, far, mate, far_mate


def at_device(tp_at, seq_at):
    return (lax.axis_index("rep"), tp_at, seq_at)


def enter(devices):
    barrier = pltpu.get_barrier_semaphore()
    for device in devices:
        pl.semaphore_signal(barrier, inc=1, device_id=device, device_id_type=MESH_ID)
    pl.semaphore_wait(barrier, len(devices))


def remote(src, dst, send, recv, device):
    return pltpu.make_async_remote_copy(
        src_ref=src,
        dst_ref=dst,
        send_sem=send,
        recv_sem=recv,
        device_id=device,
        device_id_type=MESH_ID,
    )


def gather_kernel(own_ref, all_ref, sends, recvs, local):
    tp_at, seq_at, far, mate, _ = plane_place()
    seq = lax.axis_size("seq")
    other = 1 - tp_at
    to_x = at_device(tp_at, far)
    to_y = at_device(other, seq_at)
    to_c = at_device(tp_at, mate)
    rows = own_ref.shape[0]
    part = rows // 2
    enter((to_x, to_y, to_c))

    def piece(t, s, h):
        return all_ref.at[t * seq + s, pl.ds(h * part, part)]

    def pass_on(i, t, s, h, device):
        copy = remote(piece(t, s, h), piece(t, s, h), sends.at[i], recvs.at[i], device)
        copy.start()
        return copy

    def own(i, h, device):
        copy = remote(
            own_ref.at[pl.ds(h * part, part)],
            piece(tp_at, seq_at, h),
            sends.at[i],
            recvs.at[i],
            device,
        )
        copy.start()
        return copy

    x0 = own(0, 0, to_x)
    y0 = own(1, 0, to_y)
    c0 = own(2, 0, to_c)
    x1 = own(3, 1, to_x)
    y1 = own(4, 1, to_y)
    c1 = own(5, 1, to_c)
    mine = pltpu.make_async_copy(own_ref, all_ref.at[tp_at * seq + seq_at], local)
    mine.start()
    x0.wait_recv()
    diag0 = pass_on(6, tp_at, far, 0, to_y)
    rx0 = pass_on(8, tp_at, far, 0, to_c)
    y0.wait_recv()
    ry0 = pass_on(9, other, seq_at, 0, to_c)
    y1.wait_recv()
    diag1 = pass_on(7, other, seq_at, 1, to_x)
    ry1 = pass_on(10, other, seq_at, 1, to_c)
    x1.wait_recv()
    rx1 = pass_on(11, tp_at, far, 1, to_c)
    diag0.wait_recv()
    rd0 = pass_on(12, other, far, 0, to_c)
    diag1.wait_recv()
    rd1 = pass_on(13, other, far, 1, to_c)
    for copy in (c0, c1, rx0, ry0, ry1, rx1, rd0, rd1):
        copy.wait_recv()
    for copy in (x0, y0, c0, x1, y1, c1, diag0, diag1, rx0, ry0, ry1, rx1, rd0, rd1):
        copy.wait_send()
    mine.wait()


def gather_plane(block, ident):
    rows, width = block.shape
    plane = lax.axis_size("tp") * lax.axis_size("seq")
    size = rows * width * 2
    gathered = pl.pallas_call(
        gather_kernel,
        out_shape=jax.ShapeDtypeStruct((plane, rows, width), block.dtype),
        in_specs=[pl.BlockSpec(memory_space=pltpu.VMEM)],
        out_specs=pl.BlockSpec(memory_space=pltpu.HBM),
        scratch_shapes=[
            pltpu.SemaphoreType.DMA((14,)),
            pltpu.SemaphoreType.DMA((14,)),
            pltpu.SemaphoreType.DMA,
        ],
        cost_estimate=pl.CostEstimate(
            flops=0, transcendentals=0, bytes_accessed=plane * size * 12
        ),
        compiler_params=pltpu.CompilerParams(collective_id=ident, has_side_effects=True),
        name="gather_plane",
    )(block)
    return gathered.reshape(plane * rows, width)


def add_rows(target, sources, start, count, kind):
    step = min(SUB, count)

    def body(i, carry):
        at = pl.ds(start + i * step, step)
        total = sources[0][at, :].astype(F32)
        for source in sources[1:]:
            total = total + source[at, :].astype(F32)
        target[at, :] = total.astype(kind)
        return carry

    lax.fori_loop(0, count // step, body, 0)


def scatter_kernel(part_ref, sum_ref, held, chip_in, far_in, near_in, loads, sends, recvs):
    tp_at, seq_at, far, mate, far_mate = plane_place()
    seq = lax.axis_size("seq")
    other = 1 - tp_at
    to_x = at_device(tp_at, far)
    to_y = at_device(other, seq_at)
    to_c = at_device(tp_at, mate)
    rows = sum_ref.shape[0]
    part = rows // 2
    top, low = pl.ds(0, part), pl.ds(part, part)
    enter((to_x, to_y, to_c))
    chips = ((other, far, far_mate), (tp_at, far, far_mate), (other, seq_at, mate), (tp_at, seq_at, mate))
    gives, takes = [], []
    for k, (t, s, m) in enumerate(chips):
        give = remote(
            part_ref.at[t * seq + m], chip_in.at[k], sends.at[k], recvs.at[k], to_c
        )
        give.start()
        take = pltpu.make_async_copy(part_ref.at[t * seq + s], held.at[k], loads.at[k])
        take.start()
        gives.append(give)
        takes.append(take)

    def chip_sum(k):
        takes[k].wait()
        gives[k].wait_recv()
        add_rows(held.at[k], (held.at[k], chip_in.at[k]), 0, rows, held.dtype)

    def send(i, src, dst, device):
        copy = remote(src, dst, sends.at[i], recvs.at[i], device)
        copy.start()
        return copy

    chip_sum(0)
    d0 = send(4, held.at[0, top], far_in.at[0, top], to_x)
    d1 = send(5, held.at[0, low], far_in.at[1, low], to_y)
    chip_sum(1)
    x0 = send(6, held.at[1, top], near_in.at[0, top], to_x)
    chip_sum(2)
    y1 = send(7, held.at[2, low], near_in.at[1, low], to_y)
    chip_sum(3)
    d0.wait_recv()
    add_rows(held.at[2], (held.at[2], far_in.at[0]), 0, part, held.dtype)
    y0 = send(8, held.at[2, top], near_in.at[1, top], to_y)
    d1.wait_recv()
    add_rows(held.at[1], (held.at[1], far_in.at[1]), part, part, held.dtype)
    x1 = send(9, held.at[1, low], near_in.at[0, low], to_x)
    x0.wait_recv()
    y0.wait_recv()
    add_rows(sum_ref, (held.at[3], near_in.at[0], near_in.at[1]), 0, part, sum_ref.dtype)
    y1.wait_recv()
    x1.wait_recv()
    add_rows(sum_ref, (held.at[3], near_in.at[0], near_in.at[1]), part, part, sum_ref.dtype)
    for copy in gives + [d0, d1, x0, y1, y0, x1]:
        copy.wait_send()


def scatter_plane(partial, ident):
    plane = lax.axis_size("tp") * lax.axis_size("seq")
    rows, width = partial.shape[0] // plane, partial.shape[1]
    kind = partial.dtype
    size = rows * width * 2
    return pl.pallas_call(
        scatter_kernel,
        out_shape=jax.ShapeDtypeStruct((rows, width), F32),
        in_specs=[pl.BlockSpec(memory_space=pltpu.HBM)],
        out_specs=pl.BlockSpec(memory_space=pltpu.VMEM),
        scratch_shapes=[
            pltpu.VMEM((4, rows, width), kind),
            pltpu.VMEM((4, rows, width), kind),
            pltpu.VMEM((2, rows, width), kind),
            pltpu.VMEM((2, rows, width), kind),
            pltpu.SemaphoreType.DMA((4,)),
            pltpu.SemaphoreType.DMA((10,)),
            pltpu.SemaphoreType.DMA((10,)),
        ],
        cost_estimate=pl.CostEstimate(
            flops=0, transcendentals=0, bytes_accessed=plane * size * 14
        ),
        compiler_params=pltpu.CompilerParams(
            collective_id=ident, has_side_effects=True, vmem_limit_bytes=32 << 20
        ),
        name="scatter_plane",
    )(partial.reshape(plane, rows, width))


def exchange_kernel(in_ref, out_ref, stage, local, sends, recvs):
    tp_at, seq_at, _, _, _ = plane_place()
    seq = lax.axis_size("seq")
    plane = lax.axis_size("tp") * seq
    me = tp_at * seq + seq_at
    peers = [lax.rem(me + k, plane) for k in range(1, plane)]
    devices = [at_device(peer // seq, lax.rem(peer, seq)) for peer in peers]
    enter(devices)
    copies = []
    for k, (peer, device) in enumerate(zip(peers, devices)):
        copy = remote(in_ref.at[peer], out_ref.at[me], sends.at[k], recvs.at[k], device)
        copy.start()
        copies.append(copy)
    take = pltpu.make_async_copy(in_ref.at[me], stage, local.at[0])
    take.start()
    take.wait()
    put = pltpu.make_async_copy(stage, out_ref.at[me], local.at[1])
    put.start()
    for copy in copies:
        copy.wait()
    put.wait()


def exchange_plane(blocks, ident):
    plane, rows, width = blocks.shape
    size = plane * rows * width * 2
    return pl.pallas_call(
        exchange_kernel,
        out_shape=jax.ShapeDtypeStruct(blocks.shape, blocks.dtype),
        in_specs=[pl.BlockSpec(memory_space=pltpu.HBM)],
        out_specs=pl.BlockSpec(memory_space=pltpu.HBM),
        scratch_shapes=[
            pltpu.VMEM((rows, width), blocks.dtype),
            pltpu.SemaphoreType.DMA((2,)),
            pltpu.SemaphoreType.DMA((plane - 1,)),
            pltpu.SemaphoreType.DMA((plane - 1,)),
        ],
        cost_estimate=pl.CostEstimate(flops=0, transcendentals=0, bytes_accessed=size * 20),
        compiler_params=pltpu.CompilerParams(collective_id=ident, has_side_effects=True),
        name="exchange_plane",
    )(blocks)


def ffn_kernel(
    own_ref,
    grad_ref,
    gu_hbm,
    down_hbm,
    all_ref,
    inner_ref,
    gug_ref,
    out_ref,
    sum_ref,
    gu,
    down,
    tokens,
    grads,
    wide,
    narrow,
    inner,
    gug,
    part,
    chip_in,
    far_in,
    near_in,
    sends,
    recvs,
    local,
):
    tp_at, seq_at, far, mate, _ = plane_place()
    seq = lax.axis_size("seq")
    other = 1 - tp_at
    kind = lax.rem(seq_at, 2)
    to_x = at_device(tp_at, far)
    to_y = at_device(other, seq_at)
    to_c = at_device(tp_at, mate)
    rows, width = own_ref.shape
    pair = 2 * rows
    half = rows // 2
    ff_part = narrow.shape[1]
    top, low = pl.ds(0, half), pl.ds(half, half)
    enter((to_x, to_y, to_c))

    def piece(t, s, h):
        return all_ref.at[t * seq + s, pl.ds(h * half, half)]

    def own(i, h, device):
        return remote(
            own_ref.at[pl.ds(h * half, half)],
            piece(tp_at, seq_at, h),
            sends.at[i],
            recvs.at[i],
            device,
        )

    def relay(i, t, s, h, device):
        return remote(piece(t, s, h), piece(t, s, h), sends.at[i], recvs.at[i], device)

    x0, x1 = own(0, 0, to_x), own(3, 1, to_x)
    y0, y1 = own(1, 0, to_y), own(4, 1, to_y)
    c0, c1 = own(2, 0, to_c), own(5, 1, to_c)
    diag0 = relay(6, tp_at, far, 0, to_y)
    diag1 = relay(7, other, seq_at, 1, to_x)
    rx0, rx1 = relay(8, tp_at, far, 0, to_c), relay(11, tp_at, far, 1, to_c)
    ry0, ry1 = relay(9, other, seq_at, 0, to_c), relay(10, other, seq_at, 1, to_c)
    rd0, rd1 = relay(12, other, far, 0, to_c), relay(13, other, far, 1, to_c)

    def give(c):
        return remote(
            part.at[c, 1 - kind], chip_in.at[c], sends.at[14 + c], recvs.at[14 + c], to_c
        )

    def hop(i, src, dst, device):
        return remote(src, dst, sends.at[i], recvs.at[i], device)

    def held(c):
        return part.at[c, kind]

    sum_x0 = hop(18, part.at[1, kind, top], near_in.at[0, top], to_x)
    sum_y1 = hop(19, part.at[2, kind, low], near_in.at[1, low], to_y)
    sum_d0 = hop(20, part.at[3, kind, top], far_in.at[0, top], to_x)
    sum_d1 = hop(21, part.at[3, kind, low], far_in.at[1, low], to_y)
    sum_y0 = hop(22, part.at[2, kind, top], near_in.at[1, top], to_y)
    sum_x1 = hop(23, part.at[1, kind, low], near_in.at[0, low], to_x)

    def chip_sum(c):
        give(c).wait_recv()
        add_rows(held(c), (held(c), chip_in.at[c]), 0, rows, part.dtype)

    def chip_rows(c):
        t = lax.rem(tp_at + c // 2, 2)
        s = lax.rem(seq_at + (seq // 2) * lax.rem(c, 2), seq)
        return t * seq + s - lax.rem(s, 2)

    def take_tokens(c):
        return pltpu.make_async_copy(
            all_ref.at[pl.ds(chip_rows(c), 2)], tokens.at[lax.rem(c, 2)], local.at[lax.rem(c, 2)]
        )

    def take_grads(c):
        return pltpu.make_async_copy(
            grad_ref.at[pl.ds(chip_rows(c), 2)], grads.at[lax.rem(c, 2)], local.at[2 + lax.rem(c, 2)]
        )

    def put_gug(c):
        return pltpu.make_async_copy(
            gug.at[lax.rem(c, 2)], gug_ref.at[chip_rows(c) // 2], local.at[4 + lax.rem(c, 2)]
        )

    def put_inner(c):
        return pltpu.make_async_copy(
            inner.at[c], inner_ref.at[chip_rows(c) // 2], local.at[6 + c]
        )

    def put_out(c):
        return pltpu.make_async_copy(
            tokens.at[lax.rem(c, 2)], out_ref.at[pl.ds(chip_rows(c), 2)], local.at[10 + lax.rem(c, 2)]
        )

    take_gu = pltpu.make_async_copy(gu_hbm, gu, local.at[12])
    take_down = pltpu.make_async_copy(down_hbm, down, local.at[13])
    mine = pltpu.make_async_copy(own_ref, all_ref.at[tp_at * seq + seq_at], local.at[14])

    for copy in (x0, y0, c0, x1, y1, c1, mine, take_gu, take_down, take_grads(0)):
        copy.start()
    mine.wait()
    c0.wait_recv()
    c1.wait_recv()
    take_tokens(0).start()
    take_gu.wait()
    take_down.wait()

    def after_load(c):
        @pl.when(c == 1)
        def _():
            ry0.wait_recv()
            ry1.wait_recv()
            take_tokens(2).start()
            chip_sum(0)

        @pl.when(c == 2)
        def _():
            rd0.wait_recv()
            rd1.wait_recv()
            take_tokens(3).start()
            chip_sum(1)
            sum_x0.start()

        @pl.when(c == 3)
        def _():
            chip_sum(2)
            sum_y1.start()

        @pl.when(c < 3)
        def _():
            take_grads(c + 1).start()

    def after_chip(c):
        @pl.when(c == 0)
        def _():
            x0.wait_recv()
            diag0.start()
            rx0.start()
            y0.wait_recv()
            ry0.start()
            y1.wait_recv()
            diag1.start()
            ry1.start()
            x1.wait_recv()
            rx1.start()
            rx0.wait_recv()
            rx1.wait_recv()
            take_tokens(1).start()

        @pl.when(c == 1)
        def _():
            diag0.wait_recv()
            rd0.start()
            diag1.wait_recv()
            rd1.start()

    def chip_step(c, carry):
        slot = lax.rem(c, 2)
        take_tokens(c).wait()
        wide[...] = nn(tokens[slot].reshape(pair, width), gu[...])
        after_load(c)
        take_grads(c).wait()
        narrow[...] = nn(grads[slot].reshape(pair, width), down[...])

        @pl.when(c >= 2)
        def _():
            put_gug(c - 2).wait()

        def slopes(i, carry):
            at = pl.ds(i * SUB, SUB)
            gate, upward, grad = wide[at, :ff_part], wide[at, ff_part:], narrow[at, :]
            sigmoid_gate = jax.nn.sigmoid(gate)
            silu_gate = gate * sigmoid_gate
            inner[c, at, :] = (silu_gate * upward).astype(BF)
            slope = sigmoid_gate * (1.0 + gate * (1.0 - sigmoid_gate))
            gug[slot, at, :ff_part] = (grad * upward * slope).astype(BF)
            gug[slot, at, ff_part:] = (grad * silu_gate).astype(BF)
            return carry

        lax.fori_loop(0, pair // SUB, slopes, 0)
        put_gug(c).start()
        put_inner(c).start()
        block = width // 4

        def back(n, carry):
            at = pl.ds(pl.multiple_of(n * block, block), block)
            total = nt(gug[slot], gu[at, :]).astype(part.dtype)
            part[c, :, :, at] = total.reshape(2, rows, block)
            return carry

        lax.fori_loop(0, 4, back, 0)
        give(c).start()
        after_chip(c)
        return carry

    lax.fori_loop(0, 4, chip_step, 0)

    def out_step(c, carry):
        slot = lax.rem(c, 2)

        @pl.when(c >= 2)
        def _():
            put_out(c - 2).wait()

        block = width // 4

        def out_block(n, carry):
            at = pl.ds(pl.multiple_of(n * block, block), block)
            total = nt(inner[c], down[at, :]).astype(tokens.dtype)
            tokens[slot, :, :, at] = total.reshape(2, rows, block)
            return carry

        lax.fori_loop(0, 4, out_block, 0)
        put_out(c).start()

        @pl.when(c == 0)
        def _():
            chip_sum(3)
            sum_d0.start()
            sum_d1.start()

        return carry

    lax.fori_loop(0, 4, out_step, 0)
    sum_d0.wait_recv()
    add_rows(held(2), (held(2), far_in.at[0]), 0, half, part.dtype)
    sum_y0.start()
    sum_d1.wait_recv()
    add_rows(held(1), (held(1), far_in.at[1]), half, half, part.dtype)
    sum_x1.start()
    sum_x0.wait_recv()
    sum_y0.wait_recv()
    add_rows(sum_ref, (held(0), near_in.at[0], near_in.at[1]), 0, half, sum_ref.dtype)
    sum_y1.wait_recv()
    sum_x1.wait_recv()
    add_rows(sum_ref, (held(0), near_in.at[0], near_in.at[1]), half, half, sum_ref.dtype)
    for copy in (x0, y0, c0, x1, y1, c1, diag0, diag1, rx0, ry0, ry1, rx1, rd0, rd1):
        copy.wait_send()
    for c in range(4):
        give(c).wait_send()
        put_inner(c).wait()
    for copy in (sum_x0, sum_y1, sum_d0, sum_d1, sum_y0, sum_x1):
        copy.wait_send()
    for c in (2, 3):
        put_gug(c).wait()
        put_out(c).wait()


def ffn_plane(block, grads, gu_weight, down_weight, ident):
    rows, width = block.shape
    seq = lax.axis_size("seq")
    plane = lax.axis_size("tp") * seq
    chips = plane // 2
    ff_part = down_weight.shape[1]
    shape = jax.ShapeDtypeStruct
    hbm = pl.BlockSpec(memory_space=pltpu.HBM)
    vmem = pl.BlockSpec(memory_space=pltpu.VMEM)
    tokens = plane * rows
    return pl.pallas_call(
        ffn_kernel,
        out_shape=(
            shape((plane, rows, width), BF),
            shape((chips, 2 * rows, ff_part), BF),
            shape((chips, 2 * rows, 2 * ff_part), BF),
            shape((plane, rows, width), BF),
            shape((rows, width), F32),
        ),
        in_specs=[vmem, hbm, hbm, hbm],
        out_specs=(hbm, hbm, hbm, hbm, vmem),
        scratch_shapes=[
            pltpu.VMEM(gu_weight.shape, BF),
            pltpu.VMEM(down_weight.shape, BF),
            pltpu.VMEM((2, 2, rows, width), BF),
            pltpu.VMEM((2, 2, rows, width), BF),
            pltpu.VMEM((2 * rows, 2 * ff_part), F32),
            pltpu.VMEM((2 * rows, ff_part), F32),
            pltpu.VMEM((4, 2 * rows, ff_part), BF),
            pltpu.VMEM((2, 2 * rows, 2 * ff_part), BF),
            pltpu.VMEM((4, 2, rows, width), BF),
            pltpu.VMEM((4, rows, width), BF),
            pltpu.VMEM((2, rows, width), BF),
            pltpu.VMEM((2, rows, width), BF),
            pltpu.SemaphoreType.DMA((24,)),
            pltpu.SemaphoreType.DMA((24,)),
            pltpu.SemaphoreType.DMA((15,)),
        ],
        cost_estimate=pl.CostEstimate(
            flops=12 * tokens * width * ff_part,
            transcendentals=tokens * ff_part,
            bytes_accessed=30 * tokens * width,
        ),
        compiler_params=pltpu.CompilerParams(
            collective_id=ident, has_side_effects=True, vmem_limit_bytes=60 << 20
        ),
        name="ffn_plane",
    )(block, grads, gu_weight, down_weight)


def columns(matrix, parts):
    rows, cols = matrix.shape
    return jnp.transpose(matrix.reshape(rows, parts, cols // parts), (1, 0, 2))


def uncolumns(blocks):
    parts, rows, cols = blocks.shape
    return jnp.transpose(blocks, (1, 0, 2)).reshape(rows, parts * cols)


def after(value, *earlier):
    return lax.optimization_barrier((value,) + earlier)[0]


def per_device(
    layer_input,
    pic_starts,
    skip_mask,
    gain_attn,
    w_query,
    w_key,
    w_value,
    w_out,
    gain_ffn,
    w_gate,
    w_up,
    w_down,
    cotangent,
):
    _, local_len, width = layer_input.shape
    seq = lax.axis_size("seq")
    plane = lax.axis_size("tp") * seq
    total_len = local_len * seq
    heads = H // plane
    share = plane // KV
    ff_part = w_gate.shape[1] // plane
    q_part = heads * DH
    scale = DH ** (-0.5)

    gain1 = gain_attn[:, None]
    gain2 = gain_ffn[:, None]
    wq32, wk32, wv32 = w_query.astype(F32), w_key.astype(F32), w_value.astype(F32)
    wg32, wu32 = w_gate.astype(F32), w_up.astype(F32)
    attn_pack = jnp.concatenate(
        [
            columns((wq32 * gain1).astype(BF), plane),
            jnp.repeat(columns((wk32 * gain1).astype(BF), KV), share, axis=0),
            jnp.repeat(columns((wv32 * gain1).astype(BF), KV), share, axis=0),
            columns(w_out.T, plane),
        ],
        axis=2,
    )
    attn_rows = exchange_plane(attn_pack, 0)
    attn_rows = attn_rows.reshape(-1, attn_rows.shape[2])
    attn_weight = lax.all_gather(attn_rows, "rep", axis=0, tiled=True)
    qkv_weight = attn_weight[:, : q_part + 2 * DH]
    out_weight = attn_weight[:, q_part + 2 * DH :]

    tokens = layer_input.reshape(local_len, width).astype(F32)
    keep = (1 - skip_mask).astype(F32).reshape(local_len, 1)
    upstream = cotangent.reshape(local_len, width).astype(F32)
    scale1 = rms_scale(tokens)
    norm1 = tokens * scale1

    ffn_pack = jnp.concatenate(
        [
            columns((wg32 * gain2).astype(BF), plane),
            columns((wu32 * gain2).astype(BF), plane),
            columns(w_down.T, plane),
        ],
        axis=2,
    )
    ffn_rows = exchange_plane(after(ffn_pack, attn_rows), 2)
    ffn_rows = ffn_rows.reshape(-1, ffn_rows.shape[2])
    down_weight = lax.all_gather(ffn_rows[:, 2 * ff_part :], "rep", axis=0, tiled=True)
    gu_weight = lax.all_gather(ffn_rows[:, : 2 * ff_part], "rep", axis=0, tiled=True)
    norm1_all = gather_plane(after(norm1.astype(BF), ffn_rows), 1)
    ffn_grad = gather_plane(after((keep * upstream).astype(BF), norm1_all), 3)

    other_starts = lax.ppermute(pic_starts, "tp", [(0, 1), (1, 0)])
    starts = jnp.where(
        lax.axis_index("tp") == 0,
        jnp.concatenate([pic_starts, other_starts], axis=0),
        jnp.concatenate([other_starts, pic_starts], axis=0),
    )
    positions = jnp.arange(total_len, dtype=jnp.int32)
    cos_table, sin_table = rotary_tables(positions, DH)
    allowed = jax.vmap(visible, (None, 0))(positions, starts)[:, None]
    turn = jax.vmap(rotate, (0, None, None))

    projected = nn(norm1_all, qkv_weight).reshape(TP, total_len, q_part + 2 * DH)
    queries = turn(
        projected[..., :q_part].reshape(TP, total_len, heads, DH), cos_table, sin_table
    ).astype(BF)
    keys = turn(projected[..., q_part : q_part + DH], cos_table, sin_table).astype(BF)
    values = projected[..., q_part + DH :].astype(BF)
    scores = jnp.einsum("tqhd,tkd->thqk", queries, keys, preferred_element_type=F32) * scale
    scores = jnp.where(allowed, scores, -jnp.inf)
    peak = jnp.max(scores, axis=-1, keepdims=True)
    log_total = peak + jnp.log(jnp.sum(jnp.exp(scores - peak), axis=-1, keepdims=True))
    probs = jnp.exp(scores - log_total)
    probs_low = probs.astype(BF)
    mixed = jnp.einsum("thqk,tkd->tqhd", probs_low, values, preferred_element_type=F32)
    mixed = mixed.astype(BF).reshape(TP * total_len, q_part)
    branch = scatter_plane(nt(mixed, out_weight).astype(BF), 4)
    hidden = tokens + keep * branch

    scale2 = rms_scale(hidden)
    norm2 = hidden * scale2
    norm2_all, inner, gate_up_grad, out_partial, scaled2 = ffn_plane(
        norm2.astype(BF), ffn_grad.reshape(plane, local_len, width), gu_weight, down_weight, 5
    )
    norm2_all = norm2_all.reshape(-1, width)
    inner = inner.reshape(-1, ff_part)
    gate_up_grad = gate_up_grad.reshape(-1, 2 * ff_part)
    down_partial = tn(ffn_grad, inner).astype(BF)
    down_sums = lax.psum_scatter(down_partial, "rep", scatter_dimension=0, tiled=True)
    gu_partial = tn(norm2_all, after(gate_up_grad, down_partial)).astype(BF)
    gu_sums = lax.psum_scatter(gu_partial, "rep", scatter_dimension=0, tiled=True)
    hidden_grad = upstream + scale2 * (
        scaled2 - norm2 * jnp.mean(scaled2 * norm2, axis=-1, keepdims=True)
    )

    branch_grad = gather_plane(after((keep * hidden_grad).astype(BF), gu_partial, down_partial), 7)
    mixed_grad = nn(branch_grad, out_weight).astype(BF).reshape(TP, total_len, heads, DH)
    values_grad = jnp.einsum(
        "thqk,tqhd->tkd", probs_low, mixed_grad, preferred_element_type=F32
    ).astype(BF)
    prob_grad = jnp.einsum("tqhd,tkd->thqk", mixed_grad, values, preferred_element_type=F32)
    score_grad = (
        probs * (prob_grad - jnp.sum(probs * prob_grad, axis=-1, keepdims=True))
    ).astype(BF)
    queries_grad = (
        jnp.einsum("thqk,tkd->tqhd", score_grad, keys, preferred_element_type=F32) * scale
    )
    keys_grad = (
        jnp.einsum("thqk,tqhd->tkd", score_grad, queries, preferred_element_type=F32) * scale
    )
    qkv_grad = jnp.concatenate(
        [
            turn(queries_grad, cos_table, -sin_table).astype(BF).reshape(-1, q_part),
            turn(keys_grad, cos_table, -sin_table).astype(BF).reshape(-1, DH),
            values_grad.reshape(-1, DH),
        ],
        axis=1,
    )
    attn_partial = jnp.concatenate(
        [tn(norm1_all, qkv_grad).astype(BF), tn(branch_grad, mixed).astype(BF)], axis=1
    )
    attn_partial = after(attn_partial, gu_sums, down_sums)
    attn_sums = lax.psum_scatter(attn_partial, "rep", scatter_dimension=0, tiled=True)
    scaled1 = scatter_plane(after(nt(qkv_grad, qkv_weight).astype(BF), attn_partial), 8)
    input_grad = hidden_grad + scale1 * (
        scaled1 - norm1 * jnp.mean(scaled1 * norm1, axis=-1, keepdims=True)
    )
    ffn_out = scatter_plane(after(out_partial.reshape(-1, width), scaled1), 9)
    out_hidden = (hidden + keep * ffn_out).astype(BF)

    ffn_sums = jnp.concatenate([gu_sums, down_sums], axis=1)
    ffn_sums = after(ffn_sums.reshape(plane, -1, ffn_sums.shape[1]), ffn_out)
    ffn_own = exchange_plane(ffn_sums, 10).astype(F32)
    gate_own = uncolumns(ffn_own[:, :, :ff_part])
    up_own = uncolumns(ffn_own[:, :, ff_part : 2 * ff_part])
    down_own = uncolumns(ffn_own[:, :, 2 * ff_part :])
    gain_ffn_grad = jnp.sum(gate_own * wg32, axis=1) + jnp.sum(up_own * wu32, axis=1)

    attn_own = exchange_plane(attn_sums.reshape(plane, -1, attn_sums.shape[1]), 11).astype(F32)
    query_own = uncolumns(attn_own[:, :, :q_part])
    kv_own = attn_own[:, :, q_part : q_part + 2 * DH]
    kv_own = jnp.sum(kv_own.reshape(KV, share, -1, 2 * DH), axis=1)
    key_own = uncolumns(kv_own[:, :, :DH])
    value_own = uncolumns(kv_own[:, :, DH:])
    out_own = uncolumns(attn_own[:, :, q_part + 2 * DH :])
    gain_attn_grad = (
        jnp.sum(query_own * wq32, axis=1)
        + jnp.sum(key_own * wk32, axis=1)
        + jnp.sum(value_own * wv32, axis=1)
    )
    return (
        out_hidden[None],
        input_grad[None],
        gain_attn_grad,
        query_own * gain1,
        key_own * gain1,
        value_own * gain1,
        out_own.T,
        gain_ffn_grad,
        gate_own * gain2,
        up_own * gain2,
        down_own.T,
    )


def solution(mesh):
    devices = mesh.devices
    dp, seq = devices.shape
    inner = Mesh(devices.reshape(dp // TP, TP, seq), ("rep", "tp", "seq"))
    dps = ("rep", "tp")
    every = ("rep", "tp", "seq")
    token = P(dps, "seq", None)
    row = P(every, None)
    col = P(None, every)
    return jax.shard_map(
        per_device,
        mesh=inner,
        in_specs=(
            token,
            P(dps, None),
            P(dps, "seq"),
            P(every),
            row,
            row,
            row,
            col,
            P(every),
            row,
            row,
            col,
            token,
        ),
        out_specs=(token, token, P(every), row, row, row, col, P(every), row, row, col),
        check_vma=False,
    )
```

```python
import jax
import jax.numpy as jnp
from jax import lax
from jax.experimental import pallas as pl
from jax.experimental.pallas import tpu as pltpu
from jax.sharding import Mesh
from jax.sharding import PartitionSpec as P

H = 16
KV = 4
DH = 128
PIC = 256
NPIC = 2
EPS = 1e-05
TP = 2
BF = jnp.bfloat16
F32 = jnp.float32


def rotary_tables(positions, head_dim):
    half_dim = head_dim // 2
    inverse = 10000.0 ** (-(jnp.arange(half_dim, dtype=F32) * 2.0 / head_dim))
    angles = positions.astype(F32)[:, None] * inverse[None, :]
    return (jnp.cos(angles), jnp.sin(angles))


def rotate(values, cos_table, sin_table):
    half = values.shape[-1] // 2
    shape = (cos_table.shape[0],) + (1,) * (values.ndim - 2) + (half,)
    cos_part = cos_table.reshape(shape)
    sin_part = sin_table.reshape(shape)
    first = values[..., :half]
    second = values[..., half:]
    return jnp.concatenate(
        [first * cos_part - second * sin_part, second * cos_part + first * sin_part], axis=-1
    )


def picture_ids(positions, starts):
    inside = (positions[None, :] >= starts[:, None]) & (positions[None, :] < starts[:, None] + PIC)
    labels = jnp.arange(1, NPIC + 1, dtype=jnp.int32)
    return jnp.sum(jnp.where(inside, labels[:, None], 0), axis=0)


def visible(positions, starts):
    ids = picture_ids(positions, starts)
    causal = positions[None, :] <= positions[:, None]
    same_piece = (ids[:, None] == ids[None, :]) & (ids[:, None] > 0)
    return causal | same_piece


def rms_scale(rows):
    return lax.rsqrt(jnp.mean(rows * rows, axis=-1, keepdims=True) + EPS)


def dot(left, right, contract):
    return lax.dot_general(
        left, right, ((contract[:1], contract[1:]), ((), ())), preferred_element_type=F32
    )


def nn(left, right):
    return dot(left, right, (1, 0))


def nt(left, right):
    return dot(left, right, (1, 1))


def tn(left, right):
    return dot(left, right, (0, 0))


MESH_ID = pl.DeviceIdType.MESH
SUB = 32


def plane_place():
    tp_at = lax.axis_index("tp")
    seq_at = lax.axis_index("seq")
    seq = lax.axis_size("seq")
    half = seq // 2
    far = lax.rem(seq_at + half, seq)
    mate = seq_at + 1 - 2 * lax.rem(seq_at, 2)
    far_mate = far + 1 - 2 * lax.rem(far, 2)
    return tp_at, seq_at, far, mate, far_mate


def at_device(tp_at, seq_at):
    return (lax.axis_index("rep"), tp_at, seq_at)


def enter(devices):
    barrier = pltpu.get_barrier_semaphore()
    for device in devices:
        pl.semaphore_signal(barrier, inc=1, device_id=device, device_id_type=MESH_ID)
    pl.semaphore_wait(barrier, len(devices))


def remote(src, dst, send, recv, device):
    return pltpu.make_async_remote_copy(
        src_ref=src,
        dst_ref=dst,
        send_sem=send,
        recv_sem=recv,
        device_id=device,
        device_id_type=MESH_ID,
    )


def gather_kernel(own_ref, all_ref, sends, recvs, local):
    tp_at, seq_at, far, mate, _ = plane_place()
    seq = lax.axis_size("seq")
    other = 1 - tp_at
    to_x = at_device(tp_at, far)
    to_y = at_device(other, seq_at)
    to_c = at_device(tp_at, mate)
    rows = own_ref.shape[0]
    part = rows // 2
    enter((to_x, to_y, to_c))

    def piece(t, s, h):
        return all_ref.at[t * seq + s, pl.ds(h * part, part)]

    def pass_on(i, t, s, h, device):
        copy = remote(piece(t, s, h), piece(t, s, h), sends.at[i], recvs.at[i], device)
        copy.start()
        return copy

    def own(i, h, device):
        copy = remote(
            own_ref.at[pl.ds(h * part, part)],
            piece(tp_at, seq_at, h),
            sends.at[i],
            recvs.at[i],
            device,
        )
        copy.start()
        return copy

    x0 = own(0, 0, to_x)
    y0 = own(1, 0, to_y)
    c0 = own(2, 0, to_c)
    x1 = own(3, 1, to_x)
    y1 = own(4, 1, to_y)
    c1 = own(5, 1, to_c)
    mine = pltpu.make_async_copy(own_ref, all_ref.at[tp_at * seq + seq_at], local)
    mine.start()
    x0.wait_recv()
    diag0 = pass_on(6, tp_at, far, 0, to_y)
    rx0 = pass_on(8, tp_at, far, 0, to_c)
    y0.wait_recv()
    ry0 = pass_on(9, other, seq_at, 0, to_c)
    y1.wait_recv()
    diag1 = pass_on(7, other, seq_at, 1, to_x)
    ry1 = pass_on(10, other, seq_at, 1, to_c)
    x1.wait_recv()
    rx1 = pass_on(11, tp_at, far, 1, to_c)
    diag0.wait_recv()
    rd0 = pass_on(12, other, far, 0, to_c)
    diag1.wait_recv()
    rd1 = pass_on(13, other, far, 1, to_c)
    for copy in (c0, c1, rx0, ry0, ry1, rx1, rd0, rd1):
        copy.wait_recv()
    for copy in (x0, y0, c0, x1, y1, c1, diag0, diag1, rx0, ry0, ry1, rx1, rd0, rd1):
        copy.wait_send()
    mine.wait()


def gather_plane(block, ident):
    rows, width = block.shape
    plane = lax.axis_size("tp") * lax.axis_size("seq")
    size = rows * width * 2
    gathered = pl.pallas_call(
        gather_kernel,
        out_shape=jax.ShapeDtypeStruct((plane, rows, width), block.dtype),
        in_specs=[pl.BlockSpec(memory_space=pltpu.VMEM)],
        out_specs=pl.BlockSpec(memory_space=pltpu.HBM),
        scratch_shapes=[
            pltpu.SemaphoreType.DMA((14,)),
            pltpu.SemaphoreType.DMA((14,)),
            pltpu.SemaphoreType.DMA,
        ],
        cost_estimate=pl.CostEstimate(
            flops=0, transcendentals=0, bytes_accessed=plane * size * 12
        ),
        compiler_params=pltpu.CompilerParams(collective_id=ident, has_side_effects=True),
        name="gather_plane",
    )(block)
    return gathered.reshape(plane * rows, width)


def add_rows(target, sources, start, count, kind):
    step = min(SUB, count)

    def body(i, carry):
        at = pl.ds(start + i * step, step)
        total = sources[0][at, :].astype(F32)
        for source in sources[1:]:
            total = total + source[at, :].astype(F32)
        target[at, :] = total.astype(kind)
        return carry

    lax.fori_loop(0, count // step, body, 0)


def scatter_kernel(part_ref, sum_ref, held, chip_in, far_in, near_in, loads, sends, recvs):
    tp_at, seq_at, far, mate, far_mate = plane_place()
    seq = lax.axis_size("seq")
    other = 1 - tp_at
    to_x = at_device(tp_at, far)
    to_y = at_device(other, seq_at)
    to_c = at_device(tp_at, mate)
    rows = sum_ref.shape[0]
    part = rows // 2
    top, low = pl.ds(0, part), pl.ds(part, part)
    enter((to_x, to_y, to_c))
    chips = ((other, far, far_mate), (tp_at, far, far_mate), (other, seq_at, mate), (tp_at, seq_at, mate))
    gives, takes = [], []
    for k, (t, s, m) in enumerate(chips):
        give = remote(
            part_ref.at[t * seq + m], chip_in.at[k], sends.at[k], recvs.at[k], to_c
        )
        give.start()
        take = pltpu.make_async_copy(part_ref.at[t * seq + s], held.at[k], loads.at[k])
        take.start()
        gives.append(give)
        takes.append(take)

    def chip_sum(k):
        takes[k].wait()
        gives[k].wait_recv()
        add_rows(held.at[k], (held.at[k], chip_in.at[k]), 0, rows, held.dtype)

    def send(i, src, dst, device):
        copy = remote(src, dst, sends.at[i], recvs.at[i], device)
        copy.start()
        return copy

    chip_sum(0)
    d0 = send(4, held.at[0, top], far_in.at[0, top], to_x)
    d1 = send(5, held.at[0, low], far_in.at[1, low], to_y)
    chip_sum(1)
    x0 = send(6, held.at[1, top], near_in.at[0, top], to_x)
    chip_sum(2)
    y1 = send(7, held.at[2, low], near_in.at[1, low], to_y)
    chip_sum(3)
    d0.wait_recv()
    add_rows(held.at[2], (held.at[2], far_in.at[0]), 0, part, held.dtype)
    y0 = send(8, held.at[2, top], near_in.at[1, top], to_y)
    d1.wait_recv()
    add_rows(held.at[1], (held.at[1], far_in.at[1]), part, part, held.dtype)
    x1 = send(9, held.at[1, low], near_in.at[0, low], to_x)
    x0.wait_recv()
    y0.wait_recv()
    add_rows(sum_ref, (held.at[3], near_in.at[0], near_in.at[1]), 0, part, sum_ref.dtype)
    y1.wait_recv()
    x1.wait_recv()
    add_rows(sum_ref, (held.at[3], near_in.at[0], near_in.at[1]), part, part, sum_ref.dtype)
    for copy in gives + [d0, d1, x0, y1, y0, x1]:
        copy.wait_send()


def scatter_plane(partial, ident):
    plane = lax.axis_size("tp") * lax.axis_size("seq")
    rows, width = partial.shape[0] // plane, partial.shape[1]
    kind = partial.dtype
    size = rows * width * 2
    return pl.pallas_call(
        scatter_kernel,
        out_shape=jax.ShapeDtypeStruct((rows, width), F32),
        in_specs=[pl.BlockSpec(memory_space=pltpu.HBM)],
        out_specs=pl.BlockSpec(memory_space=pltpu.VMEM),
        scratch_shapes=[
            pltpu.VMEM((4, rows, width), kind),
            pltpu.VMEM((4, rows, width), kind),
            pltpu.VMEM((2, rows, width), kind),
            pltpu.VMEM((2, rows, width), kind),
            pltpu.SemaphoreType.DMA((4,)),
            pltpu.SemaphoreType.DMA((10,)),
            pltpu.SemaphoreType.DMA((10,)),
        ],
        cost_estimate=pl.CostEstimate(
            flops=0, transcendentals=0, bytes_accessed=plane * size * 14
        ),
        compiler_params=pltpu.CompilerParams(
            collective_id=ident, has_side_effects=True, vmem_limit_bytes=32 << 20
        ),
        name="scatter_plane",
    )(partial.reshape(plane, rows, width))


def exchange_kernel(in_ref, out_ref, stage, local, sends, recvs):
    tp_at, seq_at, _, _, _ = plane_place()
    seq = lax.axis_size("seq")
    plane = lax.axis_size("tp") * seq
    me = tp_at * seq + seq_at
    peers = [lax.rem(me + k, plane) for k in range(1, plane)]
    devices = [at_device(peer // seq, lax.rem(peer, seq)) for peer in peers]
    enter(devices)
    copies = []
    for k, (peer, device) in enumerate(zip(peers, devices)):
        copy = remote(in_ref.at[peer], out_ref.at[me], sends.at[k], recvs.at[k], device)
        copy.start()
        copies.append(copy)
    take = pltpu.make_async_copy(in_ref.at[me], stage, local.at[0])
    take.start()
    take.wait()
    put = pltpu.make_async_copy(stage, out_ref.at[me], local.at[1])
    put.start()
    for copy in copies:
        copy.wait()
    put.wait()


def exchange_plane(blocks, ident):
    plane, rows, width = blocks.shape
    size = plane * rows * width * 2
    return pl.pallas_call(
        exchange_kernel,
        out_shape=jax.ShapeDtypeStruct(blocks.shape, blocks.dtype),
        in_specs=[pl.BlockSpec(memory_space=pltpu.HBM)],
        out_specs=pl.BlockSpec(memory_space=pltpu.HBM),
        scratch_shapes=[
            pltpu.VMEM((rows, width), blocks.dtype),
            pltpu.SemaphoreType.DMA((2,)),
            pltpu.SemaphoreType.DMA((plane - 1,)),
            pltpu.SemaphoreType.DMA((plane - 1,)),
        ],
        cost_estimate=pl.CostEstimate(flops=0, transcendentals=0, bytes_accessed=size * 20),
        compiler_params=pltpu.CompilerParams(collective_id=ident, has_side_effects=True),
        name="exchange_plane",
    )(blocks)


def ffn_kernel(
    own_ref,
    grad_ref,
    weight_hbm,
    all_ref,
    inner_ref,
    gug_ref,
    out_ref,
    sum_ref,
    weight,
    tokens,
    grads,
    wide,
    narrow,
    inner,
    gug,
    part,
    chip_in,
    far_in,
    near_in,
    sends,
    recvs,
    local,
):
    tp_at, seq_at, far, mate, _ = plane_place()
    seq = lax.axis_size("seq")
    other = 1 - tp_at
    kind = lax.rem(seq_at, 2)
    to_x = at_device(tp_at, far)
    to_y = at_device(other, seq_at)
    to_c = at_device(tp_at, mate)
    rows, width = own_ref.shape
    pair = 2 * rows
    half = rows // 2
    ff_part = narrow.shape[1]
    gate_up, lower = slice(0, 2 * ff_part), slice(2 * ff_part, 3 * ff_part)
    top, low = pl.ds(0, half), pl.ds(half, half)
    enter((to_x, to_y, to_c))

    def piece(t, s, h):
        return all_ref.at[t * seq + s, pl.ds(h * half, half)]

    def own(i, h, device):
        return remote(
            own_ref.at[pl.ds(h * half, half)],
            piece(tp_at, seq_at, h),
            sends.at[i],
            recvs.at[i],
            device,
        )

    def relay(i, t, s, h, device):
        return remote(piece(t, s, h), piece(t, s, h), sends.at[i], recvs.at[i], device)

    x0, x1 = own(0, 0, to_x), own(3, 1, to_x)
    y0, y1 = own(1, 0, to_y), own(4, 1, to_y)
    c0, c1 = own(2, 0, to_c), own(5, 1, to_c)
    diag0 = relay(6, tp_at, far, 0, to_y)
    diag1 = relay(7, other, seq_at, 1, to_x)
    rx0, rx1 = relay(8, tp_at, far, 0, to_c), relay(11, tp_at, far, 1, to_c)
    ry0, ry1 = relay(9, other, seq_at, 0, to_c), relay(10, other, seq_at, 1, to_c)
    rd0, rd1 = relay(12, other, far, 0, to_c), relay(13, other, far, 1, to_c)

    def give(c):
        return remote(
            part.at[c, 1 - kind], chip_in.at[c], sends.at[14 + c], recvs.at[14 + c], to_c
        )

    def hop(i, src, dst, device):
        return remote(src, dst, sends.at[i], recvs.at[i], device)

    def held(c):
        return part.at[c, kind]

    sum_x0 = hop(18, part.at[1, kind, top], near_in.at[0, top], to_x)
    sum_y1 = hop(19, part.at[2, kind, low], near_in.at[1, low], to_y)
    sum_d0 = hop(20, part.at[3, kind, top], far_in.at[0, top], to_x)
    sum_d1 = hop(21, part.at[3, kind, low], far_in.at[1, low], to_y)
    sum_y0 = hop(22, part.at[2, kind, top], near_in.at[1, top], to_y)
    sum_x1 = hop(23, part.at[1, kind, low], near_in.at[0, low], to_x)

    def chip_sum(c):
        give(c).wait_recv()
        add_rows(held(c), (held(c), chip_in.at[c]), 0, rows, part.dtype)

    def chip_rows(c):
        t = lax.rem(tp_at + c // 2, 2)
        s = lax.rem(seq_at + (seq // 2) * lax.rem(c, 2), seq)
        return t * seq + s - lax.rem(s, 2)

    def take_tokens(c):
        return pltpu.make_async_copy(
            all_ref.at[pl.ds(chip_rows(c), 2)], tokens.at[lax.rem(c, 2)], local.at[lax.rem(c, 2)]
        )

    def take_grads(c):
        return pltpu.make_async_copy(
            grad_ref.at[pl.ds(chip_rows(c), 2)], grads.at[lax.rem(c, 2)], local.at[2 + lax.rem(c, 2)]
        )

    def put_gug(c):
        return pltpu.make_async_copy(
            gug.at[lax.rem(c, 2)], gug_ref.at[chip_rows(c) // 2], local.at[4 + lax.rem(c, 2)]
        )

    def put_inner(c):
        return pltpu.make_async_copy(
            inner.at[c], inner_ref.at[chip_rows(c) // 2], local.at[6 + c]
        )

    def put_out(c):
        return pltpu.make_async_copy(
            tokens.at[lax.rem(c, 2)], out_ref.at[pl.ds(chip_rows(c), 2)], local.at[10 + lax.rem(c, 2)]
        )

    take_weight = pltpu.make_async_copy(weight_hbm, weight, local.at[12])
    mine = pltpu.make_async_copy(own_ref, all_ref.at[tp_at * seq + seq_at], local.at[13])

    for copy in (x0, y0, c0, x1, y1, c1, mine, take_weight, take_grads(0)):
        copy.start()
    mine.wait()
    c0.wait_recv()
    c1.wait_recv()
    take_tokens(0).start()
    take_weight.wait()

    def after_load(c):
        @pl.when(c == 1)
        def _():
            ry0.wait_recv()
            ry1.wait_recv()
            take_tokens(2).start()
            chip_sum(0)

        @pl.when(c == 2)
        def _():
            rd0.wait_recv()
            rd1.wait_recv()
            take_tokens(3).start()
            chip_sum(1)
            sum_x0.start()

        @pl.when(c == 3)
        def _():
            chip_sum(2)
            sum_y1.start()

        @pl.when(c < 3)
        def _():
            take_grads(c + 1).start()

    def after_chip(c):
        @pl.when(c == 0)
        def _():
            x0.wait_recv()
            diag0.start()
            rx0.start()
            y0.wait_recv()
            ry0.start()
            y1.wait_recv()
            diag1.start()
            ry1.start()
            x1.wait_recv()
            rx1.start()
            rx0.wait_recv()
            rx1.wait_recv()
            take_tokens(1).start()

        @pl.when(c == 1)
        def _():
            diag0.wait_recv()
            rd0.start()
            diag1.wait_recv()
            rd1.start()

    def chip_step(c, carry):
        slot = lax.rem(c, 2)
        take_tokens(c).wait()
        wide[...] = nn(tokens[slot].reshape(pair, width), weight[:, gate_up])
        after_load(c)
        take_grads(c).wait()
        narrow[...] = nn(grads[slot].reshape(pair, width), weight[:, lower])

        @pl.when(c >= 2)
        def _():
            put_gug(c - 2).wait()

        def slopes(i, carry):
            at = pl.ds(i * SUB, SUB)
            gate, upward, grad = wide[at, :ff_part], wide[at, ff_part:], narrow[at, :]
            sigmoid_gate = jax.nn.sigmoid(gate)
            silu_gate = gate * sigmoid_gate
            inner[c, at, :] = (silu_gate * upward).astype(BF)
            slope = sigmoid_gate * (1.0 + gate * (1.0 - sigmoid_gate))
            gug[slot, at, :ff_part] = (grad * upward * slope).astype(BF)
            gug[slot, at, ff_part:] = (grad * silu_gate).astype(BF)
            return carry

        lax.fori_loop(0, pair // SUB, slopes, 0)
        put_gug(c).start()
        put_inner(c).start()
        block = width // 4

        def back(n, carry):
            at = pl.ds(pl.multiple_of(n * block, block), block)
            total = nt(gug[slot], weight[at, gate_up]).astype(part.dtype)
            part[c, :, :, at] = total.reshape(2, rows, block)
            return carry

        lax.fori_loop(0, 4, back, 0)
        give(c).start()
        after_chip(c)
        return carry

    lax.fori_loop(0, 4, chip_step, 0)

    def out_step(c, carry):
        slot = lax.rem(c, 2)

        @pl.when(c >= 2)
        def _():
            put_out(c - 2).wait()

        block = width // 4

        def out_block(n, carry):
            at = pl.ds(pl.multiple_of(n * block, block), block)
            total = nt(inner[c], weight[at, lower]).astype(tokens.dtype)
            tokens[slot, :, :, at] = total.reshape(2, rows, block)
            return carry

        lax.fori_loop(0, 4, out_block, 0)
        put_out(c).start()

        @pl.when(c == 0)
        def _():
            chip_sum(3)
            sum_d0.start()
            sum_d1.start()

        return carry

    lax.fori_loop(0, 4, out_step, 0)
    sum_d0.wait_recv()
    add_rows(held(2), (held(2), far_in.at[0]), 0, half, part.dtype)
    sum_y0.start()
    sum_d1.wait_recv()
    add_rows(held(1), (held(1), far_in.at[1]), half, half, part.dtype)
    sum_x1.start()
    sum_x0.wait_recv()
    sum_y0.wait_recv()
    add_rows(sum_ref, (held(0), near_in.at[0], near_in.at[1]), 0, half, sum_ref.dtype)
    sum_y1.wait_recv()
    sum_x1.wait_recv()
    add_rows(sum_ref, (held(0), near_in.at[0], near_in.at[1]), half, half, sum_ref.dtype)
    for copy in (x0, y0, c0, x1, y1, c1, diag0, diag1, rx0, ry0, ry1, rx1, rd0, rd1):
        copy.wait_send()
    for c in range(4):
        give(c).wait_send()
        put_inner(c).wait()
    for copy in (sum_x0, sum_y1, sum_d0, sum_d1, sum_y0, sum_x1):
        copy.wait_send()
    for c in (2, 3):
        put_gug(c).wait()
        put_out(c).wait()


def ffn_plane(block, grads, weight, ident):
    rows, width = block.shape
    seq = lax.axis_size("seq")
    plane = lax.axis_size("tp") * seq
    chips = plane // 2
    ff_part = weight.shape[1] // 3
    shape = jax.ShapeDtypeStruct
    hbm = pl.BlockSpec(memory_space=pltpu.HBM)
    vmem = pl.BlockSpec(memory_space=pltpu.VMEM)
    tokens = plane * rows
    return pl.pallas_call(
        ffn_kernel,
        out_shape=(
            shape((plane, rows, width), BF),
            shape((chips, 2 * rows, ff_part), BF),
            shape((chips, 2 * rows, 2 * ff_part), BF),
            shape((plane, rows, width), BF),
            shape((rows, width), F32),
        ),
        in_specs=[vmem, hbm, hbm],
        out_specs=(hbm, hbm, hbm, hbm, vmem),
        scratch_shapes=[
            pltpu.VMEM(weight.shape, BF),
            pltpu.VMEM((2, 2, rows, width), BF),
            pltpu.VMEM((2, 2, rows, width), BF),
            pltpu.VMEM((2 * rows, 2 * ff_part), F32),
            pltpu.VMEM((2 * rows, ff_part), F32),
            pltpu.VMEM((4, 2 * rows, ff_part), BF),
            pltpu.VMEM((2, 2 * rows, 2 * ff_part), BF),
            pltpu.VMEM((4, 2, rows, width), BF),
            pltpu.VMEM((4, rows, width), BF),
            pltpu.VMEM((2, rows, width), BF),
            pltpu.VMEM((2, rows, width), BF),
            pltpu.SemaphoreType.DMA((24,)),
            pltpu.SemaphoreType.DMA((24,)),
            pltpu.SemaphoreType.DMA((14,)),
        ],
        cost_estimate=pl.CostEstimate(
            flops=12 * tokens * width * ff_part,
            transcendentals=tokens * ff_part,
            bytes_accessed=30 * tokens * width,
        ),
        compiler_params=pltpu.CompilerParams(
            collective_id=ident, has_side_effects=True, vmem_limit_bytes=60 << 20
        ),
        name="ffn_plane",
    )(block, grads, weight)


def finish_kernel(
    gu_ref,
    down_ref,
    gate_weight,
    up_weight,
    gain_ref,
    gate_out,
    up_out,
    down_out,
    gain_out,
    gu_in,
    down_in,
    local,
    sends,
    recvs,
):
    tp_at, seq_at, _, _, _ = plane_place()
    seq = lax.axis_size("seq")
    plane = lax.axis_size("tp") * seq
    me = tp_at * seq + seq_at
    peers = [lax.rem(me + k, plane) for k in range(1, plane)]
    devices = [at_device(peer // seq, lax.rem(peer, seq)) for peer in peers]
    enter(devices)
    copies = []
    for k, (peer, device) in enumerate(zip(peers, devices)):
        copies.append(remote(gu_ref.at[peer], gu_in.at[me], sends.at[k], recvs.at[k], device))
        i = plane - 1 + k
        copies.append(remote(down_ref.at[peer], down_in.at[me], sends.at[i], recvs.at[i], device))
    copies.append(pltpu.make_async_copy(gu_ref.at[me], gu_in.at[me], local.at[0]))
    copies.append(pltpu.make_async_copy(down_ref.at[me], down_in.at[me], local.at[1]))
    for copy in copies:
        copy.start()
    for copy in copies:
        copy.wait()
    put = pltpu.make_async_copy(down_in, down_out, local.at[2])
    put.start()
    gain = gain_ref[...]
    ff_part = down_in.shape[2]
    total = jnp.zeros(gain.shape, F32)
    for j in range(plane):
        at = slice(j * ff_part, (j + 1) * ff_part)
        for k, (out, weight) in enumerate(((gate_out, gate_weight), (up_out, up_weight))):
            own = gu_in[j, :, k * ff_part : (k + 1) * ff_part].astype(F32)
            out[:, at] = own * gain
            total = total + jnp.sum(own * weight[:, at].astype(F32), axis=1, keepdims=True)
    gain_out[...] = total
    put.wait()


def finish_plane(gu_sums, down_sums, gate_weight, up_weight, gain, ident):
    plane, rows, ff_part = down_sums.shape
    shape = jax.ShapeDtypeStruct
    hbm = pl.BlockSpec(memory_space=pltpu.HBM)
    vmem = pl.BlockSpec(memory_space=pltpu.VMEM)
    size = plane * rows * ff_part * 6
    return pl.pallas_call(
        finish_kernel,
        out_shape=(
            shape(gate_weight.shape, F32),
            shape(up_weight.shape, F32),
            shape(down_sums.shape, BF),
            shape((rows, 1), F32),
        ),
        in_specs=[hbm, hbm, vmem, vmem, vmem],
        out_specs=(vmem, vmem, hbm, vmem),
        scratch_shapes=[
            pltpu.VMEM(gu_sums.shape, BF),
            pltpu.VMEM(down_sums.shape, BF),
            pltpu.SemaphoreType.DMA((3,)),
            pltpu.SemaphoreType.DMA((2 * plane - 2,)),
            pltpu.SemaphoreType.DMA((2 * plane - 2,)),
        ],
        cost_estimate=pl.CostEstimate(flops=0, transcendentals=0, bytes_accessed=size * 20),
        compiler_params=pltpu.CompilerParams(
            collective_id=ident, has_side_effects=True, vmem_limit_bytes=24 << 20
        ),
        name="finish_plane",
    )(gu_sums, down_sums, gate_weight, up_weight, gain)


def columns(matrix, parts):
    rows, cols = matrix.shape
    return jnp.transpose(matrix.reshape(rows, parts, cols // parts), (1, 0, 2))


def uncolumns(blocks):
    parts, rows, cols = blocks.shape
    return jnp.transpose(blocks, (1, 0, 2)).reshape(rows, parts * cols)


def after(value, *earlier):
    return lax.optimization_barrier((value,) + earlier)[0]


def per_device(
    layer_input,
    pic_starts,
    skip_mask,
    gain_attn,
    w_query,
    w_key,
    w_value,
    w_out,
    gain_ffn,
    w_gate,
    w_up,
    w_down,
    cotangent,
):
    _, local_len, width = layer_input.shape
    seq = lax.axis_size("seq")
    plane = lax.axis_size("tp") * seq
    total_len = local_len * seq
    heads = H // plane
    share = plane // KV
    ff_part = w_gate.shape[1] // plane
    q_part = heads * DH
    scale = DH ** (-0.5)

    gain1 = gain_attn[:, None]
    gain2 = gain_ffn[:, None]
    wq32, wk32, wv32 = w_query.astype(F32), w_key.astype(F32), w_value.astype(F32)
    wg32, wu32 = w_gate.astype(F32), w_up.astype(F32)
    attn_pack = jnp.concatenate(
        [
            columns((wq32 * gain1).astype(BF), plane),
            jnp.repeat(columns((wk32 * gain1).astype(BF), KV), share, axis=0),
            jnp.repeat(columns((wv32 * gain1).astype(BF), KV), share, axis=0),
            columns(w_out.T, plane),
        ],
        axis=2,
    )
    attn_rows = exchange_plane(attn_pack, 0)
    attn_rows = attn_rows.reshape(-1, attn_rows.shape[2])
    attn_weight = lax.all_gather(attn_rows, "rep", axis=0, tiled=True)
    qkv_weight = attn_weight[:, : q_part + 2 * DH]
    out_weight = attn_weight[:, q_part + 2 * DH :]

    tokens = layer_input.reshape(local_len, width).astype(F32)
    keep = (1 - skip_mask).astype(F32).reshape(local_len, 1)
    upstream = cotangent.reshape(local_len, width).astype(F32)
    scale1 = rms_scale(tokens)
    norm1 = tokens * scale1

    ffn_pack = jnp.concatenate(
        [
            columns((wg32 * gain2).astype(BF), plane),
            columns((wu32 * gain2).astype(BF), plane),
            columns(w_down.T, plane),
        ],
        axis=2,
    )
    ffn_rows = exchange_plane(after(ffn_pack, attn_rows), 2)
    ffn_rows = ffn_rows.reshape(-1, ffn_rows.shape[2])
    ffn_weight = lax.all_gather(ffn_rows, "rep", axis=0, tiled=True)
    norm1_all = gather_plane(after(norm1.astype(BF), ffn_rows), 1)
    ffn_grad = gather_plane(after((keep * upstream).astype(BF), norm1_all), 3)

    other_starts = lax.ppermute(pic_starts, "tp", [(0, 1), (1, 0)])
    starts = jnp.where(
        lax.axis_index("tp") == 0,
        jnp.concatenate([pic_starts, other_starts], axis=0),
        jnp.concatenate([other_starts, pic_starts], axis=0),
    )
    positions = jnp.arange(total_len, dtype=jnp.int32)
    cos_table, sin_table = rotary_tables(positions, DH)
    allowed = jax.vmap(visible, (None, 0))(positions, starts)[:, None]
    turn = jax.vmap(rotate, (0, None, None))

    projected = nn(norm1_all, qkv_weight).reshape(TP, total_len, q_part + 2 * DH)
    queries = turn(
        projected[..., :q_part].reshape(TP, total_len, heads, DH), cos_table, sin_table
    ).astype(BF)
    keys = turn(projected[..., q_part : q_part + DH], cos_table, sin_table).astype(BF)
    values = projected[..., q_part + DH :].astype(BF)
    scores = jnp.einsum("tqhd,tkd->thqk", queries, keys, preferred_element_type=F32) * scale
    scores = jnp.where(allowed, scores, -jnp.inf)
    peak = jnp.max(scores, axis=-1, keepdims=True)
    log_total = peak + jnp.log(jnp.sum(jnp.exp(scores - peak), axis=-1, keepdims=True))
    probs = jnp.exp(scores - log_total)
    probs_low = probs.astype(BF)
    mixed = jnp.einsum("thqk,tkd->tqhd", probs_low, values, preferred_element_type=F32)
    mixed = mixed.astype(BF).reshape(TP * total_len, q_part)
    branch = scatter_plane(nt(mixed, out_weight).astype(BF), 4)
    hidden = tokens + keep * branch

    scale2 = rms_scale(hidden)
    norm2 = hidden * scale2
    norm2_all, inner, gate_up_grad, out_partial, scaled2 = ffn_plane(
        norm2.astype(BF), ffn_grad.reshape(plane, local_len, width), ffn_weight, 5
    )
    norm2_all = norm2_all.reshape(-1, width)
    inner = inner.reshape(-1, ff_part)
    gate_up_grad = gate_up_grad.reshape(-1, 2 * ff_part)
    down_partial = tn(ffn_grad, inner).astype(BF)
    down_sums = lax.psum_scatter(down_partial, "rep", scatter_dimension=0, tiled=True)
    gu_partial = tn(norm2_all, after(gate_up_grad, down_partial)).astype(BF)
    gu_sums = lax.psum_scatter(gu_partial, "rep", scatter_dimension=0, tiled=True)
    hidden_grad = upstream + scale2 * (
        scaled2 - norm2 * jnp.mean(scaled2 * norm2, axis=-1, keepdims=True)
    )

    branch_grad = gather_plane(after((keep * hidden_grad).astype(BF), gu_partial, down_partial), 7)
    mixed_grad = nn(branch_grad, out_weight).astype(BF).reshape(TP, total_len, heads, DH)
    values_grad = jnp.einsum(
        "thqk,tqhd->tkd", probs_low, mixed_grad, preferred_element_type=F32
    ).astype(BF)
    prob_grad = jnp.einsum("tqhd,tkd->thqk", mixed_grad, values, preferred_element_type=F32)
    score_grad = (
        probs * (prob_grad - jnp.sum(probs * prob_grad, axis=-1, keepdims=True))
    ).astype(BF)
    queries_grad = (
        jnp.einsum("thqk,tkd->tqhd", score_grad, keys, preferred_element_type=F32) * scale
    )
    keys_grad = (
        jnp.einsum("thqk,tqhd->tkd", score_grad, queries, preferred_element_type=F32) * scale
    )
    qkv_grad = jnp.concatenate(
        [
            turn(queries_grad, cos_table, -sin_table).astype(BF).reshape(-1, q_part),
            turn(keys_grad, cos_table, -sin_table).astype(BF).reshape(-1, DH),
            values_grad.reshape(-1, DH),
        ],
        axis=1,
    )
    attn_partial = jnp.concatenate(
        [tn(norm1_all, qkv_grad).astype(BF), tn(branch_grad, mixed).astype(BF)], axis=1
    )
    scaled1_partial = nt(qkv_grad, qkv_weight).astype(BF)
    attn_partial = after(attn_partial, gu_sums, down_sums, scaled1_partial)
    attn_sums = lax.psum_scatter(attn_partial, "rep", scatter_dimension=0, tiled=True)
    scaled1 = scatter_plane(after(scaled1_partial, attn_partial), 8)
    input_grad = hidden_grad + scale1 * (
        scaled1 - norm1 * jnp.mean(scaled1 * norm1, axis=-1, keepdims=True)
    )
    ffn_out = scatter_plane(after(out_partial.reshape(-1, width), scaled1), 9)
    out_hidden = (hidden + keep * ffn_out).astype(BF)

    gate_grad, up_grad, down_own, gain_ffn_grad = finish_plane(
        after(gu_sums.reshape(plane, -1, 2 * ff_part), ffn_out),
        down_sums.reshape(plane, -1, ff_part),
        w_gate,
        w_up,
        gain2,
        10,
    )
    down_grad = jnp.transpose(down_own, (0, 2, 1)).reshape(plane * ff_part, -1).astype(F32)

    attn_own = exchange_plane(attn_sums.reshape(plane, -1, attn_sums.shape[1]), 11).astype(F32)
    query_own = uncolumns(attn_own[:, :, :q_part])
    kv_own = attn_own[:, :, q_part : q_part + 2 * DH]
    kv_own = jnp.sum(kv_own.reshape(KV, share, -1, 2 * DH), axis=1)
    key_own = uncolumns(kv_own[:, :, :DH])
    value_own = uncolumns(kv_own[:, :, DH:])
    out_own = uncolumns(attn_own[:, :, q_part + 2 * DH :])
    gain_attn_grad = (
        jnp.sum(query_own * wq32, axis=1)
        + jnp.sum(key_own * wk32, axis=1)
        + jnp.sum(value_own * wv32, axis=1)
    )
    return (
        out_hidden[None],
        input_grad[None],
        gain_attn_grad,
        query_own * gain1,
        key_own * gain1,
        value_own * gain1,
        out_own.T,
        gain_ffn_grad[:, 0],
        gate_grad,
        up_grad,
        down_grad,
    )


def solution(mesh):
    devices = mesh.devices
    dp, seq = devices.shape
    inner = Mesh(devices.reshape(dp // TP, TP, seq), ("rep", "tp", "seq"))
    dps = ("rep", "tp")
    every = ("rep", "tp", "seq")
    token = P(dps, "seq", None)
    row = P(every, None)
    col = P(None, every)
    return jax.shard_map(
        per_device,
        mesh=inner,
        in_specs=(
            token,
            P(dps, None),
            P(dps, "seq"),
            P(every),
            row,
            row,
            row,
            col,
            P(every),
            row,
            row,
            col,
            token,
        ),
        out_specs=(token, token, P(every), row, row, row, col, P(every), row, row, col),
        check_vma=False,
    )
```

```python
import jax
import jax.numpy as jnp
from jax import lax
from jax.experimental import pallas as pl
from jax.experimental.pallas import tpu as pltpu
from jax.sharding import Mesh
from jax.sharding import PartitionSpec as P

H = 16
KV = 4
DH = 128
PIC = 256
NPIC = 2
EPS = 1e-05
TP = 2
BF = jnp.bfloat16
F32 = jnp.float32


def rotary_tables(positions, head_dim):
    half_dim = head_dim // 2
    inverse = 10000.0 ** (-(jnp.arange(half_dim, dtype=F32) * 2.0 / head_dim))
    angles = positions.astype(F32)[:, None] * inverse[None, :]
    return (jnp.cos(angles), jnp.sin(angles))


def rotate(values, cos_table, sin_table):
    half = values.shape[-1] // 2
    shape = (cos_table.shape[0],) + (1,) * (values.ndim - 2) + (half,)
    cos_part = cos_table.reshape(shape)
    sin_part = sin_table.reshape(shape)
    first = values[..., :half]
    second = values[..., half:]
    return jnp.concatenate(
        [first * cos_part - second * sin_part, second * cos_part + first * sin_part], axis=-1
    )


def picture_ids(positions, starts):
    inside = (positions[None, :] >= starts[:, None]) & (positions[None, :] < starts[:, None] + PIC)
    labels = jnp.arange(1, NPIC + 1, dtype=jnp.int32)
    return jnp.sum(jnp.where(inside, labels[:, None], 0), axis=0)


def visible(positions, starts):
    ids = picture_ids(positions, starts)
    causal = positions[None, :] <= positions[:, None]
    same_piece = (ids[:, None] == ids[None, :]) & (ids[:, None] > 0)
    return causal | same_piece


def rms_scale(rows):
    return lax.rsqrt(jnp.mean(rows * rows, axis=-1, keepdims=True) + EPS)


def dot(left, right, contract):
    return lax.dot_general(
        left, right, ((contract[:1], contract[1:]), ((), ())), preferred_element_type=F32
    )


def nn(left, right):
    return dot(left, right, (1, 0))


def nt(left, right):
    return dot(left, right, (1, 1))


def tn(left, right):
    return dot(left, right, (0, 0))


MESH_ID = pl.DeviceIdType.MESH
SUB = 32


def plane_place():
    tp_at = lax.axis_index("tp")
    seq_at = lax.axis_index("seq")
    seq = lax.axis_size("seq")
    half = seq // 2
    far = lax.rem(seq_at + half, seq)
    mate = seq_at + 1 - 2 * lax.rem(seq_at, 2)
    far_mate = far + 1 - 2 * lax.rem(far, 2)
    return tp_at, seq_at, far, mate, far_mate


def at_device(tp_at, seq_at):
    return (lax.axis_index("rep"), tp_at, seq_at)


def enter(devices):
    barrier = pltpu.get_barrier_semaphore()
    for device in devices:
        pl.semaphore_signal(barrier, inc=1, device_id=device, device_id_type=MESH_ID)
    pl.semaphore_wait(barrier, len(devices))


def remote(src, dst, send, recv, device):
    return pltpu.make_async_remote_copy(
        src_ref=src,
        dst_ref=dst,
        send_sem=send,
        recv_sem=recv,
        device_id=device,
        device_id_type=MESH_ID,
    )


def gather_kernel(own_ref, all_ref, sends, recvs, local):
    tp_at, seq_at, far, mate, _ = plane_place()
    seq = lax.axis_size("seq")
    other = 1 - tp_at
    to_x = at_device(tp_at, far)
    to_y = at_device(other, seq_at)
    to_c = at_device(tp_at, mate)
    rows = own_ref.shape[0]
    part = rows // 2
    enter((to_x, to_y, to_c))

    def piece(t, s, h):
        return all_ref.at[t * seq + s, pl.ds(h * part, part)]

    def pass_on(i, t, s, h, device):
        copy = remote(piece(t, s, h), piece(t, s, h), sends.at[i], recvs.at[i], device)
        copy.start()
        return copy

    def own(i, h, device):
        copy = remote(
            own_ref.at[pl.ds(h * part, part)],
            piece(tp_at, seq_at, h),
            sends.at[i],
            recvs.at[i],
            device,
        )
        copy.start()
        return copy

    x0 = own(0, 0, to_x)
    y0 = own(1, 0, to_y)
    c0 = own(2, 0, to_c)
    x1 = own(3, 1, to_x)
    y1 = own(4, 1, to_y)
    c1 = own(5, 1, to_c)
    mine = pltpu.make_async_copy(own_ref, all_ref.at[tp_at * seq + seq_at], local)
    mine.start()
    x0.wait_recv()
    diag0 = pass_on(6, tp_at, far, 0, to_y)
    rx0 = pass_on(8, tp_at, far, 0, to_c)
    y0.wait_recv()
    ry0 = pass_on(9, other, seq_at, 0, to_c)
    y1.wait_recv()
    diag1 = pass_on(7, other, seq_at, 1, to_x)
    ry1 = pass_on(10, other, seq_at, 1, to_c)
    x1.wait_recv()
    rx1 = pass_on(11, tp_at, far, 1, to_c)
    diag0.wait_recv()
    rd0 = pass_on(12, other, far, 0, to_c)
    diag1.wait_recv()
    rd1 = pass_on(13, other, far, 1, to_c)
    for copy in (c0, c1, rx0, ry0, ry1, rx1, rd0, rd1):
        copy.wait_recv()
    for copy in (x0, y0, c0, x1, y1, c1, diag0, diag1, rx0, ry0, ry1, rx1, rd0, rd1):
        copy.wait_send()
    mine.wait()


def gather_plane(block, ident):
    rows, width = block.shape
    plane = lax.axis_size("tp") * lax.axis_size("seq")
    size = rows * width * 2
    gathered = pl.pallas_call(
        gather_kernel,
        out_shape=jax.ShapeDtypeStruct((plane, rows, width), block.dtype),
        in_specs=[pl.BlockSpec(memory_space=pltpu.VMEM)],
        out_specs=pl.BlockSpec(memory_space=pltpu.HBM),
        scratch_shapes=[
            pltpu.SemaphoreType.DMA((14,)),
            pltpu.SemaphoreType.DMA((14,)),
            pltpu.SemaphoreType.DMA,
        ],
        cost_estimate=pl.CostEstimate(
            flops=0, transcendentals=0, bytes_accessed=plane * size * 12
        ),
        compiler_params=pltpu.CompilerParams(collective_id=ident, has_side_effects=True),
        name="gather_plane",
    )(block)
    return gathered.reshape(plane * rows, width)


def add_rows(target, sources, start, count, kind):
    step = min(SUB, count)

    def body(i, carry):
        at = pl.ds(start + i * step, step)
        total = sources[0][at, :].astype(F32)
        for source in sources[1:]:
            total = total + source[at, :].astype(F32)
        target[at, :] = total.astype(kind)
        return carry

    lax.fori_loop(0, count // step, body, 0)


def scatter_stages(part_ref, sum_ref, held, chip_in, far_in, near_in, loads, sends, recvs):
    tp_at, seq_at, far, mate, far_mate = plane_place()
    seq = lax.axis_size("seq")
    other = 1 - tp_at
    to_x = at_device(tp_at, far)
    to_y = at_device(other, seq_at)
    to_c = at_device(tp_at, mate)
    rows = sum_ref.shape[0]
    part = rows // 2
    top, low = pl.ds(0, part), pl.ds(part, part)
    chips = ((other, far, far_mate), (tp_at, far, far_mate), (other, seq_at, mate), (tp_at, seq_at, mate))
    gives = [
        remote(part_ref.at[t * seq + m], chip_in.at[k], sends.at[k], recvs.at[k], to_c)
        for k, (t, s, m) in enumerate(chips)
    ]
    takes = [
        pltpu.make_async_copy(part_ref.at[t * seq + s], held.at[k], loads.at[k])
        for k, (t, s, m) in enumerate(chips)
    ]

    def hop(i, src, dst, device):
        return remote(src, dst, sends.at[i], recvs.at[i], device)

    d0 = hop(4, held.at[0, top], far_in.at[0, top], to_x)
    d1 = hop(5, held.at[0, low], far_in.at[1, low], to_y)
    x0 = hop(6, held.at[1, top], near_in.at[0, top], to_x)
    y1 = hop(7, held.at[2, low], near_in.at[1, low], to_y)
    y0 = hop(8, held.at[2, top], near_in.at[1, top], to_y)
    x1 = hop(9, held.at[1, low], near_in.at[0, low], to_x)

    def begin():
        enter((to_x, to_y, to_c))
        for give, take in zip(gives, takes):
            give.start()
            take.start()

    def chip_sum(k):
        takes[k].wait()
        gives[k].wait_recv()
        add_rows(held.at[k], (held.at[k], chip_in.at[k]), 0, rows, held.dtype)

    def diagonal():
        chip_sum(0)
        d0.start()
        d1.start()

    def along_x():
        chip_sum(1)
        x0.start()

    def along_y():
        chip_sum(2)
        y1.start()

    def own():
        chip_sum(3)

    def fold():
        d0.wait_recv()
        add_rows(held.at[2], (held.at[2], far_in.at[0]), 0, part, held.dtype)
        y0.start()
        d1.wait_recv()
        add_rows(held.at[1], (held.at[1], far_in.at[1]), part, part, held.dtype)
        x1.start()

    def finish():
        x0.wait_recv()
        y0.wait_recv()
        add_rows(sum_ref, (held.at[3], near_in.at[0], near_in.at[1]), 0, part, sum_ref.dtype)
        y1.wait_recv()
        x1.wait_recv()
        add_rows(sum_ref, (held.at[3], near_in.at[0], near_in.at[1]), part, part, sum_ref.dtype)
        for copy in gives + [d0, d1, x0, y1, y0, x1]:
            copy.wait_send()

    return begin, diagonal, along_x, along_y, own, fold, finish


def scatter_kernel(*refs):
    for stage in scatter_stages(*refs):
        stage()


def scatter_scratch(rows, width, kind):
    return [
        pltpu.VMEM((4, rows, width), kind),
        pltpu.VMEM((4, rows, width), kind),
        pltpu.VMEM((2, rows, width), kind),
        pltpu.VMEM((2, rows, width), kind),
        pltpu.SemaphoreType.DMA((4,)),
        pltpu.SemaphoreType.DMA((10,)),
        pltpu.SemaphoreType.DMA((10,)),
    ]


def scatter_plane(partial, ident):
    plane = lax.axis_size("tp") * lax.axis_size("seq")
    rows, width = partial.shape[0] // plane, partial.shape[1]
    kind = partial.dtype
    size = rows * width * 2
    return pl.pallas_call(
        scatter_kernel,
        out_shape=jax.ShapeDtypeStruct((rows, width), F32),
        in_specs=[pl.BlockSpec(memory_space=pltpu.HBM)],
        out_specs=pl.BlockSpec(memory_space=pltpu.VMEM),
        scratch_shapes=scatter_scratch(rows, width, kind),
        cost_estimate=pl.CostEstimate(
            flops=0, transcendentals=0, bytes_accessed=plane * size * 14
        ),
        compiler_params=pltpu.CompilerParams(
            collective_id=ident, has_side_effects=True, vmem_limit_bytes=32 << 20
        ),
        name="scatter_plane",
    )(partial.reshape(plane, rows, width))


def attn_back_kernel(
    starts_ref,
    q_ref,
    k_ref,
    v_ref,
    g_ref,
    log_ref,
    cos_ref,
    sin_ref,
    part_ref,
    grad_ref,
    sum_ref,
    bias,
    turned,
    keys_sum,
    values_sum,
    *scatter,
):
    begin, diagonal, along_x, along_y, own, fold, finish = scatter_stages(
        part_ref, sum_ref, *scatter
    )
    begin()
    total, dim = cos_ref.shape
    heads = q_ref.shape[1] // dim
    blocks = total // PIC
    scale = dim ** (-0.5)
    events = {(0, 1): diagonal, (0, 2): along_x, (0, 3): along_y, (1, 0): own, (2, 2): fold}

    def unturn(rows, at):
        return rows * cos_ref[at, :] + pltpu.roll(rows, dim // 2, 1) * sin_ref[at, :]

    def head_step(i, carry):
        t, h = i // heads, lax.rem(i, heads)
        base = pl.multiple_of(t * total, total)
        cols = pl.ds(pl.multiple_of(h * dim, dim), dim)

        @pl.when(h == 0)
        def _():
            turned[...] = k_ref[pl.ds(base, total), :].T
            keys_sum[...] = jnp.zeros(keys_sum.shape, F32)
            values_sum[...] = jnp.zeros(values_sum.shape, F32)
            for b in range(blocks):
                span = min(2 * PIC, total - b * PIC)
                k_at = lax.broadcasted_iota(jnp.int32, (span, PIC), 0) + b * PIC
                q_at = lax.broadcasted_iota(jnp.int32, (span, PIC), 1) + b * PIC
                high, below = jnp.maximum(k_at, q_at), jnp.minimum(k_at, q_at)
                allowed = k_at <= q_at
                for j in range(NPIC):
                    start = starts_ref[t, j]
                    allowed = allowed | ((below >= start) & (high < start + PIC))
                bias[b, :span, :] = jnp.where(allowed, 0.0, -jnp.inf)

        for b in range(blocks):
            at = pl.ds(pl.multiple_of(base + b * PIC, PIC), PIC)
            span = min(2 * PIC, total - b * PIC)
            count = b * PIC + span
            seen = pl.ds(base, count)
            queries, grads = q_ref[at, cols], g_ref[at, cols]
            scores = nt(k_ref[seen, :], queries) * scale - log_ref[i, :, b * PIC : (b + 1) * PIC]
            late = scores[b * PIC :] + bias[b, :span, :]
            scores = jnp.concatenate([scores[: b * PIC], late], axis=0) if b else late
            probs = jnp.exp(scores)
            prob_grad = nt(v_ref[seen, :], grads)
            mean = jnp.sum(probs * prob_grad, axis=0, keepdims=True)
            score_grad = (probs * (prob_grad - mean)).astype(BF)
            values_sum[:count, :] += nn(probs.astype(BF), grads)
            keys_sum[:count, :] += nn(score_grad, queries)
            back = nn(turned[:, :count], score_grad).T * scale
            grad_ref[at, cols] = unturn(back, pl.ds(b * PIC, PIC)).astype(BF)
            for (step, block), stage in events.items():
                if block == b:
                    pl.when(i == step)(stage)

        @pl.when(h == heads - 1)
        def _():
            rows = pl.ds(base, total)
            back = unturn(keys_sum[...] * scale, pl.ds(0, total))
            grad_ref[rows, heads * dim : (heads + 1) * dim] = back.astype(BF)
            grad_ref[rows, (heads + 1) * dim :] = values_sum[...].astype(BF)

        return carry

    lax.fori_loop(0, log_ref.shape[0], head_step, 0)
    finish()


def attn_back_plane(starts, queries, keys, values, grads, log_total, cos, sin, partial, ident):
    plane = lax.axis_size("tp") * lax.axis_size("seq")
    rows, width = partial.shape[0] // plane, partial.shape[1]
    total, dim = cos.shape
    tokens, q_part = queries.shape
    hbm = pl.BlockSpec(memory_space=pltpu.HBM)
    vmem = pl.BlockSpec(memory_space=pltpu.VMEM)
    smem = pl.BlockSpec(memory_space=pltpu.SMEM)
    return pl.pallas_call(
        attn_back_kernel,
        out_shape=(
            jax.ShapeDtypeStruct((tokens, q_part + 2 * dim), BF),
            jax.ShapeDtypeStruct((rows, width), F32),
        ),
        in_specs=[smem] + [vmem] * 7 + [hbm],
        out_specs=(vmem, vmem),
        scratch_shapes=[
            pltpu.VMEM((total // PIC, 2 * PIC, PIC), F32),
            pltpu.VMEM((dim, total), BF),
            pltpu.VMEM((total, dim), F32),
            pltpu.VMEM((total, dim), F32),
        ]
        + scatter_scratch(rows, width, partial.dtype),
        cost_estimate=pl.CostEstimate(
            flops=10 * tokens * total * q_part,
            transcendentals=tokens * total * q_part // dim,
            bytes_accessed=plane * rows * width * 28,
        ),
        compiler_params=pltpu.CompilerParams(
            collective_id=ident, has_side_effects=True, vmem_limit_bytes=50 << 20
        ),
        name="attn_back_plane",
    )(starts, queries, keys, values, grads, log_total, cos, sin, partial.reshape(plane, rows, width))


def exchange_kernel(in_ref, out_ref, stage, local, sends, recvs):
    tp_at, seq_at, _, _, _ = plane_place()
    seq = lax.axis_size("seq")
    plane = lax.axis_size("tp") * seq
    me = tp_at * seq + seq_at
    peers = [lax.rem(me + k, plane) for k in range(1, plane)]
    devices = [at_device(peer // seq, lax.rem(peer, seq)) for peer in peers]
    enter(devices)
    copies = []
    for k, (peer, device) in enumerate(zip(peers, devices)):
        copy = remote(in_ref.at[peer], out_ref.at[me], sends.at[k], recvs.at[k], device)
        copy.start()
        copies.append(copy)
    take = pltpu.make_async_copy(in_ref.at[me], stage, local.at[0])
    take.start()
    take.wait()
    put = pltpu.make_async_copy(stage, out_ref.at[me], local.at[1])
    put.start()
    for copy in copies:
        copy.wait()
    put.wait()


def exchange_plane(blocks, ident):
    plane, rows, width = blocks.shape
    size = plane * rows * width * 2
    return pl.pallas_call(
        exchange_kernel,
        out_shape=jax.ShapeDtypeStruct(blocks.shape, blocks.dtype),
        in_specs=[pl.BlockSpec(memory_space=pltpu.HBM)],
        out_specs=pl.BlockSpec(memory_space=pltpu.HBM),
        scratch_shapes=[
            pltpu.VMEM((rows, width), blocks.dtype),
            pltpu.SemaphoreType.DMA((2,)),
            pltpu.SemaphoreType.DMA((plane - 1,)),
            pltpu.SemaphoreType.DMA((plane - 1,)),
        ],
        cost_estimate=pl.CostEstimate(flops=0, transcendentals=0, bytes_accessed=size * 20),
        compiler_params=pltpu.CompilerParams(collective_id=ident, has_side_effects=True),
        name="exchange_plane",
    )(blocks)


def ffn_kernel(
    own_ref,
    grad_ref,
    weight_hbm,
    all_ref,
    inner_ref,
    gug_ref,
    out_ref,
    sum_ref,
    weight,
    tokens,
    grads,
    wide,
    narrow,
    inner,
    gug,
    part,
    chip_in,
    far_in,
    near_in,
    sends,
    recvs,
    local,
):
    tp_at, seq_at, far, mate, _ = plane_place()
    seq = lax.axis_size("seq")
    other = 1 - tp_at
    kind = lax.rem(seq_at, 2)
    to_x = at_device(tp_at, far)
    to_y = at_device(other, seq_at)
    to_c = at_device(tp_at, mate)
    rows, width = own_ref.shape
    pair = 2 * rows
    half = rows // 2
    ff_part = narrow.shape[1]
    gate_up, lower = slice(0, 2 * ff_part), slice(2 * ff_part, 3 * ff_part)
    top, low = pl.ds(0, half), pl.ds(half, half)
    enter((to_x, to_y, to_c))

    def piece(t, s, h):
        return all_ref.at[t * seq + s, pl.ds(h * half, half)]

    def own(i, h, device):
        return remote(
            own_ref.at[pl.ds(h * half, half)],
            piece(tp_at, seq_at, h),
            sends.at[i],
            recvs.at[i],
            device,
        )

    def relay(i, t, s, h, device):
        return remote(piece(t, s, h), piece(t, s, h), sends.at[i], recvs.at[i], device)

    x0, x1 = own(0, 0, to_x), own(3, 1, to_x)
    y0, y1 = own(1, 0, to_y), own(4, 1, to_y)
    c0, c1 = own(2, 0, to_c), own(5, 1, to_c)
    diag0 = relay(6, tp_at, far, 0, to_y)
    diag1 = relay(7, other, seq_at, 1, to_x)
    rx0, rx1 = relay(8, tp_at, far, 0, to_c), relay(11, tp_at, far, 1, to_c)
    ry0, ry1 = relay(9, other, seq_at, 0, to_c), relay(10, other, seq_at, 1, to_c)
    rd0, rd1 = relay(12, other, far, 0, to_c), relay(13, other, far, 1, to_c)

    def give(c):
        return remote(
            part.at[c, 1 - kind], chip_in.at[c], sends.at[14 + c], recvs.at[14 + c], to_c
        )

    def hop(i, src, dst, device):
        return remote(src, dst, sends.at[i], recvs.at[i], device)

    def held(c):
        return part.at[c, kind]

    sum_x0 = hop(18, part.at[1, kind, top], near_in.at[0, top], to_x)
    sum_y1 = hop(19, part.at[2, kind, low], near_in.at[1, low], to_y)
    sum_d0 = hop(20, part.at[3, kind, top], far_in.at[0, top], to_x)
    sum_d1 = hop(21, part.at[3, kind, low], far_in.at[1, low], to_y)
    sum_y0 = hop(22, part.at[2, kind, top], near_in.at[1, top], to_y)
    sum_x1 = hop(23, part.at[1, kind, low], near_in.at[0, low], to_x)

    def chip_sum(c):
        give(c).wait_recv()
        add_rows(held(c), (held(c), chip_in.at[c]), 0, rows, part.dtype)

    def chip_rows(c):
        t = lax.rem(tp_at + c // 2, 2)
        s = lax.rem(seq_at + (seq // 2) * lax.rem(c, 2), seq)
        return t * seq + s - lax.rem(s, 2)

    def take_tokens(c):
        return pltpu.make_async_copy(
            all_ref.at[pl.ds(chip_rows(c), 2)], tokens.at[lax.rem(c, 2)], local.at[lax.rem(c, 2)]
        )

    def take_grads(c):
        return pltpu.make_async_copy(
            grad_ref.at[pl.ds(chip_rows(c), 2)], grads.at[lax.rem(c, 2)], local.at[2 + lax.rem(c, 2)]
        )

    def put_gug(c):
        return pltpu.make_async_copy(
            gug.at[lax.rem(c, 2)], gug_ref.at[chip_rows(c) // 2], local.at[4 + lax.rem(c, 2)]
        )

    def put_inner(c):
        return pltpu.make_async_copy(
            inner.at[c], inner_ref.at[chip_rows(c) // 2], local.at[6 + c]
        )

    def put_out(c):
        return pltpu.make_async_copy(
            tokens.at[lax.rem(c, 2)], out_ref.at[pl.ds(chip_rows(c), 2)], local.at[10 + lax.rem(c, 2)]
        )

    take_weight = pltpu.make_async_copy(weight_hbm, weight, local.at[12])
    mine = pltpu.make_async_copy(own_ref, all_ref.at[tp_at * seq + seq_at], local.at[13])

    for copy in (x0, y0, c0, x1, y1, c1, mine, take_weight, take_grads(0)):
        copy.start()
    mine.wait()
    c0.wait_recv()
    c1.wait_recv()
    take_tokens(0).start()
    take_weight.wait()

    def after_load(c):
        @pl.when(c == 1)
        def _():
            ry0.wait_recv()
            ry1.wait_recv()
            take_tokens(2).start()
            chip_sum(0)

        @pl.when(c == 2)
        def _():
            rd0.wait_recv()
            rd1.wait_recv()
            take_tokens(3).start()
            chip_sum(1)
            sum_x0.start()

        @pl.when(c == 3)
        def _():
            chip_sum(2)
            sum_y1.start()

        @pl.when(c < 3)
        def _():
            take_grads(c + 1).start()

    def after_chip(c):
        @pl.when(c == 0)
        def _():
            x0.wait_recv()
            diag0.start()
            rx0.start()
            y0.wait_recv()
            ry0.start()
            y1.wait_recv()
            diag1.start()
            ry1.start()
            x1.wait_recv()
            rx1.start()
            rx0.wait_recv()
            rx1.wait_recv()
            take_tokens(1).start()

        @pl.when(c == 1)
        def _():
            diag0.wait_recv()
            rd0.start()
            diag1.wait_recv()
            rd1.start()

    def chip_step(c, carry):
        slot = lax.rem(c, 2)
        take_tokens(c).wait()
        wide[...] = nn(tokens[slot].reshape(pair, width), weight[:, gate_up])
        after_load(c)
        take_grads(c).wait()
        narrow[...] = nn(grads[slot].reshape(pair, width), weight[:, lower])

        @pl.when(c >= 2)
        def _():
            put_gug(c - 2).wait()

        def slopes(i, carry):
            at = pl.ds(i * SUB, SUB)
            gate, upward, grad = wide[at, :ff_part], wide[at, ff_part:], narrow[at, :]
            sigmoid_gate = jax.nn.sigmoid(gate)
            silu_gate = gate * sigmoid_gate
            inner[c, at, :] = (silu_gate * upward).astype(BF)
            slope = sigmoid_gate * (1.0 + gate * (1.0 - sigmoid_gate))
            gug[slot, at, :ff_part] = (grad * upward * slope).astype(BF)
            gug[slot, at, ff_part:] = (grad * silu_gate).astype(BF)
            return carry

        lax.fori_loop(0, pair // SUB, slopes, 0)
        put_gug(c).start()
        put_inner(c).start()
        block = width // 4

        def back(n, carry):
            at = pl.ds(pl.multiple_of(n * block, block), block)
            total = nt(gug[slot], weight[at, gate_up]).astype(part.dtype)
            part[c, :, :, at] = total.reshape(2, rows, block)
            return carry

        lax.fori_loop(0, 4, back, 0)
        give(c).start()
        after_chip(c)
        return carry

    lax.fori_loop(0, 4, chip_step, 0)

    def out_step(c, carry):
        slot = lax.rem(c, 2)

        @pl.when(c >= 2)
        def _():
            put_out(c - 2).wait()

        block = width // 4

        def out_block(n, carry):
            at = pl.ds(pl.multiple_of(n * block, block), block)
            total = nt(inner[c], weight[at, lower]).astype(tokens.dtype)
            tokens[slot, :, :, at] = total.reshape(2, rows, block)
            return carry

        lax.fori_loop(0, 4, out_block, 0)
        put_out(c).start()

        @pl.when(c == 0)
        def _():
            chip_sum(3)
            sum_d0.start()
            sum_d1.start()

        return carry

    lax.fori_loop(0, 4, out_step, 0)
    sum_d0.wait_recv()
    add_rows(held(2), (held(2), far_in.at[0]), 0, half, part.dtype)
    sum_y0.start()
    sum_d1.wait_recv()
    add_rows(held(1), (held(1), far_in.at[1]), half, half, part.dtype)
    sum_x1.start()
    sum_x0.wait_recv()
    sum_y0.wait_recv()
    add_rows(sum_ref, (held(0), near_in.at[0], near_in.at[1]), 0, half, sum_ref.dtype)
    sum_y1.wait_recv()
    sum_x1.wait_recv()
    add_rows(sum_ref, (held(0), near_in.at[0], near_in.at[1]), half, half, sum_ref.dtype)
    for copy in (x0, y0, c0, x1, y1, c1, diag0, diag1, rx0, ry0, ry1, rx1, rd0, rd1):
        copy.wait_send()
    for c in range(4):
        give(c).wait_send()
        put_inner(c).wait()
    for copy in (sum_x0, sum_y1, sum_d0, sum_d1, sum_y0, sum_x1):
        copy.wait_send()
    for c in (2, 3):
        put_gug(c).wait()
        put_out(c).wait()


def ffn_plane(block, grads, weight, ident):
    rows, width = block.shape
    seq = lax.axis_size("seq")
    plane = lax.axis_size("tp") * seq
    chips = plane // 2
    ff_part = weight.shape[1] // 3
    shape = jax.ShapeDtypeStruct
    hbm = pl.BlockSpec(memory_space=pltpu.HBM)
    vmem = pl.BlockSpec(memory_space=pltpu.VMEM)
    tokens = plane * rows
    return pl.pallas_call(
        ffn_kernel,
        out_shape=(
            shape((plane, rows, width), BF),
            shape((chips, 2 * rows, ff_part), BF),
            shape((chips, 2 * rows, 2 * ff_part), BF),
            shape((plane, rows, width), BF),
            shape((rows, width), F32),
        ),
        in_specs=[vmem, hbm, hbm],
        out_specs=(hbm, hbm, hbm, hbm, vmem),
        scratch_shapes=[
            pltpu.VMEM(weight.shape, BF),
            pltpu.VMEM((2, 2, rows, width), BF),
            pltpu.VMEM((2, 2, rows, width), BF),
            pltpu.VMEM((2 * rows, 2 * ff_part), F32),
            pltpu.VMEM((2 * rows, ff_part), F32),
            pltpu.VMEM((4, 2 * rows, ff_part), BF),
            pltpu.VMEM((2, 2 * rows, 2 * ff_part), BF),
            pltpu.VMEM((4, 2, rows, width), BF),
            pltpu.VMEM((4, rows, width), BF),
            pltpu.VMEM((2, rows, width), BF),
            pltpu.VMEM((2, rows, width), BF),
            pltpu.SemaphoreType.DMA((24,)),
            pltpu.SemaphoreType.DMA((24,)),
            pltpu.SemaphoreType.DMA((14,)),
        ],
        cost_estimate=pl.CostEstimate(
            flops=12 * tokens * width * ff_part,
            transcendentals=tokens * ff_part,
            bytes_accessed=30 * tokens * width,
        ),
        compiler_params=pltpu.CompilerParams(
            collective_id=ident, has_side_effects=True, vmem_limit_bytes=60 << 20
        ),
        name="ffn_plane",
    )(block, grads, weight)


def finish_kernel(
    gu_ref,
    down_ref,
    gate_weight,
    up_weight,
    gain_ref,
    gate_out,
    up_out,
    down_out,
    gain_out,
    gu_in,
    down_in,
    local,
    sends,
    recvs,
):
    tp_at, seq_at, _, _, _ = plane_place()
    seq = lax.axis_size("seq")
    plane = lax.axis_size("tp") * seq
    me = tp_at * seq + seq_at
    peers = [lax.rem(me + k, plane) for k in range(1, plane)]
    devices = [at_device(peer // seq, lax.rem(peer, seq)) for peer in peers]
    enter(devices)
    copies = []
    for k, (peer, device) in enumerate(zip(peers, devices)):
        copies.append(remote(gu_ref.at[peer], gu_in.at[me], sends.at[k], recvs.at[k], device))
        i = plane - 1 + k
        copies.append(remote(down_ref.at[peer], down_in.at[me], sends.at[i], recvs.at[i], device))
    copies.append(pltpu.make_async_copy(gu_ref.at[me], gu_in.at[me], local.at[0]))
    copies.append(pltpu.make_async_copy(down_ref.at[me], down_in.at[me], local.at[1]))
    for copy in copies:
        copy.start()
    for copy in copies:
        copy.wait()
    put = pltpu.make_async_copy(down_in, down_out, local.at[2])
    put.start()
    gain = gain_ref[...]
    ff_part = down_in.shape[2]
    total = jnp.zeros(gain.shape, F32)
    for j in range(plane):
        at = slice(j * ff_part, (j + 1) * ff_part)
        for k, (out, weight) in enumerate(((gate_out, gate_weight), (up_out, up_weight))):
            own = gu_in[j, :, k * ff_part : (k + 1) * ff_part].astype(F32)
            out[:, at] = own * gain
            total = total + jnp.sum(own * weight[:, at].astype(F32), axis=1, keepdims=True)
    gain_out[...] = total
    put.wait()


def finish_plane(gu_sums, down_sums, gate_weight, up_weight, gain, ident):
    plane, rows, ff_part = down_sums.shape
    shape = jax.ShapeDtypeStruct
    hbm = pl.BlockSpec(memory_space=pltpu.HBM)
    vmem = pl.BlockSpec(memory_space=pltpu.VMEM)
    size = plane * rows * ff_part * 6
    return pl.pallas_call(
        finish_kernel,
        out_shape=(
            shape(gate_weight.shape, F32),
            shape(up_weight.shape, F32),
            shape(down_sums.shape, BF),
            shape((rows, 1), F32),
        ),
        in_specs=[hbm, hbm, vmem, vmem, vmem],
        out_specs=(vmem, vmem, hbm, vmem),
        scratch_shapes=[
            pltpu.VMEM(gu_sums.shape, BF),
            pltpu.VMEM(down_sums.shape, BF),
            pltpu.SemaphoreType.DMA((3,)),
            pltpu.SemaphoreType.DMA((2 * plane - 2,)),
            pltpu.SemaphoreType.DMA((2 * plane - 2,)),
        ],
        cost_estimate=pl.CostEstimate(flops=0, transcendentals=0, bytes_accessed=size * 20),
        compiler_params=pltpu.CompilerParams(
            collective_id=ident, has_side_effects=True, vmem_limit_bytes=24 << 20
        ),
        name="finish_plane",
    )(gu_sums, down_sums, gate_weight, up_weight, gain)


def columns(matrix, parts):
    rows, cols = matrix.shape
    return jnp.transpose(matrix.reshape(rows, parts, cols // parts), (1, 0, 2))


def uncolumns(blocks):
    parts, rows, cols = blocks.shape
    return jnp.transpose(blocks, (1, 0, 2)).reshape(rows, parts * cols)


def after(value, *earlier):
    return lax.optimization_barrier((value,) + earlier)[0]


def per_device(
    layer_input,
    pic_starts,
    skip_mask,
    gain_attn,
    w_query,
    w_key,
    w_value,
    w_out,
    gain_ffn,
    w_gate,
    w_up,
    w_down,
    cotangent,
):
    _, local_len, width = layer_input.shape
    seq = lax.axis_size("seq")
    plane = lax.axis_size("tp") * seq
    total_len = local_len * seq
    heads = H // plane
    share = plane // KV
    ff_part = w_gate.shape[1] // plane
    q_part = heads * DH
    scale = DH ** (-0.5)

    gain1 = gain_attn[:, None]
    gain2 = gain_ffn[:, None]
    wq32, wk32, wv32 = w_query.astype(F32), w_key.astype(F32), w_value.astype(F32)
    wg32, wu32 = w_gate.astype(F32), w_up.astype(F32)
    attn_pack = jnp.concatenate(
        [
            columns((wq32 * gain1).astype(BF), plane),
            jnp.repeat(columns((wk32 * gain1).astype(BF), KV), share, axis=0),
            jnp.repeat(columns((wv32 * gain1).astype(BF), KV), share, axis=0),
            columns(w_out.T, plane),
        ],
        axis=2,
    )
    attn_rows = exchange_plane(attn_pack, 0)
    attn_rows = attn_rows.reshape(-1, attn_rows.shape[2])
    attn_weight = lax.all_gather(attn_rows, "rep", axis=0, tiled=True)
    qkv_weight = attn_weight[:, : q_part + 2 * DH]
    out_weight = attn_weight[:, q_part + 2 * DH :]

    tokens = layer_input.reshape(local_len, width).astype(F32)
    keep = (1 - skip_mask).astype(F32).reshape(local_len, 1)
    upstream = cotangent.reshape(local_len, width).astype(F32)
    scale1 = rms_scale(tokens)
    norm1 = tokens * scale1

    ffn_pack = jnp.concatenate(
        [
            columns((wg32 * gain2).astype(BF), plane),
            columns((wu32 * gain2).astype(BF), plane),
            columns(w_down.T, plane),
        ],
        axis=2,
    )
    ffn_rows = exchange_plane(after(ffn_pack, attn_rows), 2)
    ffn_rows = ffn_rows.reshape(-1, ffn_rows.shape[2])
    ffn_weight = lax.all_gather(ffn_rows, "rep", axis=0, tiled=True)
    norm1_all = gather_plane(after(norm1.astype(BF), ffn_rows), 1)
    ffn_grad = gather_plane(after((keep * upstream).astype(BF), norm1_all), 3)

    other_starts = lax.ppermute(pic_starts, "tp", [(0, 1), (1, 0)])
    starts = jnp.where(
        lax.axis_index("tp") == 0,
        jnp.concatenate([pic_starts, other_starts], axis=0),
        jnp.concatenate([other_starts, pic_starts], axis=0),
    )
    positions = jnp.arange(total_len, dtype=jnp.int32)
    cos_table, sin_table = rotary_tables(positions, DH)
    allowed = jax.vmap(visible, (None, 0))(positions, starts)[:, None]
    turn = jax.vmap(rotate, (0, None, None))

    projected = nn(norm1_all, qkv_weight).reshape(TP, total_len, q_part + 2 * DH)
    queries = turn(
        projected[..., :q_part].reshape(TP, total_len, heads, DH), cos_table, sin_table
    ).astype(BF)
    keys = turn(projected[..., q_part : q_part + DH], cos_table, sin_table).astype(BF)
    values = projected[..., q_part + DH :].astype(BF)
    scores = jnp.einsum("tqhd,tkd->thqk", queries, keys, preferred_element_type=F32) * scale
    scores = jnp.where(allowed, scores, -jnp.inf)
    peak = jnp.max(scores, axis=-1, keepdims=True)
    log_total = peak + jnp.log(jnp.sum(jnp.exp(scores - peak), axis=-1, keepdims=True))
    probs = jnp.exp(scores - log_total)
    probs_low = probs.astype(BF)
    mixed = jnp.einsum("thqk,tkd->tqhd", probs_low, values, preferred_element_type=F32)
    mixed = mixed.astype(BF).reshape(TP * total_len, q_part)
    branch = scatter_plane(nt(mixed, out_weight).astype(BF), 4)
    hidden = tokens + keep * branch

    scale2 = rms_scale(hidden)
    norm2 = hidden * scale2
    norm2_all, inner, gate_up_grad, out_partial, scaled2 = ffn_plane(
        norm2.astype(BF), ffn_grad.reshape(plane, local_len, width), ffn_weight, 5
    )
    norm2_all = norm2_all.reshape(-1, width)
    inner = inner.reshape(-1, ff_part)
    gate_up_grad = gate_up_grad.reshape(-1, 2 * ff_part)
    down_partial = tn(ffn_grad, inner).astype(BF)
    down_sums = lax.psum_scatter(down_partial, "rep", scatter_dimension=0, tiled=True)
    gu_partial = tn(norm2_all, after(gate_up_grad, down_partial)).astype(BF)
    gu_sums = lax.psum_scatter(gu_partial, "rep", scatter_dimension=0, tiled=True)
    hidden_grad = upstream + scale2 * (
        scaled2 - norm2 * jnp.mean(scaled2 * norm2, axis=-1, keepdims=True)
    )

    branch_grad = gather_plane(after((keep * hidden_grad).astype(BF), gu_partial, down_partial), 7)
    mixed_grad = nn(branch_grad, out_weight).astype(BF)
    qkv_grad, ffn_out = attn_back_plane(
        starts,
        queries.reshape(-1, q_part),
        keys.reshape(-1, DH),
        values.reshape(-1, DH),
        mixed_grad,
        log_total.reshape(TP * heads, 1, total_len),
        jnp.concatenate([cos_table, cos_table], axis=1),
        jnp.concatenate([sin_table, -sin_table], axis=1),
        out_partial.reshape(-1, width),
        9,
    )
    attn_partial = jnp.concatenate(
        [tn(norm1_all, qkv_grad).astype(BF), tn(branch_grad, mixed).astype(BF)], axis=1
    )
    scaled1_partial = nt(qkv_grad, qkv_weight).astype(BF)
    attn_partial = after(attn_partial, gu_sums, down_sums, scaled1_partial)
    attn_sums = lax.psum_scatter(attn_partial, "rep", scatter_dimension=0, tiled=True)
    scaled1 = scatter_plane(after(scaled1_partial, attn_partial), 8)
    input_grad = hidden_grad + scale1 * (
        scaled1 - norm1 * jnp.mean(scaled1 * norm1, axis=-1, keepdims=True)
    )
    out_hidden = (hidden + keep * ffn_out).astype(BF)

    gate_grad, up_grad, down_own, gain_ffn_grad = finish_plane(
        after(gu_sums.reshape(plane, -1, 2 * ff_part), scaled1),
        down_sums.reshape(plane, -1, ff_part),
        w_gate,
        w_up,
        gain2,
        10,
    )
    down_grad = jnp.transpose(down_own, (0, 2, 1)).reshape(plane * ff_part, -1).astype(F32)

    attn_own = exchange_plane(attn_sums.reshape(plane, -1, attn_sums.shape[1]), 11).astype(F32)
    query_own = uncolumns(attn_own[:, :, :q_part])
    kv_own = attn_own[:, :, q_part : q_part + 2 * DH]
    kv_own = jnp.sum(kv_own.reshape(KV, share, -1, 2 * DH), axis=1)
    key_own = uncolumns(kv_own[:, :, :DH])
    value_own = uncolumns(kv_own[:, :, DH:])
    out_own = uncolumns(attn_own[:, :, q_part + 2 * DH :])
    gain_attn_grad = (
        jnp.sum(query_own * wq32, axis=1)
        + jnp.sum(key_own * wk32, axis=1)
        + jnp.sum(value_own * wv32, axis=1)
    )
    return (
        out_hidden[None],
        input_grad[None],
        gain_attn_grad,
        query_own * gain1,
        key_own * gain1,
        value_own * gain1,
        out_own.T,
        gain_ffn_grad[:, 0],
        gate_grad,
        up_grad,
        down_grad,
    )


def solution(mesh):
    devices = mesh.devices
    dp, seq = devices.shape
    inner = Mesh(devices.reshape(dp // TP, TP, seq), ("rep", "tp", "seq"))
    dps = ("rep", "tp")
    every = ("rep", "tp", "seq")
    token = P(dps, "seq", None)
    row = P(every, None)
    col = P(None, every)
    return jax.shard_map(
        per_device,
        mesh=inner,
        in_specs=(
            token,
            P(dps, None),
            P(dps, "seq"),
            P(every),
            row,
            row,
            row,
            col,
            P(every),
            row,
            row,
            col,
            token,
        ),
        out_specs=(token, token, P(every), row, row, row, col, P(every), row, row, col),
        check_vma=False,
    )
```

```python
import jax
import jax.numpy as jnp
from jax import lax
from jax.experimental import pallas as pl
from jax.experimental.pallas import tpu as pltpu
from jax.sharding import Mesh
from jax.sharding import PartitionSpec as P

H = 16
KV = 4
DH = 128
PIC = 256
NPIC = 2
EPS = 1e-05
TP = 2
BF = jnp.bfloat16
F32 = jnp.float32


def rotary_tables(positions, head_dim):
    half_dim = head_dim // 2
    inverse = 10000.0 ** (-(jnp.arange(half_dim, dtype=F32) * 2.0 / head_dim))
    angles = positions.astype(F32)[:, None] * inverse[None, :]
    return (jnp.cos(angles), jnp.sin(angles))


def rotate(values, cos_table, sin_table):
    half = values.shape[-1] // 2
    shape = (cos_table.shape[0],) + (1,) * (values.ndim - 2) + (half,)
    cos_part = cos_table.reshape(shape)
    sin_part = sin_table.reshape(shape)
    first = values[..., :half]
    second = values[..., half:]
    return jnp.concatenate(
        [first * cos_part - second * sin_part, second * cos_part + first * sin_part], axis=-1
    )


def picture_ids(positions, starts):
    inside = (positions[None, :] >= starts[:, None]) & (positions[None, :] < starts[:, None] + PIC)
    labels = jnp.arange(1, NPIC + 1, dtype=jnp.int32)
    return jnp.sum(jnp.where(inside, labels[:, None], 0), axis=0)


def visible(positions, starts):
    ids = picture_ids(positions, starts)
    causal = positions[None, :] <= positions[:, None]
    same_piece = (ids[:, None] == ids[None, :]) & (ids[:, None] > 0)
    return causal | same_piece


def rms_scale(rows):
    return lax.rsqrt(jnp.mean(rows * rows, axis=-1, keepdims=True) + EPS)


def dot(left, right, contract):
    return lax.dot_general(
        left, right, ((contract[:1], contract[1:]), ((), ())), preferred_element_type=F32
    )


def nn(left, right):
    return dot(left, right, (1, 0))


def nt(left, right):
    return dot(left, right, (1, 1))


def tn(left, right):
    return dot(left, right, (0, 0))


MESH_ID = pl.DeviceIdType.MESH
SUB = 32


def plane_place():
    tp_at = lax.axis_index("tp")
    seq_at = lax.axis_index("seq")
    seq = lax.axis_size("seq")
    half = seq // 2
    far = lax.rem(seq_at + half, seq)
    mate = seq_at + 1 - 2 * lax.rem(seq_at, 2)
    far_mate = far + 1 - 2 * lax.rem(far, 2)
    return tp_at, seq_at, far, mate, far_mate


def at_device(tp_at, seq_at):
    return (lax.axis_index("rep"), tp_at, seq_at)


def enter(devices):
    barrier = pltpu.get_barrier_semaphore()
    for device in devices:
        pl.semaphore_signal(barrier, inc=1, device_id=device, device_id_type=MESH_ID)
    pl.semaphore_wait(barrier, len(devices))


def remote(src, dst, send, recv, device):
    return pltpu.make_async_remote_copy(
        src_ref=src,
        dst_ref=dst,
        send_sem=send,
        recv_sem=recv,
        device_id=device,
        device_id_type=MESH_ID,
    )


def gather_kernel(own_ref, all_ref, sends, recvs, local):
    tp_at, seq_at, far, mate, _ = plane_place()
    seq = lax.axis_size("seq")
    other = 1 - tp_at
    to_x = at_device(tp_at, far)
    to_y = at_device(other, seq_at)
    to_c = at_device(tp_at, mate)
    rows = own_ref.shape[0]
    part = rows // 2
    enter((to_x, to_y, to_c))

    def piece(t, s, h):
        return all_ref.at[t * seq + s, pl.ds(h * part, part)]

    def pass_on(i, t, s, h, device):
        copy = remote(piece(t, s, h), piece(t, s, h), sends.at[i], recvs.at[i], device)
        copy.start()
        return copy

    def own(i, h, device):
        copy = remote(
            own_ref.at[pl.ds(h * part, part)],
            piece(tp_at, seq_at, h),
            sends.at[i],
            recvs.at[i],
            device,
        )
        copy.start()
        return copy

    x0 = own(0, 0, to_x)
    y0 = own(1, 0, to_y)
    c0 = own(2, 0, to_c)
    x1 = own(3, 1, to_x)
    y1 = own(4, 1, to_y)
    c1 = own(5, 1, to_c)
    mine = pltpu.make_async_copy(own_ref, all_ref.at[tp_at * seq + seq_at], local)
    mine.start()
    x0.wait_recv()
    diag0 = pass_on(6, tp_at, far, 0, to_y)
    rx0 = pass_on(8, tp_at, far, 0, to_c)
    y0.wait_recv()
    ry0 = pass_on(9, other, seq_at, 0, to_c)
    y1.wait_recv()
    diag1 = pass_on(7, other, seq_at, 1, to_x)
    ry1 = pass_on(10, other, seq_at, 1, to_c)
    x1.wait_recv()
    rx1 = pass_on(11, tp_at, far, 1, to_c)
    diag0.wait_recv()
    rd0 = pass_on(12, other, far, 0, to_c)
    diag1.wait_recv()
    rd1 = pass_on(13, other, far, 1, to_c)
    for copy in (c0, c1, rx0, ry0, ry1, rx1, rd0, rd1):
        copy.wait_recv()
    for copy in (x0, y0, c0, x1, y1, c1, diag0, diag1, rx0, ry0, ry1, rx1, rd0, rd1):
        copy.wait_send()
    mine.wait()


def gather_plane(block, ident):
    rows, width = block.shape
    plane = lax.axis_size("tp") * lax.axis_size("seq")
    size = rows * width * 2
    gathered = pl.pallas_call(
        gather_kernel,
        out_shape=jax.ShapeDtypeStruct((plane, rows, width), block.dtype),
        in_specs=[pl.BlockSpec(memory_space=pltpu.VMEM)],
        out_specs=pl.BlockSpec(memory_space=pltpu.HBM),
        scratch_shapes=[
            pltpu.SemaphoreType.DMA((14,)),
            pltpu.SemaphoreType.DMA((14,)),
            pltpu.SemaphoreType.DMA,
        ],
        cost_estimate=pl.CostEstimate(
            flops=0, transcendentals=0, bytes_accessed=plane * size * 12
        ),
        compiler_params=pltpu.CompilerParams(collective_id=ident, has_side_effects=True),
        name="gather_plane",
    )(block)
    return gathered.reshape(plane * rows, width)


def add_rows(target, sources, start, count, kind):
    step = min(SUB, count)

    def body(i, carry):
        at = pl.ds(start + i * step, step)
        total = sources[0][at, :].astype(F32)
        for source in sources[1:]:
            total = total + source[at, :].astype(F32)
        target[at, :] = total.astype(kind)
        return carry

    lax.fori_loop(0, count // step, body, 0)


def scatter_stages(part_ref, sum_ref, held, chip_in, far_in, near_in, loads, sends, recvs):
    tp_at, seq_at, far, mate, far_mate = plane_place()
    seq = lax.axis_size("seq")
    other = 1 - tp_at
    to_x = at_device(tp_at, far)
    to_y = at_device(other, seq_at)
    to_c = at_device(tp_at, mate)
    rows = sum_ref.shape[0]
    part = rows // 2
    top, low = pl.ds(0, part), pl.ds(part, part)
    chips = ((other, far, far_mate), (tp_at, far, far_mate), (other, seq_at, mate), (tp_at, seq_at, mate))
    gives = [
        remote(part_ref.at[t * seq + m], chip_in.at[k], sends.at[k], recvs.at[k], to_c)
        for k, (t, s, m) in enumerate(chips)
    ]
    takes = [
        pltpu.make_async_copy(part_ref.at[t * seq + s], held.at[k], loads.at[k])
        for k, (t, s, m) in enumerate(chips)
    ]

    def hop(i, src, dst, device):
        return remote(src, dst, sends.at[i], recvs.at[i], device)

    d0 = hop(4, held.at[0, top], far_in.at[0, top], to_x)
    d1 = hop(5, held.at[0, low], far_in.at[1, low], to_y)
    x0 = hop(6, held.at[1, top], near_in.at[0, top], to_x)
    y1 = hop(7, held.at[2, low], near_in.at[1, low], to_y)
    y0 = hop(8, held.at[2, top], near_in.at[1, top], to_y)
    x1 = hop(9, held.at[1, low], near_in.at[0, low], to_x)

    def begin():
        enter((to_x, to_y, to_c))
        for give, take in zip(gives, takes):
            give.start()
            take.start()

    def chip_sum(k):
        takes[k].wait()
        gives[k].wait_recv()
        add_rows(held.at[k], (held.at[k], chip_in.at[k]), 0, rows, held.dtype)

    def diagonal():
        chip_sum(0)
        d0.start()
        d1.start()

    def along_x():
        chip_sum(1)
        x0.start()

    def along_y():
        chip_sum(2)
        y1.start()

    def own():
        chip_sum(3)

    def fold():
        d0.wait_recv()
        add_rows(held.at[2], (held.at[2], far_in.at[0]), 0, part, held.dtype)
        y0.start()
        d1.wait_recv()
        add_rows(held.at[1], (held.at[1], far_in.at[1]), part, part, held.dtype)
        x1.start()

    def finish():
        x0.wait_recv()
        y0.wait_recv()
        add_rows(sum_ref, (held.at[3], near_in.at[0], near_in.at[1]), 0, part, sum_ref.dtype)
        y1.wait_recv()
        x1.wait_recv()
        add_rows(sum_ref, (held.at[3], near_in.at[0], near_in.at[1]), part, part, sum_ref.dtype)
        for copy in gives + [d0, d1, x0, y1, y0, x1]:
            copy.wait_send()

    return begin, diagonal, along_x, along_y, own, fold, finish


def scatter_kernel(*refs):
    for stage in scatter_stages(*refs):
        stage()


def scatter_scratch(rows, width, kind):
    return [
        pltpu.VMEM((4, rows, width), kind),
        pltpu.VMEM((4, rows, width), kind),
        pltpu.VMEM((2, rows, width), kind),
        pltpu.VMEM((2, rows, width), kind),
        pltpu.SemaphoreType.DMA((4,)),
        pltpu.SemaphoreType.DMA((10,)),
        pltpu.SemaphoreType.DMA((10,)),
    ]


def scatter_plane(partial, ident):
    plane = lax.axis_size("tp") * lax.axis_size("seq")
    rows, width = partial.shape[0] // plane, partial.shape[1]
    kind = partial.dtype
    size = rows * width * 2
    return pl.pallas_call(
        scatter_kernel,
        out_shape=jax.ShapeDtypeStruct((rows, width), F32),
        in_specs=[pl.BlockSpec(memory_space=pltpu.HBM)],
        out_specs=pl.BlockSpec(memory_space=pltpu.VMEM),
        scratch_shapes=scatter_scratch(rows, width, kind),
        cost_estimate=pl.CostEstimate(
            flops=0, transcendentals=0, bytes_accessed=plane * size * 14
        ),
        compiler_params=pltpu.CompilerParams(
            collective_id=ident, has_side_effects=True, vmem_limit_bytes=32 << 20
        ),
        name="scatter_plane",
    )(partial.reshape(plane, rows, width))


def attn_back_kernel(
    starts_ref,
    q_ref,
    k_ref,
    v_ref,
    g_ref,
    log_ref,
    cos_ref,
    sin_ref,
    part_ref,
    grad_ref,
    sum_ref,
    bias,
    turned,
    keys_sum,
    values_sum,
    *scatter,
):
    begin, diagonal, along_x, along_y, own, fold, finish = scatter_stages(
        part_ref, sum_ref, *scatter
    )
    begin()
    total, dim = cos_ref.shape
    heads = q_ref.shape[1] // dim
    blocks = total // PIC
    scale = dim ** (-0.5)
    events = {(0, 1): diagonal, (0, 2): along_x, (0, 3): along_y, (1, 0): own, (2, 2): fold}

    def unturn(rows, at):
        return rows * cos_ref[at, :] + pltpu.roll(rows, dim // 2, 1) * sin_ref[at, :]

    def head_step(i, carry):
        t, h = i // heads, lax.rem(i, heads)
        base = pl.multiple_of(t * total, total)
        cols = pl.ds(pl.multiple_of(h * dim, dim), dim)

        @pl.when(h == 0)
        def _():
            turned[...] = k_ref[pl.ds(base, total), :].T
            keys_sum[...] = jnp.zeros(keys_sum.shape, F32)
            values_sum[...] = jnp.zeros(values_sum.shape, F32)
            for b in range(blocks):
                span = min(2 * PIC, total - b * PIC)
                k_at = lax.broadcasted_iota(jnp.int32, (span, PIC), 0) + b * PIC
                q_at = lax.broadcasted_iota(jnp.int32, (span, PIC), 1) + b * PIC
                high, below = jnp.maximum(k_at, q_at), jnp.minimum(k_at, q_at)
                allowed = k_at <= q_at
                for j in range(NPIC):
                    start = starts_ref[t, j]
                    allowed = allowed | ((below >= start) & (high < start + PIC))
                bias[b, :span, :] = jnp.where(allowed, 0.0, -jnp.inf)

        for b in range(blocks):
            at = pl.ds(pl.multiple_of(base + b * PIC, PIC), PIC)
            span = min(2 * PIC, total - b * PIC)
            count = b * PIC + span
            seen = pl.ds(base, count)
            queries, grads = q_ref[at, cols], g_ref[at, cols]
            scores = nt(k_ref[seen, :], queries) * scale - log_ref[i, :, b * PIC : (b + 1) * PIC]
            late = scores[b * PIC :] + bias[b, :span, :]
            scores = jnp.concatenate([scores[: b * PIC], late], axis=0) if b else late
            probs = jnp.exp(scores)
            prob_grad = nt(v_ref[seen, :], grads)
            mean = jnp.sum(probs * prob_grad, axis=0, keepdims=True)
            score_grad = (probs * (prob_grad - mean)).astype(BF)
            values_sum[:count, :] += nn(probs.astype(BF), grads)
            keys_sum[:count, :] += nn(score_grad, queries)
            back = nn(turned[:, :count], score_grad).T * scale
            grad_ref[at, cols] = unturn(back, pl.ds(b * PIC, PIC)).astype(BF)
            for (step, block), stage in events.items():
                if block == b:
                    pl.when(i == step)(stage)

        @pl.when(h == heads - 1)
        def _():
            rows = pl.ds(base, total)
            back = unturn(keys_sum[...] * scale, pl.ds(0, total))
            grad_ref[rows, heads * dim : (heads + 1) * dim] = back.astype(BF)
            grad_ref[rows, (heads + 1) * dim :] = values_sum[...].astype(BF)

        return carry

    lax.fori_loop(0, log_ref.shape[0], head_step, 0)
    finish()


def attn_back_plane(starts, queries, keys, values, grads, log_total, cos, sin, partial, ident):
    plane = lax.axis_size("tp") * lax.axis_size("seq")
    rows, width = partial.shape[0] // plane, partial.shape[1]
    total, dim = cos.shape
    tokens, q_part = queries.shape
    hbm = pl.BlockSpec(memory_space=pltpu.HBM)
    vmem = pl.BlockSpec(memory_space=pltpu.VMEM)
    smem = pl.BlockSpec(memory_space=pltpu.SMEM)
    return pl.pallas_call(
        attn_back_kernel,
        out_shape=(
            jax.ShapeDtypeStruct((tokens, q_part + 2 * dim), BF),
            jax.ShapeDtypeStruct((rows, width), F32),
        ),
        in_specs=[smem] + [vmem] * 7 + [hbm],
        out_specs=(vmem, vmem),
        scratch_shapes=[
            pltpu.VMEM((total // PIC, 2 * PIC, PIC), F32),
            pltpu.VMEM((dim, total), BF),
            pltpu.VMEM((total, dim), F32),
            pltpu.VMEM((total, dim), F32),
        ]
        + scatter_scratch(rows, width, partial.dtype),
        cost_estimate=pl.CostEstimate(
            flops=10 * tokens * total * q_part,
            transcendentals=tokens * total * q_part // dim,
            bytes_accessed=plane * rows * width * 28,
        ),
        compiler_params=pltpu.CompilerParams(
            collective_id=ident, has_side_effects=True, vmem_limit_bytes=50 << 20
        ),
        name="attn_back_plane",
    )(starts, queries, keys, values, grads, log_total, cos, sin, partial.reshape(plane, rows, width))


def exchange_kernel(in_ref, out_ref, stage, local, sends, recvs):
    tp_at, seq_at, _, _, _ = plane_place()
    seq = lax.axis_size("seq")
    plane = lax.axis_size("tp") * seq
    me = tp_at * seq + seq_at
    peers = [lax.rem(me + k, plane) for k in range(1, plane)]
    devices = [at_device(peer // seq, lax.rem(peer, seq)) for peer in peers]
    enter(devices)
    copies = []
    for k, (peer, device) in enumerate(zip(peers, devices)):
        copy = remote(in_ref.at[peer], out_ref.at[me], sends.at[k], recvs.at[k], device)
        copy.start()
        copies.append(copy)
    take = pltpu.make_async_copy(in_ref.at[me], stage, local.at[0])
    take.start()
    take.wait()
    put = pltpu.make_async_copy(stage, out_ref.at[me], local.at[1])
    put.start()
    for copy in copies:
        copy.wait()
    put.wait()


def exchange_plane(blocks, ident):
    plane, rows, width = blocks.shape
    size = plane * rows * width * 2
    return pl.pallas_call(
        exchange_kernel,
        out_shape=jax.ShapeDtypeStruct(blocks.shape, blocks.dtype),
        in_specs=[pl.BlockSpec(memory_space=pltpu.HBM)],
        out_specs=pl.BlockSpec(memory_space=pltpu.HBM),
        scratch_shapes=[
            pltpu.VMEM((rows, width), blocks.dtype),
            pltpu.SemaphoreType.DMA((2,)),
            pltpu.SemaphoreType.DMA((plane - 1,)),
            pltpu.SemaphoreType.DMA((plane - 1,)),
        ],
        cost_estimate=pl.CostEstimate(flops=0, transcendentals=0, bytes_accessed=size * 20),
        compiler_params=pltpu.CompilerParams(collective_id=ident, has_side_effects=True),
        name="exchange_plane",
    )(blocks)


def ffn_kernel(
    own_ref,
    grad_ref,
    weight_hbm,
    all_ref,
    gug_ref,
    out_ref,
    down_ref,
    sum_ref,
    weight,
    tokens,
    grads,
    wide,
    narrow,
    inner,
    gug,
    stage,
    part,
    chip_in,
    far_in,
    near_in,
    sends,
    recvs,
    local,
):
    tp_at, seq_at, far, mate, _ = plane_place()
    seq = lax.axis_size("seq")
    other = 1 - tp_at
    kind = lax.rem(seq_at, 2)
    to_x = at_device(tp_at, far)
    to_y = at_device(other, seq_at)
    to_c = at_device(tp_at, mate)
    rows, width = own_ref.shape
    pair = 2 * rows
    half = rows // 2
    block = width // 4
    ff_part = narrow.shape[2]
    gate_up, lower = slice(0, 2 * ff_part), slice(2 * ff_part, 3 * ff_part)
    top, low = pl.ds(0, half), pl.ds(half, half)
    enter((to_x, to_y, to_c))

    def piece(t, s, h):
        return all_ref.at[t * seq + s, pl.ds(h * half, half)]

    def own(i, h, device):
        return remote(
            own_ref.at[pl.ds(h * half, half)],
            piece(tp_at, seq_at, h),
            sends.at[i],
            recvs.at[i],
            device,
        )

    def relay(i, t, s, h, device):
        return remote(piece(t, s, h), piece(t, s, h), sends.at[i], recvs.at[i], device)

    x0, x1 = own(0, 0, to_x), own(3, 1, to_x)
    y0, y1 = own(1, 0, to_y), own(4, 1, to_y)
    c0, c1 = own(2, 0, to_c), own(5, 1, to_c)
    diag0 = relay(6, tp_at, far, 0, to_y)
    diag1 = relay(7, other, seq_at, 1, to_x)
    rx0, rx1 = relay(8, tp_at, far, 0, to_c), relay(11, tp_at, far, 1, to_c)
    ry0, ry1 = relay(9, other, seq_at, 0, to_c), relay(10, other, seq_at, 1, to_c)
    rd0, rd1 = relay(12, other, far, 0, to_c), relay(13, other, far, 1, to_c)

    def give(c):
        return remote(
            part.at[c, 1 - kind], chip_in.at[c], sends.at[14 + c], recvs.at[14 + c], to_c
        )

    def hop(i, src, dst, device):
        return remote(src, dst, sends.at[i], recvs.at[i], device)

    def held(c):
        return part.at[c, kind]

    sum_x0 = hop(18, part.at[1, kind, top], near_in.at[0, top], to_x)
    sum_y1 = hop(19, part.at[2, kind, low], near_in.at[1, low], to_y)
    sum_d0 = hop(20, part.at[3, kind, top], far_in.at[0, top], to_x)
    sum_d1 = hop(21, part.at[3, kind, low], far_in.at[1, low], to_y)
    sum_y0 = hop(22, part.at[2, kind, top], near_in.at[1, top], to_y)
    sum_x1 = hop(23, part.at[1, kind, low], near_in.at[0, low], to_x)

    def chip_sum(c):
        give(c).wait_recv()
        add_rows(held(c), (held(c), chip_in.at[c]), 0, rows, part.dtype)

    def chip_rows(c):
        t = lax.rem(tp_at + c // 2, 2)
        s = lax.rem(seq_at + (seq // 2) * lax.rem(c, 2), seq)
        return t * seq + s - lax.rem(s, 2)

    def take_tokens(c):
        return pltpu.make_async_copy(
            all_ref.at[pl.ds(chip_rows(c), 2)], tokens.at[lax.rem(c, 2)], local.at[lax.rem(c, 2)]
        )

    def take_grads(c):
        return pltpu.make_async_copy(
            grad_ref.at[pl.ds(chip_rows(c), 2)], grads.at[c], local.at[2 + c]
        )

    def put_gug(c, slot):
        return pltpu.make_async_copy(
            gug.at[slot], gug_ref.at[chip_rows(c) // 2], local.at[6 + slot]
        )

    def put_down(n):
        slot = lax.rem(n, 2)
        return pltpu.make_async_copy(
            stage.at[slot], down_ref.at[pl.ds(n * block, block)], local.at[9 + slot]
        )

    def put_out(c):
        return pltpu.make_async_copy(
            tokens.at[lax.rem(c, 2)], out_ref.at[pl.ds(chip_rows(c), 2)], local.at[11 + lax.rem(c, 2)]
        )

    take_weight = pltpu.make_async_copy(weight_hbm, weight, local.at[13])
    mine = pltpu.make_async_copy(own_ref, all_ref.at[tp_at * seq + seq_at], local.at[14])

    for copy in (take_weight, x0, y0, c0, x1, y1, c1, mine):
        copy.start()
    for c in range(4):
        take_grads(c).start()

    def slopes(c, slot):
        def body(i, carry):
            at = pl.ds(i * SUB, SUB)
            gate, upward, grad = wide[at, :ff_part], wide[at, ff_part:], narrow[c, at, :]
            sigmoid_gate = jax.nn.sigmoid(gate)
            silu_gate = gate * sigmoid_gate
            inner[c, at, :] = (silu_gate * upward).astype(BF)
            slope = sigmoid_gate * (1.0 + gate * (1.0 - sigmoid_gate))
            gug[slot, at, :ff_part] = (grad * upward * slope).astype(BF)
            gug[slot, at, ff_part:] = (grad * silu_gate).astype(BF)
            return carry

        lax.fori_loop(0, pair // SUB, body, 0)
        put_gug(c, slot).start()

    def back(c, slot, n):
        at = pl.ds(pl.multiple_of(n * block, block), block)
        total = nt(gug[slot], weight[at, gate_up]).astype(part.dtype)
        part[c, :, :, at] = total.reshape(2, rows, block)

    def widen(slot):
        wide[...] = nn(tokens[slot].reshape(pair, width), weight[:, gate_up])

    take_weight.wait()

    def narrow_step(c, carry):
        take_grads(c).wait()
        narrow[c] = nn(grads[c].reshape(pair, width), weight[:, lower])
        return carry

    lax.fori_loop(0, 4, narrow_step, 0)
    mine.wait()
    c0.wait_recv()
    c1.wait_recv()
    take_tokens(0).start()
    x0.wait_recv()
    diag0.start()
    rx0.start()
    y0.wait_recv()
    ry0.start()
    take_tokens(0).wait()
    widen(0)
    slopes(0, 2)
    y1.wait_recv()
    diag1.start()
    ry1.start()
    x1.wait_recv()
    rx1.start()
    rx0.wait_recv()
    rx1.wait_recv()
    take_tokens(1).start()

    def chip_step(c, carry):
        slot = lax.rem(c, 2)
        take_tokens(c).wait()
        widen(slot)

        @pl.when(c == 1)
        def _():
            ry0.wait_recv()
            ry1.wait_recv()
            take_tokens(2).start()

        @pl.when(c == 2)
        def _():
            chip_sum(1)
            sum_x0.start()

        @pl.when(c == 3)
        def _():
            chip_sum(2)
            sum_y1.start()
            put_gug(1, 1).wait()

        slopes(c, slot)

        @pl.when(c == 2)
        def _():
            rd0.wait_recv()
            rd1.wait_recv()
            take_tokens(3).start()

        def back_step(n, carry):
            back(c, slot, n)
            return carry

        lax.fori_loop(0, 4, back_step, 0)
        give(c).start()

        @pl.when(c == 1)
        def _():
            diag0.wait_recv()
            rd0.start()
            diag1.wait_recv()
            rd1.start()

        return carry

    lax.fori_loop(1, 4, chip_step, 0)

    def own_step(n, carry):
        back(0, 2, n)

        @pl.when(n == 1)
        def _():
            chip_sum(3)
            sum_d0.start()
            sum_d1.start()

        return carry

    lax.fori_loop(0, 4, own_step, 0)
    give(0).start()

    def out_step(c, carry):
        slot = lax.rem(c, 2)

        @pl.when(c >= 2)
        def _():
            put_out(c - 2).wait()

        def out_block(n, carry):
            at = pl.ds(pl.multiple_of(n * block, block), block)
            total = nt(inner[c], weight[at, lower]).astype(tokens.dtype)
            tokens[slot, :, :, at] = total.reshape(2, rows, block)
            return carry

        lax.fori_loop(0, 4, out_block, 0)
        put_out(c).start()
        return carry

    lax.fori_loop(0, 4, out_step, 0)
    chip_sum(0)

    def down_step(n, carry):
        @pl.when(n == 1)
        def _():
            sum_d0.wait_recv()
            add_rows(held(2), (held(2), far_in.at[0]), 0, half, part.dtype)
            sum_y0.start()
            sum_d1.wait_recv()
            add_rows(held(1), (held(1), far_in.at[1]), half, half, part.dtype)
            sum_x1.start()

        @pl.when(n >= 2)
        def _():
            put_down(n - 2).wait()

        at = pl.ds(pl.multiple_of(n * block, block), block)
        left = grads[:, :, :, at].reshape(4 * pair, block)
        stage[lax.rem(n, 2)] = tn(left, inner[...].reshape(4 * pair, ff_part)).astype(BF)
        put_down(n).start()
        return carry

    lax.fori_loop(0, 4, down_step, 0)
    sum_x0.wait_recv()
    sum_y0.wait_recv()
    add_rows(sum_ref, (held(0), near_in.at[0], near_in.at[1]), 0, half, sum_ref.dtype)
    sum_y1.wait_recv()
    sum_x1.wait_recv()
    add_rows(sum_ref, (held(0), near_in.at[0], near_in.at[1]), half, half, sum_ref.dtype)
    for copy in (x0, y0, c0, x1, y1, c1, diag0, diag1, rx0, ry0, ry1, rx1, rd0, rd1):
        copy.wait_send()
    for c in range(4):
        give(c).wait_send()
    for copy in (sum_x0, sum_y1, sum_d0, sum_d1, sum_y0, sum_x1):
        copy.wait_send()
    for c, slot in ((0, 2), (2, 0), (3, 1)):
        put_gug(c, slot).wait()
    for c in (2, 3):
        put_out(c).wait()
        put_down(c).wait()


def ffn_plane(block, grads, weight, ident):
    rows, width = block.shape
    seq = lax.axis_size("seq")
    plane = lax.axis_size("tp") * seq
    chips = plane // 2
    ff_part = weight.shape[1] // 3
    shape = jax.ShapeDtypeStruct
    hbm = pl.BlockSpec(memory_space=pltpu.HBM)
    vmem = pl.BlockSpec(memory_space=pltpu.VMEM)
    tokens = plane * rows
    return pl.pallas_call(
        ffn_kernel,
        out_shape=(
            shape((plane, rows, width), BF),
            shape((chips, 2 * rows, 2 * ff_part), BF),
            shape((plane, rows, width), BF),
            shape((width, ff_part), BF),
            shape((rows, width), F32),
        ),
        in_specs=[vmem, hbm, hbm],
        out_specs=(hbm, hbm, hbm, hbm, vmem),
        scratch_shapes=[
            pltpu.VMEM(weight.shape, BF),
            pltpu.VMEM((2, 2, rows, width), BF),
            pltpu.VMEM((4, 2, rows, width), BF),
            pltpu.VMEM((2 * rows, 2 * ff_part), F32),
            pltpu.VMEM((4, 2 * rows, ff_part), F32),
            pltpu.VMEM((4, 2 * rows, ff_part), BF),
            pltpu.VMEM((3, 2 * rows, 2 * ff_part), BF),
            pltpu.VMEM((2, width // 4, ff_part), BF),
            pltpu.VMEM((4, 2, rows, width), BF),
            pltpu.VMEM((4, rows, width), BF),
            pltpu.VMEM((2, rows, width), BF),
            pltpu.VMEM((2, rows, width), BF),
            pltpu.SemaphoreType.DMA((24,)),
            pltpu.SemaphoreType.DMA((24,)),
            pltpu.SemaphoreType.DMA((15,)),
        ],
        cost_estimate=pl.CostEstimate(
            flops=14 * tokens * width * ff_part,
            transcendentals=tokens * ff_part,
            bytes_accessed=30 * tokens * width,
        ),
        compiler_params=pltpu.CompilerParams(
            collective_id=ident, has_side_effects=True, vmem_limit_bytes=63 << 20
        ),
        name="ffn_plane",
    )(block, grads, weight)


def finish_kernel(
    gu_ref,
    down_ref,
    gate_weight,
    up_weight,
    gain_ref,
    gate_out,
    up_out,
    down_out,
    gain_out,
    gu_in,
    down_in,
    local,
    sends,
    recvs,
):
    tp_at, seq_at, _, _, _ = plane_place()
    seq = lax.axis_size("seq")
    plane = lax.axis_size("tp") * seq
    me = tp_at * seq + seq_at
    peers = [lax.rem(me + k, plane) for k in range(1, plane)]
    devices = [at_device(peer // seq, lax.rem(peer, seq)) for peer in peers]
    enter(devices)
    copies = []
    for k, (peer, device) in enumerate(zip(peers, devices)):
        copies.append(remote(gu_ref.at[peer], gu_in.at[me], sends.at[k], recvs.at[k], device))
        i = plane - 1 + k
        copies.append(remote(down_ref.at[peer], down_in.at[me], sends.at[i], recvs.at[i], device))
    copies.append(pltpu.make_async_copy(gu_ref.at[me], gu_in.at[me], local.at[0]))
    copies.append(pltpu.make_async_copy(down_ref.at[me], down_in.at[me], local.at[1]))
    for copy in copies:
        copy.start()
    for copy in copies:
        copy.wait()
    put = pltpu.make_async_copy(down_in, down_out, local.at[2])
    put.start()
    gain = gain_ref[...]
    ff_part = down_in.shape[2]
    total = jnp.zeros(gain.shape, F32)
    for j in range(plane):
        at = slice(j * ff_part, (j + 1) * ff_part)
        for k, (out, weight) in enumerate(((gate_out, gate_weight), (up_out, up_weight))):
            own = gu_in[j, :, k * ff_part : (k + 1) * ff_part].astype(F32)
            out[:, at] = own * gain
            total = total + jnp.sum(own * weight[:, at].astype(F32), axis=1, keepdims=True)
    gain_out[...] = total
    put.wait()


def finish_plane(gu_sums, down_sums, gate_weight, up_weight, gain, ident):
    plane, rows, ff_part = down_sums.shape
    shape = jax.ShapeDtypeStruct
    hbm = pl.BlockSpec(memory_space=pltpu.HBM)
    vmem = pl.BlockSpec(memory_space=pltpu.VMEM)
    size = plane * rows * ff_part * 6
    return pl.pallas_call(
        finish_kernel,
        out_shape=(
            shape(gate_weight.shape, F32),
            shape(up_weight.shape, F32),
            shape(down_sums.shape, BF),
            shape((rows, 1), F32),
        ),
        in_specs=[hbm, hbm, vmem, vmem, vmem],
        out_specs=(vmem, vmem, hbm, vmem),
        scratch_shapes=[
            pltpu.VMEM(gu_sums.shape, BF),
            pltpu.VMEM(down_sums.shape, BF),
            pltpu.SemaphoreType.DMA((3,)),
            pltpu.SemaphoreType.DMA((2 * plane - 2,)),
            pltpu.SemaphoreType.DMA((2 * plane - 2,)),
        ],
        cost_estimate=pl.CostEstimate(flops=0, transcendentals=0, bytes_accessed=size * 20),
        compiler_params=pltpu.CompilerParams(
            collective_id=ident, has_side_effects=True, vmem_limit_bytes=24 << 20
        ),
        name="finish_plane",
    )(gu_sums, down_sums, gate_weight, up_weight, gain)


def columns(matrix, parts):
    rows, cols = matrix.shape
    return jnp.transpose(matrix.reshape(rows, parts, cols // parts), (1, 0, 2))


def uncolumns(blocks):
    parts, rows, cols = blocks.shape
    return jnp.transpose(blocks, (1, 0, 2)).reshape(rows, parts * cols)


def after(value, *earlier):
    return lax.optimization_barrier((value,) + earlier)[0]


def per_device(
    layer_input,
    pic_starts,
    skip_mask,
    gain_attn,
    w_query,
    w_key,
    w_value,
    w_out,
    gain_ffn,
    w_gate,
    w_up,
    w_down,
    cotangent,
):
    _, local_len, width = layer_input.shape
    seq = lax.axis_size("seq")
    plane = lax.axis_size("tp") * seq
    total_len = local_len * seq
    heads = H // plane
    share = plane // KV
    ff_part = w_gate.shape[1] // plane
    q_part = heads * DH
    scale = DH ** (-0.5)

    gain1 = gain_attn[:, None]
    gain2 = gain_ffn[:, None]
    wq32, wk32, wv32 = w_query.astype(F32), w_key.astype(F32), w_value.astype(F32)
    wg32, wu32 = w_gate.astype(F32), w_up.astype(F32)
    attn_pack = jnp.concatenate(
        [
            columns((wq32 * gain1).astype(BF), plane),
            jnp.repeat(columns((wk32 * gain1).astype(BF), KV), share, axis=0),
            jnp.repeat(columns((wv32 * gain1).astype(BF), KV), share, axis=0),
            columns(w_out.T, plane),
        ],
        axis=2,
    )
    attn_rows = exchange_plane(attn_pack, 0)
    attn_rows = attn_rows.reshape(-1, attn_rows.shape[2])
    attn_weight = lax.all_gather(attn_rows, "rep", axis=0, tiled=True)
    qkv_weight = attn_weight[:, : q_part + 2 * DH]
    out_weight = attn_weight[:, q_part + 2 * DH :]

    tokens = layer_input.reshape(local_len, width).astype(F32)
    keep = (1 - skip_mask).astype(F32).reshape(local_len, 1)
    upstream = cotangent.reshape(local_len, width).astype(F32)
    scale1 = rms_scale(tokens)
    norm1 = tokens * scale1

    ffn_pack = jnp.concatenate(
        [
            columns((wg32 * gain2).astype(BF), plane),
            columns((wu32 * gain2).astype(BF), plane),
            columns(w_down.T, plane),
        ],
        axis=2,
    )
    ffn_rows = exchange_plane(after(ffn_pack, attn_rows), 2)
    ffn_rows = ffn_rows.reshape(-1, ffn_rows.shape[2])
    ffn_weight = lax.all_gather(ffn_rows, "rep", axis=0, tiled=True)
    norm1_all = gather_plane(after(norm1.astype(BF), ffn_rows), 1)
    ffn_grad = gather_plane(after((keep * upstream).astype(BF), norm1_all), 3)

    other_starts = lax.ppermute(pic_starts, "tp", [(0, 1), (1, 0)])
    starts = jnp.where(
        lax.axis_index("tp") == 0,
        jnp.concatenate([pic_starts, other_starts], axis=0),
        jnp.concatenate([other_starts, pic_starts], axis=0),
    )
    positions = jnp.arange(total_len, dtype=jnp.int32)
    cos_table, sin_table = rotary_tables(positions, DH)
    allowed = jax.vmap(visible, (None, 0))(positions, starts)[:, None]
    turn = jax.vmap(rotate, (0, None, None))

    projected = nn(norm1_all, qkv_weight).reshape(TP, total_len, q_part + 2 * DH)
    queries = turn(
        projected[..., :q_part].reshape(TP, total_len, heads, DH), cos_table, sin_table
    ).astype(BF)
    keys = turn(projected[..., q_part : q_part + DH], cos_table, sin_table).astype(BF)
    values = projected[..., q_part + DH :].astype(BF)
    scores = jnp.einsum("tqhd,tkd->thqk", queries, keys, preferred_element_type=F32) * scale
    scores = jnp.where(allowed, scores, -jnp.inf)
    peak = jnp.max(scores, axis=-1, keepdims=True)
    log_total = peak + jnp.log(jnp.sum(jnp.exp(scores - peak), axis=-1, keepdims=True))
    probs = jnp.exp(scores - log_total)
    probs_low = probs.astype(BF)
    mixed = jnp.einsum("thqk,tkd->tqhd", probs_low, values, preferred_element_type=F32)
    mixed = mixed.astype(BF).reshape(TP * total_len, q_part)
    branch = scatter_plane(nt(mixed, out_weight).astype(BF), 4)
    hidden = tokens + keep * branch

    scale2 = rms_scale(hidden)
    norm2 = hidden * scale2
    norm2_all, gate_up_grad, out_partial, down_partial, scaled2 = ffn_plane(
        norm2.astype(BF), ffn_grad.reshape(plane, local_len, width), ffn_weight, 5
    )
    norm2_all = norm2_all.reshape(-1, width)
    gate_up_grad = gate_up_grad.reshape(-1, 2 * ff_part)
    down_sums = lax.psum_scatter(down_partial, "rep", scatter_dimension=0, tiled=True)
    gu_partial = tn(norm2_all, after(gate_up_grad, down_partial)).astype(BF)
    gu_sums = lax.psum_scatter(gu_partial, "rep", scatter_dimension=0, tiled=True)
    hidden_grad = upstream + scale2 * (
        scaled2 - norm2 * jnp.mean(scaled2 * norm2, axis=-1, keepdims=True)
    )

    branch_grad = gather_plane(after((keep * hidden_grad).astype(BF), gu_partial, down_partial), 7)
    mixed_grad = nn(branch_grad, out_weight).astype(BF)
    qkv_grad, ffn_out = attn_back_plane(
        starts,
        queries.reshape(-1, q_part),
        keys.reshape(-1, DH),
        values.reshape(-1, DH),
        mixed_grad,
        log_total.reshape(TP * heads, 1, total_len),
        jnp.concatenate([cos_table, cos_table], axis=1),
        jnp.concatenate([sin_table, -sin_table], axis=1),
        out_partial.reshape(-1, width),
        9,
    )
    attn_partial = jnp.concatenate(
        [tn(norm1_all, qkv_grad).astype(BF), tn(branch_grad, mixed).astype(BF)], axis=1
    )
    scaled1_partial = nt(qkv_grad, qkv_weight).astype(BF)
    attn_partial = after(attn_partial, gu_sums, down_sums, scaled1_partial)
    attn_sums = lax.psum_scatter(attn_partial, "rep", scatter_dimension=0, tiled=True)
    scaled1 = scatter_plane(after(scaled1_partial, attn_partial), 8)
    input_grad = hidden_grad + scale1 * (
        scaled1 - norm1 * jnp.mean(scaled1 * norm1, axis=-1, keepdims=True)
    )
    out_hidden = (hidden + keep * ffn_out).astype(BF)

    gate_grad, up_grad, down_own, gain_ffn_grad = finish_plane(
        after(gu_sums.reshape(plane, -1, 2 * ff_part), scaled1),
        down_sums.reshape(plane, -1, ff_part),
        w_gate,
        w_up,
        gain2,
        10,
    )
    down_grad = jnp.transpose(down_own, (0, 2, 1)).reshape(plane * ff_part, -1).astype(F32)

    attn_own = exchange_plane(attn_sums.reshape(plane, -1, attn_sums.shape[1]), 11).astype(F32)
    query_own = uncolumns(attn_own[:, :, :q_part])
    kv_own = attn_own[:, :, q_part : q_part + 2 * DH]
    kv_own = jnp.sum(kv_own.reshape(KV, share, -1, 2 * DH), axis=1)
    key_own = uncolumns(kv_own[:, :, :DH])
    value_own = uncolumns(kv_own[:, :, DH:])
    out_own = uncolumns(attn_own[:, :, q_part + 2 * DH :])
    gain_attn_grad = (
        jnp.sum(query_own * wq32, axis=1)
        + jnp.sum(key_own * wk32, axis=1)
        + jnp.sum(value_own * wv32, axis=1)
    )
    return (
        out_hidden[None],
        input_grad[None],
        gain_attn_grad,
        query_own * gain1,
        key_own * gain1,
        value_own * gain1,
        out_own.T,
        gain_ffn_grad[:, 0],
        gate_grad,
        up_grad,
        down_grad,
    )


def solution(mesh):
    devices = mesh.devices
    dp, seq = devices.shape
    inner = Mesh(devices.reshape(dp // TP, TP, seq), ("rep", "tp", "seq"))
    dps = ("rep", "tp")
    every = ("rep", "tp", "seq")
    token = P(dps, "seq", None)
    row = P(every, None)
    col = P(None, every)
    return jax.shard_map(
        per_device,
        mesh=inner,
        in_specs=(
            token,
            P(dps, None),
            P(dps, "seq"),
            P(every),
            row,
            row,
            row,
            col,
            P(every),
            row,
            row,
            col,
            token,
        ),
        out_specs=(token, token, P(every), row, row, row, col, P(every), row, row, col),
        check_vma=False,
    )
```

```python
import jax
import jax.numpy as jnp
from jax import lax
from jax.experimental import pallas as pl
from jax.experimental.pallas import tpu as pltpu
from jax.sharding import Mesh
from jax.sharding import PartitionSpec as P

H = 16
KV = 4
DH = 128
PIC = 256
NPIC = 2
EPS = 1e-05
TP = 2
BF = jnp.bfloat16
F32 = jnp.float32


def rotary_tables(positions, head_dim):
    half_dim = head_dim // 2
    inverse = 10000.0 ** (-(jnp.arange(half_dim, dtype=F32) * 2.0 / head_dim))
    angles = positions.astype(F32)[:, None] * inverse[None, :]
    return (jnp.cos(angles), jnp.sin(angles))


def rms_scale(rows):
    return lax.rsqrt(jnp.mean(rows * rows, axis=-1, keepdims=True) + EPS)


def dot(left, right, contract):
    return lax.dot_general(
        left, right, ((contract[:1], contract[1:]), ((), ())), preferred_element_type=F32
    )


def nn(left, right):
    return dot(left, right, (1, 0))


def nt(left, right):
    return dot(left, right, (1, 1))


def tn(left, right):
    return dot(left, right, (0, 0))


MESH_ID = pl.DeviceIdType.MESH
SUB = 32


def plane_place():
    tp_at = lax.axis_index("tp")
    seq_at = lax.axis_index("seq")
    seq = lax.axis_size("seq")
    half = seq // 2
    far = lax.rem(seq_at + half, seq)
    mate = seq_at + 1 - 2 * lax.rem(seq_at, 2)
    far_mate = far + 1 - 2 * lax.rem(far, 2)
    return tp_at, seq_at, far, mate, far_mate


def at_device(tp_at, seq_at):
    return (lax.axis_index("rep"), tp_at, seq_at)


def enter(devices):
    barrier = pltpu.get_barrier_semaphore()
    for device in devices:
        pl.semaphore_signal(barrier, inc=1, device_id=device, device_id_type=MESH_ID)
    pl.semaphore_wait(barrier, len(devices))


def remote(src, dst, send, recv, device):
    return pltpu.make_async_remote_copy(
        src_ref=src,
        dst_ref=dst,
        send_sem=send,
        recv_sem=recv,
        device_id=device,
        device_id_type=MESH_ID,
    )


def gather_stages(own_ref, all_ref, sends, recvs, local):
    tp_at, seq_at, far, mate, _ = plane_place()
    seq = lax.axis_size("seq")
    other = 1 - tp_at
    to_x = at_device(tp_at, far)
    to_y = at_device(other, seq_at)
    to_c = at_device(tp_at, mate)
    rows = own_ref.shape[0]
    part = rows // 2

    def piece(t, s, h):
        return all_ref.at[t * seq + s, pl.ds(h * part, part)]

    def relay(i, t, s, h, device):
        return remote(piece(t, s, h), piece(t, s, h), sends.at[i], recvs.at[i], device)

    def own(i, h, device):
        return remote(
            own_ref.at[pl.ds(h * part, part)],
            piece(tp_at, seq_at, h),
            sends.at[i],
            recvs.at[i],
            device,
        )

    x0, x1 = own(0, 0, to_x), own(3, 1, to_x)
    y0, y1 = own(1, 0, to_y), own(4, 1, to_y)
    c0, c1 = own(2, 0, to_c), own(5, 1, to_c)
    diag0 = relay(6, tp_at, far, 0, to_y)
    diag1 = relay(7, other, seq_at, 1, to_x)
    rx0, rx1 = relay(8, tp_at, far, 0, to_c), relay(11, tp_at, far, 1, to_c)
    ry0, ry1 = relay(9, other, seq_at, 0, to_c), relay(10, other, seq_at, 1, to_c)
    rd0, rd1 = relay(12, other, far, 0, to_c), relay(13, other, far, 1, to_c)
    mine = pltpu.make_async_copy(own_ref, all_ref.at[tp_at * seq + seq_at], local)

    def begin():
        enter((to_x, to_y, to_c))
        for copy in (x0, y0, c0, x1, y1, c1, mine):
            copy.start()

    def first():
        x0.wait_recv()
        diag0.start()
        rx0.start()
        y0.wait_recv()
        ry0.start()

    def second():
        y1.wait_recv()
        diag1.start()
        ry1.start()
        x1.wait_recv()
        rx1.start()

    def finish():
        diag0.wait_recv()
        rd0.start()
        diag1.wait_recv()
        rd1.start()
        for copy in (c0, c1, rx0, ry0, ry1, rx1, rd0, rd1):
            copy.wait_recv()
        for copy in (x0, y0, c0, x1, y1, c1, diag0, diag1, rx0, ry0, ry1, rx1, rd0, rd1):
            copy.wait_send()
        mine.wait()

    return begin, first, second, finish


def gather_kernel(*refs):
    for stage in gather_stages(*refs):
        stage()


GATHER_SCRATCH = (
    pltpu.SemaphoreType.DMA((14,)),
    pltpu.SemaphoreType.DMA((14,)),
    pltpu.SemaphoreType.DMA,
)


def gather_plane(block, ident):
    rows, width = block.shape
    plane = lax.axis_size("tp") * lax.axis_size("seq")
    size = rows * width * 2
    gathered = pl.pallas_call(
        gather_kernel,
        out_shape=jax.ShapeDtypeStruct((plane, rows, width), block.dtype),
        in_specs=[pl.BlockSpec(memory_space=pltpu.VMEM)],
        out_specs=pl.BlockSpec(memory_space=pltpu.HBM),
        scratch_shapes=GATHER_SCRATCH,
        cost_estimate=pl.CostEstimate(
            flops=0, transcendentals=0, bytes_accessed=plane * size * 12
        ),
        compiler_params=pltpu.CompilerParams(collective_id=ident, has_side_effects=True),
        name="gather_plane",
    )(block)
    return gathered.reshape(plane * rows, width)


def add_rows(target, sources, start, count, kind):
    step = min(SUB, count)

    def body(i, carry):
        at = pl.ds(start + i * step, step)
        total = sources[0][at, :].astype(F32)
        for source in sources[1:]:
            total = total + source[at, :].astype(F32)
        target[at, :] = total.astype(kind)
        return carry

    lax.fori_loop(0, count // step, body, 0)


def scatter_stages(part_ref, sum_ref, held, chip_in, far_in, near_in, loads, sends, recvs):
    tp_at, seq_at, far, mate, far_mate = plane_place()
    seq = lax.axis_size("seq")
    other = 1 - tp_at
    to_x = at_device(tp_at, far)
    to_y = at_device(other, seq_at)
    to_c = at_device(tp_at, mate)
    rows = sum_ref.shape[0]
    part = rows // 2
    top, low = pl.ds(0, part), pl.ds(part, part)
    chips = ((other, far, far_mate), (tp_at, far, far_mate), (other, seq_at, mate), (tp_at, seq_at, mate))
    gives = [
        remote(part_ref.at[t * seq + m], chip_in.at[k], sends.at[k], recvs.at[k], to_c)
        for k, (t, s, m) in enumerate(chips)
    ]
    takes = [
        pltpu.make_async_copy(part_ref.at[t * seq + s], held.at[k], loads.at[k])
        for k, (t, s, m) in enumerate(chips)
    ]

    def hop(i, src, dst, device):
        return remote(src, dst, sends.at[i], recvs.at[i], device)

    d0 = hop(4, held.at[0, top], far_in.at[0, top], to_x)
    d1 = hop(5, held.at[0, low], far_in.at[1, low], to_y)
    x0 = hop(6, held.at[1, top], near_in.at[0, top], to_x)
    y1 = hop(7, held.at[2, low], near_in.at[1, low], to_y)
    y0 = hop(8, held.at[2, top], near_in.at[1, top], to_y)
    x1 = hop(9, held.at[1, low], near_in.at[0, low], to_x)

    def begin():
        enter((to_x, to_y, to_c))
        for give, take in zip(gives, takes):
            give.start()
            take.start()

    def chip_sum(k):
        takes[k].wait()
        gives[k].wait_recv()
        add_rows(held.at[k], (held.at[k], chip_in.at[k]), 0, rows, held.dtype)

    def diagonal():
        chip_sum(0)
        d0.start()
        d1.start()

    def along_x():
        chip_sum(1)
        x0.start()

    def along_y():
        chip_sum(2)
        y1.start()

    def own():
        chip_sum(3)

    def fold():
        d0.wait_recv()
        add_rows(held.at[2], (held.at[2], far_in.at[0]), 0, part, held.dtype)
        y0.start()
        d1.wait_recv()
        add_rows(held.at[1], (held.at[1], far_in.at[1]), part, part, held.dtype)
        x1.start()

    def finish():
        x0.wait_recv()
        y0.wait_recv()
        add_rows(sum_ref, (held.at[3], near_in.at[0], near_in.at[1]), 0, part, sum_ref.dtype)
        y1.wait_recv()
        x1.wait_recv()
        add_rows(sum_ref, (held.at[3], near_in.at[0], near_in.at[1]), part, part, sum_ref.dtype)
        for copy in gives + [d0, d1, x0, y1, y0, x1]:
            copy.wait_send()

    return begin, diagonal, along_x, along_y, own, fold, finish


def scatter_kernel(*refs):
    for stage in scatter_stages(*refs):
        stage()


def scatter_scratch(rows, width, kind):
    return [
        pltpu.VMEM((4, rows, width), kind),
        pltpu.VMEM((4, rows, width), kind),
        pltpu.VMEM((2, rows, width), kind),
        pltpu.VMEM((2, rows, width), kind),
        pltpu.SemaphoreType.DMA((4,)),
        pltpu.SemaphoreType.DMA((10,)),
        pltpu.SemaphoreType.DMA((10,)),
    ]


def scatter_plane(partial, ident):
    plane = lax.axis_size("tp") * lax.axis_size("seq")
    rows, width = partial.shape[0] // plane, partial.shape[1]
    kind = partial.dtype
    size = rows * width * 2
    return pl.pallas_call(
        scatter_kernel,
        out_shape=jax.ShapeDtypeStruct((rows, width), F32),
        in_specs=[pl.BlockSpec(memory_space=pltpu.HBM)],
        out_specs=pl.BlockSpec(memory_space=pltpu.VMEM),
        scratch_shapes=scatter_scratch(rows, width, kind),
        cost_estimate=pl.CostEstimate(
            flops=0, transcendentals=0, bytes_accessed=plane * size * 14
        ),
        compiler_params=pltpu.CompilerParams(
            collective_id=ident, has_side_effects=True, vmem_limit_bytes=32 << 20
        ),
        name="scatter_plane",
    )(partial.reshape(plane, rows, width))


def fill_bias(bias, starts_ref, t, blocks):
    for b in range(blocks):
        span = min(2, blocks - b) * PIC
        k_at = lax.broadcasted_iota(jnp.int32, (span, PIC), 0) + b * PIC
        q_at = lax.broadcasted_iota(jnp.int32, (span, PIC), 1) + b * PIC
        high, below = jnp.maximum(k_at, q_at), jnp.minimum(k_at, q_at)
        allowed = k_at <= q_at
        for j in range(NPIC):
            start = starts_ref[t, j]
            allowed = allowed | ((below >= start) & (high < start + PIC))
        bias[b, :span, :] = jnp.where(allowed, 0.0, -jnp.inf)


def masked(scores, bias, b):
    late = scores[b * PIC :] + bias[b, : scores.shape[0] - b * PIC, :]
    return jnp.concatenate([scores[: b * PIC], late], axis=0) if b else late


def attn_front_kernel(
    starts_ref,
    projected_ref,
    cos_ref,
    sin_ref,
    own_ref,
    qkv_ref,
    mixed_ref,
    log_ref,
    all_ref,
    bias,
    turned,
    *gather,
):
    begin, first, second, finish = gather_stages(own_ref, all_ref, *gather)
    begin()
    total, dim = cos_ref.shape
    heads = mixed_ref.shape[1] // dim
    blocks = total // PIC
    scale = dim ** (-0.5)
    k_cols = slice(heads * dim, (heads + 1) * dim)
    v_cols = slice((heads + 1) * dim, (heads + 2) * dim)

    def turn(rows, at):
        return rows * cos_ref[at, :] + pltpu.roll(rows, dim // 2, 1) * sin_ref[at, :]

    def head_step(i, carry):
        t, h = i // heads, lax.rem(i, heads)
        base = pl.multiple_of(t * total, total)
        cols = pl.ds(pl.multiple_of(h * dim, dim), dim)

        @pl.when(h == 0)
        def _():
            rows = pl.ds(base, total)
            values = projected_ref[rows, v_cols].astype(BF)
            qkv_ref[rows, k_cols] = turn(projected_ref[rows, k_cols], pl.ds(0, total)).astype(BF)
            qkv_ref[rows, v_cols] = values
            turned[...] = values.T
            fill_bias(bias, starts_ref, t, blocks)

        for b in range(blocks):
            at = pl.ds(pl.multiple_of(base + b * PIC, PIC), PIC)
            count = min(b + 2, blocks) * PIC
            queries = turn(projected_ref[at, cols], pl.ds(b * PIC, PIC)).astype(BF)
            qkv_ref[at, cols] = queries
            scores = nt(qkv_ref[pl.ds(base, count), k_cols], queries) * scale
            scores = masked(scores, bias, b)
            peak = jnp.max(scores, axis=0, keepdims=True)
            weights = jnp.exp(scores - peak)
            mass = jnp.sum(weights, axis=0, keepdims=True)
            log_ref[i, :, b * PIC : (b + 1) * PIC] = peak + jnp.log(mass)
            probs = (weights * (1.0 / mass)).astype(BF)
            mixed_ref[at, cols] = nn(turned[:, :count], probs).T.astype(BF)
            if b == 0:
                pl.when(i == 2)(first)

        return carry

    lax.fori_loop(0, log_ref.shape[0], head_step, 0)
    second()
    finish()


def attn_front_plane(starts, projected, cos, sin, block, ident):
    rows, width = block.shape
    plane = lax.axis_size("tp") * lax.axis_size("seq")
    total, dim = cos.shape
    tokens, cols = projected.shape
    q_part = cols - 2 * dim
    shape = jax.ShapeDtypeStruct
    vmem = pl.BlockSpec(memory_space=pltpu.VMEM)
    smem = pl.BlockSpec(memory_space=pltpu.SMEM)
    hbm = pl.BlockSpec(memory_space=pltpu.HBM)
    return pl.pallas_call(
        attn_front_kernel,
        out_shape=(
            shape((tokens, cols), BF),
            shape((tokens, q_part), BF),
            shape((tokens * q_part // dim // total, 1, total), F32),
            shape((plane, rows, width), block.dtype),
        ),
        in_specs=[smem] + [vmem] * 4,
        out_specs=(vmem, vmem, vmem, hbm),
        scratch_shapes=[
            pltpu.VMEM((total // PIC, 2 * PIC, PIC), F32),
            pltpu.VMEM((dim, total), BF),
            *GATHER_SCRATCH,
        ],
        cost_estimate=pl.CostEstimate(
            flops=4 * tokens * total * q_part,
            transcendentals=tokens * total * q_part // dim,
            bytes_accessed=plane * rows * width * 24,
        ),
        compiler_params=pltpu.CompilerParams(
            collective_id=ident, has_side_effects=True, vmem_limit_bytes=40 << 20
        ),
        name="attn_front_plane",
    )(starts, projected, cos, sin, block)


def attn_back_kernel(
    starts_ref,
    qkv_ref,
    g_ref,
    log_ref,
    cos_ref,
    sin_ref,
    part_ref,
    grad_ref,
    sum_ref,
    bias,
    turned,
    keys_sum,
    values_sum,
    *scatter,
):
    begin, diagonal, along_x, along_y, own, fold, finish = scatter_stages(
        part_ref, sum_ref, *scatter
    )
    begin()
    total, dim = cos_ref.shape
    heads = g_ref.shape[1] // dim
    blocks = total // PIC
    scale = dim ** (-0.5)
    k_cols = slice(heads * dim, (heads + 1) * dim)
    v_cols = slice((heads + 1) * dim, (heads + 2) * dim)
    events = {(0, 1): diagonal, (0, 2): along_x, (0, 3): along_y, (1, 0): own, (2, 2): fold}

    def unturn(rows, at):
        return rows * cos_ref[at, :] - pltpu.roll(rows, dim // 2, 1) * sin_ref[at, :]

    def head_step(i, carry):
        t, h = i // heads, lax.rem(i, heads)
        base = pl.multiple_of(t * total, total)
        cols = pl.ds(pl.multiple_of(h * dim, dim), dim)

        @pl.when(h == 0)
        def _():
            turned[...] = qkv_ref[pl.ds(base, total), k_cols].T
            keys_sum[...] = jnp.zeros(keys_sum.shape, F32)
            values_sum[...] = jnp.zeros(values_sum.shape, F32)
            fill_bias(bias, starts_ref, t, blocks)

        for b in range(blocks):
            at = pl.ds(pl.multiple_of(base + b * PIC, PIC), PIC)
            count = min(b + 2, blocks) * PIC
            seen = pl.ds(base, count)
            queries, grads = qkv_ref[at, cols], g_ref[at, cols]
            scores = nt(qkv_ref[seen, k_cols], queries) * scale - log_ref[i, :, b * PIC : (b + 1) * PIC]
            probs = jnp.exp(masked(scores, bias, b))
            prob_grad = nt(qkv_ref[seen, v_cols], grads)
            mean = jnp.sum(probs * prob_grad, axis=0, keepdims=True)
            score_grad = (probs * (prob_grad - mean)).astype(BF)
            values_sum[:count, :] += nn(probs.astype(BF), grads)
            keys_sum[:count, :] += nn(score_grad, queries)
            back = nn(turned[:, :count], score_grad).T * scale
            grad_ref[at, cols] = unturn(back, pl.ds(b * PIC, PIC)).astype(BF)
            for (step, block), stage in events.items():
                if block == b:
                    pl.when(i == step)(stage)

        @pl.when(h == heads - 1)
        def _():
            rows = pl.ds(base, total)
            back = unturn(keys_sum[...] * scale, pl.ds(0, total))
            grad_ref[rows, k_cols] = back.astype(BF)
            grad_ref[rows, v_cols] = values_sum[...].astype(BF)

        return carry

    lax.fori_loop(0, log_ref.shape[0], head_step, 0)
    finish()


def attn_back_plane(starts, qkv, grads, log_total, cos, sin, partial, ident):
    plane = lax.axis_size("tp") * lax.axis_size("seq")
    rows, width = partial.shape[0] // plane, partial.shape[1]
    total, dim = cos.shape
    tokens, q_part = grads.shape
    hbm = pl.BlockSpec(memory_space=pltpu.HBM)
    vmem = pl.BlockSpec(memory_space=pltpu.VMEM)
    smem = pl.BlockSpec(memory_space=pltpu.SMEM)
    return pl.pallas_call(
        attn_back_kernel,
        out_shape=(
            jax.ShapeDtypeStruct((tokens, q_part + 2 * dim), BF),
            jax.ShapeDtypeStruct((rows, width), F32),
        ),
        in_specs=[smem] + [vmem] * 5 + [hbm],
        out_specs=(vmem, vmem),
        scratch_shapes=[
            pltpu.VMEM((total // PIC, 2 * PIC, PIC), F32),
            pltpu.VMEM((dim, total), BF),
            pltpu.VMEM((total, dim), F32),
            pltpu.VMEM((total, dim), F32),
        ]
        + scatter_scratch(rows, width, partial.dtype),
        cost_estimate=pl.CostEstimate(
            flops=10 * tokens * total * q_part,
            transcendentals=tokens * total * q_part // dim,
            bytes_accessed=plane * rows * width * 28,
        ),
        compiler_params=pltpu.CompilerParams(
            collective_id=ident, has_side_effects=True, vmem_limit_bytes=50 << 20
        ),
        name="attn_back_plane",
    )(starts, qkv, grads, log_total, cos, sin, partial.reshape(plane, rows, width))


def exchange_kernel(in_ref, out_ref, stage, local, sends, recvs):
    tp_at, seq_at, _, _, _ = plane_place()
    seq = lax.axis_size("seq")
    plane = lax.axis_size("tp") * seq
    me = tp_at * seq + seq_at
    peers = [lax.rem(me + k, plane) for k in range(1, plane)]
    devices = [at_device(peer // seq, lax.rem(peer, seq)) for peer in peers]
    enter(devices)
    copies = []
    for k, (peer, device) in enumerate(zip(peers, devices)):
        copy = remote(in_ref.at[peer], out_ref.at[me], sends.at[k], recvs.at[k], device)
        copy.start()
        copies.append(copy)
    take = pltpu.make_async_copy(in_ref.at[me], stage, local.at[0])
    take.start()
    take.wait()
    put = pltpu.make_async_copy(stage, out_ref.at[me], local.at[1])
    put.start()
    for copy in copies:
        copy.wait()
    put.wait()


def exchange_plane(blocks, ident):
    plane, rows, width = blocks.shape
    size = plane * rows * width * 2
    return pl.pallas_call(
        exchange_kernel,
        out_shape=jax.ShapeDtypeStruct(blocks.shape, blocks.dtype),
        in_specs=[pl.BlockSpec(memory_space=pltpu.HBM)],
        out_specs=pl.BlockSpec(memory_space=pltpu.HBM),
        scratch_shapes=[
            pltpu.VMEM((rows, width), blocks.dtype),
            pltpu.SemaphoreType.DMA((2,)),
            pltpu.SemaphoreType.DMA((plane - 1,)),
            pltpu.SemaphoreType.DMA((plane - 1,)),
        ],
        cost_estimate=pl.CostEstimate(flops=0, transcendentals=0, bytes_accessed=size * 20),
        compiler_params=pltpu.CompilerParams(collective_id=ident, has_side_effects=True),
        name="exchange_plane",
    )(blocks)


def ffn_kernel(
    own_ref,
    grad_ref,
    weight_hbm,
    all_ref,
    gug_ref,
    out_ref,
    down_ref,
    sum_ref,
    weight,
    tokens,
    grads,
    wide,
    narrow,
    inner,
    gug,
    stage,
    part,
    chip_in,
    far_in,
    near_in,
    sends,
    recvs,
    local,
):
    tp_at, seq_at, far, mate, _ = plane_place()
    seq = lax.axis_size("seq")
    other = 1 - tp_at
    kind = lax.rem(seq_at, 2)
    to_x = at_device(tp_at, far)
    to_y = at_device(other, seq_at)
    to_c = at_device(tp_at, mate)
    rows, width = own_ref.shape
    pair = 2 * rows
    half = rows // 2
    block = width // 4
    ff_part = narrow.shape[2]
    gate_up, lower = slice(0, 2 * ff_part), slice(2 * ff_part, 3 * ff_part)
    top, low = pl.ds(0, half), pl.ds(half, half)
    enter((to_x, to_y, to_c))

    def piece(t, s, h):
        return all_ref.at[t * seq + s, pl.ds(h * half, half)]

    def own(i, h, device):
        return remote(
            own_ref.at[pl.ds(h * half, half)],
            piece(tp_at, seq_at, h),
            sends.at[i],
            recvs.at[i],
            device,
        )

    def relay(i, t, s, h, device):
        return remote(piece(t, s, h), piece(t, s, h), sends.at[i], recvs.at[i], device)

    x0, x1 = own(0, 0, to_x), own(3, 1, to_x)
    y0, y1 = own(1, 0, to_y), own(4, 1, to_y)
    c0, c1 = own(2, 0, to_c), own(5, 1, to_c)
    diag0 = relay(6, tp_at, far, 0, to_y)
    diag1 = relay(7, other, seq_at, 1, to_x)
    rx0, rx1 = relay(8, tp_at, far, 0, to_c), relay(11, tp_at, far, 1, to_c)
    ry0, ry1 = relay(9, other, seq_at, 0, to_c), relay(10, other, seq_at, 1, to_c)
    rd0, rd1 = relay(12, other, far, 0, to_c), relay(13, other, far, 1, to_c)

    def give(c):
        return remote(
            part.at[c, 1 - kind], chip_in.at[c], sends.at[14 + c], recvs.at[14 + c], to_c
        )

    def hop(i, src, dst, device):
        return remote(src, dst, sends.at[i], recvs.at[i], device)

    def held(c):
        return part.at[c, kind]

    sum_x0 = hop(18, part.at[1, kind, top], near_in.at[0, top], to_x)
    sum_y1 = hop(19, part.at[2, kind, low], near_in.at[1, low], to_y)
    sum_d0 = hop(20, part.at[3, kind, top], far_in.at[0, top], to_x)
    sum_d1 = hop(21, part.at[3, kind, low], far_in.at[1, low], to_y)
    sum_y0 = hop(22, part.at[2, kind, top], near_in.at[1, top], to_y)
    sum_x1 = hop(23, part.at[1, kind, low], near_in.at[0, low], to_x)

    def chip_sum(c):
        give(c).wait_recv()
        add_rows(held(c), (held(c), chip_in.at[c]), 0, rows, part.dtype)

    def chip_rows(c):
        t = lax.rem(tp_at + c // 2, 2)
        s = lax.rem(seq_at + (seq // 2) * lax.rem(c, 2), seq)
        return t * seq + s - lax.rem(s, 2)

    def take_tokens(c):
        return pltpu.make_async_copy(
            all_ref.at[pl.ds(chip_rows(c), 2)], tokens.at[lax.rem(c, 2)], local.at[lax.rem(c, 2)]
        )

    def take_grads(c):
        return pltpu.make_async_copy(
            grad_ref.at[pl.ds(chip_rows(c), 2)], grads.at[c], local.at[2 + c]
        )

    def put_gug(c, slot):
        return pltpu.make_async_copy(
            gug.at[slot], gug_ref.at[chip_rows(c) // 2], local.at[6 + slot]
        )

    def put_down(n):
        slot = lax.rem(n, 2)
        return pltpu.make_async_copy(
            stage.at[slot], down_ref.at[pl.ds(n * block, block)], local.at[9 + slot]
        )

    def put_out(c):
        return pltpu.make_async_copy(
            tokens.at[lax.rem(c, 2)], out_ref.at[pl.ds(chip_rows(c), 2)], local.at[11 + lax.rem(c, 2)]
        )

    take_weight = pltpu.make_async_copy(weight_hbm, weight, local.at[13])
    mine = pltpu.make_async_copy(own_ref, all_ref.at[tp_at * seq + seq_at], local.at[14])

    for copy in (take_weight, x0, y0, c0, x1, y1, c1, mine):
        copy.start()
    for c in range(4):
        take_grads(c).start()

    def slopes(c, slot):
        def body(i, carry):
            at = pl.ds(i * SUB, SUB)
            gate, upward, grad = wide[at, :ff_part], wide[at, ff_part:], narrow[c, at, :]
            sigmoid_gate = jax.nn.sigmoid(gate)
            silu_gate = gate * sigmoid_gate
            inner[c, at, :] = (silu_gate * upward).astype(BF)
            slope = sigmoid_gate * (1.0 + gate * (1.0 - sigmoid_gate))
            gug[slot, at, :ff_part] = (grad * upward * slope).astype(BF)
            gug[slot, at, ff_part:] = (grad * silu_gate).astype(BF)
            return carry

        lax.fori_loop(0, pair // SUB, body, 0)
        put_gug(c, slot).start()

    def back(c, slot, n):
        at = pl.ds(pl.multiple_of(n * block, block), block)
        total = nt(gug[slot], weight[at, gate_up]).astype(part.dtype)
        part[c, :, :, at] = total.reshape(2, rows, block)

    def widen(slot):
        wide[...] = nn(tokens[slot].reshape(pair, width), weight[:, gate_up])

    take_weight.wait()

    def narrow_step(c, carry):
        take_grads(c).wait()
        narrow[c] = nn(grads[c].reshape(pair, width), weight[:, lower])
        return carry

    lax.fori_loop(0, 4, narrow_step, 0)
    mine.wait()
    c0.wait_recv()
    c1.wait_recv()
    take_tokens(0).start()
    x0.wait_recv()
    diag0.start()
    rx0.start()
    y0.wait_recv()
    ry0.start()
    take_tokens(0).wait()
    widen(0)
    slopes(0, 2)
    y1.wait_recv()
    diag1.start()
    ry1.start()
    x1.wait_recv()
    rx1.start()
    rx0.wait_recv()
    rx1.wait_recv()
    take_tokens(1).start()

    def chip_step(c, carry):
        slot = lax.rem(c, 2)
        take_tokens(c).wait()
        widen(slot)

        @pl.when(c == 1)
        def _():
            ry0.wait_recv()
            ry1.wait_recv()
            take_tokens(2).start()

        @pl.when(c == 2)
        def _():
            chip_sum(1)
            sum_x0.start()

        @pl.when(c == 3)
        def _():
            chip_sum(2)
            sum_y1.start()
            put_gug(1, 1).wait()

        slopes(c, slot)

        @pl.when(c == 2)
        def _():
            rd0.wait_recv()
            rd1.wait_recv()
            take_tokens(3).start()

        def back_step(n, carry):
            back(c, slot, n)
            return carry

        lax.fori_loop(0, 4, back_step, 0)
        give(c).start()

        @pl.when(c == 1)
        def _():
            diag0.wait_recv()
            rd0.start()
            diag1.wait_recv()
            rd1.start()

        return carry

    lax.fori_loop(1, 4, chip_step, 0)

    def own_step(n, carry):
        back(0, 2, n)

        @pl.when(n == 1)
        def _():
            chip_sum(3)
            sum_d0.start()
            sum_d1.start()

        return carry

    lax.fori_loop(0, 4, own_step, 0)
    give(0).start()

    def out_step(c, carry):
        slot = lax.rem(c, 2)

        @pl.when(c >= 2)
        def _():
            put_out(c - 2).wait()

        def out_block(n, carry):
            at = pl.ds(pl.multiple_of(n * block, block), block)
            total = nt(inner[c], weight[at, lower]).astype(tokens.dtype)
            tokens[slot, :, :, at] = total.reshape(2, rows, block)
            return carry

        lax.fori_loop(0, 4, out_block, 0)
        put_out(c).start()
        return carry

    lax.fori_loop(0, 4, out_step, 0)
    chip_sum(0)

    def down_step(n, carry):
        @pl.when(n == 1)
        def _():
            sum_d0.wait_recv()
            add_rows(held(2), (held(2), far_in.at[0]), 0, half, part.dtype)
            sum_y0.start()
            sum_d1.wait_recv()
            add_rows(held(1), (held(1), far_in.at[1]), half, half, part.dtype)
            sum_x1.start()

        @pl.when(n >= 2)
        def _():
            put_down(n - 2).wait()

        at = pl.ds(pl.multiple_of(n * block, block), block)
        left = grads[:, :, :, at].reshape(4 * pair, block)
        stage[lax.rem(n, 2)] = tn(left, inner[...].reshape(4 * pair, ff_part)).astype(BF)
        put_down(n).start()
        return carry

    lax.fori_loop(0, 4, down_step, 0)
    sum_x0.wait_recv()
    sum_y0.wait_recv()
    add_rows(sum_ref, (held(0), near_in.at[0], near_in.at[1]), 0, half, sum_ref.dtype)
    sum_y1.wait_recv()
    sum_x1.wait_recv()
    add_rows(sum_ref, (held(0), near_in.at[0], near_in.at[1]), half, half, sum_ref.dtype)
    for copy in (x0, y0, c0, x1, y1, c1, diag0, diag1, rx0, ry0, ry1, rx1, rd0, rd1):
        copy.wait_send()
    for c in range(4):
        give(c).wait_send()
    for copy in (sum_x0, sum_y1, sum_d0, sum_d1, sum_y0, sum_x1):
        copy.wait_send()
    for c, slot in ((0, 2), (2, 0), (3, 1)):
        put_gug(c, slot).wait()
    for c in (2, 3):
        put_out(c).wait()
        put_down(c).wait()


def ffn_plane(block, grads, weight, ident):
    rows, width = block.shape
    seq = lax.axis_size("seq")
    plane = lax.axis_size("tp") * seq
    chips = plane // 2
    ff_part = weight.shape[1] // 3
    shape = jax.ShapeDtypeStruct
    hbm = pl.BlockSpec(memory_space=pltpu.HBM)
    vmem = pl.BlockSpec(memory_space=pltpu.VMEM)
    tokens = plane * rows
    return pl.pallas_call(
        ffn_kernel,
        out_shape=(
            shape((plane, rows, width), BF),
            shape((chips, 2 * rows, 2 * ff_part), BF),
            shape((plane, rows, width), BF),
            shape((width, ff_part), BF),
            shape((rows, width), F32),
        ),
        in_specs=[vmem, hbm, hbm],
        out_specs=(hbm, hbm, hbm, hbm, vmem),
        scratch_shapes=[
            pltpu.VMEM(weight.shape, BF),
            pltpu.VMEM((2, 2, rows, width), BF),
            pltpu.VMEM((4, 2, rows, width), BF),
            pltpu.VMEM((2 * rows, 2 * ff_part), F32),
            pltpu.VMEM((4, 2 * rows, ff_part), F32),
            pltpu.VMEM((4, 2 * rows, ff_part), BF),
            pltpu.VMEM((3, 2 * rows, 2 * ff_part), BF),
            pltpu.VMEM((2, width // 4, ff_part), BF),
            pltpu.VMEM((4, 2, rows, width), BF),
            pltpu.VMEM((4, rows, width), BF),
            pltpu.VMEM((2, rows, width), BF),
            pltpu.VMEM((2, rows, width), BF),
            pltpu.SemaphoreType.DMA((24,)),
            pltpu.SemaphoreType.DMA((24,)),
            pltpu.SemaphoreType.DMA((15,)),
        ],
        cost_estimate=pl.CostEstimate(
            flops=14 * tokens * width * ff_part,
            transcendentals=tokens * ff_part,
            bytes_accessed=30 * tokens * width,
        ),
        compiler_params=pltpu.CompilerParams(
            collective_id=ident, has_side_effects=True, vmem_limit_bytes=63 << 20
        ),
        name="ffn_plane",
    )(block, grads, weight)


def finish_kernel(
    gu_ref,
    down_ref,
    gate_weight,
    up_weight,
    gain_ref,
    gate_out,
    up_out,
    down_out,
    gain_out,
    gu_in,
    down_in,
    local,
    sends,
    recvs,
):
    tp_at, seq_at, _, _, _ = plane_place()
    seq = lax.axis_size("seq")
    plane = lax.axis_size("tp") * seq
    me = tp_at * seq + seq_at
    peers = [lax.rem(me + k, plane) for k in range(1, plane)]
    devices = [at_device(peer // seq, lax.rem(peer, seq)) for peer in peers]
    enter(devices)
    copies = []
    for k, (peer, device) in enumerate(zip(peers, devices)):
        copies.append(remote(gu_ref.at[peer], gu_in.at[me], sends.at[k], recvs.at[k], device))
        i = plane - 1 + k
        copies.append(remote(down_ref.at[peer], down_in.at[me], sends.at[i], recvs.at[i], device))
    copies.append(pltpu.make_async_copy(gu_ref.at[me], gu_in.at[me], local.at[0]))
    copies.append(pltpu.make_async_copy(down_ref.at[me], down_in.at[me], local.at[1]))
    for copy in copies:
        copy.start()
    for copy in copies:
        copy.wait()
    put = pltpu.make_async_copy(down_in, down_out, local.at[2])
    put.start()
    gain = gain_ref[...]
    ff_part = down_in.shape[2]
    total = jnp.zeros(gain.shape, F32)
    for j in range(plane):
        at = slice(j * ff_part, (j + 1) * ff_part)
        for k, (out, weight) in enumerate(((gate_out, gate_weight), (up_out, up_weight))):
            own = gu_in[j, :, k * ff_part : (k + 1) * ff_part].astype(F32)
            out[:, at] = own * gain
            total = total + jnp.sum(own * weight[:, at].astype(F32), axis=1, keepdims=True)
    gain_out[...] = total
    put.wait()


def finish_plane(gu_sums, down_sums, gate_weight, up_weight, gain, ident):
    plane, rows, ff_part = down_sums.shape
    shape = jax.ShapeDtypeStruct
    hbm = pl.BlockSpec(memory_space=pltpu.HBM)
    vmem = pl.BlockSpec(memory_space=pltpu.VMEM)
    size = plane * rows * ff_part * 6
    return pl.pallas_call(
        finish_kernel,
        out_shape=(
            shape(gate_weight.shape, F32),
            shape(up_weight.shape, F32),
            shape(down_sums.shape, BF),
            shape((rows, 1), F32),
        ),
        in_specs=[hbm, hbm, vmem, vmem, vmem],
        out_specs=(vmem, vmem, hbm, vmem),
        scratch_shapes=[
            pltpu.VMEM(gu_sums.shape, BF),
            pltpu.VMEM(down_sums.shape, BF),
            pltpu.SemaphoreType.DMA((3,)),
            pltpu.SemaphoreType.DMA((2 * plane - 2,)),
            pltpu.SemaphoreType.DMA((2 * plane - 2,)),
        ],
        cost_estimate=pl.CostEstimate(flops=0, transcendentals=0, bytes_accessed=size * 20),
        compiler_params=pltpu.CompilerParams(
            collective_id=ident, has_side_effects=True, vmem_limit_bytes=24 << 20
        ),
        name="finish_plane",
    )(gu_sums, down_sums, gate_weight, up_weight, gain)


def columns(matrix, parts):
    rows, cols = matrix.shape
    return jnp.transpose(matrix.reshape(rows, parts, cols // parts), (1, 0, 2))


def uncolumns(blocks):
    parts, rows, cols = blocks.shape
    return jnp.transpose(blocks, (1, 0, 2)).reshape(rows, parts * cols)


def after(value, *earlier):
    return lax.optimization_barrier((value,) + earlier)[0]


def per_device(
    layer_input,
    pic_starts,
    skip_mask,
    gain_attn,
    w_query,
    w_key,
    w_value,
    w_out,
    gain_ffn,
    w_gate,
    w_up,
    w_down,
    cotangent,
):
    _, local_len, width = layer_input.shape
    seq = lax.axis_size("seq")
    plane = lax.axis_size("tp") * seq
    total_len = local_len * seq
    heads = H // plane
    share = plane // KV
    ff_part = w_gate.shape[1] // plane
    q_part = heads * DH

    gain1 = gain_attn[:, None]
    gain2 = gain_ffn[:, None]
    wq32, wk32, wv32 = w_query.astype(F32), w_key.astype(F32), w_value.astype(F32)
    wg32, wu32 = w_gate.astype(F32), w_up.astype(F32)
    attn_pack = jnp.concatenate(
        [
            columns((wq32 * gain1).astype(BF), plane),
            jnp.repeat(columns((wk32 * gain1).astype(BF), KV), share, axis=0),
            jnp.repeat(columns((wv32 * gain1).astype(BF), KV), share, axis=0),
            columns(w_out.T, plane),
        ],
        axis=2,
    )
    attn_rows = exchange_plane(attn_pack, 0)
    attn_rows = attn_rows.reshape(-1, attn_rows.shape[2])
    attn_weight = lax.all_gather(attn_rows, "rep", axis=0, tiled=True)
    qkv_weight = attn_weight[:, : q_part + 2 * DH]
    out_weight = attn_weight[:, q_part + 2 * DH :]

    tokens = layer_input.reshape(local_len, width).astype(F32)
    keep = (1 - skip_mask).astype(F32).reshape(local_len, 1)
    upstream = cotangent.reshape(local_len, width).astype(F32)
    scale1 = rms_scale(tokens)
    norm1 = tokens * scale1

    ffn_pack = jnp.concatenate(
        [
            columns((wg32 * gain2).astype(BF), plane),
            columns((wu32 * gain2).astype(BF), plane),
            columns(w_down.T, plane),
        ],
        axis=2,
    )
    ffn_rows = exchange_plane(after(ffn_pack, attn_rows), 2)
    ffn_rows = ffn_rows.reshape(-1, ffn_rows.shape[2])
    ffn_weight = lax.all_gather(ffn_rows, "rep", axis=0, tiled=True)
    norm1_all = gather_plane(after(norm1.astype(BF), ffn_rows), 1)
    other_starts = lax.ppermute(pic_starts, "tp", [(0, 1), (1, 0)])
    starts = jnp.where(
        lax.axis_index("tp") == 0,
        jnp.concatenate([pic_starts, other_starts], axis=0),
        jnp.concatenate([other_starts, pic_starts], axis=0),
    )
    positions = jnp.arange(total_len, dtype=jnp.int32)
    cos_table, sin_table = rotary_tables(positions, DH)
    cos = jnp.concatenate([cos_table, cos_table], axis=1)
    sin = jnp.concatenate([-sin_table, sin_table], axis=1)
    projected = nn(norm1_all, qkv_weight)
    qkv, mixed, log_total, ffn_grad = attn_front_plane(
        starts, projected, cos, sin, (keep * upstream).astype(BF), 3
    )
    branch = scatter_plane(nt(mixed, out_weight).astype(BF), 4)
    hidden = tokens + keep * branch

    scale2 = rms_scale(hidden)
    norm2 = hidden * scale2
    norm2_all, gate_up_grad, out_partial, down_partial, scaled2 = ffn_plane(
        norm2.astype(BF), ffn_grad, ffn_weight, 5
    )
    norm2_all = norm2_all.reshape(-1, width)
    gate_up_grad = gate_up_grad.reshape(-1, 2 * ff_part)
    down_sums = lax.psum_scatter(down_partial, "rep", scatter_dimension=0, tiled=True)
    gu_partial = tn(norm2_all, after(gate_up_grad, down_partial)).astype(BF)
    gu_sums = lax.psum_scatter(gu_partial, "rep", scatter_dimension=0, tiled=True)
    hidden_grad = upstream + scale2 * (
        scaled2 - norm2 * jnp.mean(scaled2 * norm2, axis=-1, keepdims=True)
    )

    branch_grad = gather_plane(after((keep * hidden_grad).astype(BF), gu_partial, down_partial), 7)
    mixed_grad = nn(branch_grad, out_weight).astype(BF)
    qkv_grad, ffn_out = attn_back_plane(
        starts,
        qkv,
        after(mixed_grad, down_sums),
        log_total,
        cos,
        sin,
        out_partial.reshape(-1, width),
        9,
    )
    attn_partial = jnp.concatenate(
        [tn(norm1_all, qkv_grad).astype(BF), tn(branch_grad, mixed).astype(BF)], axis=1
    )
    scaled1_partial = nt(qkv_grad, qkv_weight).astype(BF)
    attn_sums = lax.psum_scatter(attn_partial, "rep", scatter_dimension=0, tiled=True)
    scaled1 = scatter_plane(after(scaled1_partial, attn_partial), 8)
    input_grad = hidden_grad + scale1 * (
        scaled1 - norm1 * jnp.mean(scaled1 * norm1, axis=-1, keepdims=True)
    )
    out_hidden = (hidden + keep * ffn_out).astype(BF)

    gate_grad, up_grad, down_own, gain_ffn_grad = finish_plane(
        after(gu_sums.reshape(plane, -1, 2 * ff_part), scaled1),
        down_sums.reshape(plane, -1, ff_part),
        w_gate,
        w_up,
        gain2,
        10,
    )
    down_grad = jnp.transpose(down_own, (0, 2, 1)).reshape(plane * ff_part, -1).astype(F32)

    attn_sums = after(attn_sums, gain_ffn_grad)
    attn_own = exchange_plane(attn_sums.reshape(plane, -1, attn_sums.shape[1]), 11).astype(F32)
    query_own = uncolumns(attn_own[:, :, :q_part])
    kv_own = attn_own[:, :, q_part : q_part + 2 * DH]
    kv_own = jnp.sum(kv_own.reshape(KV, share, -1, 2 * DH), axis=1)
    key_own = uncolumns(kv_own[:, :, :DH])
    value_own = uncolumns(kv_own[:, :, DH:])
    out_own = uncolumns(attn_own[:, :, q_part + 2 * DH :])
    gain_attn_grad = (
        jnp.sum(query_own * wq32, axis=1)
        + jnp.sum(key_own * wk32, axis=1)
        + jnp.sum(value_own * wv32, axis=1)
    )
    return (
        out_hidden[None],
        input_grad[None],
        gain_attn_grad,
        query_own * gain1,
        key_own * gain1,
        value_own * gain1,
        out_own.T,
        gain_ffn_grad[:, 0],
        gate_grad,
        up_grad,
        down_grad,
    )


def solution(mesh):
    devices = mesh.devices
    dp, seq = devices.shape
    inner = Mesh(devices.reshape(dp // TP, TP, seq), ("rep", "tp", "seq"))
    dps = ("rep", "tp")
    every = ("rep", "tp", "seq")
    token = P(dps, "seq", None)
    row = P(every, None)
    col = P(None, every)
    return jax.shard_map(
        per_device,
        mesh=inner,
        in_specs=(
            token,
            P(dps, None),
            P(dps, "seq"),
            P(every),
            row,
            row,
            row,
            col,
            P(every),
            row,
            row,
            col,
            token,
        ),
        out_specs=(token, token, P(every), row, row, row, col, P(every), row, row, col),
        check_vma=False,
    )
```

```python
import jax
import jax.numpy as jnp
from jax import lax
from jax.experimental import pallas as pl
from jax.experimental.pallas import tpu as pltpu
from jax.sharding import Mesh
from jax.sharding import PartitionSpec as P

H = 16
KV = 4
DH = 128
PIC = 256
NPIC = 2
EPS = 1e-05
TP = 2
BF = jnp.bfloat16
F32 = jnp.float32


def rotary_tables(positions, head_dim):
    half_dim = head_dim // 2
    inverse = 10000.0 ** (-(jnp.arange(half_dim, dtype=F32) * 2.0 / head_dim))
    angles = positions.astype(F32)[:, None] * inverse[None, :]
    return (jnp.cos(angles), jnp.sin(angles))


def rms_scale(rows):
    return lax.rsqrt(jnp.mean(rows * rows, axis=-1, keepdims=True) + EPS)


def dot(left, right, contract):
    return lax.dot_general(
        left, right, ((contract[:1], contract[1:]), ((), ())), preferred_element_type=F32
    )


def nn(left, right):
    return dot(left, right, (1, 0))


def nt(left, right):
    return dot(left, right, (1, 1))


def tn(left, right):
    return dot(left, right, (0, 0))


MESH_ID = pl.DeviceIdType.MESH
SUB = 32


def plane_place():
    tp_at = lax.axis_index("tp")
    seq_at = lax.axis_index("seq")
    seq = lax.axis_size("seq")
    half = seq // 2
    far = lax.rem(seq_at + half, seq)
    mate = seq_at + 1 - 2 * lax.rem(seq_at, 2)
    far_mate = far + 1 - 2 * lax.rem(far, 2)
    return tp_at, seq_at, far, mate, far_mate


def at_device(tp_at, seq_at):
    return (lax.axis_index("rep"), tp_at, seq_at)


def enter(devices):
    barrier = pltpu.get_barrier_semaphore()
    for device in devices:
        pl.semaphore_signal(barrier, inc=1, device_id=device, device_id_type=MESH_ID)
    pl.semaphore_wait(barrier, len(devices))


def remote(src, dst, send, recv, device):
    return pltpu.make_async_remote_copy(
        src_ref=src,
        dst_ref=dst,
        send_sem=send,
        recv_sem=recv,
        device_id=device,
        device_id_type=MESH_ID,
    )


def gather_stages(own_ref, all_ref, sends, recvs, local):
    tp_at, seq_at, far, mate, _ = plane_place()
    seq = lax.axis_size("seq")
    other = 1 - tp_at
    to_x = at_device(tp_at, far)
    to_y = at_device(other, seq_at)
    to_c = at_device(tp_at, mate)
    rows = own_ref.shape[0]
    part = rows // 2

    def piece(t, s, h):
        return all_ref.at[t * seq + s, pl.ds(h * part, part)]

    def relay(i, t, s, h, device):
        return remote(piece(t, s, h), piece(t, s, h), sends.at[i], recvs.at[i], device)

    def own(i, h, device):
        return remote(
            own_ref.at[pl.ds(h * part, part)],
            piece(tp_at, seq_at, h),
            sends.at[i],
            recvs.at[i],
            device,
        )

    x0, x1 = own(0, 0, to_x), own(3, 1, to_x)
    y0, y1 = own(1, 0, to_y), own(4, 1, to_y)
    c0, c1 = own(2, 0, to_c), own(5, 1, to_c)
    diag0 = relay(6, tp_at, far, 0, to_y)
    diag1 = relay(7, other, seq_at, 1, to_x)
    rx0, rx1 = relay(8, tp_at, far, 0, to_c), relay(11, tp_at, far, 1, to_c)
    ry0, ry1 = relay(9, other, seq_at, 0, to_c), relay(10, other, seq_at, 1, to_c)
    rd0, rd1 = relay(12, other, far, 0, to_c), relay(13, other, far, 1, to_c)
    mine = pltpu.make_async_copy(own_ref, all_ref.at[tp_at * seq + seq_at], local)

    def begin():
        enter((to_x, to_y, to_c))
        for copy in (x0, y0, c0, x1, y1, c1, mine):
            copy.start()

    def first():
        x0.wait_recv()
        diag0.start()
        rx0.start()
        y0.wait_recv()
        ry0.start()

    def second():
        y1.wait_recv()
        diag1.start()
        ry1.start()
        x1.wait_recv()
        rx1.start()

    def finish():
        diag0.wait_recv()
        rd0.start()
        diag1.wait_recv()
        rd1.start()
        for copy in (c0, c1, rx0, ry0, ry1, rx1, rd0, rd1):
            copy.wait_recv()
        for copy in (x0, y0, c0, x1, y1, c1, diag0, diag1, rx0, ry0, ry1, rx1, rd0, rd1):
            copy.wait_send()
        mine.wait()

    return begin, first, second, finish


def gather_kernel(*refs):
    for stage in gather_stages(*refs):
        stage()


GATHER_SCRATCH = (
    pltpu.SemaphoreType.DMA((14,)),
    pltpu.SemaphoreType.DMA((14,)),
    pltpu.SemaphoreType.DMA,
)


def gather_plane(block, ident):
    rows, width = block.shape
    plane = lax.axis_size("tp") * lax.axis_size("seq")
    size = rows * width * 2
    gathered = pl.pallas_call(
        gather_kernel,
        out_shape=jax.ShapeDtypeStruct((plane, rows, width), block.dtype),
        in_specs=[pl.BlockSpec(memory_space=pltpu.VMEM)],
        out_specs=pl.BlockSpec(memory_space=pltpu.HBM),
        scratch_shapes=GATHER_SCRATCH,
        cost_estimate=pl.CostEstimate(
            flops=0, transcendentals=0, bytes_accessed=plane * size * 12
        ),
        compiler_params=pltpu.CompilerParams(collective_id=ident, has_side_effects=True),
        name="gather_plane",
    )(block)
    return gathered.reshape(plane * rows, width)


def add_rows(target, sources, start, count, kind):
    step = min(SUB, count)

    def body(i, carry):
        at = pl.ds(start + i * step, step)
        total = sources[0][at, :].astype(F32)
        for source in sources[1:]:
            total = total + source[at, :].astype(F32)
        target[at, :] = total.astype(kind)
        return carry

    lax.fori_loop(0, count // step, body, 0)


def scatter_stages(part_ref, sum_ref, held, chip_in, far_in, near_in, loads, sends, recvs):
    tp_at, seq_at, far, mate, far_mate = plane_place()
    seq = lax.axis_size("seq")
    other = 1 - tp_at
    to_x = at_device(tp_at, far)
    to_y = at_device(other, seq_at)
    to_c = at_device(tp_at, mate)
    rows = sum_ref.shape[0]
    part = rows // 2
    top, low = pl.ds(0, part), pl.ds(part, part)
    chips = ((other, far, far_mate), (tp_at, far, far_mate), (other, seq_at, mate), (tp_at, seq_at, mate))
    gives = [
        remote(part_ref.at[t * seq + m], chip_in.at[k], sends.at[k], recvs.at[k], to_c)
        for k, (t, s, m) in enumerate(chips)
    ]
    takes = [
        pltpu.make_async_copy(part_ref.at[t * seq + s], held.at[k], loads.at[k])
        for k, (t, s, m) in enumerate(chips)
    ]

    def hop(i, src, dst, device):
        return remote(src, dst, sends.at[i], recvs.at[i], device)

    d0 = hop(4, held.at[0, top], far_in.at[0, top], to_x)
    d1 = hop(5, held.at[0, low], far_in.at[1, low], to_y)
    x0 = hop(6, held.at[1, top], near_in.at[0, top], to_x)
    y1 = hop(7, held.at[2, low], near_in.at[1, low], to_y)
    y0 = hop(8, held.at[2, top], near_in.at[1, top], to_y)
    x1 = hop(9, held.at[1, low], near_in.at[0, low], to_x)

    def begin():
        enter((to_x, to_y, to_c))
        for give, take in zip(gives, takes):
            give.start()
            take.start()

    def chip_sum(k):
        takes[k].wait()
        gives[k].wait_recv()
        add_rows(held.at[k], (held.at[k], chip_in.at[k]), 0, rows, held.dtype)

    def diagonal():
        chip_sum(0)
        d0.start()
        d1.start()

    def along_x():
        chip_sum(1)
        x0.start()

    def along_y():
        chip_sum(2)
        y1.start()

    def own():
        chip_sum(3)

    def fold():
        d0.wait_recv()
        add_rows(held.at[2], (held.at[2], far_in.at[0]), 0, part, held.dtype)
        y0.start()
        d1.wait_recv()
        add_rows(held.at[1], (held.at[1], far_in.at[1]), part, part, held.dtype)
        x1.start()

    def finish():
        x0.wait_recv()
        y0.wait_recv()
        add_rows(sum_ref, (held.at[3], near_in.at[0], near_in.at[1]), 0, part, sum_ref.dtype)
        y1.wait_recv()
        x1.wait_recv()
        add_rows(sum_ref, (held.at[3], near_in.at[0], near_in.at[1]), part, part, sum_ref.dtype)
        for copy in gives + [d0, d1, x0, y1, y0, x1]:
            copy.wait_send()

    return begin, diagonal, along_x, along_y, own, fold, finish


def scatter_kernel(*refs):
    for stage in scatter_stages(*refs):
        stage()


def scatter_scratch(rows, width, kind):
    return [
        pltpu.VMEM((4, rows, width), kind),
        pltpu.VMEM((4, rows, width), kind),
        pltpu.VMEM((2, rows, width), kind),
        pltpu.VMEM((2, rows, width), kind),
        pltpu.SemaphoreType.DMA((4,)),
        pltpu.SemaphoreType.DMA((10,)),
        pltpu.SemaphoreType.DMA((10,)),
    ]


def scatter_plane(partial, ident):
    plane = lax.axis_size("tp") * lax.axis_size("seq")
    rows, width = partial.shape[0] // plane, partial.shape[1]
    kind = partial.dtype
    size = rows * width * 2
    return pl.pallas_call(
        scatter_kernel,
        out_shape=jax.ShapeDtypeStruct((rows, width), F32),
        in_specs=[pl.BlockSpec(memory_space=pltpu.HBM)],
        out_specs=pl.BlockSpec(memory_space=pltpu.VMEM),
        scratch_shapes=scatter_scratch(rows, width, kind),
        cost_estimate=pl.CostEstimate(
            flops=0, transcendentals=0, bytes_accessed=plane * size * 14
        ),
        compiler_params=pltpu.CompilerParams(
            collective_id=ident, has_side_effects=True, vmem_limit_bytes=32 << 20
        ),
        name="scatter_plane",
    )(partial.reshape(plane, rows, width))


def fill_bias(bias, starts_ref, t, blocks):
    for b in range(blocks):
        span = min(2, blocks - b) * PIC
        k_at = lax.broadcasted_iota(jnp.int32, (span, PIC), 0) + b * PIC
        q_at = lax.broadcasted_iota(jnp.int32, (span, PIC), 1) + b * PIC
        high, below = jnp.maximum(k_at, q_at), jnp.minimum(k_at, q_at)
        allowed = k_at <= q_at
        for j in range(NPIC):
            start = starts_ref[t, j]
            allowed = allowed | ((below >= start) & (high < start + PIC))
        bias[b, :span, :] = jnp.where(allowed, 0.0, -jnp.inf)


def masked(scores, bias, b):
    late = scores[b * PIC :] + bias[b, : scores.shape[0] - b * PIC, :]
    return jnp.concatenate([scores[: b * PIC], late], axis=0) if b else late


def attn_front_kernel(
    starts_ref,
    projected_ref,
    cos_ref,
    sin_ref,
    own_ref,
    qkv_ref,
    mixed_ref,
    log_ref,
    all_ref,
    bias,
    turned,
    *gather,
):
    begin, first, second, finish = gather_stages(own_ref, all_ref, *gather)
    begin()
    total, dim = cos_ref.shape
    heads = mixed_ref.shape[1] // dim
    blocks = total // PIC
    scale = dim ** (-0.5)
    k_cols = slice(heads * dim, (heads + 1) * dim)
    v_cols = slice((heads + 1) * dim, (heads + 2) * dim)

    def turn(rows, at):
        return rows * cos_ref[at, :] + pltpu.roll(rows, dim // 2, 1) * sin_ref[at, :]

    def head_step(i, carry):
        t, h = i // heads, lax.rem(i, heads)
        base = pl.multiple_of(t * total, total)
        cols = pl.ds(pl.multiple_of(h * dim, dim), dim)

        @pl.when(h == 0)
        def _():
            rows = pl.ds(base, total)
            values = projected_ref[rows, v_cols].astype(BF)
            qkv_ref[rows, k_cols] = turn(projected_ref[rows, k_cols], pl.ds(0, total)).astype(BF)
            qkv_ref[rows, v_cols] = values
            turned[...] = values.T
            fill_bias(bias, starts_ref, t, blocks)

        for b in range(blocks):
            at = pl.ds(pl.multiple_of(base + b * PIC, PIC), PIC)
            count = min(b + 2, blocks) * PIC
            queries = turn(projected_ref[at, cols], pl.ds(b * PIC, PIC)).astype(BF)
            qkv_ref[at, cols] = queries
            scores = nt(qkv_ref[pl.ds(base, count), k_cols], queries) * scale
            scores = masked(scores, bias, b)
            peak = jnp.max(scores, axis=0, keepdims=True)
            weights = jnp.exp(scores - peak)
            mass = jnp.sum(weights, axis=0, keepdims=True)
            log_ref[i, :, b * PIC : (b + 1) * PIC] = peak + jnp.log(mass)
            probs = (weights * (1.0 / mass)).astype(BF)
            mixed_ref[at, cols] = nn(turned[:, :count], probs).T.astype(BF)
            if b == 0:
                pl.when(i == 2)(first)

        return carry

    lax.fori_loop(0, log_ref.shape[0], head_step, 0)
    second()
    finish()


def attn_front_plane(starts, projected, cos, sin, block, ident):
    rows, width = block.shape
    plane = lax.axis_size("tp") * lax.axis_size("seq")
    total, dim = cos.shape
    tokens, cols = projected.shape
    q_part = cols - 2 * dim
    shape = jax.ShapeDtypeStruct
    vmem = pl.BlockSpec(memory_space=pltpu.VMEM)
    smem = pl.BlockSpec(memory_space=pltpu.SMEM)
    hbm = pl.BlockSpec(memory_space=pltpu.HBM)
    return pl.pallas_call(
        attn_front_kernel,
        out_shape=(
            shape((tokens, cols), BF),
            shape((tokens, q_part), BF),
            shape((tokens * q_part // dim // total, 1, total), F32),
            shape((plane, rows, width), block.dtype),
        ),
        in_specs=[smem] + [vmem] * 4,
        out_specs=(vmem, vmem, vmem, hbm),
        scratch_shapes=[
            pltpu.VMEM((total // PIC, 2 * PIC, PIC), F32),
            pltpu.VMEM((dim, total), BF),
            *GATHER_SCRATCH,
        ],
        cost_estimate=pl.CostEstimate(
            flops=4 * tokens * total * q_part,
            transcendentals=tokens * total * q_part // dim,
            bytes_accessed=plane * rows * width * 24,
        ),
        compiler_params=pltpu.CompilerParams(
            collective_id=ident, has_side_effects=True, vmem_limit_bytes=40 << 20
        ),
        name="attn_front_plane",
    )(starts, projected, cos, sin, block)


def attn_back_kernel(
    starts_ref,
    qkv_ref,
    g_ref,
    log_ref,
    cos_ref,
    sin_ref,
    part_ref,
    grad_ref,
    sum_ref,
    bias,
    turned,
    keys_sum,
    values_sum,
    *scatter,
):
    begin, diagonal, along_x, along_y, own, fold, finish = scatter_stages(
        part_ref, sum_ref, *scatter
    )
    begin()
    total, dim = cos_ref.shape
    heads = g_ref.shape[1] // dim
    blocks = total // PIC
    scale = dim ** (-0.5)
    k_cols = slice(heads * dim, (heads + 1) * dim)
    v_cols = slice((heads + 1) * dim, (heads + 2) * dim)
    events = {(0, 1): diagonal, (0, 2): along_x, (0, 3): along_y, (1, 0): own, (2, 2): fold}

    def unturn(rows, at):
        return rows * cos_ref[at, :] - pltpu.roll(rows, dim // 2, 1) * sin_ref[at, :]

    def head_step(i, carry):
        t, h = i // heads, lax.rem(i, heads)
        base = pl.multiple_of(t * total, total)
        cols = pl.ds(pl.multiple_of(h * dim, dim), dim)

        @pl.when(h == 0)
        def _():
            turned[...] = qkv_ref[pl.ds(base, total), k_cols].T
            keys_sum[...] = jnp.zeros(keys_sum.shape, F32)
            values_sum[...] = jnp.zeros(values_sum.shape, F32)
            fill_bias(bias, starts_ref, t, blocks)

        for b in range(blocks):
            at = pl.ds(pl.multiple_of(base + b * PIC, PIC), PIC)
            count = min(b + 2, blocks) * PIC
            seen = pl.ds(base, count)
            queries, grads = qkv_ref[at, cols], g_ref[at, cols]
            scores = nt(qkv_ref[seen, k_cols], queries) * scale - log_ref[i, :, b * PIC : (b + 1) * PIC]
            probs = jnp.exp(masked(scores, bias, b))
            prob_grad = nt(qkv_ref[seen, v_cols], grads)
            mean = jnp.sum(probs * prob_grad, axis=0, keepdims=True)
            score_grad = (probs * (prob_grad - mean)).astype(BF)
            values_sum[:count, :] += nn(probs.astype(BF), grads)
            keys_sum[:count, :] += nn(score_grad, queries)
            back = nn(turned[:, :count], score_grad).T * scale
            grad_ref[at, cols] = unturn(back, pl.ds(b * PIC, PIC)).astype(BF)
            for (step, block), stage in events.items():
                if block == b:
                    pl.when(i == step)(stage)

        @pl.when(h == heads - 1)
        def _():
            rows = pl.ds(base, total)
            back = unturn(keys_sum[...] * scale, pl.ds(0, total))
            grad_ref[rows, k_cols] = back.astype(BF)
            grad_ref[rows, v_cols] = values_sum[...].astype(BF)

        return carry

    lax.fori_loop(0, log_ref.shape[0], head_step, 0)
    finish()


def attn_back_plane(starts, qkv, grads, log_total, cos, sin, partial, ident):
    plane = lax.axis_size("tp") * lax.axis_size("seq")
    rows, width = partial.shape[0] // plane, partial.shape[1]
    total, dim = cos.shape
    tokens, q_part = grads.shape
    hbm = pl.BlockSpec(memory_space=pltpu.HBM)
    vmem = pl.BlockSpec(memory_space=pltpu.VMEM)
    smem = pl.BlockSpec(memory_space=pltpu.SMEM)
    return pl.pallas_call(
        attn_back_kernel,
        out_shape=(
            jax.ShapeDtypeStruct((tokens, q_part + 2 * dim), BF),
            jax.ShapeDtypeStruct((rows, width), F32),
        ),
        in_specs=[smem] + [vmem] * 5 + [hbm],
        out_specs=(vmem, vmem),
        scratch_shapes=[
            pltpu.VMEM((total // PIC, 2 * PIC, PIC), F32),
            pltpu.VMEM((dim, total), BF),
            pltpu.VMEM((total, dim), F32),
            pltpu.VMEM((total, dim), F32),
        ]
        + scatter_scratch(rows, width, partial.dtype),
        cost_estimate=pl.CostEstimate(
            flops=10 * tokens * total * q_part,
            transcendentals=tokens * total * q_part // dim,
            bytes_accessed=plane * rows * width * 28,
        ),
        compiler_params=pltpu.CompilerParams(
            collective_id=ident, has_side_effects=True, vmem_limit_bytes=50 << 20
        ),
        name="attn_back_plane",
    )(starts, qkv, grads, log_total, cos, sin, partial.reshape(plane, rows, width))


def exchange_kernel(in_ref, out_ref, stage, local, sends, recvs):
    tp_at, seq_at, _, _, _ = plane_place()
    seq = lax.axis_size("seq")
    plane = lax.axis_size("tp") * seq
    me = tp_at * seq + seq_at
    peers = [lax.rem(me + k, plane) for k in range(1, plane)]
    devices = [at_device(peer // seq, lax.rem(peer, seq)) for peer in peers]
    enter(devices)
    copies = []
    for k, (peer, device) in enumerate(zip(peers, devices)):
        copy = remote(in_ref.at[peer], out_ref.at[me], sends.at[k], recvs.at[k], device)
        copy.start()
        copies.append(copy)
    take = pltpu.make_async_copy(in_ref.at[me], stage, local.at[0])
    take.start()
    take.wait()
    put = pltpu.make_async_copy(stage, out_ref.at[me], local.at[1])
    put.start()
    for copy in copies:
        copy.wait()
    put.wait()


def exchange_plane(blocks, ident):
    plane, rows, width = blocks.shape
    size = plane * rows * width * 2
    return pl.pallas_call(
        exchange_kernel,
        out_shape=jax.ShapeDtypeStruct(blocks.shape, blocks.dtype),
        in_specs=[pl.BlockSpec(memory_space=pltpu.HBM)],
        out_specs=pl.BlockSpec(memory_space=pltpu.HBM),
        scratch_shapes=[
            pltpu.VMEM((rows, width), blocks.dtype),
            pltpu.SemaphoreType.DMA((2,)),
            pltpu.SemaphoreType.DMA((plane - 1,)),
            pltpu.SemaphoreType.DMA((plane - 1,)),
        ],
        cost_estimate=pl.CostEstimate(flops=0, transcendentals=0, bytes_accessed=size * 20),
        compiler_params=pltpu.CompilerParams(collective_id=ident, has_side_effects=True),
        name="exchange_plane",
    )(blocks)


def slopes(wide, narrow, inner, gug):
    ff_part = inner.shape[1]

    def body(i, carry):
        at = pl.ds(i * SUB, SUB)
        gate, upward, grad = wide[at, :ff_part], wide[at, ff_part:], narrow[at, :]
        sigmoid_gate = jax.nn.sigmoid(gate)
        silu_gate = gate * sigmoid_gate
        inner[at, :] = (silu_gate * upward).astype(BF)
        slope = sigmoid_gate * (1.0 + gate * (1.0 - sigmoid_gate))
        gug[at, :ff_part] = (grad * upward * slope).astype(BF)
        gug[at, ff_part:] = (grad * silu_gate).astype(BF)
        return carry

    lax.fori_loop(0, wide.shape[0] // SUB, body, 0)


def weight_step(n, tokens, grads, gug, inner, stage, weight_ref, sems):
    slot = lax.rem(n, 2)
    block, cols = stage.shape[1:]
    ff_part = cols // 3
    count = gug.shape[0] * gug.shape[1]

    def put(m):
        return pltpu.make_async_copy(
            stage.at[lax.rem(m, 2)], weight_ref.at[pl.ds(m * block, block)], sems[0].at[sems[1] + lax.rem(m, 2)]
        )

    @pl.when(n >= 2)
    def _():
        put(n - 2).wait()

    at = pl.ds(pl.multiple_of(n * block, block), block)
    left = tokens[:, :, :, at].reshape(count, block)
    stage[slot, :, : 2 * ff_part] = tn(left, gug[...].reshape(count, 2 * ff_part)).astype(BF)
    left = grads[:, :, :, at].reshape(count, block)
    stage[slot, :, 2 * ff_part :] = tn(left, inner[...].reshape(count, ff_part)).astype(BF)
    put(n).start()
    return put


def ffn_first_kernel(
    own_ref,
    grad_ref,
    weight_hbm,
    all_ref,
    back_ref,
    out_ref,
    grads_out,
    weight,
    tokens,
    grads,
    wide,
    narrow,
    inner,
    gug,
    stage,
    columns_stage,
    sends,
    recvs,
    local,
):
    tp_at, seq_at, far, mate, _ = plane_place()
    seq = lax.axis_size("seq")
    other = 1 - tp_at
    to_x = at_device(tp_at, far)
    to_y = at_device(other, seq_at)
    to_c = at_device(tp_at, mate)
    rows, width = own_ref.shape
    pair = 2 * rows
    half = rows // 2
    block = width // 4
    ff_part = narrow.shape[2]
    gate_up, lower = slice(0, 2 * ff_part), slice(2 * ff_part, 3 * ff_part)
    enter((to_x, to_y, to_c))

    def piece(t, s, h):
        return all_ref.at[t * seq + s, pl.ds(h * half, half)]

    def own(i, h, device):
        return remote(
            own_ref.at[pl.ds(h * half, half)],
            piece(tp_at, seq_at, h),
            sends.at[i],
            recvs.at[i],
            device,
        )

    def relay(i, t, s, h, device):
        return remote(piece(t, s, h), piece(t, s, h), sends.at[i], recvs.at[i], device)

    x0, x1 = own(0, 0, to_x), own(3, 1, to_x)
    y0, y1 = own(1, 0, to_y), own(4, 1, to_y)
    c0, c1 = own(2, 0, to_c), own(5, 1, to_c)
    diag0 = relay(6, tp_at, far, 0, to_y)
    diag1 = relay(7, other, seq_at, 1, to_x)
    rx0, rx1 = relay(8, tp_at, far, 0, to_c), relay(11, tp_at, far, 1, to_c)
    ry0, ry1 = relay(9, other, seq_at, 0, to_c), relay(10, other, seq_at, 1, to_c)
    rd0, rd1 = relay(12, other, far, 0, to_c), relay(13, other, far, 1, to_c)

    def chip_rows(c):
        t = lax.rem(tp_at + c // 2, 2)
        s = lax.rem(seq_at + (seq // 2) * lax.rem(c, 2), seq)
        return pl.ds(t * seq + s - lax.rem(s, 2), 2)

    def take_tokens(c):
        return pltpu.make_async_copy(all_ref.at[chip_rows(c)], tokens.at[c], local.at[c])

    def take_grads(c):
        return pltpu.make_async_copy(grad_ref.at[chip_rows(c)], grads.at[c], local.at[4 + c])

    def put_back(c):
        return pltpu.make_async_copy(stage.at[0], back_ref.at[chip_rows(c)], local.at[8])

    def put_out(c):
        return pltpu.make_async_copy(stage.at[1], out_ref.at[chip_rows(c)], local.at[9])

    take_weight = pltpu.make_async_copy(weight_hbm, weight, local.at[12])
    mine = pltpu.make_async_copy(own_ref, all_ref.at[tp_at * seq + seq_at], local.at[13])
    for copy in (take_weight, x0, y0, c0, x1, y1, c1, mine):
        copy.start()
    for c in range(4):
        take_grads(c).start()
    take_weight.wait()

    def narrow_step(c, carry):
        take_grads(c).wait()
        narrow[c] = nn(grads[c].reshape(pair, width), weight[:, lower])
        return carry

    lax.fori_loop(0, 4, narrow_step, 0)
    mine.wait()
    c0.wait_recv()
    c1.wait_recv()
    take_tokens(0).start()

    def chip_step(c, carry):
        take_tokens(c).wait()
        wide[...] = nn(tokens[c].reshape(pair, width), weight[:, gate_up])

        @pl.when(c == 0)
        def _():
            x0.wait_recv()
            diag0.start()
            rx0.start()
            y0.wait_recv()
            ry0.start()

        @pl.when(c == 1)
        def _():
            ry0.wait_recv()
            ry1.wait_recv()
            take_tokens(2).start()

        @pl.when(c == 2)
        def _():
            diag0.wait_recv()
            rd0.start()
            diag1.wait_recv()
            rd1.start()

        slopes(wide, narrow.at[c], inner.at[c], gug.at[c])

        @pl.when(c >= 1)
        def _():
            put_back(c - 1).wait()
            put_out(c - 1).wait()

        def back_step(n, carry):
            at = pl.ds(pl.multiple_of(n * block, block), block)
            total = nt(gug[c], weight[at, gate_up]).astype(BF)
            stage[0, :, :, at] = total.reshape(2, rows, block)
            total = nt(inner[c], weight[at, lower]).astype(BF)
            stage[1, :, :, at] = total.reshape(2, rows, block)
            return carry

        lax.fori_loop(0, 4, back_step, 0)
        put_back(c).start()
        put_out(c).start()

        @pl.when(c == 0)
        def _():
            y1.wait_recv()
            diag1.start()
            ry1.start()
            x1.wait_recv()
            rx1.start()
            rx0.wait_recv()
            rx1.wait_recv()
            take_tokens(1).start()

        @pl.when(c == 2)
        def _():
            rd0.wait_recv()
            rd1.wait_recv()
            take_tokens(3).start()

        return carry

    lax.fori_loop(0, 4, chip_step, 0)

    def grads_step(n, carry):
        weight_step(n, tokens, grads, gug, inner, columns_stage, grads_out, (local, 10))
        return carry

    lax.fori_loop(0, 4, grads_step, 0)
    for copy in (x0, y0, c0, x1, y1, c1, diag0, diag1, rx0, ry0, ry1, rx1, rd0, rd1):
        copy.wait_send()
    put_back(3).wait()
    put_out(3).wait()
    for n in (2, 3):
        pltpu.make_async_copy(
            columns_stage.at[n - 2], grads_out.at[pl.ds(n * block, block)], local.at[8 + n]
        ).wait()


def ffn_second_kernel(
    all_ref,
    grad_ref,
    weight_hbm,
    back_ref,
    first_ref,
    out_ref,
    grads_out,
    sum_ref,
    weight,
    tokens,
    grads,
    wide,
    narrow,
    inner,
    gug,
    part,
    chip_in,
    far_in,
    near_in,
    stage,
    columns_stage,
    sends,
    recvs,
    local,
):
    tp_at, seq_at, far, mate, _ = plane_place()
    seq = lax.axis_size("seq")
    kind = lax.rem(seq_at, 2)
    to_x = at_device(tp_at, far)
    to_y = at_device(1 - tp_at, seq_at)
    to_c = at_device(tp_at, mate)
    rows, width = sum_ref.shape
    pair = 2 * rows
    half = rows // 2
    block = width // 4
    ff_part = narrow.shape[1]
    gate_up, lower = slice(0, 2 * ff_part), slice(2 * ff_part, 3 * ff_part)
    top, low = pl.ds(0, half), pl.ds(half, half)
    enter((to_x, to_y, to_c))

    def chip_rows(k):
        t = lax.rem(tp_at + 1 - lax.rem(k, 2), 2)
        s = lax.rem(seq_at + (seq // 2) * (1 - k // 2), seq)
        return pl.ds(t * seq + s - lax.rem(s, 2), 2)

    def take(ref, target, sem):
        return lambda k: pltpu.make_async_copy(ref.at[chip_rows(k)], target.at[k], local.at[sem + k])

    take_tokens, take_grads, take_back = (
        take(all_ref, tokens, 0),
        take(grad_ref, grads, 4),
        take(back_ref, part, 8),
    )

    def take_first(k):
        slot = lax.rem(k, 2)
        return pltpu.make_async_copy(first_ref.at[chip_rows(k)], stage.at[slot], local.at[12 + slot])

    def put_out(k):
        slot = lax.rem(k, 2)
        return pltpu.make_async_copy(stage.at[slot], out_ref.at[chip_rows(k)], local.at[14 + slot])

    def give(k):
        return remote(part.at[k, 1 - kind], chip_in.at[k], sends.at[k], recvs.at[k], to_c)

    def held(k):
        return part.at[k, kind]

    def hop(i, src, dst, device):
        return remote(src, dst, sends.at[i], recvs.at[i], device)

    d0 = hop(4, part.at[0, kind, top], far_in.at[0, top], to_x)
    d1 = hop(5, part.at[0, kind, low], far_in.at[1, low], to_y)
    x0 = hop(6, part.at[1, kind, top], near_in.at[0, top], to_x)
    y1 = hop(7, part.at[2, kind, low], near_in.at[1, low], to_y)
    y0 = hop(8, part.at[2, kind, top], near_in.at[1, top], to_y)
    x1 = hop(9, part.at[1, kind, low], near_in.at[0, low], to_x)

    def chip_sum(k):
        give(k).wait_recv()
        add_rows(held(k), (held(k), chip_in.at[k]), 0, rows, part.dtype)

    take_weight = pltpu.make_async_copy(weight_hbm, weight, local.at[18])
    take_weight.start()
    for k in range(4):
        take_grads(k).start()
        take_tokens(k).start()
        take_back(k).start()
    take_first(0).start()
    take_weight.wait()

    def chip_step(k, carry):
        slot = lax.rem(k, 2)
        take_grads(k).wait()
        narrow[...] = nn(grads[k].reshape(pair, width), weight[:, lower])

        @pl.when(k == 1)
        def _():
            chip_sum(0)
            d0.start()
            d1.start()

        @pl.when(k == 2)
        def _():
            chip_sum(1)
            x0.start()

        @pl.when(k == 3)
        def _():
            chip_sum(2)
            y1.start()
            d0.wait_recv()
            add_rows(held(2), (held(2), far_in.at[0]), 0, half, part.dtype)
            y0.start()
            d1.wait_recv()
            add_rows(held(1), (held(1), far_in.at[1]), half, half, part.dtype)
            x1.start()

        take_tokens(k).wait()
        wide[...] = nn(tokens[k].reshape(pair, width), weight[:, gate_up])
        slopes(wide, narrow, inner.at[k], gug.at[k])
        take_back(k).wait()

        def back_step(n, carry):
            at = pl.ds(pl.multiple_of(n * block, block), block)
            total = nt(gug[k], weight[at, gate_up]).reshape(2, rows, block)
            part[k, :, :, at] = (part[k, :, :, at].astype(F32) + total).astype(part.dtype)
            return carry

        lax.fori_loop(0, 4, back_step, 0)
        give(k).start()
        take_first(k).wait()

        @pl.when(k >= 1)
        def _():
            put_out(k - 1).wait()

        @pl.when(k < 3)
        def _():
            take_first(k + 1).start()

        def out_step(n, carry):
            at = pl.ds(pl.multiple_of(n * block, block), block)
            total = nt(inner[k], weight[at, lower]).reshape(2, rows, block)
            stage[slot, :, :, at] = (stage[slot, :, :, at].astype(F32) + total).astype(stage.dtype)
            return carry

        lax.fori_loop(0, 4, out_step, 0)
        put_out(k).start()
        return carry

    lax.fori_loop(0, 4, chip_step, 0)

    def grads_step(n, carry):
        weight_step(n, tokens, grads, gug, inner, columns_stage, grads_out, (local, 16))

        @pl.when(n == 0)
        def _():
            chip_sum(3)

        return carry

    lax.fori_loop(0, 4, grads_step, 0)
    x0.wait_recv()
    y0.wait_recv()
    add_rows(sum_ref, (held(3), near_in.at[0], near_in.at[1]), 0, half, sum_ref.dtype)
    y1.wait_recv()
    x1.wait_recv()
    add_rows(sum_ref, (held(3), near_in.at[0], near_in.at[1]), half, half, sum_ref.dtype)
    for k in range(4):
        give(k).wait_send()
    for copy in (d0, d1, x0, y1, y0, x1):
        copy.wait_send()
    put_out(3).wait()
    for n in (2, 3):
        pltpu.make_async_copy(
            columns_stage.at[n - 2], grads_out.at[pl.ds(n * block, block)], local.at[14 + n]
        ).wait()


def ffn_first_plane(block, grads, weight, ident):
    rows, width = block.shape
    plane = lax.axis_size("tp") * lax.axis_size("seq")
    cols = weight.shape[1]
    ff_part = cols // 3
    shape = jax.ShapeDtypeStruct
    hbm = pl.BlockSpec(memory_space=pltpu.HBM)
    vmem = pl.BlockSpec(memory_space=pltpu.VMEM)
    tokens = plane * rows
    return pl.pallas_call(
        ffn_first_kernel,
        out_shape=(
            shape((plane, rows, width), BF),
            shape((plane, rows, width), BF),
            shape((plane, rows, width), BF),
            shape((width, cols), BF),
        ),
        in_specs=[vmem, hbm, hbm],
        out_specs=(hbm, hbm, hbm, hbm),
        scratch_shapes=[
            pltpu.VMEM(weight.shape, BF),
            pltpu.VMEM((4, 2, rows, width), BF),
            pltpu.VMEM((4, 2, rows, width), BF),
            pltpu.VMEM((2 * rows, 2 * ff_part), F32),
            pltpu.VMEM((4, 2 * rows, ff_part), F32),
            pltpu.VMEM((4, 2 * rows, ff_part), BF),
            pltpu.VMEM((4, 2 * rows, 2 * ff_part), BF),
            pltpu.VMEM((2, 2, rows, width), BF),
            pltpu.VMEM((2, width // 4, cols), BF),
            pltpu.SemaphoreType.DMA((14,)),
            pltpu.SemaphoreType.DMA((14,)),
            pltpu.SemaphoreType.DMA((14,)),
        ],
        cost_estimate=pl.CostEstimate(
            flops=18 * tokens * width * ff_part,
            transcendentals=tokens * ff_part,
            bytes_accessed=22 * tokens * width,
        ),
        compiler_params=pltpu.CompilerParams(
            collective_id=ident, has_side_effects=True, vmem_limit_bytes=60 << 20
        ),
        name="ffn_first_plane",
    )(block, grads, weight)


def ffn_second_plane(block, grads, weight, back, first, ident):
    plane, rows, width = block.shape
    cols = weight.shape[1]
    ff_part = cols // 3
    shape = jax.ShapeDtypeStruct
    hbm = pl.BlockSpec(memory_space=pltpu.HBM)
    vmem = pl.BlockSpec(memory_space=pltpu.VMEM)
    tokens = plane * rows
    return pl.pallas_call(
        ffn_second_kernel,
        out_shape=(
            shape((plane, rows, width), BF),
            shape((width, cols), BF),
            shape((rows, width), F32),
        ),
        in_specs=[hbm] * 5,
        out_specs=(hbm, hbm, vmem),
        scratch_shapes=[
            pltpu.VMEM(weight.shape, BF),
            pltpu.VMEM((4, 2, rows, width), BF),
            pltpu.VMEM((4, 2, rows, width), BF),
            pltpu.VMEM((2 * rows, 2 * ff_part), F32),
            pltpu.VMEM((2 * rows, ff_part), F32),
            pltpu.VMEM((4, 2 * rows, ff_part), BF),
            pltpu.VMEM((4, 2 * rows, 2 * ff_part), BF),
            pltpu.VMEM((4, 2, rows, width), BF),
            pltpu.VMEM((4, rows, width), BF),
            pltpu.VMEM((2, rows, width), BF),
            pltpu.VMEM((2, rows, width), BF),
            pltpu.VMEM((2, 2, rows, width), BF),
            pltpu.VMEM((2, width // 4, cols), BF),
            pltpu.SemaphoreType.DMA((10,)),
            pltpu.SemaphoreType.DMA((10,)),
            pltpu.SemaphoreType.DMA((19,)),
        ],
        cost_estimate=pl.CostEstimate(
            flops=18 * tokens * width * ff_part,
            transcendentals=tokens * ff_part,
            bytes_accessed=22 * tokens * width,
        ),
        compiler_params=pltpu.CompilerParams(
            collective_id=ident, has_side_effects=True, vmem_limit_bytes=63 << 20
        ),
        name="ffn_second_plane",
    )(block, grads, weight, back, first)


def finish_kernel(
    first_ref,
    second_ref,
    gate_weight,
    up_weight,
    gain_ref,
    gate_out,
    up_out,
    down_first,
    down_second,
    gain_out,
    first_in,
    second_in,
    local,
    sends,
    recvs,
):
    tp_at, seq_at, _, _, _ = plane_place()
    seq = lax.axis_size("seq")
    plane = lax.axis_size("tp") * seq
    me = tp_at * seq + seq_at
    peers = [lax.rem(me + k, plane) for k in range(1, plane)]
    devices = [at_device(peer // seq, lax.rem(peer, seq)) for peer in peers]
    enter(devices)
    copies = []
    for k, (peer, device) in enumerate(zip(peers, devices)):
        i = plane - 1 + k
        copies.append(remote(first_ref.at[peer], first_in.at[me], sends.at[k], recvs.at[k], device))
        copies.append(remote(second_ref.at[peer], second_in.at[me], sends.at[i], recvs.at[i], device))
    copies.append(pltpu.make_async_copy(first_ref.at[me], first_in.at[me], local.at[0]))
    copies.append(pltpu.make_async_copy(second_ref.at[me], second_in.at[me], local.at[1]))
    for copy in copies:
        copy.start()
    for copy in copies:
        copy.wait()
    gain = gain_ref[...]
    sizes = [ref.shape[2] // 3 for ref in (first_in, second_in)]
    total = jnp.zeros(gain.shape, F32)
    for j in range(plane):
        start = j * sum(sizes)
        for ref, down, size in ((first_in, down_first, sizes[0]), (second_in, down_second, sizes[1])):
            at = slice(start, start + size)
            start += size
            for k, (out, weight) in enumerate(((gate_out, gate_weight), (up_out, up_weight))):
                own = ref[j, :, k * size : (k + 1) * size].astype(F32)
                out[:, at] = own * gain
                total = total + jnp.sum(own * weight[:, at].astype(F32), axis=1, keepdims=True)
            down[j] = ref[j, :, 2 * size :]
    gain_out[...] = total


def finish_plane(first, second, gate_weight, up_weight, gain, ident):
    plane, rows, _ = first.shape
    shape = jax.ShapeDtypeStruct
    hbm = pl.BlockSpec(memory_space=pltpu.HBM)
    vmem = pl.BlockSpec(memory_space=pltpu.VMEM)
    size = plane * rows * gate_weight.shape[1] * 6 // plane
    return pl.pallas_call(
        finish_kernel,
        out_shape=(
            shape(gate_weight.shape, F32),
            shape(up_weight.shape, F32),
            shape((plane, rows, first.shape[2] // 3), BF),
            shape((plane, rows, second.shape[2] // 3), BF),
            shape((rows, 1), F32),
        ),
        in_specs=[hbm, hbm, vmem, vmem, vmem],
        out_specs=(vmem,) * 5,
        scratch_shapes=[
            pltpu.VMEM(first.shape, BF),
            pltpu.VMEM(second.shape, BF),
            pltpu.SemaphoreType.DMA((2,)),
            pltpu.SemaphoreType.DMA((2 * plane - 2,)),
            pltpu.SemaphoreType.DMA((2 * plane - 2,)),
        ],
        cost_estimate=pl.CostEstimate(flops=0, transcendentals=0, bytes_accessed=size * 20),
        compiler_params=pltpu.CompilerParams(
            collective_id=ident, has_side_effects=True, vmem_limit_bytes=24 << 20
        ),
        name="finish_plane",
    )(first, second, gate_weight, up_weight, gain)


def columns(matrix, parts):
    rows, cols = matrix.shape
    return jnp.transpose(matrix.reshape(rows, parts, cols // parts), (1, 0, 2))


def uncolumns(blocks):
    parts, rows, cols = blocks.shape
    return jnp.transpose(blocks, (1, 0, 2)).reshape(rows, parts * cols)


def after(value, *earlier):
    return lax.optimization_barrier((value,) + earlier)[0]


def per_device(
    layer_input,
    pic_starts,
    skip_mask,
    gain_attn,
    w_query,
    w_key,
    w_value,
    w_out,
    gain_ffn,
    w_gate,
    w_up,
    w_down,
    cotangent,
):
    _, local_len, width = layer_input.shape
    seq = lax.axis_size("seq")
    plane = lax.axis_size("tp") * seq
    total_len = local_len * seq
    heads = H // plane
    share = plane // KV
    ff_part = w_gate.shape[1] // plane
    q_part = heads * DH

    gain1 = gain_attn[:, None]
    gain2 = gain_ffn[:, None]
    wq32, wk32, wv32 = w_query.astype(F32), w_key.astype(F32), w_value.astype(F32)
    wg32, wu32 = w_gate.astype(F32), w_up.astype(F32)
    attn_pack = jnp.concatenate(
        [
            columns((wq32 * gain1).astype(BF), plane),
            jnp.repeat(columns((wk32 * gain1).astype(BF), KV), share, axis=0),
            jnp.repeat(columns((wv32 * gain1).astype(BF), KV), share, axis=0),
            columns(w_out.T, plane),
        ],
        axis=2,
    )
    attn_rows = exchange_plane(attn_pack, 0)
    attn_rows = attn_rows.reshape(-1, attn_rows.shape[2])
    attn_weight = lax.all_gather(attn_rows, "rep", axis=0, tiled=True)
    qkv_weight = attn_weight[:, : q_part + 2 * DH]
    out_weight = attn_weight[:, q_part + 2 * DH :]

    tokens = layer_input.reshape(local_len, width).astype(F32)
    keep = (1 - skip_mask).astype(F32).reshape(local_len, 1)
    upstream = cotangent.reshape(local_len, width).astype(F32)
    scale1 = rms_scale(tokens)
    norm1 = tokens * scale1

    first_part = (ff_part // 2 + DH - 1) // DH * DH
    split = ((0, first_part), (first_part, ff_part))
    ffn_parts = (
        columns((wg32 * gain2).astype(BF), plane),
        columns((wu32 * gain2).astype(BF), plane),
        columns(w_down.T, plane),
    )
    ffn_pack = jnp.concatenate([m[:, :, a:b] for a, b in split for m in ffn_parts], axis=2)
    ffn_rows = exchange_plane(after(ffn_pack, attn_rows), 2)
    ffn_rows = ffn_rows.reshape(-1, ffn_rows.shape[2])
    first_weight = lax.all_gather(ffn_rows[:, : 3 * first_part], "rep", axis=0, tiled=True)
    second_rows = after(ffn_rows[:, 3 * first_part :], ffn_rows)
    second_weight = lax.all_gather(second_rows, "rep", axis=0, tiled=True)
    norm1_all = gather_plane(after(norm1.astype(BF), ffn_rows), 1)
    other_starts = lax.ppermute(pic_starts, "tp", [(0, 1), (1, 0)])
    starts = jnp.where(
        lax.axis_index("tp") == 0,
        jnp.concatenate([pic_starts, other_starts], axis=0),
        jnp.concatenate([other_starts, pic_starts], axis=0),
    )
    positions = jnp.arange(total_len, dtype=jnp.int32)
    cos_table, sin_table = rotary_tables(positions, DH)
    cos = jnp.concatenate([cos_table, cos_table], axis=1)
    sin = jnp.concatenate([-sin_table, sin_table], axis=1)
    projected = nn(norm1_all, qkv_weight)
    qkv, mixed, log_total, ffn_grad = attn_front_plane(
        starts, projected, cos, sin, (keep * upstream).astype(BF), 3
    )
    branch = scatter_plane(nt(mixed, out_weight).astype(BF), 4)
    hidden = tokens + keep * branch

    scale2 = rms_scale(hidden)
    norm2 = hidden * scale2
    norm2_all, back_first, out_first, first_partial = ffn_first_plane(
        norm2.astype(BF), ffn_grad, first_weight, 5
    )
    first_sums = lax.psum_scatter(first_partial, "rep", scatter_dimension=0, tiled=True)
    out_partial, second_partial, scaled2 = ffn_second_plane(
        norm2_all, ffn_grad, second_weight, back_first, out_first, 6
    )
    second_sums = lax.psum_scatter(second_partial, "rep", scatter_dimension=0, tiled=True)
    hidden_grad = upstream + scale2 * (
        scaled2 - norm2 * jnp.mean(scaled2 * norm2, axis=-1, keepdims=True)
    )

    branch_grad = gather_plane((keep * hidden_grad).astype(BF), 7)
    mixed_grad = nn(branch_grad, out_weight).astype(BF)
    qkv_grad, ffn_out = attn_back_plane(
        starts,
        qkv,
        after(mixed_grad, first_sums),
        log_total,
        cos,
        sin,
        out_partial.reshape(-1, width),
        9,
    )
    attn_partial = jnp.concatenate(
        [tn(norm1_all, qkv_grad).astype(BF), tn(branch_grad, mixed).astype(BF)], axis=1
    )
    scaled1_partial = nt(qkv_grad, qkv_weight).astype(BF)
    attn_sums = lax.psum_scatter(attn_partial, "rep", scatter_dimension=0, tiled=True)
    scaled1 = scatter_plane(after(scaled1_partial, attn_partial), 8)
    input_grad = hidden_grad + scale1 * (
        scaled1 - norm1 * jnp.mean(scaled1 * norm1, axis=-1, keepdims=True)
    )
    out_hidden = (hidden + keep * ffn_out).astype(BF)

    gate_grad, up_grad, down_first, down_second, gain_ffn_grad = finish_plane(
        after(first_sums.reshape(plane, -1, first_sums.shape[1]), scaled1),
        second_sums.reshape(plane, -1, second_sums.shape[1]),
        w_gate,
        w_up,
        gain2,
        10,
    )
    down_own = jnp.concatenate([down_first, down_second], axis=2)
    down_grad = jnp.transpose(down_own, (0, 2, 1)).reshape(plane * ff_part, -1).astype(F32)

    attn_sums = after(attn_sums, gain_ffn_grad)
    attn_own = exchange_plane(attn_sums.reshape(plane, -1, attn_sums.shape[1]), 11).astype(F32)
    query_own = uncolumns(attn_own[:, :, :q_part])
    kv_own = attn_own[:, :, q_part : q_part + 2 * DH]
    kv_own = jnp.sum(kv_own.reshape(KV, share, -1, 2 * DH), axis=1)
    key_own = uncolumns(kv_own[:, :, :DH])
    value_own = uncolumns(kv_own[:, :, DH:])
    out_own = uncolumns(attn_own[:, :, q_part + 2 * DH :])
    gain_attn_grad = (
        jnp.sum(query_own * wq32, axis=1)
        + jnp.sum(key_own * wk32, axis=1)
        + jnp.sum(value_own * wv32, axis=1)
    )
    return (
        out_hidden[None],
        input_grad[None],
        gain_attn_grad,
        query_own * gain1,
        key_own * gain1,
        value_own * gain1,
        out_own.T,
        gain_ffn_grad[:, 0],
        gate_grad,
        up_grad,
        down_grad,
    )


def solution(mesh):
    devices = mesh.devices
    dp, seq = devices.shape
    inner = Mesh(devices.reshape(dp // TP, TP, seq), ("rep", "tp", "seq"))
    dps = ("rep", "tp")
    every = ("rep", "tp", "seq")
    token = P(dps, "seq", None)
    row = P(every, None)
    col = P(None, every)
    return jax.shard_map(
        per_device,
        mesh=inner,
        in_specs=(
            token,
            P(dps, None),
            P(dps, "seq"),
            P(every),
            row,
            row,
            row,
            col,
            P(every),
            row,
            row,
            col,
            token,
        ),
        out_specs=(token, token, P(every), row, row, row, col, P(every), row, row, col),
        check_vma=False,
    )
```

```python
import jax
import jax.numpy as jnp
from jax import lax
from jax.experimental import pallas as pl
from jax.experimental.pallas import tpu as pltpu
from jax.sharding import Mesh
from jax.sharding import PartitionSpec as P

H = 16
KV = 4
DH = 128
PIC = 256
NPIC = 2
EPS = 1e-05
TP = 2
BF = jnp.bfloat16
F32 = jnp.float32


def rotary_tables(positions, head_dim):
    half_dim = head_dim // 2
    inverse = 10000.0 ** (-(jnp.arange(half_dim, dtype=F32) * 2.0 / head_dim))
    angles = positions.astype(F32)[:, None] * inverse[None, :]
    return (jnp.cos(angles), jnp.sin(angles))


def rms_scale(rows):
    return lax.rsqrt(jnp.mean(rows * rows, axis=-1, keepdims=True) + EPS)


def dot(left, right, contract):
    return lax.dot_general(
        left, right, ((contract[:1], contract[1:]), ((), ())), preferred_element_type=F32
    )


def nn(left, right):
    return dot(left, right, (1, 0))


def nt(left, right):
    return dot(left, right, (1, 1))


def tn(left, right):
    return dot(left, right, (0, 0))


MESH_ID = pl.DeviceIdType.MESH
SUB = 32


def plane_place():
    tp_at = lax.axis_index("tp")
    seq_at = lax.axis_index("seq")
    seq = lax.axis_size("seq")
    half = seq // 2
    far = lax.rem(seq_at + half, seq)
    mate = seq_at + 1 - 2 * lax.rem(seq_at, 2)
    far_mate = far + 1 - 2 * lax.rem(far, 2)
    return tp_at, seq_at, far, mate, far_mate


def at_device(tp_at, seq_at):
    return (lax.axis_index("rep"), tp_at, seq_at)


def enter(devices):
    barrier = pltpu.get_barrier_semaphore()
    for device in devices:
        pl.semaphore_signal(barrier, inc=1, device_id=device, device_id_type=MESH_ID)
    pl.semaphore_wait(barrier, len(devices))


def remote(src, dst, send, recv, device):
    return pltpu.make_async_remote_copy(
        src_ref=src,
        dst_ref=dst,
        send_sem=send,
        recv_sem=recv,
        device_id=device,
        device_id_type=MESH_ID,
    )


def gather_stages(own_ref, all_ref, sends, recvs, local):
    tp_at, seq_at, far, mate, _ = plane_place()
    seq = lax.axis_size("seq")
    other = 1 - tp_at
    to_x = at_device(tp_at, far)
    to_y = at_device(other, seq_at)
    to_c = at_device(tp_at, mate)
    rows = own_ref.shape[0]
    part = rows // 2

    def piece(t, s, h):
        return all_ref.at[t * seq + s, pl.ds(h * part, part)]

    def relay(i, t, s, h, device):
        return remote(piece(t, s, h), piece(t, s, h), sends.at[i], recvs.at[i], device)

    def own(i, h, device):
        return remote(
            own_ref.at[pl.ds(h * part, part)],
            piece(tp_at, seq_at, h),
            sends.at[i],
            recvs.at[i],
            device,
        )

    x0, x1 = own(0, 0, to_x), own(3, 1, to_x)
    y0, y1 = own(1, 0, to_y), own(4, 1, to_y)
    c0, c1 = own(2, 0, to_c), own(5, 1, to_c)
    diag0 = relay(6, tp_at, far, 0, to_y)
    diag1 = relay(7, other, seq_at, 1, to_x)
    rx0, rx1 = relay(8, tp_at, far, 0, to_c), relay(11, tp_at, far, 1, to_c)
    ry0, ry1 = relay(9, other, seq_at, 0, to_c), relay(10, other, seq_at, 1, to_c)
    rd0, rd1 = relay(12, other, far, 0, to_c), relay(13, other, far, 1, to_c)
    mine = pltpu.make_async_copy(own_ref, all_ref.at[tp_at * seq + seq_at], local)

    def begin(peers=(to_x, to_y, to_c)):
        enter(peers)
        for copy in (x0, y0, c0, x1, y1, c1, mine):
            copy.start()

    def first():
        x0.wait_recv()
        diag0.start()
        rx0.start()
        y0.wait_recv()
        ry0.start()

    def second():
        y1.wait_recv()
        diag1.start()
        ry1.start()
        x1.wait_recv()
        rx1.start()

    def finish():
        diag0.wait_recv()
        rd0.start()
        diag1.wait_recv()
        rd1.start()
        for copy in (c0, c1, rx0, ry0, ry1, rx1, rd0, rd1):
            copy.wait_recv()
        for copy in (x0, y0, c0, x1, y1, c1, diag0, diag1, rx0, ry0, ry1, rx1, rd0, rd1):
            copy.wait_send()
        mine.wait()

    return begin, first, second, finish


def gather_kernel(*refs):
    for stage in gather_stages(*refs):
        stage()


GATHER_SCRATCH = (
    pltpu.SemaphoreType.DMA((14,)),
    pltpu.SemaphoreType.DMA((14,)),
    pltpu.SemaphoreType.DMA,
)


def gather_plane(block, ident):
    rows, width = block.shape
    plane = lax.axis_size("tp") * lax.axis_size("seq")
    size = rows * width * 2
    gathered = pl.pallas_call(
        gather_kernel,
        out_shape=jax.ShapeDtypeStruct((plane, rows, width), block.dtype),
        in_specs=[pl.BlockSpec(memory_space=pltpu.VMEM)],
        out_specs=pl.BlockSpec(memory_space=pltpu.HBM),
        scratch_shapes=GATHER_SCRATCH,
        cost_estimate=pl.CostEstimate(
            flops=0, transcendentals=0, bytes_accessed=plane * size * 12
        ),
        compiler_params=pltpu.CompilerParams(collective_id=ident, has_side_effects=True),
        name="gather_plane",
    )(block)
    return gathered.reshape(plane * rows, width)


def spread_kernel(
    own_ref, first_ref, second_ref, all_ref, first_out, second_out, first_own, second_own, copies, *gather
):
    begin, first, second, finish = gather_stages(own_ref, all_ref, *gather)
    tp_at, seq_at, _, _, _ = plane_place()
    seq = lax.axis_size("seq")
    plane = lax.axis_size("tp") * seq
    me = tp_at * seq + seq_at
    peers = [lax.rem(me + k, plane) for k in range(1, plane)]
    devices = [at_device(peer // seq, lax.rem(peer, seq)) for peer in peers]
    sends, recvs, local = copies.at[0], copies.at[1], copies.at[2]
    begin(devices)
    moves, keeps = [], []
    for n, (ref, out, kept) in enumerate(
        ((first_ref, first_out, first_own), (second_ref, second_out, second_own))
    ):
        for k, (peer, device) in enumerate(zip(peers, devices)):
            i = n * (plane - 1) + k
            moves.append(remote(ref.at[peer], out.at[me], sends.at[i], recvs.at[i], device))
        keeps.append(
            (
                pltpu.make_async_copy(ref.at[me], kept, local.at[2 * n]),
                pltpu.make_async_copy(kept, out.at[me], local.at[2 * n + 1]),
            )
        )
    for move in moves:
        move.start()
    for take, put in keeps:
        take.start()
    for take, put in keeps:
        take.wait()
        put.start()
    first()
    second()
    for move in moves:
        move.wait()
    for take, put in keeps:
        put.wait()
    finish()


def spread_plane(block, first, second, ident):
    rows, width = block.shape
    plane = lax.axis_size("tp") * lax.axis_size("seq")
    hbm = pl.BlockSpec(memory_space=pltpu.HBM)
    vmem = pl.BlockSpec(memory_space=pltpu.VMEM)
    size = plane * rows * width * 2
    return pl.pallas_call(
        spread_kernel,
        out_shape=(
            jax.ShapeDtypeStruct((plane, rows, width), block.dtype),
            jax.ShapeDtypeStruct(first.shape, first.dtype),
            jax.ShapeDtypeStruct(second.shape, second.dtype),
        ),
        in_specs=[vmem, hbm, hbm],
        out_specs=(hbm, hbm, hbm),
        scratch_shapes=[
            pltpu.VMEM(first.shape[1:], first.dtype),
            pltpu.VMEM(second.shape[1:], second.dtype),
            pltpu.SemaphoreType.DMA((3, 2 * plane)),
            *GATHER_SCRATCH,
        ],
        cost_estimate=pl.CostEstimate(flops=0, transcendentals=0, bytes_accessed=size * 16),
        compiler_params=pltpu.CompilerParams(collective_id=ident, has_side_effects=True),
        name="spread_plane",
    )(block, first, second)


def add_rows(target, sources, start, count, kind):
    step = min(SUB, count)

    def body(i, carry):
        at = pl.ds(start + i * step, step)
        total = sources[0][at, :].astype(F32)
        for source in sources[1:]:
            total = total + source[at, :].astype(F32)
        target[at, :] = total.astype(kind)
        return carry

    lax.fori_loop(0, count // step, body, 0)


def scatter_stages(part_ref, sum_ref, held, chip_in, far_in, near_in, loads, sends, recvs):
    tp_at, seq_at, far, mate, far_mate = plane_place()
    seq = lax.axis_size("seq")
    other = 1 - tp_at
    to_x = at_device(tp_at, far)
    to_y = at_device(other, seq_at)
    to_c = at_device(tp_at, mate)
    rows = sum_ref.shape[0]
    part = rows // 2
    top, low = pl.ds(0, part), pl.ds(part, part)
    chips = ((other, far, far_mate), (tp_at, far, far_mate), (other, seq_at, mate), (tp_at, seq_at, mate))
    gives = [
        remote(part_ref.at[t * seq + m], chip_in.at[k], sends.at[k], recvs.at[k], to_c)
        for k, (t, s, m) in enumerate(chips)
    ]
    takes = [
        pltpu.make_async_copy(part_ref.at[t * seq + s], held.at[k], loads.at[k])
        for k, (t, s, m) in enumerate(chips)
    ]

    def hop(i, src, dst, device):
        return remote(src, dst, sends.at[i], recvs.at[i], device)

    d0 = hop(4, held.at[0, top], far_in.at[0, top], to_x)
    d1 = hop(5, held.at[0, low], far_in.at[1, low], to_y)
    x0 = hop(6, held.at[1, top], near_in.at[0, top], to_x)
    y1 = hop(7, held.at[2, low], near_in.at[1, low], to_y)
    y0 = hop(8, held.at[2, top], near_in.at[1, top], to_y)
    x1 = hop(9, held.at[1, low], near_in.at[0, low], to_x)

    def begin():
        enter((to_x, to_y, to_c))
        for give, take in zip(gives, takes):
            give.start()
            take.start()

    def chip_sum(k):
        takes[k].wait()
        gives[k].wait_recv()
        add_rows(held.at[k], (held.at[k], chip_in.at[k]), 0, rows, held.dtype)

    def diagonal():
        chip_sum(0)
        d0.start()
        d1.start()

    def along_x():
        chip_sum(1)
        x0.start()

    def along_y():
        chip_sum(2)
        y1.start()

    def own():
        chip_sum(3)

    def fold():
        d0.wait_recv()
        add_rows(held.at[2], (held.at[2], far_in.at[0]), 0, part, held.dtype)
        y0.start()
        d1.wait_recv()
        add_rows(held.at[1], (held.at[1], far_in.at[1]), part, part, held.dtype)
        x1.start()

    def finish():
        x0.wait_recv()
        y0.wait_recv()
        add_rows(sum_ref, (held.at[3], near_in.at[0], near_in.at[1]), 0, part, sum_ref.dtype)
        y1.wait_recv()
        x1.wait_recv()
        add_rows(sum_ref, (held.at[3], near_in.at[0], near_in.at[1]), part, part, sum_ref.dtype)
        for copy in gives + [d0, d1, x0, y1, y0, x1]:
            copy.wait_send()

    return begin, diagonal, along_x, along_y, own, fold, finish


def scatter_kernel(*refs):
    for stage in scatter_stages(*refs):
        stage()


def scatter_scratch(rows, width, kind):
    return [
        pltpu.VMEM((4, rows, width), kind),
        pltpu.VMEM((4, rows, width), kind),
        pltpu.VMEM((2, rows, width), kind),
        pltpu.VMEM((2, rows, width), kind),
        pltpu.SemaphoreType.DMA((4,)),
        pltpu.SemaphoreType.DMA((10,)),
        pltpu.SemaphoreType.DMA((10,)),
    ]


def scatter_plane(partial, ident):
    plane = lax.axis_size("tp") * lax.axis_size("seq")
    rows, width = partial.shape[0] // plane, partial.shape[1]
    kind = partial.dtype
    size = rows * width * 2
    return pl.pallas_call(
        scatter_kernel,
        out_shape=jax.ShapeDtypeStruct((rows, width), F32),
        in_specs=[pl.BlockSpec(memory_space=pltpu.HBM)],
        out_specs=pl.BlockSpec(memory_space=pltpu.VMEM),
        scratch_shapes=scatter_scratch(rows, width, kind),
        cost_estimate=pl.CostEstimate(
            flops=0, transcendentals=0, bytes_accessed=plane * size * 14
        ),
        compiler_params=pltpu.CompilerParams(
            collective_id=ident, has_side_effects=True, vmem_limit_bytes=32 << 20
        ),
        name="scatter_plane",
    )(partial.reshape(plane, rows, width))


def fill_bias(bias, starts_ref, t, blocks):
    for b in range(blocks):
        span = min(2, blocks - b) * PIC
        k_at = lax.broadcasted_iota(jnp.int32, (span, PIC), 0) + b * PIC
        q_at = lax.broadcasted_iota(jnp.int32, (span, PIC), 1) + b * PIC
        high, below = jnp.maximum(k_at, q_at), jnp.minimum(k_at, q_at)
        allowed = k_at <= q_at
        for j in range(NPIC):
            start = starts_ref[t, j]
            allowed = allowed | ((below >= start) & (high < start + PIC))
        bias[b, :span, :] = jnp.where(allowed, 0.0, -jnp.inf)


def masked(scores, bias, b):
    late = scores[b * PIC :] + bias[b, : scores.shape[0] - b * PIC, :]
    return jnp.concatenate([scores[: b * PIC], late], axis=0) if b else late


def attn_front_kernel(
    starts_ref,
    norm_hbm,
    weight_hbm,
    cos_ref,
    sin_ref,
    own_ref,
    qkv_ref,
    mixed_ref,
    log_ref,
    out_ref,
    all_ref,
    bias,
    turned,
    norm,
    weight,
    projected,
    stage,
    local,
    *gather,
):
    begin, first, second, finish = gather_stages(own_ref, all_ref, *gather)
    total, dim = cos_ref.shape
    take_weight = pltpu.make_async_copy(weight_hbm, weight, local.at[0])
    take_weight.start()

    def take_norm(t):
        rows = pl.ds(t * total, total)
        return pltpu.make_async_copy(norm_hbm.at[rows], norm.at[t], local.at[1 + t])

    def put_out(t, n):
        rows = pl.ds(t * total + n * (total // 2), total // 2)
        return pltpu.make_async_copy(stage.at[n], out_ref.at[rows], local.at[1 + TP + n])

    for t in range(TP):
        take_norm(t).start()
    begin()
    take_weight.wait()
    heads = mixed_ref.shape[1] // dim
    blocks = total // PIC
    scale = dim ** (-0.5)
    k_cols = slice(heads * dim, (heads + 1) * dim)
    v_cols = slice((heads + 1) * dim, (heads + 2) * dim)

    def turn(rows, at):
        return rows * cos_ref[at, :] + pltpu.roll(rows, dim // 2, 1) * sin_ref[at, :]

    def head_step(i, carry):
        t, h = i // heads, lax.rem(i, heads)
        base = pl.multiple_of(t * total, total)
        cols = pl.ds(pl.multiple_of(h * dim, dim), dim)

        @pl.when(h == 0)
        def _():
            rows = pl.ds(base, total)
            take_norm(t).wait()

            def project(n, carry):
                some = pl.ds(pl.multiple_of(n * PIC, PIC), PIC)
                projected[some, :] = nn(norm[t, some, :], weight[:, : (heads + 2) * dim])
                return carry

            lax.fori_loop(0, blocks, project, 0)
            values = projected[:, v_cols].astype(BF)
            qkv_ref[rows, k_cols] = turn(projected[:, k_cols], pl.ds(0, total)).astype(BF)
            qkv_ref[rows, v_cols] = values
            turned[...] = values.T
            fill_bias(bias, starts_ref, t, blocks)

        for b in range(blocks):
            at = pl.ds(pl.multiple_of(base + b * PIC, PIC), PIC)
            count = min(b + 2, blocks) * PIC
            queries = turn(projected[b * PIC : (b + 1) * PIC, cols], pl.ds(b * PIC, PIC)).astype(BF)
            qkv_ref[at, cols] = queries
            scores = nt(qkv_ref[pl.ds(base, count), k_cols], queries) * scale
            scores = masked(scores, bias, b)
            peak = jnp.max(scores, axis=0, keepdims=True)
            weights = jnp.exp(scores - peak)
            mass = jnp.sum(weights, axis=0, keepdims=True)
            log_ref[i, :, b * PIC : (b + 1) * PIC] = peak + jnp.log(mass)
            probs = (weights * (1.0 / mass)).astype(BF)
            mixed_ref[at, cols] = nn(turned[:, :count], probs).T.astype(BF)
            if b == 0:
                pl.when(i == 1)(first)
                pl.when(i == 3)(second)

        @pl.when(h == heads - 1)
        def _():
            for n in range(2):

                @pl.when(t >= 1)
                def _():
                    put_out(t - 1, n).wait()

                rows = pl.ds(pl.multiple_of(base + n * (total // 2), total // 2), total // 2)
                block = stage.shape[2] // 4

                def out_step(m, carry):
                    some = pl.ds(pl.multiple_of(m * block, block), block)
                    partial = nt(mixed_ref[rows, :], weight[some, (heads + 2) * dim :])
                    stage[n, :, some] = partial.astype(BF)
                    return carry

                lax.fori_loop(0, 4, out_step, 0)
                put_out(t, n).start()

        return carry

    lax.fori_loop(0, log_ref.shape[0], head_step, 0)
    finish()
    for n in range(2):
        put_out(TP - 1, n).wait()


def attn_front_plane(starts, norm, weight, cos, sin, block, ident):
    rows, width = block.shape
    plane = lax.axis_size("tp") * lax.axis_size("seq")
    total, dim = cos.shape
    tokens = norm.shape[0]
    q_part = weight.shape[1] // 2 - dim
    shape = jax.ShapeDtypeStruct
    vmem = pl.BlockSpec(memory_space=pltpu.VMEM)
    smem = pl.BlockSpec(memory_space=pltpu.SMEM)
    hbm = pl.BlockSpec(memory_space=pltpu.HBM)
    return pl.pallas_call(
        attn_front_kernel,
        out_shape=(
            shape((tokens, q_part + 2 * dim), BF),
            shape((tokens, q_part), BF),
            shape((tokens * q_part // dim // total, 1, total), F32),
            shape(norm.shape, BF),
            shape((plane, rows, width), block.dtype),
        ),
        in_specs=[smem, hbm, hbm, vmem, vmem, vmem],
        out_specs=(vmem, vmem, vmem, hbm, hbm),
        scratch_shapes=[
            pltpu.VMEM((total // PIC, 2 * PIC, PIC), F32),
            pltpu.VMEM((dim, total), BF),
            pltpu.VMEM((TP, total, width), BF),
            pltpu.VMEM(weight.shape, BF),
            pltpu.VMEM((total, q_part + 2 * dim), F32),
            pltpu.VMEM((2, total // 2, width), BF),
            pltpu.SemaphoreType.DMA((3 + TP,)),
            *GATHER_SCRATCH,
        ],
        cost_estimate=pl.CostEstimate(
            flops=4 * tokens * total * q_part,
            transcendentals=tokens * total * q_part // dim,
            bytes_accessed=plane * rows * width * 24,
        ),
        compiler_params=pltpu.CompilerParams(
            collective_id=ident, has_side_effects=True, vmem_limit_bytes=40 << 20
        ),
        name="attn_front_plane",
    )(starts, norm, weight, cos, sin, block)


def attn_back_kernel(
    starts_ref,
    qkv_ref,
    g_ref,
    log_ref,
    cos_ref,
    sin_ref,
    part_ref,
    grad_ref,
    sum_ref,
    bias,
    turned,
    keys_sum,
    values_sum,
    *scatter,
):
    begin, diagonal, along_x, along_y, own, fold, finish = scatter_stages(
        part_ref, sum_ref, *scatter
    )
    begin()
    total, dim = cos_ref.shape
    heads = g_ref.shape[1] // dim
    blocks = total // PIC
    scale = dim ** (-0.5)
    k_cols = slice(heads * dim, (heads + 1) * dim)
    v_cols = slice((heads + 1) * dim, (heads + 2) * dim)
    events = {(0, 1): diagonal, (0, 2): along_x, (0, 3): along_y, (1, 0): own, (2, 2): fold}

    def unturn(rows, at):
        return rows * cos_ref[at, :] - pltpu.roll(rows, dim // 2, 1) * sin_ref[at, :]

    def head_step(i, carry):
        t, h = i // heads, lax.rem(i, heads)
        base = pl.multiple_of(t * total, total)
        cols = pl.ds(pl.multiple_of(h * dim, dim), dim)

        @pl.when(h == 0)
        def _():
            turned[...] = qkv_ref[pl.ds(base, total), k_cols].T
            keys_sum[...] = jnp.zeros(keys_sum.shape, F32)
            values_sum[...] = jnp.zeros(values_sum.shape, F32)
            fill_bias(bias, starts_ref, t, blocks)

        for b in range(blocks):
            at = pl.ds(pl.multiple_of(base + b * PIC, PIC), PIC)
            count = min(b + 2, blocks) * PIC
            seen = pl.ds(base, count)
            queries, grads = qkv_ref[at, cols], g_ref[at, cols]
            scores = nt(qkv_ref[seen, k_cols], queries) * scale - log_ref[i, :, b * PIC : (b + 1) * PIC]
            probs = jnp.exp(masked(scores, bias, b))
            prob_grad = nt(qkv_ref[seen, v_cols], grads)
            mean = jnp.sum(probs * prob_grad, axis=0, keepdims=True)
            score_grad = (probs * (prob_grad - mean)).astype(BF)
            values_sum[:count, :] += nn(probs.astype(BF), grads)
            keys_sum[:count, :] += nn(score_grad, queries)
            back = nn(turned[:, :count], score_grad).T * scale
            grad_ref[at, cols] = unturn(back, pl.ds(b * PIC, PIC)).astype(BF)
            for (step, block), stage in events.items():
                if block == b:
                    pl.when(i == step)(stage)

        @pl.when(h == heads - 1)
        def _():
            rows = pl.ds(base, total)
            back = unturn(keys_sum[...] * scale, pl.ds(0, total))
            grad_ref[rows, k_cols] = back.astype(BF)
            grad_ref[rows, v_cols] = values_sum[...].astype(BF)

        return carry

    lax.fori_loop(0, log_ref.shape[0], head_step, 0)
    finish()


def attn_back_plane(starts, qkv, grads, log_total, cos, sin, partial, ident):
    plane = lax.axis_size("tp") * lax.axis_size("seq")
    rows, width = partial.shape[0] // plane, partial.shape[1]
    total, dim = cos.shape
    tokens, q_part = grads.shape
    hbm = pl.BlockSpec(memory_space=pltpu.HBM)
    vmem = pl.BlockSpec(memory_space=pltpu.VMEM)
    smem = pl.BlockSpec(memory_space=pltpu.SMEM)
    return pl.pallas_call(
        attn_back_kernel,
        out_shape=(
            jax.ShapeDtypeStruct((tokens, q_part + 2 * dim), BF),
            jax.ShapeDtypeStruct((rows, width), F32),
        ),
        in_specs=[smem] + [vmem] * 5 + [hbm],
        out_specs=(vmem, vmem),
        scratch_shapes=[
            pltpu.VMEM((total // PIC, 2 * PIC, PIC), F32),
            pltpu.VMEM((dim, total), BF),
            pltpu.VMEM((total, dim), F32),
            pltpu.VMEM((total, dim), F32),
        ]
        + scatter_scratch(rows, width, partial.dtype),
        cost_estimate=pl.CostEstimate(
            flops=10 * tokens * total * q_part,
            transcendentals=tokens * total * q_part // dim,
            bytes_accessed=plane * rows * width * 28,
        ),
        compiler_params=pltpu.CompilerParams(
            collective_id=ident, has_side_effects=True, vmem_limit_bytes=50 << 20
        ),
        name="attn_back_plane",
    )(starts, qkv, grads, log_total, cos, sin, partial.reshape(plane, rows, width))


def exchange_kernel(in_ref, out_ref, stage, local, sends, recvs):
    tp_at, seq_at, _, _, _ = plane_place()
    seq = lax.axis_size("seq")
    plane = lax.axis_size("tp") * seq
    me = tp_at * seq + seq_at
    peers = [lax.rem(me + k, plane) for k in range(1, plane)]
    devices = [at_device(peer // seq, lax.rem(peer, seq)) for peer in peers]
    enter(devices)
    copies = []
    for k, (peer, device) in enumerate(zip(peers, devices)):
        copy = remote(in_ref.at[peer], out_ref.at[me], sends.at[k], recvs.at[k], device)
        copy.start()
        copies.append(copy)
    take = pltpu.make_async_copy(in_ref.at[me], stage, local.at[0])
    take.start()
    take.wait()
    put = pltpu.make_async_copy(stage, out_ref.at[me], local.at[1])
    put.start()
    for copy in copies:
        copy.wait()
    put.wait()


def exchange_plane(blocks, ident):
    plane, rows, width = blocks.shape
    size = plane * rows * width * 2
    return pl.pallas_call(
        exchange_kernel,
        out_shape=jax.ShapeDtypeStruct(blocks.shape, blocks.dtype),
        in_specs=[pl.BlockSpec(memory_space=pltpu.HBM)],
        out_specs=pl.BlockSpec(memory_space=pltpu.HBM),
        scratch_shapes=[
            pltpu.VMEM((rows, width), blocks.dtype),
            pltpu.SemaphoreType.DMA((2,)),
            pltpu.SemaphoreType.DMA((plane - 1,)),
            pltpu.SemaphoreType.DMA((plane - 1,)),
        ],
        cost_estimate=pl.CostEstimate(flops=0, transcendentals=0, bytes_accessed=size * 20),
        compiler_params=pltpu.CompilerParams(collective_id=ident, has_side_effects=True),
        name="exchange_plane",
    )(blocks)


def slopes(wide, narrow, inner, gug):
    ff_part = inner.shape[1]

    def body(i, carry):
        at = pl.ds(i * SUB, SUB)
        gate, upward, grad = wide[at, :ff_part], wide[at, ff_part:], narrow[at, :]
        sigmoid_gate = jax.nn.sigmoid(gate)
        silu_gate = gate * sigmoid_gate
        inner[at, :] = (silu_gate * upward).astype(BF)
        slope = sigmoid_gate * (1.0 + gate * (1.0 - sigmoid_gate))
        gug[at, :ff_part] = (grad * upward * slope).astype(BF)
        gug[at, ff_part:] = (grad * silu_gate).astype(BF)
        return carry

    lax.fori_loop(0, wide.shape[0] // SUB, body, 0)


def weight_step(n, tokens, grads, gug, inner, stage, weight_ref, sems):
    slot = lax.rem(n, 2)
    block, cols = stage.shape[1:]
    ff_part = cols // 3
    count = gug.shape[0] * gug.shape[1]

    def put(m):
        return pltpu.make_async_copy(
            stage.at[lax.rem(m, 2)], weight_ref.at[pl.ds(m * block, block)], sems[0].at[sems[1] + lax.rem(m, 2)]
        )

    @pl.when(n >= 2)
    def _():
        put(n - 2).wait()

    at = pl.ds(pl.multiple_of(n * block, block), block)
    left = tokens[:, :, :, at].reshape(count, block)
    stage[slot, :, : 2 * ff_part] = tn(left, gug[...].reshape(count, 2 * ff_part)).astype(BF)
    left = grads[:, :, :, at].reshape(count, block)
    stage[slot, :, 2 * ff_part :] = tn(left, inner[...].reshape(count, ff_part)).astype(BF)
    put(n).start()
    return put


def ffn_first_kernel(
    own_ref,
    grad_ref,
    weight_hbm,
    all_ref,
    back_ref,
    out_ref,
    grads_out,
    weight,
    tokens,
    grads,
    wide,
    narrow,
    inner,
    gug,
    stage,
    columns_stage,
    sends,
    recvs,
    local,
):
    tp_at, seq_at, far, mate, _ = plane_place()
    seq = lax.axis_size("seq")
    other = 1 - tp_at
    to_x = at_device(tp_at, far)
    to_y = at_device(other, seq_at)
    to_c = at_device(tp_at, mate)
    rows, width = own_ref.shape
    pair = 2 * rows
    half = rows // 2
    block = width // 4
    ff_part = narrow.shape[2]
    gate_up, lower = slice(0, 2 * ff_part), slice(2 * ff_part, 3 * ff_part)
    enter((to_x, to_y, to_c))

    def piece(t, s, h):
        return all_ref.at[t * seq + s, pl.ds(h * half, half)]

    def own(i, h, device):
        return remote(
            own_ref.at[pl.ds(h * half, half)],
            piece(tp_at, seq_at, h),
            sends.at[i],
            recvs.at[i],
            device,
        )

    def relay(i, t, s, h, device):
        return remote(piece(t, s, h), piece(t, s, h), sends.at[i], recvs.at[i], device)

    x0, x1 = own(0, 0, to_x), own(3, 1, to_x)
    y0, y1 = own(1, 0, to_y), own(4, 1, to_y)
    c0, c1 = own(2, 0, to_c), own(5, 1, to_c)
    diag0 = relay(6, tp_at, far, 0, to_y)
    diag1 = relay(7, other, seq_at, 1, to_x)
    rx0, rx1 = relay(8, tp_at, far, 0, to_c), relay(11, tp_at, far, 1, to_c)
    ry0, ry1 = relay(9, other, seq_at, 0, to_c), relay(10, other, seq_at, 1, to_c)
    rd0, rd1 = relay(12, other, far, 0, to_c), relay(13, other, far, 1, to_c)

    def chip_rows(c):
        t = lax.rem(tp_at + c // 2, 2)
        s = lax.rem(seq_at + (seq // 2) * lax.rem(c, 2), seq)
        return pl.ds(t * seq + s - lax.rem(s, 2), 2)

    def take_tokens(c):
        return pltpu.make_async_copy(all_ref.at[chip_rows(c)], tokens.at[c], local.at[c])

    def take_grads(c):
        return pltpu.make_async_copy(grad_ref.at[chip_rows(c)], grads.at[c], local.at[4 + c])

    def put_back(c):
        return pltpu.make_async_copy(stage.at[0], back_ref.at[chip_rows(c)], local.at[8])

    def put_out(c):
        return pltpu.make_async_copy(stage.at[1], out_ref.at[chip_rows(c)], local.at[9])

    take_weight = pltpu.make_async_copy(weight_hbm, weight, local.at[12])
    mine = pltpu.make_async_copy(own_ref, all_ref.at[tp_at * seq + seq_at], local.at[13])
    for copy in (take_weight, x0, y0, c0, x1, y1, c1, mine):
        copy.start()
    for c in range(4):
        take_grads(c).start()
    take_weight.wait()

    def narrow_step(c, carry):
        take_grads(c).wait()
        narrow[c] = nn(grads[c].reshape(pair, width), weight[:, lower])
        return carry

    lax.fori_loop(0, 4, narrow_step, 0)
    mine.wait()
    c0.wait_recv()
    c1.wait_recv()
    take_tokens(0).start()

    def chip_step(c, carry):
        take_tokens(c).wait()
        wide[...] = nn(tokens[c].reshape(pair, width), weight[:, gate_up])

        @pl.when(c == 0)
        def _():
            x0.wait_recv()
            diag0.start()
            rx0.start()
            y0.wait_recv()
            ry0.start()

        @pl.when(c == 1)
        def _():
            ry0.wait_recv()
            ry1.wait_recv()
            take_tokens(2).start()

        @pl.when(c == 2)
        def _():
            diag0.wait_recv()
            rd0.start()
            diag1.wait_recv()
            rd1.start()

        slopes(wide, narrow.at[c], inner.at[c], gug.at[c])

        @pl.when(c >= 1)
        def _():
            put_back(c - 1).wait()
            put_out(c - 1).wait()

        def back_step(n, carry):
            at = pl.ds(pl.multiple_of(n * block, block), block)
            total = nt(gug[c], weight[at, gate_up]).astype(BF)
            stage[0, :, :, at] = total.reshape(2, rows, block)
            total = nt(inner[c], weight[at, lower]).astype(BF)
            stage[1, :, :, at] = total.reshape(2, rows, block)
            return carry

        lax.fori_loop(0, 4, back_step, 0)
        put_back(c).start()
        put_out(c).start()

        @pl.when(c == 0)
        def _():
            y1.wait_recv()
            diag1.start()
            ry1.start()
            x1.wait_recv()
            rx1.start()
            rx0.wait_recv()
            rx1.wait_recv()
            take_tokens(1).start()

        @pl.when(c == 2)
        def _():
            rd0.wait_recv()
            rd1.wait_recv()
            take_tokens(3).start()

        return carry

    lax.fori_loop(0, 4, chip_step, 0)

    def grads_step(n, carry):
        weight_step(n, tokens, grads, gug, inner, columns_stage, grads_out, (local, 10))
        return carry

    lax.fori_loop(0, 4, grads_step, 0)
    for copy in (x0, y0, c0, x1, y1, c1, diag0, diag1, rx0, ry0, ry1, rx1, rd0, rd1):
        copy.wait_send()
    put_back(3).wait()
    put_out(3).wait()
    for n in (2, 3):
        pltpu.make_async_copy(
            columns_stage.at[n - 2], grads_out.at[pl.ds(n * block, block)], local.at[8 + n]
        ).wait()


def ffn_second_kernel(
    all_ref,
    grad_ref,
    weight_hbm,
    back_ref,
    first_ref,
    out_ref,
    grads_out,
    sum_ref,
    weight,
    tokens,
    grads,
    wide,
    narrow,
    inner,
    gug,
    part,
    chip_in,
    far_in,
    near_in,
    stage,
    columns_stage,
    sends,
    recvs,
    local,
):
    tp_at, seq_at, far, mate, _ = plane_place()
    seq = lax.axis_size("seq")
    kind = lax.rem(seq_at, 2)
    to_x = at_device(tp_at, far)
    to_y = at_device(1 - tp_at, seq_at)
    to_c = at_device(tp_at, mate)
    rows, width = sum_ref.shape
    pair = 2 * rows
    half = rows // 2
    block = width // 4
    ff_part = narrow.shape[1]
    gate_up, lower = slice(0, 2 * ff_part), slice(2 * ff_part, 3 * ff_part)
    top, low = pl.ds(0, half), pl.ds(half, half)
    enter((to_x, to_y, to_c))

    def chip_rows(k):
        t = lax.rem(tp_at + 1 - lax.rem(k, 2), 2)
        s = lax.rem(seq_at + (seq // 2) * (1 - k // 2), seq)
        return pl.ds(t * seq + s - lax.rem(s, 2), 2)

    def take(ref, target, sem):
        return lambda k: pltpu.make_async_copy(ref.at[chip_rows(k)], target.at[k], local.at[sem + k])

    take_tokens, take_grads, take_back = (
        take(all_ref, tokens, 0),
        take(grad_ref, grads, 4),
        take(back_ref, part, 8),
    )

    def take_first(k):
        slot = lax.rem(k, 2)
        return pltpu.make_async_copy(first_ref.at[chip_rows(k)], stage.at[slot], local.at[12 + slot])

    def put_out(k):
        slot = lax.rem(k, 2)
        return pltpu.make_async_copy(stage.at[slot], out_ref.at[chip_rows(k)], local.at[14 + slot])

    def give(k):
        return remote(part.at[k, 1 - kind], chip_in.at[k], sends.at[k], recvs.at[k], to_c)

    def held(k):
        return part.at[k, kind]

    def hop(i, src, dst, device):
        return remote(src, dst, sends.at[i], recvs.at[i], device)

    d0 = hop(4, part.at[0, kind, top], far_in.at[0, top], to_x)
    d1 = hop(5, part.at[0, kind, low], far_in.at[1, low], to_y)
    x0 = hop(6, part.at[1, kind, top], near_in.at[0, top], to_x)
    y1 = hop(7, part.at[2, kind, low], near_in.at[1, low], to_y)
    y0 = hop(8, part.at[2, kind, top], near_in.at[1, top], to_y)
    x1 = hop(9, part.at[1, kind, low], near_in.at[0, low], to_x)

    def chip_sum(k):
        give(k).wait_recv()
        add_rows(held(k), (held(k), chip_in.at[k]), 0, rows, part.dtype)

    take_weight = pltpu.make_async_copy(weight_hbm, weight, local.at[18])
    take_weight.start()
    for k in range(4):
        take_grads(k).start()
        take_tokens(k).start()
        take_back(k).start()
    take_first(0).start()
    take_weight.wait()

    def chip_step(k, carry):
        slot = lax.rem(k, 2)
        take_grads(k).wait()
        narrow[...] = nn(grads[k].reshape(pair, width), weight[:, lower])

        @pl.when(k == 1)
        def _():
            chip_sum(0)
            d0.start()
            d1.start()

        @pl.when(k == 2)
        def _():
            chip_sum(1)
            x0.start()

        @pl.when(k == 3)
        def _():
            chip_sum(2)
            y1.start()
            d0.wait_recv()
            add_rows(held(2), (held(2), far_in.at[0]), 0, half, part.dtype)
            y0.start()
            d1.wait_recv()
            add_rows(held(1), (held(1), far_in.at[1]), half, half, part.dtype)
            x1.start()

        take_tokens(k).wait()
        wide[...] = nn(tokens[k].reshape(pair, width), weight[:, gate_up])
        slopes(wide, narrow, inner.at[k], gug.at[k])
        take_back(k).wait()

        def back_step(n, carry):
            at = pl.ds(pl.multiple_of(n * block, block), block)
            total = nt(gug[k], weight[at, gate_up]).reshape(2, rows, block)
            part[k, :, :, at] = (part[k, :, :, at].astype(F32) + total).astype(part.dtype)
            return carry

        lax.fori_loop(0, 4, back_step, 0)
        give(k).start()
        take_first(k).wait()

        @pl.when(k >= 1)
        def _():
            put_out(k - 1).wait()

        @pl.when(k < 3)
        def _():
            take_first(k + 1).start()

        def out_step(n, carry):
            at = pl.ds(pl.multiple_of(n * block, block), block)
            total = nt(inner[k], weight[at, lower]).reshape(2, rows, block)
            stage[slot, :, :, at] = (stage[slot, :, :, at].astype(F32) + total).astype(stage.dtype)
            return carry

        lax.fori_loop(0, 4, out_step, 0)
        put_out(k).start()
        return carry

    lax.fori_loop(0, 4, chip_step, 0)

    def grads_step(n, carry):
        weight_step(n, tokens, grads, gug, inner, columns_stage, grads_out, (local, 16))

        @pl.when(n == 0)
        def _():
            chip_sum(3)

        return carry

    lax.fori_loop(0, 4, grads_step, 0)
    x0.wait_recv()
    y0.wait_recv()
    add_rows(sum_ref, (held(3), near_in.at[0], near_in.at[1]), 0, half, sum_ref.dtype)
    y1.wait_recv()
    x1.wait_recv()
    add_rows(sum_ref, (held(3), near_in.at[0], near_in.at[1]), half, half, sum_ref.dtype)
    for k in range(4):
        give(k).wait_send()
    for copy in (d0, d1, x0, y1, y0, x1):
        copy.wait_send()
    put_out(3).wait()
    for n in (2, 3):
        pltpu.make_async_copy(
            columns_stage.at[n - 2], grads_out.at[pl.ds(n * block, block)], local.at[14 + n]
        ).wait()


def ffn_first_plane(block, grads, weight, ident):
    rows, width = block.shape
    plane = lax.axis_size("tp") * lax.axis_size("seq")
    cols = weight.shape[1]
    ff_part = cols // 3
    shape = jax.ShapeDtypeStruct
    hbm = pl.BlockSpec(memory_space=pltpu.HBM)
    vmem = pl.BlockSpec(memory_space=pltpu.VMEM)
    tokens = plane * rows
    return pl.pallas_call(
        ffn_first_kernel,
        out_shape=(
            shape((plane, rows, width), BF),
            shape((plane, rows, width), BF),
            shape((plane, rows, width), BF),
            shape((width, cols), BF),
        ),
        in_specs=[vmem, hbm, hbm],
        out_specs=(hbm, hbm, hbm, hbm),
        scratch_shapes=[
            pltpu.VMEM(weight.shape, BF),
            pltpu.VMEM((4, 2, rows, width), BF),
            pltpu.VMEM((4, 2, rows, width), BF),
            pltpu.VMEM((2 * rows, 2 * ff_part), F32),
            pltpu.VMEM((4, 2 * rows, ff_part), F32),
            pltpu.VMEM((4, 2 * rows, ff_part), BF),
            pltpu.VMEM((4, 2 * rows, 2 * ff_part), BF),
            pltpu.VMEM((2, 2, rows, width), BF),
            pltpu.VMEM((2, width // 4, cols), BF),
            pltpu.SemaphoreType.DMA((14,)),
            pltpu.SemaphoreType.DMA((14,)),
            pltpu.SemaphoreType.DMA((14,)),
        ],
        cost_estimate=pl.CostEstimate(
            flops=18 * tokens * width * ff_part,
            transcendentals=tokens * ff_part,
            bytes_accessed=22 * tokens * width,
        ),
        compiler_params=pltpu.CompilerParams(
            collective_id=ident, has_side_effects=True, vmem_limit_bytes=60 << 20
        ),
        name="ffn_first_plane",
    )(block, grads, weight)


def ffn_second_plane(block, grads, weight, back, first, ident):
    plane, rows, width = block.shape
    cols = weight.shape[1]
    ff_part = cols // 3
    shape = jax.ShapeDtypeStruct
    hbm = pl.BlockSpec(memory_space=pltpu.HBM)
    vmem = pl.BlockSpec(memory_space=pltpu.VMEM)
    tokens = plane * rows
    return pl.pallas_call(
        ffn_second_kernel,
        out_shape=(
            shape((plane, rows, width), BF),
            shape((width, cols), BF),
            shape((rows, width), F32),
        ),
        in_specs=[hbm] * 5,
        out_specs=(hbm, hbm, vmem),
        scratch_shapes=[
            pltpu.VMEM(weight.shape, BF),
            pltpu.VMEM((4, 2, rows, width), BF),
            pltpu.VMEM((4, 2, rows, width), BF),
            pltpu.VMEM((2 * rows, 2 * ff_part), F32),
            pltpu.VMEM((2 * rows, ff_part), F32),
            pltpu.VMEM((4, 2 * rows, ff_part), BF),
            pltpu.VMEM((4, 2 * rows, 2 * ff_part), BF),
            pltpu.VMEM((4, 2, rows, width), BF),
            pltpu.VMEM((4, rows, width), BF),
            pltpu.VMEM((2, rows, width), BF),
            pltpu.VMEM((2, rows, width), BF),
            pltpu.VMEM((2, 2, rows, width), BF),
            pltpu.VMEM((2, width // 4, cols), BF),
            pltpu.SemaphoreType.DMA((10,)),
            pltpu.SemaphoreType.DMA((10,)),
            pltpu.SemaphoreType.DMA((19,)),
        ],
        cost_estimate=pl.CostEstimate(
            flops=18 * tokens * width * ff_part,
            transcendentals=tokens * ff_part,
            bytes_accessed=22 * tokens * width,
        ),
        compiler_params=pltpu.CompilerParams(
            collective_id=ident, has_side_effects=True, vmem_limit_bytes=63 << 20
        ),
        name="ffn_second_plane",
    )(block, grads, weight, back, first)


def finish_kernel(
    first_ref,
    second_ref,
    gate_weight,
    up_weight,
    gain_ref,
    gate_out,
    up_out,
    down_first,
    down_second,
    gain_out,
    first_in,
    second_in,
    local,
    sends,
    recvs,
):
    tp_at, seq_at, _, _, _ = plane_place()
    seq = lax.axis_size("seq")
    plane = lax.axis_size("tp") * seq
    me = tp_at * seq + seq_at
    peers = [lax.rem(me + k, plane) for k in range(1, plane)]
    devices = [at_device(peer // seq, lax.rem(peer, seq)) for peer in peers]
    enter(devices)
    copies = []
    for k, (peer, device) in enumerate(zip(peers, devices)):
        i = plane - 1 + k
        copies.append(remote(first_ref.at[peer], first_in.at[me], sends.at[k], recvs.at[k], device))
        copies.append(remote(second_ref.at[peer], second_in.at[me], sends.at[i], recvs.at[i], device))
    copies.append(pltpu.make_async_copy(first_ref.at[me], first_in.at[me], local.at[0]))
    copies.append(pltpu.make_async_copy(second_ref.at[me], second_in.at[me], local.at[1]))
    for copy in copies:
        copy.start()
    for copy in copies:
        copy.wait()
    gain = gain_ref[...]
    sizes = [ref.shape[2] // 3 for ref in (first_in, second_in)]
    total = jnp.zeros(gain.shape, F32)
    for j in range(plane):
        start = j * sum(sizes)
        for ref, down, size in ((first_in, down_first, sizes[0]), (second_in, down_second, sizes[1])):
            at = slice(start, start + size)
            start += size
            for k, (out, weight) in enumerate(((gate_out, gate_weight), (up_out, up_weight))):
                own = ref[j, :, k * size : (k + 1) * size].astype(F32)
                out[:, at] = own * gain
                total = total + jnp.sum(own * weight[:, at].astype(F32), axis=1, keepdims=True)
            down[j] = ref[j, :, 2 * size :]
    gain_out[...] = total


def finish_plane(first, second, gate_weight, up_weight, gain, ident):
    plane, rows, _ = first.shape
    shape = jax.ShapeDtypeStruct
    hbm = pl.BlockSpec(memory_space=pltpu.HBM)
    vmem = pl.BlockSpec(memory_space=pltpu.VMEM)
    size = plane * rows * gate_weight.shape[1] * 6 // plane
    return pl.pallas_call(
        finish_kernel,
        out_shape=(
            shape(gate_weight.shape, F32),
            shape(up_weight.shape, F32),
            shape((plane, rows, first.shape[2] // 3), BF),
            shape((plane, rows, second.shape[2] // 3), BF),
            shape((rows, 1), F32),
        ),
        in_specs=[hbm, hbm, vmem, vmem, vmem],
        out_specs=(vmem,) * 5,
        scratch_shapes=[
            pltpu.VMEM(first.shape, BF),
            pltpu.VMEM(second.shape, BF),
            pltpu.SemaphoreType.DMA((2,)),
            pltpu.SemaphoreType.DMA((2 * plane - 2,)),
            pltpu.SemaphoreType.DMA((2 * plane - 2,)),
        ],
        cost_estimate=pl.CostEstimate(flops=0, transcendentals=0, bytes_accessed=size * 20),
        compiler_params=pltpu.CompilerParams(
            collective_id=ident, has_side_effects=True, vmem_limit_bytes=24 << 20
        ),
        name="finish_plane",
    )(first, second, gate_weight, up_weight, gain)


def columns(matrix, parts):
    rows, cols = matrix.shape
    return jnp.transpose(matrix.reshape(rows, parts, cols // parts), (1, 0, 2))


def uncolumns(blocks):
    parts, rows, cols = blocks.shape
    return jnp.transpose(blocks, (1, 0, 2)).reshape(rows, parts * cols)


def after(value, *earlier):
    return lax.optimization_barrier((value,) + earlier)[0]


def per_device(
    layer_input,
    pic_starts,
    skip_mask,
    gain_attn,
    w_query,
    w_key,
    w_value,
    w_out,
    gain_ffn,
    w_gate,
    w_up,
    w_down,
    cotangent,
):
    _, local_len, width = layer_input.shape
    seq = lax.axis_size("seq")
    plane = lax.axis_size("tp") * seq
    total_len = local_len * seq
    heads = H // plane
    share = plane // KV
    ff_part = w_gate.shape[1] // plane
    q_part = heads * DH

    gain1 = gain_attn[:, None]
    gain2 = gain_ffn[:, None]
    wq32, wk32, wv32 = w_query.astype(F32), w_key.astype(F32), w_value.astype(F32)
    wg32, wu32 = w_gate.astype(F32), w_up.astype(F32)
    attn_pack = jnp.concatenate(
        [
            columns((wq32 * gain1).astype(BF), plane),
            jnp.repeat(columns((wk32 * gain1).astype(BF), KV), share, axis=0),
            jnp.repeat(columns((wv32 * gain1).astype(BF), KV), share, axis=0),
            columns(w_out.T, plane),
        ],
        axis=2,
    )
    attn_rows = exchange_plane(attn_pack, 0)
    attn_rows = attn_rows.reshape(-1, attn_rows.shape[2])
    attn_weight = lax.all_gather(attn_rows, "rep", axis=0, tiled=True)
    qkv_weight = attn_weight[:, : q_part + 2 * DH]
    out_weight = attn_weight[:, q_part + 2 * DH :]

    tokens = layer_input.reshape(local_len, width).astype(F32)
    keep = (1 - skip_mask).astype(F32).reshape(local_len, 1)
    upstream = cotangent.reshape(local_len, width).astype(F32)
    scale1 = rms_scale(tokens)
    norm1 = tokens * scale1

    first_part = (ff_part // 2 + DH - 1) // DH * DH
    split = ((0, first_part), (first_part, ff_part))
    ffn_parts = (
        columns((wg32 * gain2).astype(BF), plane),
        columns((wu32 * gain2).astype(BF), plane),
        columns(w_down.T, plane),
    )
    first_pack, second_pack = (
        jnp.concatenate([m[:, :, a:b] for m in ffn_parts], axis=2) for a, b in split
    )
    norm1_all, first_rows, second_rows = spread_plane(
        after(norm1.astype(BF), attn_rows), first_pack, second_pack, 1
    )
    first_rows = first_rows.reshape(-1, first_rows.shape[2])
    second_rows = second_rows.reshape(-1, second_rows.shape[2])
    first_weight = lax.all_gather(first_rows, "rep", axis=0, tiled=True)
    second_weight = lax.all_gather(second_rows, "rep", axis=0, tiled=True)
    norm1_all = norm1_all.reshape(-1, width)

    other_starts = lax.ppermute(pic_starts, "tp", [(0, 1), (1, 0)])
    starts = jnp.where(
        lax.axis_index("tp") == 0,
        jnp.concatenate([pic_starts, other_starts], axis=0),
        jnp.concatenate([other_starts, pic_starts], axis=0),
    )
    positions = jnp.arange(total_len, dtype=jnp.int32)
    cos_table, sin_table = rotary_tables(positions, DH)
    cos = jnp.concatenate([cos_table, cos_table], axis=1)
    sin = jnp.concatenate([-sin_table, sin_table], axis=1)
    qkv, mixed, log_total, branch_partial, ffn_grad = attn_front_plane(
        starts, norm1_all, attn_weight, cos, sin, (keep * upstream).astype(BF), 3
    )
    branch = scatter_plane(branch_partial, 4)
    hidden = tokens + keep * branch

    scale2 = rms_scale(hidden)
    norm2 = hidden * scale2
    norm2_all, back_first, out_first, first_partial = ffn_first_plane(
        norm2.astype(BF), ffn_grad, first_weight, 5
    )
    first_sums = lax.psum_scatter(first_partial, "rep", scatter_dimension=0, tiled=True)
    out_partial, second_partial, scaled2 = ffn_second_plane(
        norm2_all, ffn_grad, second_weight, back_first, out_first, 6
    )
    second_sums = lax.psum_scatter(second_partial, "rep", scatter_dimension=0, tiled=True)
    hidden_grad = upstream + scale2 * (
        scaled2 - norm2 * jnp.mean(scaled2 * norm2, axis=-1, keepdims=True)
    )

    branch_grad = gather_plane((keep * hidden_grad).astype(BF), 7)
    mixed_grad = nn(branch_grad, out_weight).astype(BF)
    qkv_grad, ffn_out = attn_back_plane(
        starts,
        qkv,
        after(mixed_grad, first_sums),
        log_total,
        cos,
        sin,
        out_partial.reshape(-1, width),
        9,
    )
    attn_partial = jnp.concatenate(
        [tn(norm1_all, qkv_grad).astype(BF), tn(branch_grad, mixed).astype(BF)], axis=1
    )
    scaled1_partial = nt(qkv_grad, qkv_weight).astype(BF)
    attn_sums = lax.psum_scatter(attn_partial, "rep", scatter_dimension=0, tiled=True)
    scaled1 = scatter_plane(after(scaled1_partial, attn_partial), 8)
    input_grad = hidden_grad + scale1 * (
        scaled1 - norm1 * jnp.mean(scaled1 * norm1, axis=-1, keepdims=True)
    )
    out_hidden = (hidden + keep * ffn_out).astype(BF)

    gate_grad, up_grad, down_first, down_second, gain_ffn_grad = finish_plane(
        after(first_sums.reshape(plane, -1, first_sums.shape[1]), scaled1),
        second_sums.reshape(plane, -1, second_sums.shape[1]),
        w_gate,
        w_up,
        gain2,
        10,
    )
    down_own = jnp.concatenate([down_first, down_second], axis=2)
    down_grad = jnp.transpose(down_own, (0, 2, 1)).reshape(plane * ff_part, -1).astype(F32)

    attn_sums = after(attn_sums, gain_ffn_grad)
    attn_own = exchange_plane(attn_sums.reshape(plane, -1, attn_sums.shape[1]), 11).astype(F32)
    query_own = uncolumns(attn_own[:, :, :q_part])
    kv_own = attn_own[:, :, q_part : q_part + 2 * DH]
    kv_own = jnp.sum(kv_own.reshape(KV, share, -1, 2 * DH), axis=1)
    key_own = uncolumns(kv_own[:, :, :DH])
    value_own = uncolumns(kv_own[:, :, DH:])
    out_own = uncolumns(attn_own[:, :, q_part + 2 * DH :])
    gain_attn_grad = (
        jnp.sum(query_own * wq32, axis=1)
        + jnp.sum(key_own * wk32, axis=1)
        + jnp.sum(value_own * wv32, axis=1)
    )
    return (
        out_hidden[None],
        input_grad[None],
        gain_attn_grad,
        query_own * gain1,
        key_own * gain1,
        value_own * gain1,
        out_own.T,
        gain_ffn_grad[:, 0],
        gate_grad,
        up_grad,
        down_grad,
    )


def solution(mesh):
    devices = mesh.devices
    dp, seq = devices.shape
    inner = Mesh(devices.reshape(dp // TP, TP, seq), ("rep", "tp", "seq"))
    dps = ("rep", "tp")
    every = ("rep", "tp", "seq")
    token = P(dps, "seq", None)
    row = P(every, None)
    col = P(None, every)
    return jax.shard_map(
        per_device,
        mesh=inner,
        in_specs=(
            token,
            P(dps, None),
            P(dps, "seq"),
            P(every),
            row,
            row,
            row,
            col,
            P(every),
            row,
            row,
            col,
            token,
        ),
        out_specs=(token, token, P(every), row, row, row, col, P(every), row, row, col),
        check_vma=False,
    )
```

```python
import jax
import jax.numpy as jnp
from jax import lax
from jax.experimental import pallas as pl
from jax.experimental.pallas import tpu as pltpu
from jax.sharding import Mesh
from jax.sharding import PartitionSpec as P

H = 16
KV = 4
DH = 128
PIC = 256
NPIC = 2
EPS = 1e-05
TP = 2
BF = jnp.bfloat16
F32 = jnp.float32


def rotary_tables(positions, head_dim):
    half_dim = head_dim // 2
    inverse = 10000.0 ** (-(jnp.arange(half_dim, dtype=F32) * 2.0 / head_dim))
    angles = positions.astype(F32)[:, None] * inverse[None, :]
    return (jnp.cos(angles), jnp.sin(angles))


def rms_scale(rows):
    return lax.rsqrt(jnp.mean(rows * rows, axis=-1, keepdims=True) + EPS)


def dot(left, right, contract):
    return lax.dot_general(
        left, right, ((contract[:1], contract[1:]), ((), ())), preferred_element_type=F32
    )


def nn(left, right):
    return dot(left, right, (1, 0))


def nt(left, right):
    return dot(left, right, (1, 1))


def tn(left, right):
    return dot(left, right, (0, 0))


MESH_ID = pl.DeviceIdType.MESH
SUB = 32


def plane_place():
    tp_at = lax.axis_index("tp")
    seq_at = lax.axis_index("seq")
    seq = lax.axis_size("seq")
    half = seq // 2
    far = lax.rem(seq_at + half, seq)
    mate = seq_at + 1 - 2 * lax.rem(seq_at, 2)
    far_mate = far + 1 - 2 * lax.rem(far, 2)
    return tp_at, seq_at, far, mate, far_mate


def at_device(tp_at, seq_at):
    return (lax.axis_index("rep"), tp_at, seq_at)


def enter(devices):
    barrier = pltpu.get_barrier_semaphore()
    for device in devices:
        pl.semaphore_signal(barrier, inc=1, device_id=device, device_id_type=MESH_ID)
    pl.semaphore_wait(barrier, len(devices))


def remote(src, dst, send, recv, device):
    return pltpu.make_async_remote_copy(
        src_ref=src,
        dst_ref=dst,
        send_sem=send,
        recv_sem=recv,
        device_id=device,
        device_id_type=MESH_ID,
    )


def gather_stages(own_ref, all_ref, sends, recvs, local):
    tp_at, seq_at, far, mate, _ = plane_place()
    seq = lax.axis_size("seq")
    other = 1 - tp_at
    to_x = at_device(tp_at, far)
    to_y = at_device(other, seq_at)
    to_c = at_device(tp_at, mate)
    rows = own_ref.shape[0]
    part = rows // 2

    def piece(t, s, h):
        return all_ref.at[t * seq + s, pl.ds(h * part, part)]

    def relay(i, t, s, h, device):
        return remote(piece(t, s, h), piece(t, s, h), sends.at[i], recvs.at[i], device)

    def own(i, h, device):
        return remote(
            own_ref.at[pl.ds(h * part, part)],
            piece(tp_at, seq_at, h),
            sends.at[i],
            recvs.at[i],
            device,
        )

    x0, x1 = own(0, 0, to_x), own(3, 1, to_x)
    y0, y1 = own(1, 0, to_y), own(4, 1, to_y)
    c0, c1 = own(2, 0, to_c), own(5, 1, to_c)
    diag0 = relay(6, tp_at, far, 0, to_y)
    diag1 = relay(7, other, seq_at, 1, to_x)
    rx0, rx1 = relay(8, tp_at, far, 0, to_c), relay(11, tp_at, far, 1, to_c)
    ry0, ry1 = relay(9, other, seq_at, 0, to_c), relay(10, other, seq_at, 1, to_c)
    rd0, rd1 = relay(12, other, far, 0, to_c), relay(13, other, far, 1, to_c)
    mine = pltpu.make_async_copy(own_ref, all_ref.at[tp_at * seq + seq_at], local)

    def begin(peers=(to_x, to_y, to_c)):
        enter(peers)
        for copy in (x0, y0, c0, x1, y1, c1, mine):
            copy.start()

    def first():
        x0.wait_recv()
        diag0.start()
        rx0.start()
        y0.wait_recv()
        ry0.start()

    def second():
        y1.wait_recv()
        diag1.start()
        ry1.start()
        x1.wait_recv()
        rx1.start()

    def finish():
        diag0.wait_recv()
        rd0.start()
        diag1.wait_recv()
        rd1.start()
        for copy in (c0, c1, rx0, ry0, ry1, rx1, rd0, rd1):
            copy.wait_recv()
        for copy in (x0, y0, c0, x1, y1, c1, diag0, diag1, rx0, ry0, ry1, rx1, rd0, rd1):
            copy.wait_send()
        mine.wait()

    return begin, first, second, finish


def gather_kernel(*refs):
    for stage in gather_stages(*refs):
        stage()


GATHER_SCRATCH = (
    pltpu.SemaphoreType.DMA((14,)),
    pltpu.SemaphoreType.DMA((14,)),
    pltpu.SemaphoreType.DMA,
)


def gather_plane(block, ident):
    rows, width = block.shape
    plane = lax.axis_size("tp") * lax.axis_size("seq")
    size = rows * width * 2
    gathered = pl.pallas_call(
        gather_kernel,
        out_shape=jax.ShapeDtypeStruct((plane, rows, width), block.dtype),
        in_specs=[pl.BlockSpec(memory_space=pltpu.VMEM)],
        out_specs=pl.BlockSpec(memory_space=pltpu.HBM),
        scratch_shapes=GATHER_SCRATCH,
        cost_estimate=pl.CostEstimate(
            flops=0, transcendentals=0, bytes_accessed=plane * size * 12
        ),
        compiler_params=pltpu.CompilerParams(collective_id=ident, has_side_effects=True),
        name="gather_plane",
    )(block)
    return gathered.reshape(plane * rows, width)


def spread_kernel(
    own_ref, move_ref, all_ref, move_out, kept, copies, *gather
):
    begin, first, second, finish = gather_stages(own_ref, all_ref, *gather)
    tp_at, seq_at, _, _, _ = plane_place()
    seq = lax.axis_size("seq")
    plane = lax.axis_size("tp") * seq
    me = tp_at * seq + seq_at
    peers = [lax.rem(me + k, plane) for k in range(1, plane)]
    devices = [at_device(peer // seq, lax.rem(peer, seq)) for peer in peers]
    sends, recvs, local = copies.at[0], copies.at[1], copies.at[2]
    begin(devices)
    moves = [
        remote(move_ref.at[peer], move_out.at[me], sends.at[k], recvs.at[k], device)
        for k, (peer, device) in enumerate(zip(peers, devices))
    ]
    for move in moves:
        move.start()
    take = pltpu.make_async_copy(move_ref.at[me], kept, local.at[0])
    put = pltpu.make_async_copy(kept, move_out.at[me], local.at[1])
    take.start()
    take.wait()
    put.start()
    first()
    second()
    for move in moves:
        move.wait()
    put.wait()
    finish()


def spread_plane(block, blocks, ident):
    rows, width = block.shape
    plane = lax.axis_size("tp") * lax.axis_size("seq")
    hbm = pl.BlockSpec(memory_space=pltpu.HBM)
    vmem = pl.BlockSpec(memory_space=pltpu.VMEM)
    size = plane * rows * width * 2
    return pl.pallas_call(
        spread_kernel,
        out_shape=(
            jax.ShapeDtypeStruct((plane, rows, width), block.dtype),
            jax.ShapeDtypeStruct(blocks.shape, blocks.dtype),
        ),
        in_specs=[vmem, hbm],
        out_specs=(hbm, hbm),
        scratch_shapes=[
            pltpu.VMEM(blocks.shape[1:], blocks.dtype),
            pltpu.SemaphoreType.DMA((3, plane)),
            *GATHER_SCRATCH,
        ],
        cost_estimate=pl.CostEstimate(flops=0, transcendentals=0, bytes_accessed=size * 16),
        compiler_params=pltpu.CompilerParams(collective_id=ident, has_side_effects=True),
        name="spread_plane",
    )(block, blocks)


def add_rows(target, sources, start, count, kind):
    step = min(SUB, count)

    def body(i, carry):
        at = pl.ds(start + i * step, step)
        total = sources[0][at, :].astype(F32)
        for source in sources[1:]:
            total = total + source[at, :].astype(F32)
        target[at, :] = total.astype(kind)
        return carry

    lax.fori_loop(0, count // step, body, 0)


def scatter_stages(part_ref, sum_ref, held, chip_in, far_in, near_in, loads, sends, recvs):
    tp_at, seq_at, far, mate, far_mate = plane_place()
    seq = lax.axis_size("seq")
    other = 1 - tp_at
    to_x = at_device(tp_at, far)
    to_y = at_device(other, seq_at)
    to_c = at_device(tp_at, mate)
    rows = sum_ref.shape[0]
    part = rows // 2
    top, low = pl.ds(0, part), pl.ds(part, part)
    chips = ((other, far, far_mate), (tp_at, far, far_mate), (other, seq_at, mate), (tp_at, seq_at, mate))
    gives = [
        remote(part_ref.at[t * seq + m], chip_in.at[k], sends.at[k], recvs.at[k], to_c)
        for k, (t, s, m) in enumerate(chips)
    ]
    takes = [
        pltpu.make_async_copy(part_ref.at[t * seq + s], held.at[k], loads.at[k])
        for k, (t, s, m) in enumerate(chips)
    ]

    def hop(i, src, dst, device):
        return remote(src, dst, sends.at[i], recvs.at[i], device)

    d0 = hop(4, held.at[0, top], far_in.at[0, top], to_x)
    d1 = hop(5, held.at[0, low], far_in.at[1, low], to_y)
    x0 = hop(6, held.at[1, top], near_in.at[0, top], to_x)
    y1 = hop(7, held.at[2, low], near_in.at[1, low], to_y)
    y0 = hop(8, held.at[2, top], near_in.at[1, top], to_y)
    x1 = hop(9, held.at[1, low], near_in.at[0, low], to_x)

    def begin():
        enter((to_x, to_y, to_c))
        for give, take in zip(gives, takes):
            give.start()
            take.start()

    def chip_sum(k):
        takes[k].wait()
        gives[k].wait_recv()
        add_rows(held.at[k], (held.at[k], chip_in.at[k]), 0, rows, held.dtype)

    def diagonal():
        chip_sum(0)
        d0.start()
        d1.start()

    def along_x():
        chip_sum(1)
        x0.start()

    def along_y():
        chip_sum(2)
        y1.start()

    def own():
        chip_sum(3)

    def fold():
        d0.wait_recv()
        add_rows(held.at[2], (held.at[2], far_in.at[0]), 0, part, held.dtype)
        y0.start()
        d1.wait_recv()
        add_rows(held.at[1], (held.at[1], far_in.at[1]), part, part, held.dtype)
        x1.start()

    def finish():
        x0.wait_recv()
        y0.wait_recv()
        add_rows(sum_ref, (held.at[3], near_in.at[0], near_in.at[1]), 0, part, sum_ref.dtype)
        y1.wait_recv()
        x1.wait_recv()
        add_rows(sum_ref, (held.at[3], near_in.at[0], near_in.at[1]), part, part, sum_ref.dtype)
        for copy in gives + [d0, d1, x0, y1, y0, x1]:
            copy.wait_send()

    return begin, diagonal, along_x, along_y, own, fold, finish


def scatter_kernel(*refs):
    for stage in scatter_stages(*refs):
        stage()


def scatter_scratch(rows, width, kind):
    return [
        pltpu.VMEM((4, rows, width), kind),
        pltpu.VMEM((4, rows, width), kind),
        pltpu.VMEM((2, rows, width), kind),
        pltpu.VMEM((2, rows, width), kind),
        pltpu.SemaphoreType.DMA((4,)),
        pltpu.SemaphoreType.DMA((10,)),
        pltpu.SemaphoreType.DMA((10,)),
    ]


def scatter_plane(partial, ident):
    plane = lax.axis_size("tp") * lax.axis_size("seq")
    rows, width = partial.shape[0] // plane, partial.shape[1]
    kind = partial.dtype
    size = rows * width * 2
    return pl.pallas_call(
        scatter_kernel,
        out_shape=jax.ShapeDtypeStruct((rows, width), F32),
        in_specs=[pl.BlockSpec(memory_space=pltpu.HBM)],
        out_specs=pl.BlockSpec(memory_space=pltpu.VMEM),
        scratch_shapes=scatter_scratch(rows, width, kind),
        cost_estimate=pl.CostEstimate(
            flops=0, transcendentals=0, bytes_accessed=plane * size * 14
        ),
        compiler_params=pltpu.CompilerParams(
            collective_id=ident, has_side_effects=True, vmem_limit_bytes=60 << 20
        ),
        name="scatter_plane",
    )(partial.reshape(plane, rows, width))


def fill_bias(bias, starts_ref, t, blocks):
    for b in range(blocks):
        span = min(2, blocks - b) * PIC
        k_at = lax.broadcasted_iota(jnp.int32, (span, PIC), 0) + b * PIC
        q_at = lax.broadcasted_iota(jnp.int32, (span, PIC), 1) + b * PIC
        high, below = jnp.maximum(k_at, q_at), jnp.minimum(k_at, q_at)
        allowed = k_at <= q_at
        for j in range(NPIC):
            start = starts_ref[t, j]
            allowed = allowed | ((below >= start) & (high < start + PIC))
        bias[b, :span, :] = jnp.where(allowed, 0.0, -jnp.inf)


def masked(scores, bias, b):
    late = scores[b * PIC :] + bias[b, : scores.shape[0] - b * PIC, :]
    return jnp.concatenate([scores[: b * PIC], late], axis=0) if b else late


def attn_front_kernel(
    starts_ref,
    norm_hbm,
    weight_hbm,
    cos_ref,
    sin_ref,
    own_ref,
    qkv_ref,
    mixed_ref,
    log_ref,
    out_ref,
    all_ref,
    bias,
    turned,
    norm,
    weight,
    projected,
    stage,
    local,
    *gather,
):
    begin, first, second, finish = gather_stages(own_ref, all_ref, *gather)
    total, dim = cos_ref.shape
    take_weight = pltpu.make_async_copy(weight_hbm, weight, local.at[0])
    take_weight.start()

    def take_norm(t):
        rows = pl.ds(t * total, total)
        return pltpu.make_async_copy(norm_hbm.at[rows], norm.at[t], local.at[1 + t])

    def put_out(t, n):
        rows = pl.ds(t * total + n * (total // 2), total // 2)
        return pltpu.make_async_copy(stage.at[n], out_ref.at[rows], local.at[1 + TP + n])

    for t in range(TP):
        take_norm(t).start()
    begin()
    take_weight.wait()
    heads = mixed_ref.shape[1] // dim
    blocks = total // PIC
    scale = dim ** (-0.5)
    k_cols = slice(heads * dim, (heads + 1) * dim)
    v_cols = slice((heads + 1) * dim, (heads + 2) * dim)

    def turn(rows, at):
        return rows * cos_ref[at, :] + pltpu.roll(rows, dim // 2, 1) * sin_ref[at, :]

    def head_step(i, carry):
        t, h = i // heads, lax.rem(i, heads)
        base = pl.multiple_of(t * total, total)
        cols = pl.ds(pl.multiple_of(h * dim, dim), dim)

        @pl.when(h == 0)
        def _():
            rows = pl.ds(base, total)
            take_norm(t).wait()

            def project(n, carry):
                some = pl.ds(pl.multiple_of(n * PIC, PIC), PIC)
                projected[some, :] = nn(norm[t, some, :], weight[:, : (heads + 2) * dim])
                return carry

            lax.fori_loop(0, blocks, project, 0)
            values = projected[:, v_cols].astype(BF)
            qkv_ref[rows, k_cols] = turn(projected[:, k_cols], pl.ds(0, total)).astype(BF)
            qkv_ref[rows, v_cols] = values
            turned[...] = values.T
            fill_bias(bias, starts_ref, t, blocks)

        for b in range(blocks):
            at = pl.ds(pl.multiple_of(base + b * PIC, PIC), PIC)
            count = min(b + 2, blocks) * PIC
            queries = turn(projected[b * PIC : (b + 1) * PIC, cols], pl.ds(b * PIC, PIC)).astype(BF)
            qkv_ref[at, cols] = queries
            scores = nt(qkv_ref[pl.ds(base, count), k_cols], queries) * scale
            scores = masked(scores, bias, b)
            peak = jnp.max(scores, axis=0, keepdims=True)
            weights = jnp.exp(scores - peak)
            mass = jnp.sum(weights, axis=0, keepdims=True)
            log_ref[i, :, b * PIC : (b + 1) * PIC] = peak + jnp.log(mass)
            probs = (weights * (1.0 / mass)).astype(BF)
            mixed_ref[at, cols] = nn(turned[:, :count], probs).T.astype(BF)
            if b == 0:
                pl.when(i == 1)(first)
                pl.when(i == 3)(second)

        @pl.when(h == heads - 1)
        def _():
            for n in range(2):

                @pl.when(t >= 1)
                def _():
                    put_out(t - 1, n).wait()

                rows = pl.ds(pl.multiple_of(base + n * (total // 2), total // 2), total // 2)
                block = stage.shape[2] // 4

                def out_step(m, carry):
                    some = pl.ds(pl.multiple_of(m * block, block), block)
                    partial = nt(mixed_ref[rows, :], weight[some, (heads + 2) * dim :])
                    stage[n, :, some] = partial.astype(BF)
                    return carry

                lax.fori_loop(0, 4, out_step, 0)
                put_out(t, n).start()

        return carry

    lax.fori_loop(0, log_ref.shape[0], head_step, 0)
    finish()
    for n in range(2):
        put_out(TP - 1, n).wait()


def attn_front_plane(starts, norm, weight, cos, sin, block, ident):
    rows, width = block.shape
    plane = lax.axis_size("tp") * lax.axis_size("seq")
    total, dim = cos.shape
    tokens = norm.shape[0]
    q_part = weight.shape[1] // 2 - dim
    shape = jax.ShapeDtypeStruct
    vmem = pl.BlockSpec(memory_space=pltpu.VMEM)
    smem = pl.BlockSpec(memory_space=pltpu.SMEM)
    hbm = pl.BlockSpec(memory_space=pltpu.HBM)
    return pl.pallas_call(
        attn_front_kernel,
        out_shape=(
            shape((tokens, q_part + 2 * dim), BF),
            shape((tokens, q_part), BF),
            shape((tokens * q_part // dim // total, 1, total), F32),
            shape(norm.shape, BF),
            shape((plane, rows, width), block.dtype),
        ),
        in_specs=[smem, hbm, hbm, vmem, vmem, vmem],
        out_specs=(vmem, vmem, vmem, hbm, hbm),
        scratch_shapes=[
            pltpu.VMEM((total // PIC, 2 * PIC, PIC), F32),
            pltpu.VMEM((dim, total), BF),
            pltpu.VMEM((TP, total, width), BF),
            pltpu.VMEM(weight.shape, BF),
            pltpu.VMEM((total, q_part + 2 * dim), F32),
            pltpu.VMEM((2, total // 2, width), BF),
            pltpu.SemaphoreType.DMA((3 + TP,)),
            *GATHER_SCRATCH,
        ],
        cost_estimate=pl.CostEstimate(
            flops=4 * tokens * total * q_part,
            transcendentals=tokens * total * q_part // dim,
            bytes_accessed=plane * rows * width * 24,
        ),
        compiler_params=pltpu.CompilerParams(
            collective_id=ident, has_side_effects=True, vmem_limit_bytes=40 << 20
        ),
        name="attn_front_plane",
    )(starts, norm, weight, cos, sin, block)


def attn_back_kernel(
    starts_ref,
    qkv_ref,
    g_ref,
    log_ref,
    cos_ref,
    sin_ref,
    part_ref,
    grad_ref,
    sum_ref,
    bias,
    turned,
    keys_sum,
    values_sum,
    *scatter,
):
    begin, diagonal, along_x, along_y, own, fold, finish = scatter_stages(
        part_ref, sum_ref, *scatter
    )
    begin()
    total, dim = cos_ref.shape
    heads = g_ref.shape[1] // dim
    blocks = total // PIC
    scale = dim ** (-0.5)
    k_cols = slice(heads * dim, (heads + 1) * dim)
    v_cols = slice((heads + 1) * dim, (heads + 2) * dim)
    events = {(0, 1): diagonal, (0, 2): along_x, (0, 3): along_y, (1, 0): own, (2, 2): fold}

    def unturn(rows, at):
        return rows * cos_ref[at, :] - pltpu.roll(rows, dim // 2, 1) * sin_ref[at, :]

    def head_step(i, carry):
        t, h = i // heads, lax.rem(i, heads)
        base = pl.multiple_of(t * total, total)
        cols = pl.ds(pl.multiple_of(h * dim, dim), dim)

        @pl.when(h == 0)
        def _():
            turned[...] = qkv_ref[pl.ds(base, total), k_cols].T
            keys_sum[...] = jnp.zeros(keys_sum.shape, F32)
            values_sum[...] = jnp.zeros(values_sum.shape, F32)
            fill_bias(bias, starts_ref, t, blocks)

        for b in range(blocks):
            at = pl.ds(pl.multiple_of(base + b * PIC, PIC), PIC)
            count = min(b + 2, blocks) * PIC
            seen = pl.ds(base, count)
            queries, grads = qkv_ref[at, cols], g_ref[at, cols]
            scores = nt(qkv_ref[seen, k_cols], queries) * scale - log_ref[i, :, b * PIC : (b + 1) * PIC]
            probs = jnp.exp(masked(scores, bias, b))
            prob_grad = nt(qkv_ref[seen, v_cols], grads)
            mean = jnp.sum(probs * prob_grad, axis=0, keepdims=True)
            score_grad = (probs * (prob_grad - mean)).astype(BF)
            values_sum[:count, :] += nn(probs.astype(BF), grads)
            keys_sum[:count, :] += nn(score_grad, queries)
            back = nn(turned[:, :count], score_grad).T * scale
            grad_ref[at, cols] = unturn(back, pl.ds(b * PIC, PIC)).astype(BF)
            for (step, block), stage in events.items():
                if block == b:
                    pl.when(i == step)(stage)

        @pl.when(h == heads - 1)
        def _():
            rows = pl.ds(base, total)
            back = unturn(keys_sum[...] * scale, pl.ds(0, total))
            grad_ref[rows, k_cols] = back.astype(BF)
            grad_ref[rows, v_cols] = values_sum[...].astype(BF)

        return carry

    lax.fori_loop(0, log_ref.shape[0], head_step, 0)
    finish()


def attn_back_plane(starts, qkv, grads, log_total, cos, sin, partial, ident):
    plane = lax.axis_size("tp") * lax.axis_size("seq")
    rows, width = partial.shape[0] // plane, partial.shape[1]
    total, dim = cos.shape
    tokens, q_part = grads.shape
    hbm = pl.BlockSpec(memory_space=pltpu.HBM)
    vmem = pl.BlockSpec(memory_space=pltpu.VMEM)
    smem = pl.BlockSpec(memory_space=pltpu.SMEM)
    return pl.pallas_call(
        attn_back_kernel,
        out_shape=(
            jax.ShapeDtypeStruct((tokens, q_part + 2 * dim), BF),
            jax.ShapeDtypeStruct((rows, width), F32),
        ),
        in_specs=[smem] + [vmem] * 5 + [hbm],
        out_specs=(vmem, vmem),
        scratch_shapes=[
            pltpu.VMEM((total // PIC, 2 * PIC, PIC), F32),
            pltpu.VMEM((dim, total), BF),
            pltpu.VMEM((total, dim), F32),
            pltpu.VMEM((total, dim), F32),
        ]
        + scatter_scratch(rows, width, partial.dtype),
        cost_estimate=pl.CostEstimate(
            flops=10 * tokens * total * q_part,
            transcendentals=tokens * total * q_part // dim,
            bytes_accessed=plane * rows * width * 28,
        ),
        compiler_params=pltpu.CompilerParams(
            collective_id=ident, has_side_effects=True, vmem_limit_bytes=50 << 20
        ),
        name="attn_back_plane",
    )(starts, qkv, grads, log_total, cos, sin, partial.reshape(plane, rows, width))


def exchange_kernel(in_ref, out_ref, stage, local, sends, recvs):
    tp_at, seq_at, _, _, _ = plane_place()
    seq = lax.axis_size("seq")
    plane = lax.axis_size("tp") * seq
    me = tp_at * seq + seq_at
    peers = [lax.rem(me + k, plane) for k in range(1, plane)]
    devices = [at_device(peer // seq, lax.rem(peer, seq)) for peer in peers]
    enter(devices)
    copies = []
    for k, (peer, device) in enumerate(zip(peers, devices)):
        copy = remote(in_ref.at[peer], out_ref.at[me], sends.at[k], recvs.at[k], device)
        copy.start()
        copies.append(copy)
    take = pltpu.make_async_copy(in_ref.at[me], stage, local.at[0])
    take.start()
    take.wait()
    put = pltpu.make_async_copy(stage, out_ref.at[me], local.at[1])
    put.start()
    for copy in copies:
        copy.wait()
    put.wait()


def exchange_plane(blocks, ident):
    plane, rows, width = blocks.shape
    size = plane * rows * width * 2
    return pl.pallas_call(
        exchange_kernel,
        out_shape=jax.ShapeDtypeStruct(blocks.shape, blocks.dtype),
        in_specs=[pl.BlockSpec(memory_space=pltpu.HBM)],
        out_specs=pl.BlockSpec(memory_space=pltpu.HBM),
        scratch_shapes=[
            pltpu.VMEM((rows, width), blocks.dtype),
            pltpu.SemaphoreType.DMA((2,)),
            pltpu.SemaphoreType.DMA((plane - 1,)),
            pltpu.SemaphoreType.DMA((plane - 1,)),
        ],
        cost_estimate=pl.CostEstimate(flops=0, transcendentals=0, bytes_accessed=size * 20),
        compiler_params=pltpu.CompilerParams(collective_id=ident, has_side_effects=True),
        name="exchange_plane",
    )(blocks)


def slopes(wide, narrow, inner, gug):
    ff_part = inner.shape[1]

    def body(i, carry):
        at = pl.ds(i * SUB, SUB)
        gate, upward, grad = wide[at, :ff_part], wide[at, ff_part:], narrow[at, :]
        sigmoid_gate = jax.nn.sigmoid(gate)
        silu_gate = gate * sigmoid_gate
        inner[at, :] = (silu_gate * upward).astype(BF)
        slope = sigmoid_gate * (1.0 + gate * (1.0 - sigmoid_gate))
        gug[at, :ff_part] = (grad * upward * slope).astype(BF)
        gug[at, ff_part:] = (grad * silu_gate).astype(BF)
        return carry

    lax.fori_loop(0, wide.shape[0] // SUB, body, 0)


def weight_step(n, tokens, grads, gug, inner, stage, weight_ref, sems):
    slot = lax.rem(n, 2)
    block, cols = stage.shape[1:]
    ff_part = cols // 3
    count = gug.shape[0] * gug.shape[1]

    def put(m):
        return pltpu.make_async_copy(
            stage.at[lax.rem(m, 2)], weight_ref.at[pl.ds(m * block, block)], sems[0].at[sems[1] + lax.rem(m, 2)]
        )

    @pl.when(n >= 2)
    def _():
        put(n - 2).wait()

    at = pl.ds(pl.multiple_of(n * block, block), block)
    left = tokens[:, :, :, at].reshape(count, block)
    stage[slot, :, : 2 * ff_part] = tn(left, gug[...].reshape(count, 2 * ff_part)).astype(BF)
    left = grads[:, :, :, at].reshape(count, block)
    stage[slot, :, 2 * ff_part :] = tn(left, inner[...].reshape(count, ff_part)).astype(BF)
    put(n).start()
    return put


def ffn_first_kernel(
    own_ref,
    grad_ref,
    weight_hbm,
    all_ref,
    back_ref,
    out_ref,
    grads_out,
    weight,
    tokens,
    grads,
    wide,
    narrow,
    inner,
    gug,
    stage,
    columns_stage,
    sends,
    recvs,
    local,
):
    tp_at, seq_at, far, mate, _ = plane_place()
    seq = lax.axis_size("seq")
    other = 1 - tp_at
    to_x = at_device(tp_at, far)
    to_y = at_device(other, seq_at)
    to_c = at_device(tp_at, mate)
    rows, width = own_ref.shape
    pair = 2 * rows
    half = rows // 2
    block = width // 4
    ff_part = narrow.shape[2]
    gate_up, lower = slice(0, 2 * ff_part), slice(2 * ff_part, 3 * ff_part)
    enter((to_x, to_y, to_c))

    def piece(t, s, h):
        return all_ref.at[t * seq + s, pl.ds(h * half, half)]

    def own(i, h, device):
        return remote(
            own_ref.at[pl.ds(h * half, half)],
            piece(tp_at, seq_at, h),
            sends.at[i],
            recvs.at[i],
            device,
        )

    def relay(i, t, s, h, device):
        return remote(piece(t, s, h), piece(t, s, h), sends.at[i], recvs.at[i], device)

    x0, x1 = own(0, 0, to_x), own(3, 1, to_x)
    y0, y1 = own(1, 0, to_y), own(4, 1, to_y)
    c0, c1 = own(2, 0, to_c), own(5, 1, to_c)
    diag0 = relay(6, tp_at, far, 0, to_y)
    diag1 = relay(7, other, seq_at, 1, to_x)
    rx0, rx1 = relay(8, tp_at, far, 0, to_c), relay(11, tp_at, far, 1, to_c)
    ry0, ry1 = relay(9, other, seq_at, 0, to_c), relay(10, other, seq_at, 1, to_c)
    rd0, rd1 = relay(12, other, far, 0, to_c), relay(13, other, far, 1, to_c)

    def chip_rows(c):
        t = lax.rem(tp_at + c // 2, 2)
        s = lax.rem(seq_at + (seq // 2) * lax.rem(c, 2), seq)
        return pl.ds(t * seq + s - lax.rem(s, 2), 2)

    def take_tokens(c):
        return pltpu.make_async_copy(all_ref.at[chip_rows(c)], tokens.at[c], local.at[c])

    def take_grads(c):
        return pltpu.make_async_copy(grad_ref.at[chip_rows(c)], grads.at[c], local.at[4 + c])

    def put_back(c):
        return pltpu.make_async_copy(stage.at[0], back_ref.at[chip_rows(c)], local.at[8])

    def put_out(c):
        return pltpu.make_async_copy(stage.at[1], out_ref.at[chip_rows(c)], local.at[9])

    take_weight = pltpu.make_async_copy(weight_hbm, weight, local.at[12])
    mine = pltpu.make_async_copy(own_ref, all_ref.at[tp_at * seq + seq_at], local.at[13])
    for copy in (take_weight, x0, y0, c0, x1, y1, c1, mine):
        copy.start()
    for c in range(4):
        take_grads(c).start()
    take_weight.wait()

    def narrow_step(c, carry):
        take_grads(c).wait()
        narrow[c] = nn(grads[c].reshape(pair, width), weight[:, lower])
        return carry

    lax.fori_loop(0, 4, narrow_step, 0)
    mine.wait()
    c0.wait_recv()
    c1.wait_recv()
    take_tokens(0).start()

    def chip_step(c, carry):
        take_tokens(c).wait()
        wide[...] = nn(tokens[c].reshape(pair, width), weight[:, gate_up])

        @pl.when(c == 0)
        def _():
            x0.wait_recv()
            diag0.start()
            rx0.start()
            y0.wait_recv()
            ry0.start()

        @pl.when(c == 1)
        def _():
            ry0.wait_recv()
            ry1.wait_recv()
            take_tokens(2).start()

        @pl.when(c == 2)
        def _():
            diag0.wait_recv()
            rd0.start()
            diag1.wait_recv()
            rd1.start()

        slopes(wide, narrow.at[c], inner.at[c], gug.at[c])

        @pl.when(c >= 1)
        def _():
            put_back(c - 1).wait()
            put_out(c - 1).wait()

        def back_step(n, carry):
            at = pl.ds(pl.multiple_of(n * block, block), block)
            total = nt(gug[c], weight[at, gate_up]).astype(BF)
            stage[0, :, :, at] = total.reshape(2, rows, block)
            total = nt(inner[c], weight[at, lower]).astype(BF)
            stage[1, :, :, at] = total.reshape(2, rows, block)
            return carry

        lax.fori_loop(0, 4, back_step, 0)
        put_back(c).start()
        put_out(c).start()

        @pl.when(c == 0)
        def _():
            y1.wait_recv()
            diag1.start()
            ry1.start()
            x1.wait_recv()
            rx1.start()
            rx0.wait_recv()
            rx1.wait_recv()
            take_tokens(1).start()

        @pl.when(c == 2)
        def _():
            rd0.wait_recv()
            rd1.wait_recv()
            take_tokens(3).start()

        return carry

    lax.fori_loop(0, 4, chip_step, 0)

    def grads_step(n, carry):
        weight_step(n, tokens, grads, gug, inner, columns_stage, grads_out, (local, 10))
        return carry

    lax.fori_loop(0, 4, grads_step, 0)
    for copy in (x0, y0, c0, x1, y1, c1, diag0, diag1, rx0, ry0, ry1, rx1, rd0, rd1):
        copy.wait_send()
    put_back(3).wait()
    put_out(3).wait()
    for n in (2, 3):
        pltpu.make_async_copy(
            columns_stage.at[n - 2], grads_out.at[pl.ds(n * block, block)], local.at[8 + n]
        ).wait()


def ffn_second_kernel(
    all_ref,
    grad_ref,
    weight_hbm,
    back_ref,
    first_ref,
    out_ref,
    grads_out,
    sum_ref,
    weight,
    tokens,
    grads,
    wide,
    narrow,
    inner,
    gug,
    part,
    chip_in,
    far_in,
    near_in,
    stage,
    columns_stage,
    sends,
    recvs,
    local,
):
    tp_at, seq_at, far, mate, _ = plane_place()
    seq = lax.axis_size("seq")
    kind = lax.rem(seq_at, 2)
    to_x = at_device(tp_at, far)
    to_y = at_device(1 - tp_at, seq_at)
    to_c = at_device(tp_at, mate)
    rows, width = sum_ref.shape
    pair = 2 * rows
    half = rows // 2
    block = width // 4
    ff_part = narrow.shape[1]
    gate_up, lower = slice(0, 2 * ff_part), slice(2 * ff_part, 3 * ff_part)
    top, low = pl.ds(0, half), pl.ds(half, half)
    enter((to_x, to_y, to_c))

    def chip_rows(k):
        t = lax.rem(tp_at + 1 - lax.rem(k, 2), 2)
        s = lax.rem(seq_at + (seq // 2) * (1 - k // 2), seq)
        return pl.ds(t * seq + s - lax.rem(s, 2), 2)

    def take(ref, target, sem):
        return lambda k: pltpu.make_async_copy(ref.at[chip_rows(k)], target.at[k], local.at[sem + k])

    take_tokens, take_grads, take_back = (
        take(all_ref, tokens, 0),
        take(grad_ref, grads, 4),
        take(back_ref, part, 8),
    )

    def take_first(k):
        slot = lax.rem(k, 2)
        return pltpu.make_async_copy(first_ref.at[chip_rows(k)], stage.at[slot], local.at[12 + slot])

    def put_out(k):
        slot = lax.rem(k, 2)
        return pltpu.make_async_copy(stage.at[slot], out_ref.at[chip_rows(k)], local.at[14 + slot])

    def give(k):
        return remote(part.at[k, 1 - kind], chip_in.at[k], sends.at[k], recvs.at[k], to_c)

    def held(k):
        return part.at[k, kind]

    def hop(i, src, dst, device):
        return remote(src, dst, sends.at[i], recvs.at[i], device)

    d0 = hop(4, part.at[0, kind, top], far_in.at[0, top], to_x)
    d1 = hop(5, part.at[0, kind, low], far_in.at[1, low], to_y)
    x0 = hop(6, part.at[1, kind, top], near_in.at[0, top], to_x)
    y1 = hop(7, part.at[2, kind, low], near_in.at[1, low], to_y)
    y0 = hop(8, part.at[2, kind, top], near_in.at[1, top], to_y)
    x1 = hop(9, part.at[1, kind, low], near_in.at[0, low], to_x)

    def chip_sum(k):
        give(k).wait_recv()
        add_rows(held(k), (held(k), chip_in.at[k]), 0, rows, part.dtype)

    take_weight = pltpu.make_async_copy(weight_hbm, weight, local.at[18])
    take_weight.start()
    for k in range(4):
        take_grads(k).start()
        take_tokens(k).start()
        take_back(k).start()
    take_first(0).start()
    take_weight.wait()

    def chip_step(k, carry):
        slot = lax.rem(k, 2)
        take_grads(k).wait()
        narrow[...] = nn(grads[k].reshape(pair, width), weight[:, lower])

        @pl.when(k == 1)
        def _():
            chip_sum(0)
            d0.start()
            d1.start()

        @pl.when(k == 2)
        def _():
            chip_sum(1)
            x0.start()

        @pl.when(k == 3)
        def _():
            chip_sum(2)
            y1.start()
            d0.wait_recv()
            add_rows(held(2), (held(2), far_in.at[0]), 0, half, part.dtype)
            y0.start()
            d1.wait_recv()
            add_rows(held(1), (held(1), far_in.at[1]), half, half, part.dtype)
            x1.start()

        take_tokens(k).wait()
        wide[...] = nn(tokens[k].reshape(pair, width), weight[:, gate_up])
        slopes(wide, narrow, inner.at[k], gug.at[k])
        take_back(k).wait()

        def back_step(n, carry):
            at = pl.ds(pl.multiple_of(n * block, block), block)
            total = nt(gug[k], weight[at, gate_up]).reshape(2, rows, block)
            part[k, :, :, at] = (part[k, :, :, at].astype(F32) + total).astype(part.dtype)
            return carry

        lax.fori_loop(0, 4, back_step, 0)
        give(k).start()
        take_first(k).wait()

        @pl.when(k >= 1)
        def _():
            put_out(k - 1).wait()

        @pl.when(k < 3)
        def _():
            take_first(k + 1).start()

        def out_step(n, carry):
            at = pl.ds(pl.multiple_of(n * block, block), block)
            total = nt(inner[k], weight[at, lower]).reshape(2, rows, block)
            stage[slot, :, :, at] = (stage[slot, :, :, at].astype(F32) + total).astype(stage.dtype)
            return carry

        lax.fori_loop(0, 4, out_step, 0)
        put_out(k).start()
        return carry

    lax.fori_loop(0, 4, chip_step, 0)

    def grads_step(n, carry):
        weight_step(n, tokens, grads, gug, inner, columns_stage, grads_out, (local, 16))

        @pl.when(n == 0)
        def _():
            chip_sum(3)

        return carry

    lax.fori_loop(0, 4, grads_step, 0)
    x0.wait_recv()
    y0.wait_recv()
    add_rows(sum_ref, (held(3), near_in.at[0], near_in.at[1]), 0, half, sum_ref.dtype)
    y1.wait_recv()
    x1.wait_recv()
    add_rows(sum_ref, (held(3), near_in.at[0], near_in.at[1]), half, half, sum_ref.dtype)
    for k in range(4):
        give(k).wait_send()
    for copy in (d0, d1, x0, y1, y0, x1):
        copy.wait_send()
    put_out(3).wait()
    for n in (2, 3):
        pltpu.make_async_copy(
            columns_stage.at[n - 2], grads_out.at[pl.ds(n * block, block)], local.at[14 + n]
        ).wait()


def ffn_first_plane(block, grads, weight, ident):
    rows, width = block.shape
    plane = lax.axis_size("tp") * lax.axis_size("seq")
    cols = weight.shape[1]
    ff_part = cols // 3
    shape = jax.ShapeDtypeStruct
    hbm = pl.BlockSpec(memory_space=pltpu.HBM)
    vmem = pl.BlockSpec(memory_space=pltpu.VMEM)
    tokens = plane * rows
    return pl.pallas_call(
        ffn_first_kernel,
        out_shape=(
            shape((plane, rows, width), BF),
            shape((plane, rows, width), BF),
            shape((plane, rows, width), BF),
            shape((width, cols), BF),
        ),
        in_specs=[vmem, hbm, hbm],
        out_specs=(hbm, hbm, hbm, hbm),
        scratch_shapes=[
            pltpu.VMEM(weight.shape, BF),
            pltpu.VMEM((4, 2, rows, width), BF),
            pltpu.VMEM((4, 2, rows, width), BF),
            pltpu.VMEM((2 * rows, 2 * ff_part), F32),
            pltpu.VMEM((4, 2 * rows, ff_part), F32),
            pltpu.VMEM((4, 2 * rows, ff_part), BF),
            pltpu.VMEM((4, 2 * rows, 2 * ff_part), BF),
            pltpu.VMEM((2, 2, rows, width), BF),
            pltpu.VMEM((2, width // 4, cols), BF),
            pltpu.SemaphoreType.DMA((14,)),
            pltpu.SemaphoreType.DMA((14,)),
            pltpu.SemaphoreType.DMA((14,)),
        ],
        cost_estimate=pl.CostEstimate(
            flops=18 * tokens * width * ff_part,
            transcendentals=tokens * ff_part,
            bytes_accessed=22 * tokens * width,
        ),
        compiler_params=pltpu.CompilerParams(
            collective_id=ident, has_side_effects=True, vmem_limit_bytes=60 << 20
        ),
        name="ffn_first_plane",
    )(block, grads, weight)


def ffn_second_plane(block, grads, weight, back, first, ident):
    plane, rows, width = block.shape
    cols = weight.shape[1]
    ff_part = cols // 3
    shape = jax.ShapeDtypeStruct
    hbm = pl.BlockSpec(memory_space=pltpu.HBM)
    vmem = pl.BlockSpec(memory_space=pltpu.VMEM)
    tokens = plane * rows
    return pl.pallas_call(
        ffn_second_kernel,
        out_shape=(
            shape((plane, rows, width), BF),
            shape((width, cols), BF),
            shape((rows, width), F32),
        ),
        in_specs=[hbm] * 5,
        out_specs=(hbm, hbm, vmem),
        scratch_shapes=[
            pltpu.VMEM(weight.shape, BF),
            pltpu.VMEM((4, 2, rows, width), BF),
            pltpu.VMEM((4, 2, rows, width), BF),
            pltpu.VMEM((2 * rows, 2 * ff_part), F32),
            pltpu.VMEM((2 * rows, ff_part), F32),
            pltpu.VMEM((4, 2 * rows, ff_part), BF),
            pltpu.VMEM((4, 2 * rows, 2 * ff_part), BF),
            pltpu.VMEM((4, 2, rows, width), BF),
            pltpu.VMEM((4, rows, width), BF),
            pltpu.VMEM((2, rows, width), BF),
            pltpu.VMEM((2, rows, width), BF),
            pltpu.VMEM((2, 2, rows, width), BF),
            pltpu.VMEM((2, width // 4, cols), BF),
            pltpu.SemaphoreType.DMA((10,)),
            pltpu.SemaphoreType.DMA((10,)),
            pltpu.SemaphoreType.DMA((19,)),
        ],
        cost_estimate=pl.CostEstimate(
            flops=18 * tokens * width * ff_part,
            transcendentals=tokens * ff_part,
            bytes_accessed=22 * tokens * width,
        ),
        compiler_params=pltpu.CompilerParams(
            collective_id=ident, has_side_effects=True, vmem_limit_bytes=63 << 20
        ),
        name="ffn_second_plane",
    )(block, grads, weight, back, first)


def finish_kernel(
    first_ref,
    second_ref,
    attn_ref,
    gate_weight,
    up_weight,
    query_weight,
    key_weight,
    value_weight,
    gain2_ref,
    gain1_ref,
    gate_out,
    up_out,
    down_first,
    down_second,
    gain2_out,
    query_out,
    key_out,
    value_out,
    out_out,
    gain1_out,
    first_in,
    second_in,
    attn_in,
    local,
    sends,
    recvs,
):
    tp_at, seq_at, _, _, _ = plane_place()
    seq = lax.axis_size("seq")
    plane = lax.axis_size("tp") * seq
    me = tp_at * seq + seq_at
    peers = [lax.rem(me + k, plane) for k in range(1, plane)]
    devices = [at_device(peer // seq, lax.rem(peer, seq)) for peer in peers]
    enter(devices)
    groups = []
    for n, (ref, into) in enumerate(
        ((first_ref, first_in), (second_ref, second_in), (attn_ref, attn_in))
    ):
        copies = [pltpu.make_async_copy(ref.at[me], into.at[me], local.at[n])]
        for k, (peer, device) in enumerate(zip(peers, devices)):
            i = n * (plane - 1) + k
            copies.append(remote(ref.at[peer], into.at[me], sends.at[i], recvs.at[i], device))
        for copy in copies:
            copy.start()
        groups.append(copies)

    def arrive(n):
        for copy in groups[n]:
            copy.wait()

    gain = gain2_ref[...]
    sizes = [ref.shape[2] // 3 for ref in (first_in, second_in)]
    total = jnp.zeros(gain.shape, F32)
    for n, (ref, down) in enumerate(((first_in, down_first), (second_in, down_second))):
        arrive(n)
        size = sizes[n]
        for j in range(plane):
            start = j * sum(sizes) + n * sizes[0]
            at = slice(start, start + size)
            for k, (out, weight) in enumerate(((gate_out, gate_weight), (up_out, up_weight))):
                own = ref[j, :, k * size : (k + 1) * size].astype(F32)
                out[:, at] = own * gain
                total = total + jnp.sum(own * weight[:, at].astype(F32), axis=1, keepdims=True)
            down[j] = ref[j, :, 2 * size :]
    gain2_out[...] = total

    arrive(2)
    gain = gain1_ref[...]
    q_part = query_out.shape[1] // plane
    share = plane // KV
    total = jnp.zeros(gain.shape, F32)
    for j in range(plane):
        at = slice(j * q_part, (j + 1) * q_part)
        own = attn_in[j, :, :q_part].astype(F32)
        query_out[:, at] = own * gain
        total = total + jnp.sum(own * query_weight[:, at].astype(F32), axis=1, keepdims=True)
        out_out[:, at] = attn_in[j, :, q_part + 2 * DH :].astype(F32)
    for j in range(KV):
        at = slice(j * DH, (j + 1) * DH)
        for k, (out, weight) in enumerate(((key_out, key_weight), (value_out, value_weight))):
            cols = slice(q_part + k * DH, q_part + (k + 1) * DH)
            own = attn_in[j * share, :, cols].astype(F32)
            for i in range(1, share):
                own = own + attn_in[j * share + i, :, cols].astype(F32)
            out[:, at] = own * gain
            total = total + jnp.sum(own * weight[:, at].astype(F32), axis=1, keepdims=True)
    gain1_out[...] = total


def finish_plane(first, second, attn, weights, gain2, gain1, ident):
    plane, rows, _ = first.shape
    shape = jax.ShapeDtypeStruct
    hbm = pl.BlockSpec(memory_space=pltpu.HBM)
    vmem = pl.BlockSpec(memory_space=pltpu.VMEM)
    gate, up, query, key, value = (shape(w.shape, F32) for w in weights)
    column = shape((rows, 1), F32)
    size = (first.size + second.size + attn.size) * 2
    return pl.pallas_call(
        finish_kernel,
        out_shape=(
            gate,
            up,
            shape((plane, rows, first.shape[2] // 3), BF),
            shape((plane, rows, second.shape[2] // 3), BF),
            column,
            query,
            key,
            value,
            query,
            column,
        ),
        in_specs=[hbm] * 3 + [vmem] * 7,
        out_specs=(vmem,) * 10,
        scratch_shapes=[
            pltpu.VMEM(first.shape, BF),
            pltpu.VMEM(second.shape, BF),
            pltpu.VMEM(attn.shape, BF),
            pltpu.SemaphoreType.DMA((3,)),
            pltpu.SemaphoreType.DMA((3 * plane - 3,)),
            pltpu.SemaphoreType.DMA((3 * plane - 3,)),
        ],
        cost_estimate=pl.CostEstimate(flops=0, transcendentals=0, bytes_accessed=size * 20),
        compiler_params=pltpu.CompilerParams(
            collective_id=ident, has_side_effects=True, vmem_limit_bytes=32 << 20
        ),
        name="finish_plane",
    )(first, second, attn, *weights, gain2, gain1)


def columns(matrix, parts):
    rows, cols = matrix.shape
    return jnp.transpose(matrix.reshape(rows, parts, cols // parts), (1, 0, 2))


def uncolumns(blocks):
    parts, rows, cols = blocks.shape
    return jnp.transpose(blocks, (1, 0, 2)).reshape(rows, parts * cols)


def after(value, *earlier):
    return lax.optimization_barrier((value,) + earlier)[0]


def per_device(
    layer_input,
    pic_starts,
    skip_mask,
    gain_attn,
    w_query,
    w_key,
    w_value,
    w_out,
    gain_ffn,
    w_gate,
    w_up,
    w_down,
    cotangent,
):
    _, local_len, width = layer_input.shape
    seq = lax.axis_size("seq")
    plane = lax.axis_size("tp") * seq
    total_len = local_len * seq
    heads = H // plane
    share = plane // KV
    ff_part = w_gate.shape[1] // plane
    q_part = heads * DH

    gain1 = gain_attn[:, None]
    gain2 = gain_ffn[:, None]
    wq32, wk32, wv32 = w_query.astype(F32), w_key.astype(F32), w_value.astype(F32)
    wg32, wu32 = w_gate.astype(F32), w_up.astype(F32)
    attn_pack = jnp.concatenate(
        [
            columns((wq32 * gain1).astype(BF), plane),
            jnp.repeat(columns((wk32 * gain1).astype(BF), KV), share, axis=0),
            jnp.repeat(columns((wv32 * gain1).astype(BF), KV), share, axis=0),
            columns(w_out.T, plane),
        ],
        axis=2,
    )
    attn_rows = exchange_plane(attn_pack, 0)
    attn_rows = attn_rows.reshape(-1, attn_rows.shape[2])
    attn_weight = lax.all_gather(attn_rows, "rep", axis=0, tiled=True)
    qkv_weight = attn_weight[:, : q_part + 2 * DH]
    out_weight = attn_weight[:, q_part + 2 * DH :]

    tokens = layer_input.reshape(local_len, width).astype(F32)
    keep = (1 - skip_mask).astype(F32).reshape(local_len, 1)
    upstream = cotangent.reshape(local_len, width).astype(F32)
    scale1 = rms_scale(tokens)
    norm1 = tokens * scale1

    first_part = (ff_part // 2 + DH - 1) // DH * DH
    split = ((0, first_part), (first_part, ff_part))
    ffn_parts = (
        columns((wg32 * gain2).astype(BF), plane),
        columns((wu32 * gain2).astype(BF), plane),
        columns(w_down.T, plane),
    )
    first_pack, second_pack = (
        jnp.concatenate([m[:, :, a:b] for m in ffn_parts], axis=2) for a, b in split
    )
    first_rows = exchange_plane(after(first_pack, attn_rows), 2)
    norm1_all, second_rows = spread_plane(after(norm1.astype(BF), first_rows), second_pack, 1)
    first_rows = first_rows.reshape(-1, first_rows.shape[2])
    second_rows = second_rows.reshape(-1, second_rows.shape[2])
    first_weight = lax.all_gather(first_rows, "rep", axis=0, tiled=True)
    second_weight = lax.all_gather(second_rows, "rep", axis=0, tiled=True)
    norm1_all = norm1_all.reshape(-1, width)

    other_starts = lax.ppermute(pic_starts, "tp", [(0, 1), (1, 0)])
    starts = jnp.where(
        lax.axis_index("tp") == 0,
        jnp.concatenate([pic_starts, other_starts], axis=0),
        jnp.concatenate([other_starts, pic_starts], axis=0),
    )
    positions = jnp.arange(total_len, dtype=jnp.int32)
    cos_table, sin_table = rotary_tables(positions, DH)
    cos = jnp.concatenate([cos_table, cos_table], axis=1)
    sin = jnp.concatenate([-sin_table, sin_table], axis=1)
    qkv, mixed, log_total, branch_partial, ffn_grad = attn_front_plane(
        starts, norm1_all, attn_weight, cos, sin, (keep * upstream).astype(BF), 3
    )
    branch = scatter_plane(branch_partial, 4)
    hidden = tokens + keep * branch

    scale2 = rms_scale(hidden)
    norm2 = hidden * scale2
    norm2_all, back_first, out_first, first_partial = ffn_first_plane(
        norm2.astype(BF), ffn_grad, first_weight, 5
    )
    first_sums = lax.psum_scatter(first_partial, "rep", scatter_dimension=0, tiled=True)
    out_partial, second_partial, scaled2 = ffn_second_plane(
        norm2_all, ffn_grad, second_weight, back_first, out_first, 6
    )
    second_sums = lax.psum_scatter(second_partial, "rep", scatter_dimension=0, tiled=True)
    hidden_grad = upstream + scale2 * (
        scaled2 - norm2 * jnp.mean(scaled2 * norm2, axis=-1, keepdims=True)
    )

    branch_grad = gather_plane((keep * hidden_grad).astype(BF), 7)
    mixed_grad = nn(branch_grad, out_weight).astype(BF)
    qkv_grad, ffn_out = attn_back_plane(
        starts,
        qkv,
        after(mixed_grad, first_sums),
        log_total,
        cos,
        sin,
        out_partial.reshape(-1, width),
        9,
    )
    attn_partial = jnp.concatenate(
        [tn(norm1_all, qkv_grad).astype(BF), tn(branch_grad, mixed).astype(BF)], axis=1
    )
    scaled1_partial = nt(qkv_grad, qkv_weight).astype(BF)
    attn_sums = lax.psum_scatter(attn_partial, "rep", scatter_dimension=0, tiled=True)
    scaled1 = scatter_plane(after(scaled1_partial, attn_partial, second_sums), 8)
    input_grad = hidden_grad + scale1 * (
        scaled1 - norm1 * jnp.mean(scaled1 * norm1, axis=-1, keepdims=True)
    )
    out_hidden = (hidden + keep * ffn_out).astype(BF)

    gate_grad, up_grad, down_first, down_second, gain2_grad, *attn_grads = finish_plane(
        after(first_sums, input_grad, out_hidden).reshape(plane, -1, first_sums.shape[1]),
        second_sums.reshape(plane, -1, second_sums.shape[1]),
        attn_sums.reshape(plane, -1, attn_sums.shape[1]),
        (w_gate, w_up, w_query, w_key, w_value),
        gain2,
        gain1,
        10,
    )
    query_grad, key_grad, value_grad, out_grad, gain1_grad = attn_grads
    down_own = jnp.concatenate([down_first, down_second], axis=2)
    down_grad = jnp.transpose(down_own, (0, 2, 1)).reshape(plane * ff_part, -1).astype(F32)
    return (
        out_hidden[None],
        input_grad[None],
        gain1_grad[:, 0],
        query_grad,
        key_grad,
        value_grad,
        out_grad.T,
        gain2_grad[:, 0],
        gate_grad,
        up_grad,
        down_grad,
    )


def solution(mesh):
    devices = mesh.devices
    dp, seq = devices.shape
    inner = Mesh(devices.reshape(dp // TP, TP, seq), ("rep", "tp", "seq"))
    dps = ("rep", "tp")
    every = ("rep", "tp", "seq")
    token = P(dps, "seq", None)
    row = P(every, None)
    col = P(None, every)
    return jax.shard_map(
        per_device,
        mesh=inner,
        in_specs=(
            token,
            P(dps, None),
            P(dps, "seq"),
            P(every),
            row,
            row,
            row,
            col,
            P(every),
            row,
            row,
            col,
            token,
        ),
        out_specs=(token, token, P(every), row, row, row, col, P(every), row, row, col),
        check_vma=False,
    )
```

```python
import jax
import jax.numpy as jnp
from jax import lax
from jax.experimental import pallas as pl
from jax.experimental.pallas import tpu as pltpu
from jax.sharding import Mesh
from jax.sharding import PartitionSpec as P

H = 16
KV = 4
DH = 128
PIC = 256
NPIC = 2
EPS = 1e-05
TP = 2
BF = jnp.bfloat16
F32 = jnp.float32


def rotary_tables(positions, head_dim):
    half_dim = head_dim // 2
    inverse = 10000.0 ** (-(jnp.arange(half_dim, dtype=F32) * 2.0 / head_dim))
    angles = positions.astype(F32)[:, None] * inverse[None, :]
    return (jnp.cos(angles), jnp.sin(angles))


def rms_scale(rows):
    return lax.rsqrt(jnp.mean(rows * rows, axis=-1, keepdims=True) + EPS)


def dot(left, right, contract):
    return lax.dot_general(
        left, right, ((contract[:1], contract[1:]), ((), ())), preferred_element_type=F32
    )


def nn(left, right):
    return dot(left, right, (1, 0))


def nt(left, right):
    return dot(left, right, (1, 1))


def tn(left, right):
    return dot(left, right, (0, 0))


MESH_ID = pl.DeviceIdType.MESH
SUB = 32


def plane_place():
    tp_at = lax.axis_index("tp")
    seq_at = lax.axis_index("seq")
    seq = lax.axis_size("seq")
    half = seq // 2
    far = lax.rem(seq_at + half, seq)
    mate = seq_at + 1 - 2 * lax.rem(seq_at, 2)
    far_mate = far + 1 - 2 * lax.rem(far, 2)
    return tp_at, seq_at, far, mate, far_mate


def at_device(tp_at, seq_at):
    return (lax.axis_index("rep"), tp_at, seq_at)


def enter(devices):
    barrier = pltpu.get_barrier_semaphore()
    for device in devices:
        pl.semaphore_signal(barrier, inc=1, device_id=device, device_id_type=MESH_ID)
    pl.semaphore_wait(barrier, len(devices))


def remote(src, dst, send, recv, device):
    return pltpu.make_async_remote_copy(
        src_ref=src,
        dst_ref=dst,
        send_sem=send,
        recv_sem=recv,
        device_id=device,
        device_id_type=MESH_ID,
    )


def gather_stages(own_ref, all_ref, sends, recvs, local):
    tp_at, seq_at, far, mate, _ = plane_place()
    seq = lax.axis_size("seq")
    other = 1 - tp_at
    to_x = at_device(tp_at, far)
    to_y = at_device(other, seq_at)
    to_c = at_device(tp_at, mate)
    rows = own_ref.shape[0]
    part = rows // 2

    def piece(t, s, h):
        return all_ref.at[t * seq + s, pl.ds(h * part, part)]

    def relay(i, t, s, h, device):
        return remote(piece(t, s, h), piece(t, s, h), sends.at[i], recvs.at[i], device)

    def own(i, h, device):
        return remote(
            own_ref.at[pl.ds(h * part, part)],
            piece(tp_at, seq_at, h),
            sends.at[i],
            recvs.at[i],
            device,
        )

    x0, x1 = own(0, 0, to_x), own(3, 1, to_x)
    y0, y1 = own(1, 0, to_y), own(4, 1, to_y)
    c0, c1 = own(2, 0, to_c), own(5, 1, to_c)
    diag0 = relay(6, tp_at, far, 0, to_y)
    diag1 = relay(7, other, seq_at, 1, to_x)
    rx0, rx1 = relay(8, tp_at, far, 0, to_c), relay(11, tp_at, far, 1, to_c)
    ry0, ry1 = relay(9, other, seq_at, 0, to_c), relay(10, other, seq_at, 1, to_c)
    rd0, rd1 = relay(12, other, far, 0, to_c), relay(13, other, far, 1, to_c)
    mine = pltpu.make_async_copy(own_ref, all_ref.at[tp_at * seq + seq_at], local)

    def begin(peers=(to_x, to_y, to_c)):
        enter(peers)
        for copy in (x0, y0, c0, x1, y1, c1, mine):
            copy.start()

    def first():
        x0.wait_recv()
        diag0.start()
        rx0.start()
        y0.wait_recv()
        ry0.start()

    def second():
        y1.wait_recv()
        diag1.start()
        ry1.start()
        x1.wait_recv()
        rx1.start()

    def far_start():
        diag0.wait_recv()
        rd0.start()
        diag1.wait_recv()
        rd1.start()

    def near_arrive():
        mine.wait()
        for copy in (c0, c1, rx0, ry0, ry1, rx1):
            copy.wait_recv()

    def far_arrive():
        rd0.wait_recv()
        rd1.wait_recv()
        for copy in (x0, y0, c0, x1, y1, c1, diag0, diag1, rx0, ry0, ry1, rx1, rd0, rd1):
            copy.wait_send()

    return begin, first, second, near_arrive, far_start, far_arrive


GATHER_SCRATCH = (
    pltpu.SemaphoreType.DMA((14,)),
    pltpu.SemaphoreType.DMA((14,)),
    pltpu.SemaphoreType.DMA,
)


def gather_mix_kernel(
    own_ref, mixed_ref, weight_ref, all_ref, grad_ref, columns_ref, tokens, total, local, *gather
):
    begin, first, second, near_arrive, far_start, far_arrive = gather_stages(
        own_ref, all_ref, *gather
    )
    tp_at, seq_at, _, _, _ = plane_place()
    seq = lax.axis_size("seq")
    rows, width = own_ref.shape
    pair = 2 * rows
    block = width // 4
    begin()

    def chip_rows(c):
        t = lax.rem(tp_at + c // 2, 2)
        s = lax.rem(seq_at + (seq // 2) * lax.rem(c, 2), seq)
        return t * seq + s - lax.rem(s, 2)

    def take(c):
        return pltpu.make_async_copy(
            all_ref.at[pl.ds(chip_rows(c), 2)], tokens.at[c], local.at[c]
        )

    total[...] = jnp.zeros(total.shape, F32)

    def chip_step(c, carry):
        take(c).wait()
        at = pl.ds(pl.multiple_of(chip_rows(c) * rows, pair), pair)
        chip = nn(tokens[c].reshape(pair, width), weight_ref[...])
        grad_ref[at, :] = chip.astype(BF)

        def grads_step(n, carry):
            some = pl.ds(pl.multiple_of(n * block, block), block)
            total[some, :] += tn(tokens[c, :, :, some].reshape(pair, block), mixed_ref[at, :])
            return carry

        lax.fori_loop(0, 4, grads_step, 0)
        return carry

    first()
    second()
    near_arrive()
    for c in range(3):
        take(c).start()
    lax.fori_loop(0, 3, chip_step, 0)
    far_start()
    far_arrive()
    take(3).start()
    chip_step(3, 0)
    columns_ref[...] = total[...].astype(BF)


def gather_mix_plane(block, mixed, weight, ident):
    rows, width = block.shape
    plane = lax.axis_size("tp") * lax.axis_size("seq")
    tokens, q_part = mixed.shape
    shape = jax.ShapeDtypeStruct
    hbm = pl.BlockSpec(memory_space=pltpu.HBM)
    vmem = pl.BlockSpec(memory_space=pltpu.VMEM)
    return pl.pallas_call(
        gather_mix_kernel,
        out_shape=(
            shape((plane, rows, width), BF),
            shape((tokens, q_part), BF),
            shape((width, q_part), BF),
        ),
        in_specs=[vmem] * 3,
        out_specs=(hbm, vmem, vmem),
        scratch_shapes=[
            pltpu.VMEM((4, 2, rows, width), BF),
            pltpu.VMEM((width, q_part), F32),
            pltpu.SemaphoreType.DMA((4,)),
            *GATHER_SCRATCH,
        ],
        cost_estimate=pl.CostEstimate(
            flops=4 * tokens * width * q_part,
            transcendentals=0,
            bytes_accessed=plane * rows * width * 24,
        ),
        compiler_params=pltpu.CompilerParams(
            collective_id=ident, has_side_effects=True, vmem_limit_bytes=40 << 20
        ),
        name="gather_mix_plane",
    )(block, mixed, weight)


def spread_kernel(
    own_ref, move_ref, all_ref, move_out, kept, copies, *gather
):
    begin, first, second, *last = gather_stages(own_ref, all_ref, *gather)
    tp_at, seq_at, _, _, _ = plane_place()
    seq = lax.axis_size("seq")
    plane = lax.axis_size("tp") * seq
    me = tp_at * seq + seq_at
    peers = [lax.rem(me + k, plane) for k in range(1, plane)]
    devices = [at_device(peer // seq, lax.rem(peer, seq)) for peer in peers]
    sends, recvs, local = copies.at[0], copies.at[1], copies.at[2]
    begin(devices)
    moves = [
        remote(move_ref.at[peer], move_out.at[me], sends.at[k], recvs.at[k], device)
        for k, (peer, device) in enumerate(zip(peers, devices))
    ]
    for move in moves:
        move.start()
    take = pltpu.make_async_copy(move_ref.at[me], kept, local.at[0])
    put = pltpu.make_async_copy(kept, move_out.at[me], local.at[1])
    take.start()
    take.wait()
    put.start()
    first()
    second()
    for move in moves:
        move.wait()
    put.wait()
    for stage in last:
        stage()


def spread_plane(block, blocks, ident):
    rows, width = block.shape
    plane = lax.axis_size("tp") * lax.axis_size("seq")
    hbm = pl.BlockSpec(memory_space=pltpu.HBM)
    vmem = pl.BlockSpec(memory_space=pltpu.VMEM)
    size = plane * rows * width * 2
    return pl.pallas_call(
        spread_kernel,
        out_shape=(
            jax.ShapeDtypeStruct((plane, rows, width), block.dtype),
            jax.ShapeDtypeStruct(blocks.shape, blocks.dtype),
        ),
        in_specs=[vmem, hbm],
        out_specs=(hbm, hbm),
        scratch_shapes=[
            pltpu.VMEM(blocks.shape[1:], blocks.dtype),
            pltpu.SemaphoreType.DMA((3, plane)),
            *GATHER_SCRATCH,
        ],
        cost_estimate=pl.CostEstimate(flops=0, transcendentals=0, bytes_accessed=size * 16),
        compiler_params=pltpu.CompilerParams(collective_id=ident, has_side_effects=True),
        name="spread_plane",
    )(block, blocks)


def add_rows(target, sources, start, count, kind):
    step = min(SUB, count)

    def body(i, carry):
        at = pl.ds(start + i * step, step)
        total = sources[0][at, :].astype(F32)
        for source in sources[1:]:
            total = total + source[at, :].astype(F32)
        target[at, :] = total.astype(kind)
        return carry

    lax.fori_loop(0, count // step, body, 0)


def scatter_stages(part_ref, sum_ref, held, chip_in, far_in, near_in, loads, sends, recvs):
    tp_at, seq_at, far, mate, far_mate = plane_place()
    seq = lax.axis_size("seq")
    other = 1 - tp_at
    to_x = at_device(tp_at, far)
    to_y = at_device(other, seq_at)
    to_c = at_device(tp_at, mate)
    rows = sum_ref.shape[0]
    part = rows // 2
    top, low = pl.ds(0, part), pl.ds(part, part)
    chips = ((other, far, far_mate), (tp_at, far, far_mate), (other, seq_at, mate), (tp_at, seq_at, mate))
    gives = [
        remote(part_ref.at[t * seq + m], chip_in.at[k], sends.at[k], recvs.at[k], to_c)
        for k, (t, s, m) in enumerate(chips)
    ]
    takes = [
        pltpu.make_async_copy(part_ref.at[t * seq + s], held.at[k], loads.at[k])
        for k, (t, s, m) in enumerate(chips)
    ]

    def hop(i, src, dst, device):
        return remote(src, dst, sends.at[i], recvs.at[i], device)

    d0 = hop(4, held.at[0, top], far_in.at[0, top], to_x)
    d1 = hop(5, held.at[0, low], far_in.at[1, low], to_y)
    x0 = hop(6, held.at[1, top], near_in.at[0, top], to_x)
    y1 = hop(7, held.at[2, low], near_in.at[1, low], to_y)
    y0 = hop(8, held.at[2, top], near_in.at[1, top], to_y)
    x1 = hop(9, held.at[1, low], near_in.at[0, low], to_x)

    def begin():
        enter((to_x, to_y, to_c))
        for give, take in zip(gives, takes):
            give.start()
            take.start()

    def chip_sum(k):
        takes[k].wait()
        gives[k].wait_recv()
        add_rows(held.at[k], (held.at[k], chip_in.at[k]), 0, rows, held.dtype)

    def diagonal():
        chip_sum(0)
        d0.start()
        d1.start()

    def along_x():
        chip_sum(1)
        x0.start()

    def along_y():
        chip_sum(2)
        y1.start()

    def own():
        chip_sum(3)

    def fold():
        d0.wait_recv()
        add_rows(held.at[2], (held.at[2], far_in.at[0]), 0, part, held.dtype)
        y0.start()
        d1.wait_recv()
        add_rows(held.at[1], (held.at[1], far_in.at[1]), part, part, held.dtype)
        x1.start()

    def finish():
        x0.wait_recv()
        y0.wait_recv()
        add_rows(sum_ref, (held.at[3], near_in.at[0], near_in.at[1]), 0, part, sum_ref.dtype)
        y1.wait_recv()
        x1.wait_recv()
        add_rows(sum_ref, (held.at[3], near_in.at[0], near_in.at[1]), part, part, sum_ref.dtype)
        for copy in gives + [d0, d1, x0, y1, y0, x1]:
            copy.wait_send()

    return begin, diagonal, along_x, along_y, own, fold, finish


def scatter_kernel(*refs):
    for stage in scatter_stages(*refs):
        stage()


def scatter_scratch(rows, width, kind):
    return [
        pltpu.VMEM((4, rows, width), kind),
        pltpu.VMEM((4, rows, width), kind),
        pltpu.VMEM((2, rows, width), kind),
        pltpu.VMEM((2, rows, width), kind),
        pltpu.SemaphoreType.DMA((4,)),
        pltpu.SemaphoreType.DMA((10,)),
        pltpu.SemaphoreType.DMA((10,)),
    ]


def scatter_plane(partial, ident):
    plane = lax.axis_size("tp") * lax.axis_size("seq")
    rows, width = partial.shape[0] // plane, partial.shape[1]
    kind = partial.dtype
    size = rows * width * 2
    return pl.pallas_call(
        scatter_kernel,
        out_shape=jax.ShapeDtypeStruct((rows, width), F32),
        in_specs=[pl.BlockSpec(memory_space=pltpu.HBM)],
        out_specs=pl.BlockSpec(memory_space=pltpu.VMEM),
        scratch_shapes=scatter_scratch(rows, width, kind),
        cost_estimate=pl.CostEstimate(
            flops=0, transcendentals=0, bytes_accessed=plane * size * 14
        ),
        compiler_params=pltpu.CompilerParams(
            collective_id=ident, has_side_effects=True, vmem_limit_bytes=60 << 20
        ),
        name="scatter_plane",
    )(partial.reshape(plane, rows, width))


def fill_bias(bias, starts_ref, t, blocks):
    for b in range(blocks):
        span = min(2, blocks - b) * PIC
        k_at = lax.broadcasted_iota(jnp.int32, (span, PIC), 0) + b * PIC
        q_at = lax.broadcasted_iota(jnp.int32, (span, PIC), 1) + b * PIC
        high, below = jnp.maximum(k_at, q_at), jnp.minimum(k_at, q_at)
        allowed = k_at <= q_at
        for j in range(NPIC):
            start = starts_ref[t, j]
            allowed = allowed | ((below >= start) & (high < start + PIC))
        bias[b, :span, :] = jnp.where(allowed, 0.0, -jnp.inf)


def masked(scores, bias, b):
    late = scores[b * PIC :] + bias[b, : scores.shape[0] - b * PIC, :]
    return jnp.concatenate([scores[: b * PIC], late], axis=0) if b else late


def attn_front_kernel(
    starts_ref,
    norm_hbm,
    weight_hbm,
    cos_ref,
    sin_ref,
    own_ref,
    qkv_ref,
    mixed_ref,
    log_ref,
    out_ref,
    all_ref,
    bias,
    turned,
    norm,
    weight,
    projected,
    stage,
    local,
    *gather,
):
    begin, first, second, *last = gather_stages(own_ref, all_ref, *gather)
    total, dim = cos_ref.shape
    take_weight = pltpu.make_async_copy(weight_hbm, weight, local.at[0])
    take_weight.start()

    def take_norm(t):
        rows = pl.ds(t * total, total)
        return pltpu.make_async_copy(norm_hbm.at[rows], norm.at[t], local.at[1 + t])

    def put_out(t, n):
        rows = pl.ds(t * total + n * (total // 2), total // 2)
        return pltpu.make_async_copy(stage.at[n], out_ref.at[rows], local.at[1 + TP + n])

    for t in range(TP):
        take_norm(t).start()
    begin()
    take_weight.wait()
    heads = mixed_ref.shape[1] // dim
    blocks = total // PIC
    scale = dim ** (-0.5)
    k_cols = slice(heads * dim, (heads + 1) * dim)
    v_cols = slice((heads + 1) * dim, (heads + 2) * dim)

    def turn(rows, at):
        return rows * cos_ref[at, :] + pltpu.roll(rows, dim // 2, 1) * sin_ref[at, :]

    def head_step(i, carry):
        t, h = i // heads, lax.rem(i, heads)
        base = pl.multiple_of(t * total, total)
        cols = pl.ds(pl.multiple_of(h * dim, dim), dim)

        @pl.when(h == 0)
        def _():
            rows = pl.ds(base, total)
            take_norm(t).wait()

            def project(n, carry):
                some = pl.ds(pl.multiple_of(n * PIC, PIC), PIC)
                projected[some, :] = nn(norm[t, some, :], weight[:, : (heads + 2) * dim])
                return carry

            lax.fori_loop(0, blocks, project, 0)
            values = projected[:, v_cols].astype(BF)
            qkv_ref[rows, k_cols] = turn(projected[:, k_cols], pl.ds(0, total)).astype(BF)
            qkv_ref[rows, v_cols] = values
            turned[...] = values.T
            fill_bias(bias, starts_ref, t, blocks)

        for b in range(blocks):
            at = pl.ds(pl.multiple_of(base + b * PIC, PIC), PIC)
            count = min(b + 2, blocks) * PIC
            queries = turn(projected[b * PIC : (b + 1) * PIC, cols], pl.ds(b * PIC, PIC)).astype(BF)
            qkv_ref[at, cols] = queries
            scores = nt(qkv_ref[pl.ds(base, count), k_cols], queries) * scale
            scores = masked(scores, bias, b)
            peak = jnp.max(scores, axis=0, keepdims=True)
            weights = jnp.exp(scores - peak)
            mass = jnp.sum(weights, axis=0, keepdims=True)
            log_ref[i, :, b * PIC : (b + 1) * PIC] = peak + jnp.log(mass)
            probs = (weights * (1.0 / mass)).astype(BF)
            mixed_ref[at, cols] = nn(turned[:, :count], probs).T.astype(BF)
            if b == 0:
                pl.when(i == 1)(first)
                pl.when(i == 3)(second)

        @pl.when(h == heads - 1)
        def _():
            for n in range(2):

                @pl.when(t >= 1)
                def _():
                    put_out(t - 1, n).wait()

                rows = pl.ds(pl.multiple_of(base + n * (total // 2), total // 2), total // 2)
                block = stage.shape[2] // 4

                def out_step(m, carry):
                    some = pl.ds(pl.multiple_of(m * block, block), block)
                    partial = nt(mixed_ref[rows, :], weight[some, (heads + 2) * dim :])
                    stage[n, :, some] = partial.astype(BF)
                    return carry

                lax.fori_loop(0, 4, out_step, 0)
                put_out(t, n).start()

        return carry

    lax.fori_loop(0, log_ref.shape[0], head_step, 0)
    for stage_step in last:
        stage_step()
    for n in range(2):
        put_out(TP - 1, n).wait()


def attn_front_plane(starts, norm, weight, cos, sin, block, ident):
    rows, width = block.shape
    plane = lax.axis_size("tp") * lax.axis_size("seq")
    total, dim = cos.shape
    tokens = norm.shape[0]
    q_part = weight.shape[1] // 2 - dim
    shape = jax.ShapeDtypeStruct
    vmem = pl.BlockSpec(memory_space=pltpu.VMEM)
    smem = pl.BlockSpec(memory_space=pltpu.SMEM)
    hbm = pl.BlockSpec(memory_space=pltpu.HBM)
    return pl.pallas_call(
        attn_front_kernel,
        out_shape=(
            shape((tokens, q_part + 2 * dim), BF),
            shape((tokens, q_part), BF),
            shape((tokens * q_part // dim // total, 1, total), F32),
            shape(norm.shape, BF),
            shape((plane, rows, width), block.dtype),
        ),
        in_specs=[smem, hbm, hbm, vmem, vmem, vmem],
        out_specs=(vmem, vmem, vmem, hbm, hbm),
        scratch_shapes=[
            pltpu.VMEM((total // PIC, 2 * PIC, PIC), F32),
            pltpu.VMEM((dim, total), BF),
            pltpu.VMEM((TP, total, width), BF),
            pltpu.VMEM(weight.shape, BF),
            pltpu.VMEM((total, q_part + 2 * dim), F32),
            pltpu.VMEM((2, total // 2, width), BF),
            pltpu.SemaphoreType.DMA((3 + TP,)),
            *GATHER_SCRATCH,
        ],
        cost_estimate=pl.CostEstimate(
            flops=4 * tokens * total * q_part,
            transcendentals=tokens * total * q_part // dim,
            bytes_accessed=plane * rows * width * 24,
        ),
        compiler_params=pltpu.CompilerParams(
            collective_id=ident, has_side_effects=True, vmem_limit_bytes=40 << 20
        ),
        name="attn_front_plane",
    )(starts, norm, weight, cos, sin, block)


def attn_back_kernel(
    starts_ref,
    qkv_ref,
    g_ref,
    log_ref,
    cos_ref,
    sin_ref,
    part_ref,
    grad_ref,
    sum_ref,
    bias,
    turned,
    keys_sum,
    values_sum,
    *scatter,
):
    begin, diagonal, along_x, along_y, own, fold, finish = scatter_stages(
        part_ref, sum_ref, *scatter
    )
    begin()
    total, dim = cos_ref.shape
    heads = g_ref.shape[1] // dim
    blocks = total // PIC
    scale = dim ** (-0.5)
    k_cols = slice(heads * dim, (heads + 1) * dim)
    v_cols = slice((heads + 1) * dim, (heads + 2) * dim)
    events = {(0, 1): diagonal, (0, 2): along_x, (0, 3): along_y, (1, 0): own, (2, 2): fold}

    def unturn(rows, at):
        return rows * cos_ref[at, :] - pltpu.roll(rows, dim // 2, 1) * sin_ref[at, :]

    def head_step(i, carry):
        t, h = i // heads, lax.rem(i, heads)
        base = pl.multiple_of(t * total, total)
        cols = pl.ds(pl.multiple_of(h * dim, dim), dim)

        @pl.when(h == 0)
        def _():
            turned[...] = qkv_ref[pl.ds(base, total), k_cols].T
            keys_sum[...] = jnp.zeros(keys_sum.shape, F32)
            values_sum[...] = jnp.zeros(values_sum.shape, F32)
            fill_bias(bias, starts_ref, t, blocks)

        for b in range(blocks):
            at = pl.ds(pl.multiple_of(base + b * PIC, PIC), PIC)
            count = min(b + 2, blocks) * PIC
            seen = pl.ds(base, count)
            queries, grads = qkv_ref[at, cols], g_ref[at, cols]
            scores = nt(qkv_ref[seen, k_cols], queries) * scale - log_ref[i, :, b * PIC : (b + 1) * PIC]
            probs = jnp.exp(masked(scores, bias, b))
            prob_grad = nt(qkv_ref[seen, v_cols], grads)
            mean = jnp.sum(probs * prob_grad, axis=0, keepdims=True)
            score_grad = (probs * (prob_grad - mean)).astype(BF)
            values_sum[:count, :] += nn(probs.astype(BF), grads)
            keys_sum[:count, :] += nn(score_grad, queries)
            back = nn(turned[:, :count], score_grad).T * scale
            grad_ref[at, cols] = unturn(back, pl.ds(b * PIC, PIC)).astype(BF)
            for (step, block), stage in events.items():
                if block == b:
                    pl.when(i == step)(stage)

        @pl.when(h == heads - 1)
        def _():
            rows = pl.ds(base, total)
            back = unturn(keys_sum[...] * scale, pl.ds(0, total))
            grad_ref[rows, k_cols] = back.astype(BF)
            grad_ref[rows, v_cols] = values_sum[...].astype(BF)

        return carry

    lax.fori_loop(0, log_ref.shape[0], head_step, 0)
    finish()


def attn_back_plane(starts, qkv, grads, log_total, cos, sin, partial, ident):
    plane = lax.axis_size("tp") * lax.axis_size("seq")
    rows, width = partial.shape[0] // plane, partial.shape[1]
    total, dim = cos.shape
    tokens, q_part = grads.shape
    hbm = pl.BlockSpec(memory_space=pltpu.HBM)
    vmem = pl.BlockSpec(memory_space=pltpu.VMEM)
    smem = pl.BlockSpec(memory_space=pltpu.SMEM)
    return pl.pallas_call(
        attn_back_kernel,
        out_shape=(
            jax.ShapeDtypeStruct((tokens, q_part + 2 * dim), BF),
            jax.ShapeDtypeStruct((rows, width), F32),
        ),
        in_specs=[smem] + [vmem] * 5 + [hbm],
        out_specs=(vmem, vmem),
        scratch_shapes=[
            pltpu.VMEM((total // PIC, 2 * PIC, PIC), F32),
            pltpu.VMEM((dim, total), BF),
            pltpu.VMEM((total, dim), F32),
            pltpu.VMEM((total, dim), F32),
        ]
        + scatter_scratch(rows, width, partial.dtype),
        cost_estimate=pl.CostEstimate(
            flops=10 * tokens * total * q_part,
            transcendentals=tokens * total * q_part // dim,
            bytes_accessed=plane * rows * width * 28,
        ),
        compiler_params=pltpu.CompilerParams(
            collective_id=ident, has_side_effects=True, vmem_limit_bytes=50 << 20
        ),
        name="attn_back_plane",
    )(starts, qkv, grads, log_total, cos, sin, partial.reshape(plane, rows, width))


def exchange_kernel(in_ref, out_ref, stage, local, sends, recvs):
    tp_at, seq_at, _, _, _ = plane_place()
    seq = lax.axis_size("seq")
    plane = lax.axis_size("tp") * seq
    me = tp_at * seq + seq_at
    peers = [lax.rem(me + k, plane) for k in range(1, plane)]
    devices = [at_device(peer // seq, lax.rem(peer, seq)) for peer in peers]
    enter(devices)
    copies = []
    for k, (peer, device) in enumerate(zip(peers, devices)):
        copy = remote(in_ref.at[peer], out_ref.at[me], sends.at[k], recvs.at[k], device)
        copy.start()
        copies.append(copy)
    take = pltpu.make_async_copy(in_ref.at[me], stage, local.at[0])
    take.start()
    take.wait()
    put = pltpu.make_async_copy(stage, out_ref.at[me], local.at[1])
    put.start()
    for copy in copies:
        copy.wait()
    put.wait()


def exchange_plane(blocks, ident):
    plane, rows, width = blocks.shape
    size = plane * rows * width * 2
    return pl.pallas_call(
        exchange_kernel,
        out_shape=jax.ShapeDtypeStruct(blocks.shape, blocks.dtype),
        in_specs=[pl.BlockSpec(memory_space=pltpu.HBM)],
        out_specs=pl.BlockSpec(memory_space=pltpu.HBM),
        scratch_shapes=[
            pltpu.VMEM((rows, width), blocks.dtype),
            pltpu.SemaphoreType.DMA((2,)),
            pltpu.SemaphoreType.DMA((plane - 1,)),
            pltpu.SemaphoreType.DMA((plane - 1,)),
        ],
        cost_estimate=pl.CostEstimate(flops=0, transcendentals=0, bytes_accessed=size * 20),
        compiler_params=pltpu.CompilerParams(collective_id=ident, has_side_effects=True),
        name="exchange_plane",
    )(blocks)


def slopes(wide, narrow, inner, gug):
    ff_part = inner.shape[1]

    def body(i, carry):
        at = pl.ds(i * SUB, SUB)
        gate, upward, grad = wide[at, :ff_part], wide[at, ff_part:], narrow[at, :]
        sigmoid_gate = jax.nn.sigmoid(gate)
        silu_gate = gate * sigmoid_gate
        inner[at, :] = (silu_gate * upward).astype(BF)
        slope = sigmoid_gate * (1.0 + gate * (1.0 - sigmoid_gate))
        gug[at, :ff_part] = (grad * upward * slope).astype(BF)
        gug[at, ff_part:] = (grad * silu_gate).astype(BF)
        return carry

    lax.fori_loop(0, wide.shape[0] // SUB, body, 0)


def weight_step(n, tokens, grads, gug, inner, stage, weight_ref, sems):
    slot = lax.rem(n, 2)
    block, cols = stage.shape[1:]
    ff_part = cols // 3
    count = gug.shape[0] * gug.shape[1]

    def put(m):
        return pltpu.make_async_copy(
            stage.at[lax.rem(m, 2)], weight_ref.at[pl.ds(m * block, block)], sems[0].at[sems[1] + lax.rem(m, 2)]
        )

    @pl.when(n >= 2)
    def _():
        put(n - 2).wait()

    at = pl.ds(pl.multiple_of(n * block, block), block)
    left = tokens[:, :, :, at].reshape(count, block)
    stage[slot, :, : 2 * ff_part] = tn(left, gug[...].reshape(count, 2 * ff_part)).astype(BF)
    left = grads[:, :, :, at].reshape(count, block)
    stage[slot, :, 2 * ff_part :] = tn(left, inner[...].reshape(count, ff_part)).astype(BF)
    put(n).start()
    return put


def ffn_first_kernel(
    own_ref,
    grad_ref,
    weight_hbm,
    all_ref,
    back_ref,
    out_ref,
    grads_out,
    weight,
    tokens,
    grads,
    wide,
    narrow,
    inner,
    gug,
    stage,
    columns_stage,
    sends,
    recvs,
    local,
):
    tp_at, seq_at, far, mate, _ = plane_place()
    seq = lax.axis_size("seq")
    other = 1 - tp_at
    to_x = at_device(tp_at, far)
    to_y = at_device(other, seq_at)
    to_c = at_device(tp_at, mate)
    rows, width = own_ref.shape
    pair = 2 * rows
    half = rows // 2
    block = width // 4
    ff_part = narrow.shape[2]
    gate_up, lower = slice(0, 2 * ff_part), slice(2 * ff_part, 3 * ff_part)
    enter((to_x, to_y, to_c))

    def piece(t, s, h):
        return all_ref.at[t * seq + s, pl.ds(h * half, half)]

    def own(i, h, device):
        return remote(
            own_ref.at[pl.ds(h * half, half)],
            piece(tp_at, seq_at, h),
            sends.at[i],
            recvs.at[i],
            device,
        )

    def relay(i, t, s, h, device):
        return remote(piece(t, s, h), piece(t, s, h), sends.at[i], recvs.at[i], device)

    x0, x1 = own(0, 0, to_x), own(3, 1, to_x)
    y0, y1 = own(1, 0, to_y), own(4, 1, to_y)
    c0, c1 = own(2, 0, to_c), own(5, 1, to_c)
    diag0 = relay(6, tp_at, far, 0, to_y)
    diag1 = relay(7, other, seq_at, 1, to_x)
    rx0, rx1 = relay(8, tp_at, far, 0, to_c), relay(11, tp_at, far, 1, to_c)
    ry0, ry1 = relay(9, other, seq_at, 0, to_c), relay(10, other, seq_at, 1, to_c)
    rd0, rd1 = relay(12, other, far, 0, to_c), relay(13, other, far, 1, to_c)

    def chip_rows(c):
        t = lax.rem(tp_at + c // 2, 2)
        s = lax.rem(seq_at + (seq // 2) * lax.rem(c, 2), seq)
        return pl.ds(t * seq + s - lax.rem(s, 2), 2)

    def take_tokens(c):
        return pltpu.make_async_copy(all_ref.at[chip_rows(c)], tokens.at[c], local.at[c])

    def take_grads(c):
        return pltpu.make_async_copy(grad_ref.at[chip_rows(c)], grads.at[c], local.at[4 + c])

    def put_back(c):
        return pltpu.make_async_copy(stage.at[0], back_ref.at[chip_rows(c)], local.at[8])

    def put_out(c):
        return pltpu.make_async_copy(stage.at[1], out_ref.at[chip_rows(c)], local.at[9])

    take_weight = pltpu.make_async_copy(weight_hbm, weight, local.at[12])
    mine = pltpu.make_async_copy(own_ref, all_ref.at[tp_at * seq + seq_at], local.at[13])
    for copy in (take_weight, x0, y0, c0, x1, y1, c1, mine):
        copy.start()
    for c in range(4):
        take_grads(c).start()
    take_weight.wait()

    def narrow_step(c, carry):
        take_grads(c).wait()
        narrow[c] = nn(grads[c].reshape(pair, width), weight[:, lower])
        return carry

    lax.fori_loop(0, 4, narrow_step, 0)
    mine.wait()
    c0.wait_recv()
    c1.wait_recv()
    take_tokens(0).start()

    def chip_step(c, carry):
        take_tokens(c).wait()
        wide[...] = nn(tokens[c].reshape(pair, width), weight[:, gate_up])

        @pl.when(c == 0)
        def _():
            x0.wait_recv()
            diag0.start()
            rx0.start()
            y0.wait_recv()
            ry0.start()

        @pl.when(c == 1)
        def _():
            ry0.wait_recv()
            ry1.wait_recv()
            take_tokens(2).start()

        @pl.when(c == 2)
        def _():
            diag0.wait_recv()
            rd0.start()
            diag1.wait_recv()
            rd1.start()

        slopes(wide, narrow.at[c], inner.at[c], gug.at[c])

        @pl.when(c >= 1)
        def _():
            put_back(c - 1).wait()
            put_out(c - 1).wait()

        def back_step(n, carry):
            at = pl.ds(pl.multiple_of(n * block, block), block)
            total = nt(gug[c], weight[at, gate_up]).astype(BF)
            stage[0, :, :, at] = total.reshape(2, rows, block)
            total = nt(inner[c], weight[at, lower]).astype(BF)
            stage[1, :, :, at] = total.reshape(2, rows, block)
            return carry

        lax.fori_loop(0, 4, back_step, 0)
        put_back(c).start()
        put_out(c).start()

        @pl.when(c == 0)
        def _():
            y1.wait_recv()
            diag1.start()
            ry1.start()
            x1.wait_recv()
            rx1.start()
            rx0.wait_recv()
            rx1.wait_recv()
            take_tokens(1).start()

        @pl.when(c == 2)
        def _():
            rd0.wait_recv()
            rd1.wait_recv()
            take_tokens(3).start()

        return carry

    lax.fori_loop(0, 4, chip_step, 0)

    def grads_step(n, carry):
        weight_step(n, tokens, grads, gug, inner, columns_stage, grads_out, (local, 10))
        return carry

    lax.fori_loop(0, 4, grads_step, 0)
    for copy in (x0, y0, c0, x1, y1, c1, diag0, diag1, rx0, ry0, ry1, rx1, rd0, rd1):
        copy.wait_send()
    put_back(3).wait()
    put_out(3).wait()
    for n in (2, 3):
        pltpu.make_async_copy(
            columns_stage.at[n - 2], grads_out.at[pl.ds(n * block, block)], local.at[8 + n]
        ).wait()


def ffn_second_kernel(
    all_ref,
    grad_ref,
    weight_hbm,
    back_ref,
    first_ref,
    out_ref,
    grads_out,
    sum_ref,
    weight,
    tokens,
    grads,
    wide,
    narrow,
    inner,
    gug,
    part,
    chip_in,
    far_in,
    near_in,
    stage,
    columns_stage,
    sends,
    recvs,
    local,
):
    tp_at, seq_at, far, mate, _ = plane_place()
    seq = lax.axis_size("seq")
    kind = lax.rem(seq_at, 2)
    to_x = at_device(tp_at, far)
    to_y = at_device(1 - tp_at, seq_at)
    to_c = at_device(tp_at, mate)
    rows, width = sum_ref.shape
    pair = 2 * rows
    half = rows // 2
    block = width // 4
    ff_part = narrow.shape[1]
    gate_up, lower = slice(0, 2 * ff_part), slice(2 * ff_part, 3 * ff_part)
    top, low = pl.ds(0, half), pl.ds(half, half)
    enter((to_x, to_y, to_c))

    def chip_rows(k):
        t = lax.rem(tp_at + 1 - lax.rem(k, 2), 2)
        s = lax.rem(seq_at + (seq // 2) * (1 - k // 2), seq)
        return pl.ds(t * seq + s - lax.rem(s, 2), 2)

    def take(ref, target, sem):
        return lambda k: pltpu.make_async_copy(ref.at[chip_rows(k)], target.at[k], local.at[sem + k])

    take_tokens, take_grads, take_back = (
        take(all_ref, tokens, 0),
        take(grad_ref, grads, 4),
        take(back_ref, part, 8),
    )

    def take_first(k):
        slot = lax.rem(k, 2)
        return pltpu.make_async_copy(first_ref.at[chip_rows(k)], stage.at[slot], local.at[12 + slot])

    def put_out(k):
        slot = lax.rem(k, 2)
        return pltpu.make_async_copy(stage.at[slot], out_ref.at[chip_rows(k)], local.at[14 + slot])

    def give(k):
        return remote(part.at[k, 1 - kind], chip_in.at[k], sends.at[k], recvs.at[k], to_c)

    def held(k):
        return part.at[k, kind]

    def hop(i, src, dst, device):
        return remote(src, dst, sends.at[i], recvs.at[i], device)

    d0 = hop(4, part.at[0, kind, top], far_in.at[0, top], to_x)
    d1 = hop(5, part.at[0, kind, low], far_in.at[1, low], to_y)
    x0 = hop(6, part.at[1, kind, top], near_in.at[0, top], to_x)
    y1 = hop(7, part.at[2, kind, low], near_in.at[1, low], to_y)
    y0 = hop(8, part.at[2, kind, top], near_in.at[1, top], to_y)
    x1 = hop(9, part.at[1, kind, low], near_in.at[0, low], to_x)

    def chip_sum(k):
        give(k).wait_recv()
        add_rows(held(k), (held(k), chip_in.at[k]), 0, rows, part.dtype)

    take_weight = pltpu.make_async_copy(weight_hbm, weight, local.at[18])
    take_weight.start()
    for k in range(4):
        take_grads(k).start()
        take_tokens(k).start()
        take_back(k).start()
    take_first(0).start()
    take_weight.wait()

    def chip_step(k, carry):
        slot = lax.rem(k, 2)
        take_grads(k).wait()
        narrow[...] = nn(grads[k].reshape(pair, width), weight[:, lower])

        @pl.when(k == 1)
        def _():
            chip_sum(0)
            d0.start()
            d1.start()

        @pl.when(k == 2)
        def _():
            chip_sum(1)
            x0.start()

        @pl.when(k == 3)
        def _():
            chip_sum(2)
            y1.start()
            d0.wait_recv()
            add_rows(held(2), (held(2), far_in.at[0]), 0, half, part.dtype)
            y0.start()
            d1.wait_recv()
            add_rows(held(1), (held(1), far_in.at[1]), half, half, part.dtype)
            x1.start()

        take_tokens(k).wait()
        wide[...] = nn(tokens[k].reshape(pair, width), weight[:, gate_up])
        slopes(wide, narrow, inner.at[k], gug.at[k])
        take_back(k).wait()

        def back_step(n, carry):
            at = pl.ds(pl.multiple_of(n * block, block), block)
            total = nt(gug[k], weight[at, gate_up]).reshape(2, rows, block)
            part[k, :, :, at] = (part[k, :, :, at].astype(F32) + total).astype(part.dtype)
            return carry

        lax.fori_loop(0, 4, back_step, 0)
        give(k).start()
        take_first(k).wait()

        @pl.when(k >= 1)
        def _():
            put_out(k - 1).wait()

        @pl.when(k < 3)
        def _():
            take_first(k + 1).start()

        def out_step(n, carry):
            at = pl.ds(pl.multiple_of(n * block, block), block)
            total = nt(inner[k], weight[at, lower]).reshape(2, rows, block)
            stage[slot, :, :, at] = (stage[slot, :, :, at].astype(F32) + total).astype(stage.dtype)
            return carry

        lax.fori_loop(0, 4, out_step, 0)
        put_out(k).start()
        return carry

    lax.fori_loop(0, 4, chip_step, 0)

    def grads_step(n, carry):
        weight_step(n, tokens, grads, gug, inner, columns_stage, grads_out, (local, 16))

        @pl.when(n == 0)
        def _():
            chip_sum(3)

        return carry

    lax.fori_loop(0, 4, grads_step, 0)
    x0.wait_recv()
    y0.wait_recv()
    add_rows(sum_ref, (held(3), near_in.at[0], near_in.at[1]), 0, half, sum_ref.dtype)
    y1.wait_recv()
    x1.wait_recv()
    add_rows(sum_ref, (held(3), near_in.at[0], near_in.at[1]), half, half, sum_ref.dtype)
    for k in range(4):
        give(k).wait_send()
    for copy in (d0, d1, x0, y1, y0, x1):
        copy.wait_send()
    put_out(3).wait()
    for n in (2, 3):
        pltpu.make_async_copy(
            columns_stage.at[n - 2], grads_out.at[pl.ds(n * block, block)], local.at[14 + n]
        ).wait()


def ffn_first_plane(block, grads, weight, ident):
    rows, width = block.shape
    plane = lax.axis_size("tp") * lax.axis_size("seq")
    cols = weight.shape[1]
    ff_part = cols // 3
    shape = jax.ShapeDtypeStruct
    hbm = pl.BlockSpec(memory_space=pltpu.HBM)
    vmem = pl.BlockSpec(memory_space=pltpu.VMEM)
    tokens = plane * rows
    return pl.pallas_call(
        ffn_first_kernel,
        out_shape=(
            shape((plane, rows, width), BF),
            shape((plane, rows, width), BF),
            shape((plane, rows, width), BF),
            shape((width, cols), BF),
        ),
        in_specs=[vmem, hbm, hbm],
        out_specs=(hbm, hbm, hbm, hbm),
        scratch_shapes=[
            pltpu.VMEM(weight.shape, BF),
            pltpu.VMEM((4, 2, rows, width), BF),
            pltpu.VMEM((4, 2, rows, width), BF),
            pltpu.VMEM((2 * rows, 2 * ff_part), F32),
            pltpu.VMEM((4, 2 * rows, ff_part), F32),
            pltpu.VMEM((4, 2 * rows, ff_part), BF),
            pltpu.VMEM((4, 2 * rows, 2 * ff_part), BF),
            pltpu.VMEM((2, 2, rows, width), BF),
            pltpu.VMEM((2, width // 4, cols), BF),
            pltpu.SemaphoreType.DMA((14,)),
            pltpu.SemaphoreType.DMA((14,)),
            pltpu.SemaphoreType.DMA((14,)),
        ],
        cost_estimate=pl.CostEstimate(
            flops=18 * tokens * width * ff_part,
            transcendentals=tokens * ff_part,
            bytes_accessed=22 * tokens * width,
        ),
        compiler_params=pltpu.CompilerParams(
            collective_id=ident, has_side_effects=True, vmem_limit_bytes=60 << 20
        ),
        name="ffn_first_plane",
    )(block, grads, weight)


def ffn_second_plane(block, grads, weight, back, first, ident):
    plane, rows, width = block.shape
    cols = weight.shape[1]
    ff_part = cols // 3
    shape = jax.ShapeDtypeStruct
    hbm = pl.BlockSpec(memory_space=pltpu.HBM)
    vmem = pl.BlockSpec(memory_space=pltpu.VMEM)
    tokens = plane * rows
    return pl.pallas_call(
        ffn_second_kernel,
        out_shape=(
            shape((plane, rows, width), BF),
            shape((width, cols), BF),
            shape((rows, width), F32),
        ),
        in_specs=[hbm] * 5,
        out_specs=(hbm, hbm, vmem),
        scratch_shapes=[
            pltpu.VMEM(weight.shape, BF),
            pltpu.VMEM((4, 2, rows, width), BF),
            pltpu.VMEM((4, 2, rows, width), BF),
            pltpu.VMEM((2 * rows, 2 * ff_part), F32),
            pltpu.VMEM((2 * rows, ff_part), F32),
            pltpu.VMEM((4, 2 * rows, ff_part), BF),
            pltpu.VMEM((4, 2 * rows, 2 * ff_part), BF),
            pltpu.VMEM((4, 2, rows, width), BF),
            pltpu.VMEM((4, rows, width), BF),
            pltpu.VMEM((2, rows, width), BF),
            pltpu.VMEM((2, rows, width), BF),
            pltpu.VMEM((2, 2, rows, width), BF),
            pltpu.VMEM((2, width // 4, cols), BF),
            pltpu.SemaphoreType.DMA((10,)),
            pltpu.SemaphoreType.DMA((10,)),
            pltpu.SemaphoreType.DMA((19,)),
        ],
        cost_estimate=pl.CostEstimate(
            flops=18 * tokens * width * ff_part,
            transcendentals=tokens * ff_part,
            bytes_accessed=22 * tokens * width,
        ),
        compiler_params=pltpu.CompilerParams(
            collective_id=ident, has_side_effects=True, vmem_limit_bytes=63 << 20
        ),
        name="ffn_second_plane",
    )(block, grads, weight, back, first)


def exchange_all_kernel(
    first_ref, second_ref, attn_ref, first_in, second_in, attn_in, local, sends, recvs
):
    tp_at, seq_at, _, _, _ = plane_place()
    seq = lax.axis_size("seq")
    plane = lax.axis_size("tp") * seq
    me = tp_at * seq + seq_at
    peers = [lax.rem(me + k, plane) for k in range(1, plane)]
    devices = [at_device(peer // seq, lax.rem(peer, seq)) for peer in peers]
    enter(devices)
    groups = []
    for n, (ref, into) in enumerate(
        ((first_ref, first_in), (second_ref, second_in), (attn_ref, attn_in))
    ):
        copies = [pltpu.make_async_copy(ref.at[me], into.at[me], local.at[n])]
        for k, (peer, device) in enumerate(zip(peers, devices)):
            i = n * (plane - 1) + k
            copies.append(remote(ref.at[peer], into.at[me], sends.at[i], recvs.at[i], device))
        for copy in copies:
            copy.start()
        groups.append(copies)

    for copies in groups:
        for copy in copies:
            copy.wait()


def exchange_all_plane(blocks, ident):
    plane = blocks[0].shape[0]
    hbm = pl.BlockSpec(memory_space=pltpu.HBM)
    vmem = pl.BlockSpec(memory_space=pltpu.VMEM)
    size = sum(block.size for block in blocks) * 2
    return pl.pallas_call(
        exchange_all_kernel,
        out_shape=tuple(jax.ShapeDtypeStruct(b.shape, b.dtype) for b in blocks),
        in_specs=[hbm] * 3,
        out_specs=(vmem,) * 3,
        scratch_shapes=[
            pltpu.SemaphoreType.DMA((3,)),
            pltpu.SemaphoreType.DMA((3 * plane - 3,)),
            pltpu.SemaphoreType.DMA((3 * plane - 3,)),
        ],
        cost_estimate=pl.CostEstimate(flops=0, transcendentals=0, bytes_accessed=size * 20),
        compiler_params=pltpu.CompilerParams(collective_id=ident, has_side_effects=True),
        name="exchange_all_plane",
    )(*blocks)


def finish_kernel(
    first_in,
    second_in,
    attn_in,
    gate_weight,
    up_weight,
    query_weight,
    key_weight,
    value_weight,
    gain2_ref,
    gain1_ref,
    gate_out,
    up_out,
    down_out,
    gain2_out,
    query_out,
    key_out,
    value_out,
    out_out,
    gain1_out,
):
    plane = first_in.shape[0]
    gain = gain2_ref[...]
    sizes = [ref.shape[2] // 3 for ref in (first_in, second_in)]
    total = jnp.zeros(gain.shape, F32)
    for n, ref in enumerate((first_in, second_in)):
        size = sizes[n]
        for j in range(plane):
            start = j * sum(sizes) + n * sizes[0]
            at = slice(start, start + size)
            for k, (out, weight) in enumerate(((gate_out, gate_weight), (up_out, up_weight))):
                own = ref[j, :, k * size : (k + 1) * size].astype(F32)
                out[:, at] = own * gain
                total = total + jnp.sum(own * weight[:, at].astype(F32), axis=1, keepdims=True)
            down_out[at, :] = ref[j, :, 2 * size :].astype(F32).T
    gain2_out[...] = total

    gain = gain1_ref[...]
    q_part = query_out.shape[1] // plane
    share = plane // KV
    total = jnp.zeros(gain.shape, F32)
    for j in range(plane):
        at = slice(j * q_part, (j + 1) * q_part)
        own = attn_in[j, :, :q_part].astype(F32)
        query_out[:, at] = own * gain
        total = total + jnp.sum(own * query_weight[:, at].astype(F32), axis=1, keepdims=True)
        out_out[at, :] = attn_in[j, :, q_part + 2 * DH :].astype(F32).T
    for j in range(KV):
        at = slice(j * DH, (j + 1) * DH)
        for k, (out, weight) in enumerate(((key_out, key_weight), (value_out, value_weight))):
            cols = slice(q_part + k * DH, q_part + (k + 1) * DH)
            own = attn_in[j * share, :, cols].astype(F32)
            for i in range(1, share):
                own = own + attn_in[j * share + i, :, cols].astype(F32)
            out[:, at] = own * gain
            total = total + jnp.sum(own * weight[:, at].astype(F32), axis=1, keepdims=True)
    gain1_out[...] = total


def finish(first, second, attn, weights, gain2, gain1):
    rows = first.shape[1]
    shape = jax.ShapeDtypeStruct
    vmem = pl.BlockSpec(memory_space=pltpu.VMEM)
    gate, up, query, key, value = (shape(w.shape, F32) for w in weights)
    down, out = (shape(w.shape[::-1], F32) for w in (gate, query))
    column = shape((rows, 1), F32)
    return pl.pallas_call(
        finish_kernel,
        out_shape=(gate, up, down, column, query, key, value, out, column),
        in_specs=[vmem] * 10,
        out_specs=(vmem,) * 9,
        cost_estimate=pl.CostEstimate(
            flops=4 * gate.size, transcendentals=0, bytes_accessed=16 * gate.size
        ),
        compiler_params=pltpu.CompilerParams(vmem_limit_bytes=40 << 20),
        name="finish",
    )(first, second, attn, *weights, gain2, gain1)


def columns(matrix, parts):
    rows, cols = matrix.shape
    return jnp.transpose(matrix.reshape(rows, parts, cols // parts), (1, 0, 2))


def uncolumns(blocks):
    parts, rows, cols = blocks.shape
    return jnp.transpose(blocks, (1, 0, 2)).reshape(rows, parts * cols)


def after(value, *earlier):
    return lax.optimization_barrier((value,) + earlier)[0]


def per_device(
    layer_input,
    pic_starts,
    skip_mask,
    gain_attn,
    w_query,
    w_key,
    w_value,
    w_out,
    gain_ffn,
    w_gate,
    w_up,
    w_down,
    cotangent,
):
    _, local_len, width = layer_input.shape
    seq = lax.axis_size("seq")
    plane = lax.axis_size("tp") * seq
    total_len = local_len * seq
    heads = H // plane
    share = plane // KV
    ff_part = w_gate.shape[1] // plane
    q_part = heads * DH

    gain1 = gain_attn[:, None]
    gain2 = gain_ffn[:, None]
    wq32, wk32, wv32 = w_query.astype(F32), w_key.astype(F32), w_value.astype(F32)
    wg32, wu32 = w_gate.astype(F32), w_up.astype(F32)
    attn_pack = jnp.concatenate(
        [
            columns((wq32 * gain1).astype(BF), plane),
            jnp.repeat(columns((wk32 * gain1).astype(BF), KV), share, axis=0),
            jnp.repeat(columns((wv32 * gain1).astype(BF), KV), share, axis=0),
            columns(w_out.T, plane),
        ],
        axis=2,
    )
    attn_rows = exchange_plane(attn_pack, 0)
    attn_rows = attn_rows.reshape(-1, attn_rows.shape[2])
    attn_weight = lax.all_gather(attn_rows, "rep", axis=0, tiled=True)
    qkv_weight = attn_weight[:, : q_part + 2 * DH]
    out_weight = attn_weight[:, q_part + 2 * DH :]

    tokens = layer_input.reshape(local_len, width).astype(F32)
    keep = (1 - skip_mask).astype(F32).reshape(local_len, 1)
    upstream = cotangent.reshape(local_len, width).astype(F32)
    scale1 = rms_scale(tokens)
    norm1 = tokens * scale1

    first_part = (ff_part // 2 + DH - 1) // DH * DH
    split = ((0, first_part), (first_part, ff_part))
    ffn_parts = (
        columns((wg32 * gain2).astype(BF), plane),
        columns((wu32 * gain2).astype(BF), plane),
        columns(w_down.T, plane),
    )
    first_pack, second_pack = (
        jnp.concatenate([m[:, :, a:b] for m in ffn_parts], axis=2) for a, b in split
    )
    first_rows = exchange_plane(after(first_pack, attn_rows), 2)
    norm1_all, second_rows = spread_plane(after(norm1.astype(BF), first_rows), second_pack, 1)
    first_rows = first_rows.reshape(-1, first_rows.shape[2])
    second_rows = second_rows.reshape(-1, second_rows.shape[2])
    first_weight = lax.all_gather(first_rows, "rep", axis=0, tiled=True)
    second_weight = lax.all_gather(second_rows, "rep", axis=0, tiled=True)
    norm1_all = norm1_all.reshape(-1, width)

    other_starts = lax.ppermute(pic_starts, "tp", [(0, 1), (1, 0)])
    starts = jnp.where(
        lax.axis_index("tp") == 0,
        jnp.concatenate([pic_starts, other_starts], axis=0),
        jnp.concatenate([other_starts, pic_starts], axis=0),
    )
    positions = jnp.arange(total_len, dtype=jnp.int32)
    cos_table, sin_table = rotary_tables(positions, DH)
    cos = jnp.concatenate([cos_table, cos_table], axis=1)
    sin = jnp.concatenate([-sin_table, sin_table], axis=1)
    qkv, mixed, log_total, branch_partial, ffn_grad = attn_front_plane(
        starts, norm1_all, attn_weight, cos, sin, (keep * upstream).astype(BF), 3
    )
    branch = scatter_plane(branch_partial, 4)
    hidden = tokens + keep * branch

    scale2 = rms_scale(hidden)
    norm2 = hidden * scale2
    norm2_all, back_first, out_first, first_partial = ffn_first_plane(
        norm2.astype(BF), ffn_grad, first_weight, 5
    )
    first_sums = lax.psum_scatter(first_partial, "rep", scatter_dimension=0, tiled=True)
    out_partial, second_partial, scaled2 = ffn_second_plane(
        norm2_all, ffn_grad, second_weight, back_first, out_first, 6
    )
    second_sums = lax.psum_scatter(second_partial, "rep", scatter_dimension=0, tiled=True)
    hidden_grad = upstream + scale2 * (
        scaled2 - norm2 * jnp.mean(scaled2 * norm2, axis=-1, keepdims=True)
    )

    _, mixed_grad, out_columns = gather_mix_plane(
        (keep * hidden_grad).astype(BF), mixed, out_weight, 7
    )
    qkv_grad, ffn_out = attn_back_plane(
        starts,
        qkv,
        after(mixed_grad, first_sums),
        log_total,
        cos,
        sin,
        out_partial.reshape(-1, width),
        9,
    )
    attn_partial = jnp.concatenate(
        [tn(norm1_all, qkv_grad).astype(BF), out_columns], axis=1
    )
    scaled1_partial = nt(qkv_grad, qkv_weight).astype(BF)
    attn_sums = lax.psum_scatter(attn_partial, "rep", scatter_dimension=0, tiled=True)
    scaled1 = scatter_plane(after(scaled1_partial, attn_partial, second_sums), 8)
    input_grad = hidden_grad + scale1 * (
        scaled1 - norm1 * jnp.mean(scaled1 * norm1, axis=-1, keepdims=True)
    )
    out_hidden = (hidden + keep * ffn_out).astype(BF)

    sums = exchange_all_plane(
        (
            after(first_sums, input_grad, out_hidden).reshape(plane, -1, first_sums.shape[1]),
            second_sums.reshape(plane, -1, second_sums.shape[1]),
            attn_sums.reshape(plane, -1, attn_sums.shape[1]),
        ),
        10,
    )
    weights = (w_gate, w_up, w_query, w_key, w_value)
    gate_grad, up_grad, down_grad, gain2_grad, *attn_grads = finish(*sums, weights, gain2, gain1)
    query_grad, key_grad, value_grad, out_grad, gain1_grad = attn_grads
    return (
        out_hidden[None],
        input_grad[None],
        gain1_grad[:, 0],
        query_grad,
        key_grad,
        value_grad,
        out_grad,
        gain2_grad[:, 0],
        gate_grad,
        up_grad,
        down_grad,
    )


def solution(mesh):
    devices = mesh.devices
    dp, seq = devices.shape
    inner = Mesh(devices.reshape(dp // TP, TP, seq), ("rep", "tp", "seq"))
    dps = ("rep", "tp")
    every = ("rep", "tp", "seq")
    token = P(dps, "seq", None)
    row = P(every, None)
    col = P(None, every)
    return jax.shard_map(
        per_device,
        mesh=inner,
        in_specs=(
            token,
            P(dps, None),
            P(dps, "seq"),
            P(every),
            row,
            row,
            row,
            col,
            P(every),
            row,
            row,
            col,
            token,
        ),
        out_specs=(token, token, P(every), row, row, row, col, P(every), row, row, col),
        check_vma=False,
    )
```

```python
import jax
import jax.numpy as jnp
from jax import lax
from jax.experimental import pallas as pl
from jax.experimental.pallas import tpu as pltpu
from jax.sharding import Mesh
from jax.sharding import PartitionSpec as P

H = 16
KV = 4
DH = 128
PIC = 256
NPIC = 2
EPS = 1e-05
TP = 2
BF = jnp.bfloat16
F32 = jnp.float32


def rotary_tables(positions, head_dim):
    half_dim = head_dim // 2
    inverse = 10000.0 ** (-(jnp.arange(half_dim, dtype=F32) * 2.0 / head_dim))
    angles = positions.astype(F32)[:, None] * inverse[None, :]
    return (jnp.cos(angles), jnp.sin(angles))


def rms_scale(rows):
    return lax.rsqrt(jnp.mean(rows * rows, axis=-1, keepdims=True) + EPS)


def dot(left, right, contract):
    return lax.dot_general(
        left, right, ((contract[:1], contract[1:]), ((), ())), preferred_element_type=F32
    )


def nn(left, right):
    return dot(left, right, (1, 0))


def nt(left, right):
    return dot(left, right, (1, 1))


def tn(left, right):
    return dot(left, right, (0, 0))


MESH_ID = pl.DeviceIdType.MESH
SUB = 32


def plane_place():
    tp_at = lax.axis_index("tp")
    seq_at = lax.axis_index("seq")
    seq = lax.axis_size("seq")
    half = seq // 2
    far = lax.rem(seq_at + half, seq)
    mate = seq_at + 1 - 2 * lax.rem(seq_at, 2)
    far_mate = far + 1 - 2 * lax.rem(far, 2)
    return tp_at, seq_at, far, mate, far_mate


def at_device(tp_at, seq_at):
    return (lax.axis_index("rep"), tp_at, seq_at)


def enter(devices):
    barrier = pltpu.get_barrier_semaphore()
    for device in devices:
        pl.semaphore_signal(barrier, inc=1, device_id=device, device_id_type=MESH_ID)
    pl.semaphore_wait(barrier, len(devices))


def remote(src, dst, send, recv, device):
    return pltpu.make_async_remote_copy(
        src_ref=src,
        dst_ref=dst,
        send_sem=send,
        recv_sem=recv,
        device_id=device,
        device_id_type=MESH_ID,
    )


def gather_stages(own_ref, all_ref, sends, recvs, local):
    tp_at, seq_at, far, mate, _ = plane_place()
    seq = lax.axis_size("seq")
    other = 1 - tp_at
    to_x = at_device(tp_at, far)
    to_y = at_device(other, seq_at)
    to_c = at_device(tp_at, mate)
    rows = own_ref.shape[0]
    part = rows // 2

    def piece(t, s, h):
        return all_ref.at[t * seq + s, pl.ds(h * part, part)]

    def relay(i, t, s, h, device):
        return remote(piece(t, s, h), piece(t, s, h), sends.at[i], recvs.at[i], device)

    def own(i, h, device):
        return remote(
            own_ref.at[pl.ds(h * part, part)],
            piece(tp_at, seq_at, h),
            sends.at[i],
            recvs.at[i],
            device,
        )

    x0, x1 = own(0, 0, to_x), own(3, 1, to_x)
    y0, y1 = own(1, 0, to_y), own(4, 1, to_y)
    c0, c1 = own(2, 0, to_c), own(5, 1, to_c)
    diag0 = relay(6, tp_at, far, 0, to_y)
    diag1 = relay(7, other, seq_at, 1, to_x)
    rx0, rx1 = relay(8, tp_at, far, 0, to_c), relay(11, tp_at, far, 1, to_c)
    ry0, ry1 = relay(9, other, seq_at, 0, to_c), relay(10, other, seq_at, 1, to_c)
    rd0, rd1 = relay(12, other, far, 0, to_c), relay(13, other, far, 1, to_c)
    mine = pltpu.make_async_copy(own_ref, all_ref.at[tp_at * seq + seq_at], local)

    def begin(peers=(to_x, to_y, to_c)):
        enter(peers)
        for copy in (x0, y0, c0, x1, y1, c1, mine):
            copy.start()

    def first():
        x0.wait_recv()
        diag0.start()
        rx0.start()
        y0.wait_recv()
        ry0.start()

    def second():
        y1.wait_recv()
        diag1.start()
        ry1.start()
        x1.wait_recv()
        rx1.start()

    def far_start():
        diag0.wait_recv()
        rd0.start()
        diag1.wait_recv()
        rd1.start()

    def near_arrive():
        mine.wait()
        for copy in (c0, c1, rx0, ry0, ry1, rx1):
            copy.wait_recv()

    def far_arrive():
        rd0.wait_recv()
        rd1.wait_recv()
        for copy in (x0, y0, c0, x1, y1, c1, diag0, diag1, rx0, ry0, ry1, rx1, rd0, rd1):
            copy.wait_send()

    return begin, first, second, near_arrive, far_start, far_arrive


GATHER_SCRATCH = (
    pltpu.SemaphoreType.DMA((14,)),
    pltpu.SemaphoreType.DMA((14,)),
    pltpu.SemaphoreType.DMA,
)


def gather_mix_kernel(
    own_ref, mixed_ref, weight_ref, all_ref, grad_ref, columns_ref, tokens, total, local, *gather
):
    begin, first, second, near_arrive, far_start, far_arrive = gather_stages(
        own_ref, all_ref, *gather
    )
    tp_at, seq_at, _, _, _ = plane_place()
    seq = lax.axis_size("seq")
    rows, width = own_ref.shape
    pair = 2 * rows
    block = width // 4
    begin()

    def chip_rows(c):
        t = lax.rem(tp_at + c // 2, 2)
        s = lax.rem(seq_at + (seq // 2) * lax.rem(c, 2), seq)
        return t * seq + s - lax.rem(s, 2)

    def take(c):
        return pltpu.make_async_copy(
            all_ref.at[pl.ds(chip_rows(c), 2)], tokens.at[c], local.at[c]
        )

    total[...] = jnp.zeros(total.shape, F32)

    def chip_step(c, carry):
        take(c).wait()
        at = pl.ds(pl.multiple_of(chip_rows(c) * rows, pair), pair)
        chip = nn(tokens[c].reshape(pair, width), weight_ref[...])
        grad_ref[at, :] = chip.astype(BF)

        def grads_step(n, carry):
            some = pl.ds(pl.multiple_of(n * block, block), block)
            total[some, :] += tn(tokens[c, :, :, some].reshape(pair, block), mixed_ref[at, :])
            return carry

        lax.fori_loop(0, 4, grads_step, 0)
        return carry

    first()
    second()
    near_arrive()
    for c in range(3):
        take(c).start()
    lax.fori_loop(0, 3, chip_step, 0)
    far_start()
    far_arrive()
    take(3).start()
    chip_step(3, 0)
    columns_ref[...] = total[...].astype(BF)


def gather_mix_plane(block, mixed, weight, ident):
    rows, width = block.shape
    plane = lax.axis_size("tp") * lax.axis_size("seq")
    tokens, q_part = mixed.shape
    shape = jax.ShapeDtypeStruct
    hbm = pl.BlockSpec(memory_space=pltpu.HBM)
    vmem = pl.BlockSpec(memory_space=pltpu.VMEM)
    return pl.pallas_call(
        gather_mix_kernel,
        out_shape=(
            shape((plane, rows, width), BF),
            shape((tokens, q_part), BF),
            shape((width, q_part), BF),
        ),
        in_specs=[vmem] * 3,
        out_specs=(hbm, vmem, vmem),
        scratch_shapes=[
            pltpu.VMEM((4, 2, rows, width), BF),
            pltpu.VMEM((width, q_part), F32),
            pltpu.SemaphoreType.DMA((4,)),
            *GATHER_SCRATCH,
        ],
        cost_estimate=pl.CostEstimate(
            flops=4 * tokens * width * q_part,
            transcendentals=0,
            bytes_accessed=plane * rows * width * 24,
        ),
        compiler_params=pltpu.CompilerParams(
            collective_id=ident, has_side_effects=True, vmem_limit_bytes=40 << 20
        ),
        name="gather_mix_plane",
    )(block, mixed, weight)


def spread_kernel(
    own_ref, move_ref, all_ref, move_out, kept, copies, *gather
):
    begin, first, second, *last = gather_stages(own_ref, all_ref, *gather)
    tp_at, seq_at, _, _, _ = plane_place()
    seq = lax.axis_size("seq")
    plane = lax.axis_size("tp") * seq
    me = tp_at * seq + seq_at
    peers = [lax.rem(me + k, plane) for k in range(1, plane)]
    devices = [at_device(peer // seq, lax.rem(peer, seq)) for peer in peers]
    sends, recvs, local = copies.at[0], copies.at[1], copies.at[2]
    begin(devices)
    moves = [
        remote(move_ref.at[peer], move_out.at[me], sends.at[k], recvs.at[k], device)
        for k, (peer, device) in enumerate(zip(peers, devices))
    ]
    for move in moves:
        move.start()
    take = pltpu.make_async_copy(move_ref.at[me], kept, local.at[0])
    put = pltpu.make_async_copy(kept, move_out.at[me], local.at[1])
    take.start()
    take.wait()
    put.start()
    first()
    second()
    for move in moves:
        move.wait()
    put.wait()
    for stage in last:
        stage()


def spread_plane(block, blocks, ident):
    rows, width = block.shape
    plane = lax.axis_size("tp") * lax.axis_size("seq")
    hbm = pl.BlockSpec(memory_space=pltpu.HBM)
    vmem = pl.BlockSpec(memory_space=pltpu.VMEM)
    size = plane * rows * width * 2
    return pl.pallas_call(
        spread_kernel,
        out_shape=(
            jax.ShapeDtypeStruct((plane, rows, width), block.dtype),
            jax.ShapeDtypeStruct(blocks.shape, blocks.dtype),
        ),
        in_specs=[vmem, hbm],
        out_specs=(hbm, hbm),
        scratch_shapes=[
            pltpu.VMEM(blocks.shape[1:], blocks.dtype),
            pltpu.SemaphoreType.DMA((3, plane)),
            *GATHER_SCRATCH,
        ],
        cost_estimate=pl.CostEstimate(flops=0, transcendentals=0, bytes_accessed=size * 16),
        compiler_params=pltpu.CompilerParams(collective_id=ident, has_side_effects=True),
        name="spread_plane",
    )(block, blocks)


def add_rows(target, sources, start, count, kind):
    step = min(SUB, count)

    def body(i, carry):
        at = pl.ds(start + i * step, step)
        total = sources[0][at, :].astype(F32)
        for source in sources[1:]:
            total = total + source[at, :].astype(F32)
        target[at, :] = total.astype(kind)
        return carry

    lax.fori_loop(0, count // step, body, 0)


def scatter_stages(part_ref, sum_ref, held, chip_in, far_in, near_in, loads, sends, recvs):
    tp_at, seq_at, far, mate, far_mate = plane_place()
    seq = lax.axis_size("seq")
    other = 1 - tp_at
    to_x = at_device(tp_at, far)
    to_y = at_device(other, seq_at)
    to_c = at_device(tp_at, mate)
    rows = sum_ref.shape[0]
    part = rows // 2
    top, low = pl.ds(0, part), pl.ds(part, part)
    chips = ((other, far, far_mate), (tp_at, far, far_mate), (other, seq_at, mate), (tp_at, seq_at, mate))
    gives = [
        remote(part_ref.at[t * seq + m], chip_in.at[k], sends.at[k], recvs.at[k], to_c)
        for k, (t, s, m) in enumerate(chips)
    ]
    takes = [
        pltpu.make_async_copy(part_ref.at[t * seq + s], held.at[k], loads.at[k])
        for k, (t, s, m) in enumerate(chips)
    ]

    def hop(i, src, dst, device):
        return remote(src, dst, sends.at[i], recvs.at[i], device)

    d0 = hop(4, held.at[0, top], far_in.at[0, top], to_x)
    d1 = hop(5, held.at[0, low], far_in.at[1, low], to_y)
    x0 = hop(6, held.at[1, top], near_in.at[0, top], to_x)
    y1 = hop(7, held.at[2, low], near_in.at[1, low], to_y)
    y0 = hop(8, held.at[2, top], near_in.at[1, top], to_y)
    x1 = hop(9, held.at[1, low], near_in.at[0, low], to_x)

    def begin():
        enter((to_x, to_y, to_c))
        for give, take in zip(gives, takes):
            give.start()
            take.start()

    def chip_sum(k):
        takes[k].wait()
        gives[k].wait_recv()
        add_rows(held.at[k], (held.at[k], chip_in.at[k]), 0, rows, held.dtype)

    def diagonal():
        chip_sum(0)
        d0.start()
        d1.start()

    def along_x():
        chip_sum(1)
        x0.start()

    def along_y():
        chip_sum(2)
        y1.start()

    def own():
        chip_sum(3)

    def fold():
        d0.wait_recv()
        add_rows(held.at[2], (held.at[2], far_in.at[0]), 0, part, held.dtype)
        y0.start()
        d1.wait_recv()
        add_rows(held.at[1], (held.at[1], far_in.at[1]), part, part, held.dtype)
        x1.start()

    def finish():
        x0.wait_recv()
        y0.wait_recv()
        add_rows(sum_ref, (held.at[3], near_in.at[0], near_in.at[1]), 0, part, sum_ref.dtype)
        y1.wait_recv()
        x1.wait_recv()
        add_rows(sum_ref, (held.at[3], near_in.at[0], near_in.at[1]), part, part, sum_ref.dtype)
        for copy in gives + [d0, d1, x0, y1, y0, x1]:
            copy.wait_send()

    return begin, diagonal, along_x, along_y, own, fold, finish


def scatter_kernel(*refs):
    for stage in scatter_stages(*refs):
        stage()


def scatter_scratch(rows, width, kind):
    return [
        pltpu.VMEM((4, rows, width), kind),
        pltpu.VMEM((4, rows, width), kind),
        pltpu.VMEM((2, rows, width), kind),
        pltpu.VMEM((2, rows, width), kind),
        pltpu.SemaphoreType.DMA((4,)),
        pltpu.SemaphoreType.DMA((10,)),
        pltpu.SemaphoreType.DMA((10,)),
    ]


def scatter_plane(partial, ident):
    plane = lax.axis_size("tp") * lax.axis_size("seq")
    rows, width = partial.shape[0] // plane, partial.shape[1]
    kind = partial.dtype
    size = rows * width * 2
    return pl.pallas_call(
        scatter_kernel,
        out_shape=jax.ShapeDtypeStruct((rows, width), F32),
        in_specs=[pl.BlockSpec(memory_space=pltpu.HBM)],
        out_specs=pl.BlockSpec(memory_space=pltpu.VMEM),
        scratch_shapes=scatter_scratch(rows, width, kind),
        cost_estimate=pl.CostEstimate(
            flops=0, transcendentals=0, bytes_accessed=plane * size * 14
        ),
        compiler_params=pltpu.CompilerParams(
            collective_id=ident, has_side_effects=True, vmem_limit_bytes=60 << 20
        ),
        name="scatter_plane",
    )(partial.reshape(plane, rows, width))


def fill_bias(bias, starts_ref, t, blocks):
    for b in range(blocks):
        span = min(2, blocks - b) * PIC
        k_at = lax.broadcasted_iota(jnp.int32, (span, PIC), 0) + b * PIC
        q_at = lax.broadcasted_iota(jnp.int32, (span, PIC), 1) + b * PIC
        high, below = jnp.maximum(k_at, q_at), jnp.minimum(k_at, q_at)
        allowed = k_at <= q_at
        for j in range(NPIC):
            start = starts_ref[t, j]
            allowed = allowed | ((below >= start) & (high < start + PIC))
        bias[b, :span, :] = jnp.where(allowed, 0.0, -jnp.inf)


def masked(scores, bias, b):
    late = scores[b * PIC :] + bias[b, : scores.shape[0] - b * PIC, :]
    return jnp.concatenate([scores[: b * PIC], late], axis=0) if b else late


def attn_front_kernel(
    starts_ref,
    norm_hbm,
    weight_hbm,
    cos_ref,
    sin_ref,
    own_ref,
    qkv_ref,
    mixed_ref,
    log_ref,
    out_ref,
    all_ref,
    bias,
    turned,
    norm,
    weight,
    projected,
    stage,
    local,
    *gather,
):
    begin, first, second, *last = gather_stages(own_ref, all_ref, *gather)
    total, dim = cos_ref.shape
    take_weight = pltpu.make_async_copy(weight_hbm, weight, local.at[0])
    take_weight.start()

    def take_norm(t):
        rows = pl.ds(t * total, total)
        return pltpu.make_async_copy(norm_hbm.at[rows], norm.at[t], local.at[1 + t])

    def put_out(t, n):
        rows = pl.ds(t * total + n * (total // 2), total // 2)
        return pltpu.make_async_copy(stage.at[n], out_ref.at[rows], local.at[1 + TP + n])

    for t in range(TP):
        take_norm(t).start()
    begin()
    take_weight.wait()
    heads = mixed_ref.shape[1] // dim
    blocks = total // PIC
    scale = dim ** (-0.5)
    k_cols = slice(heads * dim, (heads + 1) * dim)
    v_cols = slice((heads + 1) * dim, (heads + 2) * dim)

    def turn(rows, at):
        return rows * cos_ref[at, :] + pltpu.roll(rows, dim // 2, 1) * sin_ref[at, :]

    def head_step(i, carry):
        t, h = i // heads, lax.rem(i, heads)
        base = pl.multiple_of(t * total, total)
        cols = pl.ds(pl.multiple_of(h * dim, dim), dim)

        @pl.when(h == 0)
        def _():
            rows = pl.ds(base, total)
            take_norm(t).wait()

            def project(n, carry):
                some = pl.ds(pl.multiple_of(n * PIC, PIC), PIC)
                projected[some, :] = nn(norm[t, some, :], weight[:, : (heads + 2) * dim])
                return carry

            lax.fori_loop(0, blocks, project, 0)
            values = projected[:, v_cols].astype(BF)
            qkv_ref[rows, k_cols] = turn(projected[:, k_cols], pl.ds(0, total)).astype(BF)
            qkv_ref[rows, v_cols] = values
            turned[...] = values.T
            fill_bias(bias, starts_ref, t, blocks)

        for b in range(blocks):
            at = pl.ds(pl.multiple_of(base + b * PIC, PIC), PIC)
            count = min(b + 2, blocks) * PIC
            queries = turn(projected[b * PIC : (b + 1) * PIC, cols], pl.ds(b * PIC, PIC)).astype(BF)
            qkv_ref[at, cols] = queries
            scores = nt(qkv_ref[pl.ds(base, count), k_cols], queries) * scale
            scores = masked(scores, bias, b)
            peak = jnp.max(scores, axis=0, keepdims=True)
            weights = jnp.exp(scores - peak)
            mass = jnp.sum(weights, axis=0, keepdims=True)
            log_ref[i, :, b * PIC : (b + 1) * PIC] = peak + jnp.log(mass)
            probs = (weights * (1.0 / mass)).astype(BF)
            mixed_ref[at, cols] = nn(turned[:, :count], probs).T.astype(BF)
            if b == 0:
                pl.when(i == 1)(first)
                pl.when(i == 3)(second)

        @pl.when(h == heads - 1)
        def _():
            for n in range(2):

                @pl.when(t >= 1)
                def _():
                    put_out(t - 1, n).wait()

                rows = pl.ds(pl.multiple_of(base + n * (total // 2), total // 2), total // 2)
                block = stage.shape[2] // 4

                def out_step(m, carry):
                    some = pl.ds(pl.multiple_of(m * block, block), block)
                    partial = nt(mixed_ref[rows, :], weight[some, (heads + 2) * dim :])
                    stage[n, :, some] = partial.astype(BF)
                    return carry

                lax.fori_loop(0, 4, out_step, 0)
                put_out(t, n).start()

        return carry

    lax.fori_loop(0, log_ref.shape[0], head_step, 0)
    for stage_step in last:
        stage_step()
    for n in range(2):
        put_out(TP - 1, n).wait()


def attn_front_plane(starts, norm, weight, cos, sin, block, ident):
    rows, width = block.shape
    plane = lax.axis_size("tp") * lax.axis_size("seq")
    total, dim = cos.shape
    tokens = norm.shape[0]
    q_part = weight.shape[1] // 2 - dim
    shape = jax.ShapeDtypeStruct
    vmem = pl.BlockSpec(memory_space=pltpu.VMEM)
    smem = pl.BlockSpec(memory_space=pltpu.SMEM)
    hbm = pl.BlockSpec(memory_space=pltpu.HBM)
    return pl.pallas_call(
        attn_front_kernel,
        out_shape=(
            shape((tokens, q_part + 2 * dim), BF),
            shape((tokens, q_part), BF),
            shape((tokens * q_part // dim // total, 1, total), F32),
            shape(norm.shape, BF),
            shape((plane, rows, width), block.dtype),
        ),
        in_specs=[smem, hbm, hbm, vmem, vmem, vmem],
        out_specs=(vmem, vmem, vmem, hbm, hbm),
        scratch_shapes=[
            pltpu.VMEM((total // PIC, 2 * PIC, PIC), F32),
            pltpu.VMEM((dim, total), BF),
            pltpu.VMEM((TP, total, width), BF),
            pltpu.VMEM(weight.shape, BF),
            pltpu.VMEM((total, q_part + 2 * dim), F32),
            pltpu.VMEM((2, total // 2, width), BF),
            pltpu.SemaphoreType.DMA((3 + TP,)),
            *GATHER_SCRATCH,
        ],
        cost_estimate=pl.CostEstimate(
            flops=4 * tokens * total * q_part,
            transcendentals=tokens * total * q_part // dim,
            bytes_accessed=plane * rows * width * 24,
        ),
        compiler_params=pltpu.CompilerParams(
            collective_id=ident, has_side_effects=True, vmem_limit_bytes=40 << 20
        ),
        name="attn_front_plane",
    )(starts, norm, weight, cos, sin, block)


def attn_back_kernel(
    starts_ref,
    qkv_ref,
    g_ref,
    log_ref,
    cos_ref,
    sin_ref,
    part_ref,
    grad_ref,
    sum_ref,
    bias,
    turned,
    keys_sum,
    values_sum,
    *scatter,
):
    begin, diagonal, along_x, along_y, own, fold, finish = scatter_stages(
        part_ref, sum_ref, *scatter
    )
    begin()
    total, dim = cos_ref.shape
    heads = g_ref.shape[1] // dim
    blocks = total // PIC
    scale = dim ** (-0.5)
    k_cols = slice(heads * dim, (heads + 1) * dim)
    v_cols = slice((heads + 1) * dim, (heads + 2) * dim)
    events = {(0, 1): diagonal, (0, 2): along_x, (0, 3): along_y, (1, 0): own, (2, 2): fold}

    def unturn(rows, at):
        return rows * cos_ref[at, :] - pltpu.roll(rows, dim // 2, 1) * sin_ref[at, :]

    def head_step(i, carry):
        t, h = i // heads, lax.rem(i, heads)
        base = pl.multiple_of(t * total, total)
        cols = pl.ds(pl.multiple_of(h * dim, dim), dim)

        @pl.when(h == 0)
        def _():
            turned[...] = qkv_ref[pl.ds(base, total), k_cols].T
            keys_sum[...] = jnp.zeros(keys_sum.shape, F32)
            values_sum[...] = jnp.zeros(values_sum.shape, F32)
            fill_bias(bias, starts_ref, t, blocks)

        for b in range(blocks):
            at = pl.ds(pl.multiple_of(base + b * PIC, PIC), PIC)
            count = min(b + 2, blocks) * PIC
            seen = pl.ds(base, count)
            queries, grads = qkv_ref[at, cols], g_ref[at, cols]
            scores = nt(qkv_ref[seen, k_cols], queries) * scale - log_ref[i, :, b * PIC : (b + 1) * PIC]
            probs = jnp.exp(masked(scores, bias, b))
            prob_grad = nt(qkv_ref[seen, v_cols], grads)
            mean = jnp.sum(probs * prob_grad, axis=0, keepdims=True)
            score_grad = (probs * (prob_grad - mean)).astype(BF)
            values_sum[:count, :] += nn(probs.astype(BF), grads)
            keys_sum[:count, :] += nn(score_grad, queries)
            back = nn(turned[:, :count], score_grad).T * scale
            grad_ref[at, cols] = unturn(back, pl.ds(b * PIC, PIC)).astype(BF)
            for (step, block), stage in events.items():
                if block == b:
                    pl.when(i == step)(stage)

        @pl.when(h == heads - 1)
        def _():
            rows = pl.ds(base, total)
            back = unturn(keys_sum[...] * scale, pl.ds(0, total))
            grad_ref[rows, k_cols] = back.astype(BF)
            grad_ref[rows, v_cols] = values_sum[...].astype(BF)

        return carry

    lax.fori_loop(0, log_ref.shape[0], head_step, 0)
    finish()


def attn_back_plane(starts, qkv, grads, log_total, cos, sin, partial, ident):
    plane = lax.axis_size("tp") * lax.axis_size("seq")
    rows, width = partial.shape[0] // plane, partial.shape[1]
    total, dim = cos.shape
    tokens, q_part = grads.shape
    hbm = pl.BlockSpec(memory_space=pltpu.HBM)
    vmem = pl.BlockSpec(memory_space=pltpu.VMEM)
    smem = pl.BlockSpec(memory_space=pltpu.SMEM)
    return pl.pallas_call(
        attn_back_kernel,
        out_shape=(
            jax.ShapeDtypeStruct((tokens, q_part + 2 * dim), BF),
            jax.ShapeDtypeStruct((rows, width), F32),
        ),
        in_specs=[smem] + [vmem] * 5 + [hbm],
        out_specs=(vmem, vmem),
        scratch_shapes=[
            pltpu.VMEM((total // PIC, 2 * PIC, PIC), F32),
            pltpu.VMEM((dim, total), BF),
            pltpu.VMEM((total, dim), F32),
            pltpu.VMEM((total, dim), F32),
        ]
        + scatter_scratch(rows, width, partial.dtype),
        cost_estimate=pl.CostEstimate(
            flops=10 * tokens * total * q_part,
            transcendentals=tokens * total * q_part // dim,
            bytes_accessed=plane * rows * width * 28,
        ),
        compiler_params=pltpu.CompilerParams(
            collective_id=ident, has_side_effects=True, vmem_limit_bytes=50 << 20
        ),
        name="attn_back_plane",
    )(starts, qkv, grads, log_total, cos, sin, partial.reshape(plane, rows, width))


def exchange_kernel(in_ref, out_ref, stage, local, sends, recvs):
    tp_at, seq_at, _, _, _ = plane_place()
    seq = lax.axis_size("seq")
    plane = lax.axis_size("tp") * seq
    me = tp_at * seq + seq_at
    peers = [lax.rem(me + k, plane) for k in range(1, plane)]
    devices = [at_device(peer // seq, lax.rem(peer, seq)) for peer in peers]
    enter(devices)
    copies = []
    for k, (peer, device) in enumerate(zip(peers, devices)):
        copy = remote(in_ref.at[peer], out_ref.at[me], sends.at[k], recvs.at[k], device)
        copy.start()
        copies.append(copy)
    take = pltpu.make_async_copy(in_ref.at[me], stage, local.at[0])
    take.start()
    take.wait()
    put = pltpu.make_async_copy(stage, out_ref.at[me], local.at[1])
    put.start()
    for copy in copies:
        copy.wait()
    put.wait()


def exchange_plane(blocks, ident):
    plane, rows, width = blocks.shape
    size = plane * rows * width * 2
    return pl.pallas_call(
        exchange_kernel,
        out_shape=jax.ShapeDtypeStruct(blocks.shape, blocks.dtype),
        in_specs=[pl.BlockSpec(memory_space=pltpu.HBM)],
        out_specs=pl.BlockSpec(memory_space=pltpu.HBM),
        scratch_shapes=[
            pltpu.VMEM((rows, width), blocks.dtype),
            pltpu.SemaphoreType.DMA((2,)),
            pltpu.SemaphoreType.DMA((plane - 1,)),
            pltpu.SemaphoreType.DMA((plane - 1,)),
        ],
        cost_estimate=pl.CostEstimate(flops=0, transcendentals=0, bytes_accessed=size * 20),
        compiler_params=pltpu.CompilerParams(collective_id=ident, has_side_effects=True),
        name="exchange_plane",
    )(blocks)


def slopes(wide, narrow, inner, gug):
    ff_part = inner.shape[1]

    def body(i, carry):
        at = pl.ds(i * SUB, SUB)
        gate, upward, grad = wide[at, :ff_part], wide[at, ff_part:], narrow[at, :]
        sigmoid_gate = jax.nn.sigmoid(gate)
        silu_gate = gate * sigmoid_gate
        inner[at, :] = (silu_gate * upward).astype(BF)
        slope = sigmoid_gate * (1.0 + gate * (1.0 - sigmoid_gate))
        gug[at, :ff_part] = (grad * upward * slope).astype(BF)
        gug[at, ff_part:] = (grad * silu_gate).astype(BF)
        return carry

    lax.fori_loop(0, wide.shape[0] // SUB, body, 0)


def weight_step(n, tokens, grads, gug, inner, stage, weight_ref, sems):
    slot = lax.rem(n, 2)
    block, cols = stage.shape[1:]
    ff_part = cols // 3
    count = gug.shape[0] * gug.shape[1]

    def put(m):
        return pltpu.make_async_copy(
            stage.at[lax.rem(m, 2)], weight_ref.at[pl.ds(m * block, block)], sems[0].at[sems[1] + lax.rem(m, 2)]
        )

    @pl.when(n >= 2)
    def _():
        put(n - 2).wait()

    at = pl.ds(pl.multiple_of(n * block, block), block)
    left = tokens[:, :, :, at].reshape(count, block)
    stage[slot, :, : 2 * ff_part] = tn(left, gug[...].reshape(count, 2 * ff_part)).astype(BF)
    left = grads[:, :, :, at].reshape(count, block)
    stage[slot, :, 2 * ff_part :] = tn(left, inner[...].reshape(count, ff_part)).astype(BF)
    put(n).start()
    return put


def ffn_first_kernel(
    own_ref,
    grad_ref,
    weight_hbm,
    all_ref,
    back_ref,
    out_ref,
    grads_out,
    weight,
    tokens,
    grads,
    wide,
    narrow,
    inner,
    gug,
    stage,
    columns_stage,
    sends,
    recvs,
    local,
):
    tp_at, seq_at, far, mate, _ = plane_place()
    seq = lax.axis_size("seq")
    other = 1 - tp_at
    to_x = at_device(tp_at, far)
    to_y = at_device(other, seq_at)
    to_c = at_device(tp_at, mate)
    rows, width = own_ref.shape
    pair = 2 * rows
    half = rows // 2
    block = width // 4
    ff_part = narrow.shape[2]
    gate_up, lower = slice(0, 2 * ff_part), slice(2 * ff_part, 3 * ff_part)
    enter((to_x, to_y, to_c))

    def piece(t, s, h):
        return all_ref.at[t * seq + s, pl.ds(h * half, half)]

    def own(i, h, device):
        return remote(
            own_ref.at[pl.ds(h * half, half)],
            piece(tp_at, seq_at, h),
            sends.at[i],
            recvs.at[i],
            device,
        )

    def relay(i, t, s, h, device):
        return remote(piece(t, s, h), piece(t, s, h), sends.at[i], recvs.at[i], device)

    x0, x1 = own(0, 0, to_x), own(3, 1, to_x)
    y0, y1 = own(1, 0, to_y), own(4, 1, to_y)
    c0, c1 = own(2, 0, to_c), own(5, 1, to_c)
    diag0 = relay(6, tp_at, far, 0, to_y)
    diag1 = relay(7, other, seq_at, 1, to_x)
    rx0, rx1 = relay(8, tp_at, far, 0, to_c), relay(11, tp_at, far, 1, to_c)
    ry0, ry1 = relay(9, other, seq_at, 0, to_c), relay(10, other, seq_at, 1, to_c)
    rd0, rd1 = relay(12, other, far, 0, to_c), relay(13, other, far, 1, to_c)

    def chip_rows(c):
        t = lax.rem(tp_at + c // 2, 2)
        s = lax.rem(seq_at + (seq // 2) * lax.rem(c, 2), seq)
        return pl.ds(t * seq + s - lax.rem(s, 2), 2)

    def take_tokens(c):
        return pltpu.make_async_copy(all_ref.at[chip_rows(c)], tokens.at[c], local.at[c])

    def take_grads(c):
        return pltpu.make_async_copy(grad_ref.at[chip_rows(c)], grads.at[c], local.at[4 + c])

    def put_back(c):
        return pltpu.make_async_copy(stage.at[0], back_ref.at[chip_rows(c)], local.at[8])

    def put_out(c):
        return pltpu.make_async_copy(stage.at[1], out_ref.at[chip_rows(c)], local.at[9])

    take_weight = pltpu.make_async_copy(weight_hbm, weight, local.at[12])
    mine = pltpu.make_async_copy(own_ref, all_ref.at[tp_at * seq + seq_at], local.at[13])
    for copy in (take_weight, x0, y0, c0, x1, y1, c1, mine):
        copy.start()
    for c in range(4):
        take_grads(c).start()
    take_weight.wait()

    def narrow_step(c, carry):
        take_grads(c).wait()
        narrow[c] = nn(grads[c].reshape(pair, width), weight[:, lower])
        return carry

    lax.fori_loop(0, 4, narrow_step, 0)
    mine.wait()
    c0.wait_recv()
    c1.wait_recv()
    take_tokens(0).start()

    def chip_step(c, carry):
        take_tokens(c).wait()
        wide[...] = nn(tokens[c].reshape(pair, width), weight[:, gate_up])

        @pl.when(c == 0)
        def _():
            x0.wait_recv()
            diag0.start()
            rx0.start()
            y0.wait_recv()
            ry0.start()

        @pl.when(c == 1)
        def _():
            ry0.wait_recv()
            ry1.wait_recv()
            take_tokens(2).start()

        @pl.when(c == 2)
        def _():
            diag0.wait_recv()
            rd0.start()
            diag1.wait_recv()
            rd1.start()

        slopes(wide, narrow.at[c], inner.at[c], gug.at[c])

        @pl.when(c >= 1)
        def _():
            put_back(c - 1).wait()
            put_out(c - 1).wait()

        def back_step(n, carry):
            at = pl.ds(pl.multiple_of(n * block, block), block)
            total = nt(gug[c], weight[at, gate_up]).astype(BF)
            stage[0, :, :, at] = total.reshape(2, rows, block)
            total = nt(inner[c], weight[at, lower]).astype(BF)
            stage[1, :, :, at] = total.reshape(2, rows, block)
            return carry

        lax.fori_loop(0, 4, back_step, 0)
        put_back(c).start()
        put_out(c).start()

        @pl.when(c == 0)
        def _():
            y1.wait_recv()
            diag1.start()
            ry1.start()
            x1.wait_recv()
            rx1.start()
            rx0.wait_recv()
            rx1.wait_recv()
            take_tokens(1).start()

        @pl.when(c == 2)
        def _():
            rd0.wait_recv()
            rd1.wait_recv()
            take_tokens(3).start()

        return carry

    lax.fori_loop(0, 4, chip_step, 0)

    def grads_step(n, carry):
        weight_step(n, tokens, grads, gug, inner, columns_stage, grads_out, (local, 10))
        return carry

    lax.fori_loop(0, 4, grads_step, 0)
    for copy in (x0, y0, c0, x1, y1, c1, diag0, diag1, rx0, ry0, ry1, rx1, rd0, rd1):
        copy.wait_send()
    put_back(3).wait()
    put_out(3).wait()
    for n in (2, 3):
        pltpu.make_async_copy(
            columns_stage.at[n - 2], grads_out.at[pl.ds(n * block, block)], local.at[8 + n]
        ).wait()


def ffn_second_kernel(
    all_ref,
    grad_ref,
    weight_hbm,
    back_ref,
    first_ref,
    out_ref,
    grads_out,
    sum_ref,
    weight,
    tokens,
    grads,
    wide,
    narrow,
    inner,
    gug,
    part,
    chip_in,
    far_in,
    near_in,
    stage,
    columns_stage,
    sends,
    recvs,
    local,
):
    tp_at, seq_at, far, mate, _ = plane_place()
    seq = lax.axis_size("seq")
    kind = lax.rem(seq_at, 2)
    to_x = at_device(tp_at, far)
    to_y = at_device(1 - tp_at, seq_at)
    to_c = at_device(tp_at, mate)
    rows, width = sum_ref.shape
    pair = 2 * rows
    half = rows // 2
    block = width // 4
    ff_part = narrow.shape[1]
    gate_up, lower = slice(0, 2 * ff_part), slice(2 * ff_part, 3 * ff_part)
    top, low = pl.ds(0, half), pl.ds(half, half)
    enter((to_x, to_y, to_c))

    def chip_rows(k):
        t = lax.rem(tp_at + 1 - lax.rem(k, 2), 2)
        s = lax.rem(seq_at + (seq // 2) * (1 - k // 2), seq)
        return pl.ds(t * seq + s - lax.rem(s, 2), 2)

    def take(ref, target, sem):
        return lambda k: pltpu.make_async_copy(ref.at[chip_rows(k)], target.at[k], local.at[sem + k])

    take_tokens, take_grads, take_back = (
        take(all_ref, tokens, 0),
        take(grad_ref, grads, 4),
        take(back_ref, part, 8),
    )

    def take_first(k):
        slot = lax.rem(k, 2)
        return pltpu.make_async_copy(first_ref.at[chip_rows(k)], stage.at[slot], local.at[12 + slot])

    def put_out(k):
        slot = lax.rem(k, 2)
        return pltpu.make_async_copy(stage.at[slot], out_ref.at[chip_rows(k)], local.at[14 + slot])

    def give(k):
        return remote(part.at[k, 1 - kind], chip_in.at[k], sends.at[k], recvs.at[k], to_c)

    def held(k):
        return part.at[k, kind]

    def hop(i, src, dst, device):
        return remote(src, dst, sends.at[i], recvs.at[i], device)

    d0 = hop(4, part.at[0, kind, top], far_in.at[0, top], to_x)
    d1 = hop(5, part.at[0, kind, low], far_in.at[1, low], to_y)
    x0 = hop(6, part.at[1, kind, top], near_in.at[0, top], to_x)
    y1 = hop(7, part.at[2, kind, low], near_in.at[1, low], to_y)
    y0 = hop(8, part.at[2, kind, top], near_in.at[1, top], to_y)
    x1 = hop(9, part.at[1, kind, low], near_in.at[0, low], to_x)

    def chip_sum(k):
        give(k).wait_recv()
        add_rows(held(k), (held(k), chip_in.at[k]), 0, rows, part.dtype)

    take_weight = pltpu.make_async_copy(weight_hbm, weight, local.at[18])
    take_weight.start()
    for k in range(4):
        take_grads(k).start()
        take_tokens(k).start()
        take_back(k).start()
    take_first(0).start()
    take_weight.wait()

    def chip_step(k, carry):
        slot = lax.rem(k, 2)
        take_grads(k).wait()
        narrow[...] = nn(grads[k].reshape(pair, width), weight[:, lower])

        @pl.when(k == 1)
        def _():
            chip_sum(0)
            d0.start()
            d1.start()

        @pl.when(k == 2)
        def _():
            chip_sum(1)
            x0.start()

        @pl.when(k == 3)
        def _():
            chip_sum(2)
            y1.start()
            d0.wait_recv()
            add_rows(held(2), (held(2), far_in.at[0]), 0, half, part.dtype)
            y0.start()
            d1.wait_recv()
            add_rows(held(1), (held(1), far_in.at[1]), half, half, part.dtype)
            x1.start()

        take_tokens(k).wait()
        wide[...] = nn(tokens[k].reshape(pair, width), weight[:, gate_up])
        slopes(wide, narrow, inner.at[k], gug.at[k])
        take_back(k).wait()

        def back_step(n, carry):
            at = pl.ds(pl.multiple_of(n * block, block), block)
            total = nt(gug[k], weight[at, gate_up]).reshape(2, rows, block)
            part[k, :, :, at] = (part[k, :, :, at].astype(F32) + total).astype(part.dtype)
            return carry

        lax.fori_loop(0, 4, back_step, 0)
        give(k).start()
        take_first(k).wait()

        @pl.when(k >= 1)
        def _():
            put_out(k - 1).wait()

        @pl.when(k < 3)
        def _():
            take_first(k + 1).start()

        def out_step(n, carry):
            at = pl.ds(pl.multiple_of(n * block, block), block)
            total = nt(inner[k], weight[at, lower]).reshape(2, rows, block)
            stage[slot, :, :, at] = (stage[slot, :, :, at].astype(F32) + total).astype(stage.dtype)
            return carry

        lax.fori_loop(0, 4, out_step, 0)
        put_out(k).start()
        return carry

    lax.fori_loop(0, 4, chip_step, 0)

    def grads_step(n, carry):
        weight_step(n, tokens, grads, gug, inner, columns_stage, grads_out, (local, 16))

        @pl.when(n == 0)
        def _():
            chip_sum(3)

        return carry

    lax.fori_loop(0, 4, grads_step, 0)
    x0.wait_recv()
    y0.wait_recv()
    add_rows(sum_ref, (held(3), near_in.at[0], near_in.at[1]), 0, half, sum_ref.dtype)
    y1.wait_recv()
    x1.wait_recv()
    add_rows(sum_ref, (held(3), near_in.at[0], near_in.at[1]), half, half, sum_ref.dtype)
    for k in range(4):
        give(k).wait_send()
    for copy in (d0, d1, x0, y1, y0, x1):
        copy.wait_send()
    put_out(3).wait()
    for n in (2, 3):
        pltpu.make_async_copy(
            columns_stage.at[n - 2], grads_out.at[pl.ds(n * block, block)], local.at[14 + n]
        ).wait()


def ffn_first_plane(block, grads, weight, ident):
    rows, width = block.shape
    plane = lax.axis_size("tp") * lax.axis_size("seq")
    cols = weight.shape[1]
    ff_part = cols // 3
    shape = jax.ShapeDtypeStruct
    hbm = pl.BlockSpec(memory_space=pltpu.HBM)
    vmem = pl.BlockSpec(memory_space=pltpu.VMEM)
    tokens = plane * rows
    return pl.pallas_call(
        ffn_first_kernel,
        out_shape=(
            shape((plane, rows, width), BF),
            shape((plane, rows, width), BF),
            shape((plane, rows, width), BF),
            shape((width, cols), BF),
        ),
        in_specs=[vmem, hbm, hbm],
        out_specs=(hbm, hbm, hbm, hbm),
        scratch_shapes=[
            pltpu.VMEM(weight.shape, BF),
            pltpu.VMEM((4, 2, rows, width), BF),
            pltpu.VMEM((4, 2, rows, width), BF),
            pltpu.VMEM((2 * rows, 2 * ff_part), F32),
            pltpu.VMEM((4, 2 * rows, ff_part), F32),
            pltpu.VMEM((4, 2 * rows, ff_part), BF),
            pltpu.VMEM((4, 2 * rows, 2 * ff_part), BF),
            pltpu.VMEM((2, 2, rows, width), BF),
            pltpu.VMEM((2, width // 4, cols), BF),
            pltpu.SemaphoreType.DMA((14,)),
            pltpu.SemaphoreType.DMA((14,)),
            pltpu.SemaphoreType.DMA((14,)),
        ],
        cost_estimate=pl.CostEstimate(
            flops=18 * tokens * width * ff_part,
            transcendentals=tokens * ff_part,
            bytes_accessed=22 * tokens * width,
        ),
        compiler_params=pltpu.CompilerParams(
            collective_id=ident, has_side_effects=True, vmem_limit_bytes=60 << 20
        ),
        name="ffn_first_plane",
    )(block, grads, weight)


def ffn_second_plane(block, grads, weight, back, first, ident):
    plane, rows, width = block.shape
    cols = weight.shape[1]
    ff_part = cols // 3
    shape = jax.ShapeDtypeStruct
    hbm = pl.BlockSpec(memory_space=pltpu.HBM)
    vmem = pl.BlockSpec(memory_space=pltpu.VMEM)
    tokens = plane * rows
    return pl.pallas_call(
        ffn_second_kernel,
        out_shape=(
            shape((plane, rows, width), BF),
            shape((width, cols), BF),
            shape((rows, width), F32),
        ),
        in_specs=[hbm] * 5,
        out_specs=(hbm, hbm, vmem),
        scratch_shapes=[
            pltpu.VMEM(weight.shape, BF),
            pltpu.VMEM((4, 2, rows, width), BF),
            pltpu.VMEM((4, 2, rows, width), BF),
            pltpu.VMEM((2 * rows, 2 * ff_part), F32),
            pltpu.VMEM((2 * rows, ff_part), F32),
            pltpu.VMEM((4, 2 * rows, ff_part), BF),
            pltpu.VMEM((4, 2 * rows, 2 * ff_part), BF),
            pltpu.VMEM((4, 2, rows, width), BF),
            pltpu.VMEM((4, rows, width), BF),
            pltpu.VMEM((2, rows, width), BF),
            pltpu.VMEM((2, rows, width), BF),
            pltpu.VMEM((2, 2, rows, width), BF),
            pltpu.VMEM((2, width // 4, cols), BF),
            pltpu.SemaphoreType.DMA((10,)),
            pltpu.SemaphoreType.DMA((10,)),
            pltpu.SemaphoreType.DMA((19,)),
        ],
        cost_estimate=pl.CostEstimate(
            flops=18 * tokens * width * ff_part,
            transcendentals=tokens * ff_part,
            bytes_accessed=22 * tokens * width,
        ),
        compiler_params=pltpu.CompilerParams(
            collective_id=ident, has_side_effects=True, vmem_limit_bytes=63 << 20
        ),
        name="ffn_second_plane",
    )(block, grads, weight, back, first)


def exchange_all_kernel(*refs):
    *blocks, local, sends, recvs = refs
    count = len(blocks) // 2
    tp_at, seq_at, _, _, _ = plane_place()
    seq = lax.axis_size("seq")
    plane = lax.axis_size("tp") * seq
    me = tp_at * seq + seq_at
    peers = [lax.rem(me + k, plane) for k in range(1, plane)]
    devices = [at_device(peer // seq, lax.rem(peer, seq)) for peer in peers]
    enter(devices)
    groups = []
    for n, (ref, into) in enumerate(zip(blocks[:count], blocks[count:])):
        copies = [pltpu.make_async_copy(ref.at[me], into.at[me], local.at[n])]
        for k, (peer, device) in enumerate(zip(peers, devices)):
            i = n * (plane - 1) + k
            copies.append(remote(ref.at[peer], into.at[me], sends.at[i], recvs.at[i], device))
        for copy in copies:
            copy.start()
        groups.append(copies)

    for copies in groups:
        for copy in copies:
            copy.wait()


def exchange_all_plane(blocks, ident):
    plane, count = blocks[0].shape[0], len(blocks)
    hbm = pl.BlockSpec(memory_space=pltpu.HBM)
    vmem = pl.BlockSpec(memory_space=pltpu.VMEM)
    size = sum(block.size for block in blocks) * 2
    return pl.pallas_call(
        exchange_all_kernel,
        out_shape=tuple(jax.ShapeDtypeStruct(b.shape, b.dtype) for b in blocks),
        in_specs=[hbm] * count,
        out_specs=(vmem,) * count,
        scratch_shapes=[
            pltpu.SemaphoreType.DMA((count,)),
            pltpu.SemaphoreType.DMA((count * (plane - 1),)),
            pltpu.SemaphoreType.DMA((count * (plane - 1),)),
        ],
        cost_estimate=pl.CostEstimate(flops=0, transcendentals=0, bytes_accessed=size * 20),
        compiler_params=pltpu.CompilerParams(collective_id=ident, has_side_effects=True),
        name="exchange_all_plane",
    )(*blocks)


def attn_grads_kernel(
    norm_hbm,
    grad_ref,
    columns_ref,
    weight_hbm,
    move_ref,
    grads_out,
    back_out,
    move_out,
    norm,
    weight,
    stage,
    back,
    kept,
    local,
    sends,
    recvs,
):
    tp_at, seq_at, _, _, _ = plane_place()
    seq = lax.axis_size("seq")
    plane = lax.axis_size("tp") * seq
    me = tp_at * seq + seq_at
    tokens, width = norm.shape
    cols = grad_ref.shape[1]
    block, some = width // 4, tokens // 4
    peers = [lax.rem(me + k, plane) for k in range(1, plane)]
    devices = [at_device(peer // seq, lax.rem(peer, seq)) for peer in peers]

    def at(n):
        return pl.ds(pl.multiple_of(n * block, block), block)

    def take(n):
        return pltpu.make_async_copy(norm_hbm.at[:, at(n)], norm.at[:, at(n)], local.at[n])

    def put(n):
        slot = lax.rem(n, 2)
        return pltpu.make_async_copy(stage.at[slot], grads_out.at[at(n)], local.at[4 + slot])

    def put_back(n):
        slot = lax.rem(n, 2)
        rows = pl.ds(pl.multiple_of(n * some, some), some)
        return pltpu.make_async_copy(back.at[slot], back_out.at[rows], local.at[6 + slot])

    for n in range(4):
        take(n).start()
    take_weight = pltpu.make_async_copy(weight_hbm, weight, local.at[8])
    take_weight.start()
    take_kept = pltpu.make_async_copy(move_ref.at[me], kept, local.at[9])
    put_kept = pltpu.make_async_copy(kept, move_out.at[me], local.at[10])
    take_kept.start()
    enter(devices)
    moves = [
        remote(move_ref.at[peer], move_out.at[me], sends.at[k], recvs.at[k], device)
        for k, (peer, device) in enumerate(zip(peers, devices))
    ]
    for move in moves:
        move.start()

    def grads_step(n, carry):
        @pl.when(n >= 2)
        def _():
            put(n - 2).wait()

        slot = lax.rem(n, 2)
        take(n).wait()
        stage[slot, :, :cols] = tn(norm[:, at(n)], grad_ref[...]).astype(BF)
        stage[slot, :, cols:] = columns_ref[at(n), :]
        put(n).start()
        return carry

    lax.fori_loop(0, 4, grads_step, 0)
    take_kept.wait()
    put_kept.start()
    take_weight.wait()

    def back_step(n, carry):
        @pl.when(n >= 2)
        def _():
            put_back(n - 2).wait()

        slot = lax.rem(n, 2)
        left = grad_ref[pl.ds(pl.multiple_of(n * some, some), some), :]

        def back_block(m, carry):
            back[slot, :, at(m)] = nt(left, weight[at(m), :cols]).astype(BF)
            return carry

        lax.fori_loop(0, 4, back_block, 0)
        put_back(n).start()
        return carry

    lax.fori_loop(0, 4, back_step, 0)
    for n in (2, 3):
        put(n).wait()
        put_back(n).wait()
    for move in moves:
        move.wait()
    put_kept.wait()


def attn_grads_plane(norm, grads, columns, weight, blocks, ident):
    tokens, width = norm.shape
    plane = blocks.shape[0]
    shape = jax.ShapeDtypeStruct
    hbm = pl.BlockSpec(memory_space=pltpu.HBM)
    vmem = pl.BlockSpec(memory_space=pltpu.VMEM)
    return pl.pallas_call(
        attn_grads_kernel,
        out_shape=(
            shape(weight.shape, BF),
            shape((tokens, width), BF),
            shape(blocks.shape, blocks.dtype),
        ),
        in_specs=[hbm, vmem, vmem, hbm, hbm],
        out_specs=(hbm,) * 3,
        scratch_shapes=[
            pltpu.VMEM(norm.shape, BF),
            pltpu.VMEM(weight.shape, BF),
            pltpu.VMEM((2, width // 4, weight.shape[1]), BF),
            pltpu.VMEM((2, tokens // 4, width), BF),
            pltpu.VMEM(blocks.shape[1:], blocks.dtype),
            pltpu.SemaphoreType.DMA((11,)),
            pltpu.SemaphoreType.DMA((plane - 1,)),
            pltpu.SemaphoreType.DMA((plane - 1,)),
        ],
        cost_estimate=pl.CostEstimate(
            flops=4 * tokens * width * grads.shape[1],
            transcendentals=0,
            bytes_accessed=12 * tokens * width,
        ),
        compiler_params=pltpu.CompilerParams(
            collective_id=ident, has_side_effects=True, vmem_limit_bytes=48 << 20
        ),
        name="attn_grads_plane",
    )(norm, grads, columns, weight, blocks)


def finish_kernel(
    first_in,
    second_in,
    attn_in,
    gate_weight,
    up_weight,
    query_weight,
    key_weight,
    value_weight,
    gain2_ref,
    gain1_ref,
    gate_out,
    up_out,
    down_out,
    gain2_out,
    query_out,
    key_out,
    value_out,
    out_out,
    gain1_out,
):
    plane = first_in.shape[0]
    gain = gain2_ref[...]
    sizes = [ref.shape[2] // 3 for ref in (first_in, second_in)]
    total = jnp.zeros(gain.shape, F32)
    for n, ref in enumerate((first_in, second_in)):
        size = sizes[n]
        for j in range(plane):
            start = j * sum(sizes) + n * sizes[0]
            at = slice(start, start + size)
            for k, (out, weight) in enumerate(((gate_out, gate_weight), (up_out, up_weight))):
                own = ref[j, :, k * size : (k + 1) * size].astype(F32)
                out[:, at] = own * gain
                total = total + jnp.sum(own * weight[:, at].astype(F32), axis=1, keepdims=True)
            down_out[at, :] = ref[j, :, 2 * size :].astype(F32).T
    gain2_out[...] = total

    gain = gain1_ref[...]
    q_part = query_out.shape[1] // plane
    share = plane // KV
    total = jnp.zeros(gain.shape, F32)
    for j in range(plane):
        at = slice(j * q_part, (j + 1) * q_part)
        own = attn_in[j, :, :q_part].astype(F32)
        query_out[:, at] = own * gain
        total = total + jnp.sum(own * query_weight[:, at].astype(F32), axis=1, keepdims=True)
        out_out[at, :] = attn_in[j, :, q_part + 2 * DH :].astype(F32).T
    for j in range(KV):
        at = slice(j * DH, (j + 1) * DH)
        for k, (out, weight) in enumerate(((key_out, key_weight), (value_out, value_weight))):
            cols = slice(q_part + k * DH, q_part + (k + 1) * DH)
            own = attn_in[j * share, :, cols].astype(F32)
            for i in range(1, share):
                own = own + attn_in[j * share + i, :, cols].astype(F32)
            out[:, at] = own * gain
            total = total + jnp.sum(own * weight[:, at].astype(F32), axis=1, keepdims=True)
    gain1_out[...] = total


def finish(first, second, attn, weights, gain2, gain1):
    rows = first.shape[1]
    shape = jax.ShapeDtypeStruct
    vmem = pl.BlockSpec(memory_space=pltpu.VMEM)
    gate, up, query, key, value = (shape(w.shape, F32) for w in weights)
    down, out = (shape(w.shape[::-1], F32) for w in (gate, query))
    column = shape((rows, 1), F32)
    return pl.pallas_call(
        finish_kernel,
        out_shape=(gate, up, down, column, query, key, value, out, column),
        in_specs=[vmem] * 10,
        out_specs=(vmem,) * 9,
        cost_estimate=pl.CostEstimate(
            flops=4 * gate.size, transcendentals=0, bytes_accessed=16 * gate.size
        ),
        compiler_params=pltpu.CompilerParams(vmem_limit_bytes=40 << 20),
        name="finish",
    )(first, second, attn, *weights, gain2, gain1)


def columns(matrix, parts):
    rows, cols = matrix.shape
    return jnp.transpose(matrix.reshape(rows, parts, cols // parts), (1, 0, 2))


def uncolumns(blocks):
    parts, rows, cols = blocks.shape
    return jnp.transpose(blocks, (1, 0, 2)).reshape(rows, parts * cols)


def after(value, *earlier):
    return lax.optimization_barrier((value,) + earlier)[0]


def per_device(
    layer_input,
    pic_starts,
    skip_mask,
    gain_attn,
    w_query,
    w_key,
    w_value,
    w_out,
    gain_ffn,
    w_gate,
    w_up,
    w_down,
    cotangent,
):
    _, local_len, width = layer_input.shape
    seq = lax.axis_size("seq")
    plane = lax.axis_size("tp") * seq
    total_len = local_len * seq
    heads = H // plane
    share = plane // KV
    ff_part = w_gate.shape[1] // plane
    q_part = heads * DH

    gain1 = gain_attn[:, None]
    gain2 = gain_ffn[:, None]
    wq32, wk32, wv32 = w_query.astype(F32), w_key.astype(F32), w_value.astype(F32)
    wg32, wu32 = w_gate.astype(F32), w_up.astype(F32)
    attn_pack = jnp.concatenate(
        [
            columns((wq32 * gain1).astype(BF), plane),
            jnp.repeat(columns((wk32 * gain1).astype(BF), KV), share, axis=0),
            jnp.repeat(columns((wv32 * gain1).astype(BF), KV), share, axis=0),
            columns(w_out.T, plane),
        ],
        axis=2,
    )
    attn_rows = exchange_plane(attn_pack, 0)
    attn_rows = attn_rows.reshape(-1, attn_rows.shape[2])
    attn_weight = lax.all_gather(attn_rows, "rep", axis=0, tiled=True)
    qkv_weight = attn_weight[:, : q_part + 2 * DH]
    out_weight = attn_weight[:, q_part + 2 * DH :]

    tokens = layer_input.reshape(local_len, width).astype(F32)
    keep = (1 - skip_mask).astype(F32).reshape(local_len, 1)
    upstream = cotangent.reshape(local_len, width).astype(F32)
    scale1 = rms_scale(tokens)
    norm1 = tokens * scale1

    first_part = (ff_part // 2 + DH - 1) // DH * DH
    split = ((0, first_part), (first_part, ff_part))
    ffn_parts = (
        columns((wg32 * gain2).astype(BF), plane),
        columns((wu32 * gain2).astype(BF), plane),
        columns(w_down.T, plane),
    )
    first_pack, second_pack = (
        jnp.concatenate([m[:, :, a:b] for m in ffn_parts], axis=2) for a, b in split
    )
    first_rows = exchange_plane(after(first_pack, attn_rows), 2)
    norm1_all, second_rows = spread_plane(after(norm1.astype(BF), first_rows), second_pack, 1)
    first_rows = first_rows.reshape(-1, first_rows.shape[2])
    second_rows = second_rows.reshape(-1, second_rows.shape[2])
    first_weight = lax.all_gather(first_rows, "rep", axis=0, tiled=True)
    second_weight = lax.all_gather(second_rows, "rep", axis=0, tiled=True)
    norm1_all = norm1_all.reshape(-1, width)

    other_starts = lax.ppermute(pic_starts, "tp", [(0, 1), (1, 0)])
    starts = jnp.where(
        lax.axis_index("tp") == 0,
        jnp.concatenate([pic_starts, other_starts], axis=0),
        jnp.concatenate([other_starts, pic_starts], axis=0),
    )
    positions = jnp.arange(total_len, dtype=jnp.int32)
    cos_table, sin_table = rotary_tables(positions, DH)
    cos = jnp.concatenate([cos_table, cos_table], axis=1)
    sin = jnp.concatenate([-sin_table, sin_table], axis=1)
    qkv, mixed, log_total, branch_partial, ffn_grad = attn_front_plane(
        starts, norm1_all, attn_weight, cos, sin, (keep * upstream).astype(BF), 3
    )
    branch = scatter_plane(branch_partial, 4)
    hidden = tokens + keep * branch

    scale2 = rms_scale(hidden)
    norm2 = hidden * scale2
    norm2_all, back_first, out_first, first_partial = ffn_first_plane(
        norm2.astype(BF), ffn_grad, first_weight, 5
    )
    first_sums = lax.psum_scatter(first_partial, "rep", scatter_dimension=0, tiled=True)
    out_partial, second_partial, scaled2 = ffn_second_plane(
        norm2_all, ffn_grad, second_weight, back_first, out_first, 6
    )
    second_sums = lax.psum_scatter(second_partial, "rep", scatter_dimension=0, tiled=True)
    hidden_grad = upstream + scale2 * (
        scaled2 - norm2 * jnp.mean(scaled2 * norm2, axis=-1, keepdims=True)
    )

    _, mixed_grad, out_columns = gather_mix_plane(
        (keep * hidden_grad).astype(BF), mixed, out_weight, 7
    )
    qkv_grad, ffn_out = attn_back_plane(
        starts,
        qkv,
        after(mixed_grad, first_sums),
        log_total,
        cos,
        sin,
        out_partial.reshape(-1, width),
        9,
    )
    attn_partial, scaled1_partial, first_own = attn_grads_plane(
        norm1_all,
        qkv_grad,
        out_columns,
        attn_weight,
        first_sums.reshape(plane, -1, first_sums.shape[1]),
        11,
    )
    attn_sums = lax.psum_scatter(attn_partial, "rep", scatter_dimension=0, tiled=True)
    scaled1 = scatter_plane(after(scaled1_partial, second_sums), 8)
    input_grad = hidden_grad + scale1 * (
        scaled1 - norm1 * jnp.mean(scaled1 * norm1, axis=-1, keepdims=True)
    )
    out_hidden = (hidden + keep * ffn_out).astype(BF)

    sums = exchange_all_plane(
        (
            after(second_sums, input_grad, out_hidden).reshape(plane, -1, second_sums.shape[1]),
            attn_sums.reshape(plane, -1, attn_sums.shape[1]),
        ),
        10,
    )
    weights = (w_gate, w_up, w_query, w_key, w_value)
    gate_grad, up_grad, down_grad, gain2_grad, *attn_grads = finish(first_own, *sums, weights, gain2, gain1)
    query_grad, key_grad, value_grad, out_grad, gain1_grad = attn_grads
    return (
        out_hidden[None],
        input_grad[None],
        gain1_grad[:, 0],
        query_grad,
        key_grad,
        value_grad,
        out_grad,
        gain2_grad[:, 0],
        gate_grad,
        up_grad,
        down_grad,
    )


def solution(mesh):
    devices = mesh.devices
    dp, seq = devices.shape
    inner = Mesh(devices.reshape(dp // TP, TP, seq), ("rep", "tp", "seq"))
    dps = ("rep", "tp")
    every = ("rep", "tp", "seq")
    token = P(dps, "seq", None)
    row = P(every, None)
    col = P(None, every)
    return jax.shard_map(
        per_device,
        mesh=inner,
        in_specs=(
            token,
            P(dps, None),
            P(dps, "seq"),
            P(every),
            row,
            row,
            row,
            col,
            P(every),
            row,
            row,
            col,
            token,
        ),
        out_specs=(token, token, P(every), row, row, row, col, P(every), row, row, col),
        check_vma=False,
    )
```

```python
import jax
import jax.numpy as jnp
from jax import lax
from jax.experimental import pallas as pl
from jax.experimental.pallas import tpu as pltpu
from jax.sharding import Mesh
from jax.sharding import PartitionSpec as P

H = 16
KV = 4
DH = 128
PIC = 256
NPIC = 2
EPS = 1e-05
TP = 2
BF = jnp.bfloat16
F32 = jnp.float32


def rotary_tables(positions, head_dim):
    half_dim = head_dim // 2
    inverse = 10000.0 ** (-(jnp.arange(half_dim, dtype=F32) * 2.0 / head_dim))
    angles = positions.astype(F32)[:, None] * inverse[None, :]
    return (jnp.cos(angles), jnp.sin(angles))


def rms_scale(rows):
    return lax.rsqrt(jnp.mean(rows * rows, axis=-1, keepdims=True) + EPS)


def dot(left, right, contract):
    return lax.dot_general(
        left, right, ((contract[:1], contract[1:]), ((), ())), preferred_element_type=F32
    )


def nn(left, right):
    return dot(left, right, (1, 0))


def nt(left, right):
    return dot(left, right, (1, 1))


def tn(left, right):
    return dot(left, right, (0, 0))


MESH_ID = pl.DeviceIdType.MESH
SUB = 32


def plane_place():
    tp_at = lax.axis_index("tp")
    seq_at = lax.axis_index("seq")
    seq = lax.axis_size("seq")
    half = seq // 2
    far = lax.rem(seq_at + half, seq)
    mate = seq_at + 1 - 2 * lax.rem(seq_at, 2)
    far_mate = far + 1 - 2 * lax.rem(far, 2)
    return tp_at, seq_at, far, mate, far_mate


def at_device(tp_at, seq_at):
    return (lax.axis_index("rep"), tp_at, seq_at)


def enter(devices):
    barrier = pltpu.get_barrier_semaphore()
    for device in devices:
        pl.semaphore_signal(barrier, inc=1, device_id=device, device_id_type=MESH_ID)
    pl.semaphore_wait(barrier, len(devices))


def remote(src, dst, send, recv, device):
    return pltpu.make_async_remote_copy(
        src_ref=src,
        dst_ref=dst,
        send_sem=send,
        recv_sem=recv,
        device_id=device,
        device_id_type=MESH_ID,
    )


def gather_stages(own_ref, all_ref, sends, recvs, local):
    tp_at, seq_at, far, mate, _ = plane_place()
    seq = lax.axis_size("seq")
    other = 1 - tp_at
    to_x = at_device(tp_at, far)
    to_y = at_device(other, seq_at)
    to_c = at_device(tp_at, mate)
    rows = own_ref.shape[0]
    part = rows // 2

    def piece(t, s, h):
        return all_ref.at[t * seq + s, pl.ds(h * part, part)]

    def relay(i, t, s, h, device):
        return remote(piece(t, s, h), piece(t, s, h), sends.at[i], recvs.at[i], device)

    def own(i, h, device):
        return remote(
            own_ref.at[pl.ds(h * part, part)],
            piece(tp_at, seq_at, h),
            sends.at[i],
            recvs.at[i],
            device,
        )

    x0, x1 = own(0, 0, to_x), own(3, 1, to_x)
    y0, y1 = own(1, 0, to_y), own(4, 1, to_y)
    c0, c1 = own(2, 0, to_c), own(5, 1, to_c)
    diag0 = relay(6, tp_at, far, 0, to_y)
    diag1 = relay(7, other, seq_at, 1, to_x)
    rx0, rx1 = relay(8, tp_at, far, 0, to_c), relay(11, tp_at, far, 1, to_c)
    ry0, ry1 = relay(9, other, seq_at, 0, to_c), relay(10, other, seq_at, 1, to_c)
    rd0, rd1 = relay(12, other, far, 0, to_c), relay(13, other, far, 1, to_c)
    mine = pltpu.make_async_copy(own_ref, all_ref.at[tp_at * seq + seq_at], local)

    def begin(peers=(to_x, to_y, to_c)):
        enter(peers)
        for copy in (x0, y0, c0, x1, y1, c1, mine):
            copy.start()

    def first():
        x0.wait_recv()
        diag0.start()
        rx0.start()
        y0.wait_recv()
        ry0.start()

    def second():
        y1.wait_recv()
        diag1.start()
        ry1.start()
        x1.wait_recv()
        rx1.start()

    def far_start():
        diag0.wait_recv()
        rd0.start()
        diag1.wait_recv()
        rd1.start()

    def near_arrive():
        mine.wait()
        for copy in (c0, c1, rx0, ry0, ry1, rx1):
            copy.wait_recv()

    def far_arrive():
        rd0.wait_recv()
        rd1.wait_recv()
        for copy in (x0, y0, c0, x1, y1, c1, diag0, diag1, rx0, ry0, ry1, rx1, rd0, rd1):
            copy.wait_send()

    return begin, first, second, near_arrive, far_start, far_arrive


GATHER_SCRATCH = (
    pltpu.SemaphoreType.DMA((14,)),
    pltpu.SemaphoreType.DMA((14,)),
    pltpu.SemaphoreType.DMA,
)


def gather_mix_kernel(
    own_ref, mixed_ref, weight_ref, all_ref, grad_ref, columns_ref, tokens, total, local, *gather
):
    begin, first, second, near_arrive, far_start, far_arrive = gather_stages(
        own_ref, all_ref, *gather
    )
    tp_at, seq_at, _, _, _ = plane_place()
    seq = lax.axis_size("seq")
    rows, width = own_ref.shape
    pair = 2 * rows
    block = width // 4
    begin()

    def chip_rows(c):
        t = lax.rem(tp_at + c // 2, 2)
        s = lax.rem(seq_at + (seq // 2) * lax.rem(c, 2), seq)
        return t * seq + s - lax.rem(s, 2)

    def take(c):
        return pltpu.make_async_copy(
            all_ref.at[pl.ds(chip_rows(c), 2)], tokens.at[c], local.at[c]
        )

    total[...] = jnp.zeros(total.shape, F32)

    def chip_step(c, carry):
        take(c).wait()
        at = pl.ds(pl.multiple_of(chip_rows(c) * rows, pair), pair)
        chip = nn(tokens[c].reshape(pair, width), weight_ref[...])
        grad_ref[at, :] = chip.astype(BF)

        def grads_step(n, carry):
            some = pl.ds(pl.multiple_of(n * block, block), block)
            total[some, :] += tn(tokens[c, :, :, some].reshape(pair, block), mixed_ref[at, :])
            return carry

        lax.fori_loop(0, 4, grads_step, 0)
        return carry

    first()
    second()
    near_arrive()
    for c in range(3):
        take(c).start()
    lax.fori_loop(0, 3, chip_step, 0)
    far_start()
    far_arrive()
    take(3).start()
    chip_step(3, 0)
    columns_ref[...] = total[...].astype(BF)


def gather_mix_plane(block, mixed, weight, ident):
    rows, width = block.shape
    plane = lax.axis_size("tp") * lax.axis_size("seq")
    tokens, q_part = mixed.shape
    shape = jax.ShapeDtypeStruct
    hbm = pl.BlockSpec(memory_space=pltpu.HBM)
    vmem = pl.BlockSpec(memory_space=pltpu.VMEM)
    return pl.pallas_call(
        gather_mix_kernel,
        out_shape=(
            shape((plane, rows, width), BF),
            shape((tokens, q_part), BF),
            shape((width, q_part), BF),
        ),
        in_specs=[vmem] * 3,
        out_specs=(hbm, vmem, vmem),
        scratch_shapes=[
            pltpu.VMEM((4, 2, rows, width), BF),
            pltpu.VMEM((width, q_part), F32),
            pltpu.SemaphoreType.DMA((4,)),
            *GATHER_SCRATCH,
        ],
        cost_estimate=pl.CostEstimate(
            flops=4 * tokens * width * q_part,
            transcendentals=0,
            bytes_accessed=plane * rows * width * 24,
        ),
        compiler_params=pltpu.CompilerParams(
            collective_id=ident, has_side_effects=True, vmem_limit_bytes=40 << 20
        ),
        name="gather_mix_plane",
    )(block, mixed, weight)


def spread_kernel(
    own_ref, move_ref, all_ref, move_out, kept, copies, *gather
):
    begin, first, second, *last = gather_stages(own_ref, all_ref, *gather)
    tp_at, seq_at, _, _, _ = plane_place()
    seq = lax.axis_size("seq")
    plane = lax.axis_size("tp") * seq
    me = tp_at * seq + seq_at
    peers = [lax.rem(me + k, plane) for k in range(1, plane)]
    devices = [at_device(peer // seq, lax.rem(peer, seq)) for peer in peers]
    sends, recvs, local = copies.at[0], copies.at[1], copies.at[2]
    begin(devices)
    moves = [
        remote(move_ref.at[peer], move_out.at[me], sends.at[k], recvs.at[k], device)
        for k, (peer, device) in enumerate(zip(peers, devices))
    ]
    for move in moves:
        move.start()
    take = pltpu.make_async_copy(move_ref.at[me], kept, local.at[0])
    put = pltpu.make_async_copy(kept, move_out.at[me], local.at[1])
    take.start()
    take.wait()
    put.start()
    first()
    second()
    for move in moves:
        move.wait()
    put.wait()
    for stage in last:
        stage()


def spread_plane(block, blocks, ident):
    rows, width = block.shape
    plane = lax.axis_size("tp") * lax.axis_size("seq")
    hbm = pl.BlockSpec(memory_space=pltpu.HBM)
    vmem = pl.BlockSpec(memory_space=pltpu.VMEM)
    size = plane * rows * width * 2
    return pl.pallas_call(
        spread_kernel,
        out_shape=(
            jax.ShapeDtypeStruct((plane, rows, width), block.dtype),
            jax.ShapeDtypeStruct(blocks.shape, blocks.dtype),
        ),
        in_specs=[vmem, hbm],
        out_specs=(hbm, hbm),
        scratch_shapes=[
            pltpu.VMEM(blocks.shape[1:], blocks.dtype),
            pltpu.SemaphoreType.DMA((3, plane)),
            *GATHER_SCRATCH,
        ],
        cost_estimate=pl.CostEstimate(flops=0, transcendentals=0, bytes_accessed=size * 16),
        compiler_params=pltpu.CompilerParams(collective_id=ident, has_side_effects=True),
        name="spread_plane",
    )(block, blocks)


def add_rows(target, sources, start, count, kind):
    step = min(SUB, count)

    def body(i, carry):
        at = pl.ds(start + i * step, step)
        total = sources[0][at, :].astype(F32)
        for source in sources[1:]:
            total = total + source[at, :].astype(F32)
        target[at, :] = total.astype(kind)
        return carry

    lax.fori_loop(0, count // step, body, 0)


def scatter_stages(part_ref, sum_ref, held, chip_in, far_in, near_in, loads, sends, recvs):
    tp_at, seq_at, far, mate, far_mate = plane_place()
    seq = lax.axis_size("seq")
    other = 1 - tp_at
    to_x = at_device(tp_at, far)
    to_y = at_device(other, seq_at)
    to_c = at_device(tp_at, mate)
    rows = sum_ref.shape[0]
    part = rows // 2
    top, low = pl.ds(0, part), pl.ds(part, part)
    chips = ((other, far, far_mate), (tp_at, far, far_mate), (other, seq_at, mate), (tp_at, seq_at, mate))
    gives = [
        remote(part_ref.at[t * seq + m], chip_in.at[k], sends.at[k], recvs.at[k], to_c)
        for k, (t, s, m) in enumerate(chips)
    ]
    takes = [
        pltpu.make_async_copy(part_ref.at[t * seq + s], held.at[k], loads.at[k])
        for k, (t, s, m) in enumerate(chips)
    ]

    def hop(i, src, dst, device):
        return remote(src, dst, sends.at[i], recvs.at[i], device)

    d0 = hop(4, held.at[0, top], far_in.at[0, top], to_x)
    d1 = hop(5, held.at[0, low], far_in.at[1, low], to_y)
    x0 = hop(6, held.at[1, top], near_in.at[0, top], to_x)
    y1 = hop(7, held.at[2, low], near_in.at[1, low], to_y)
    y0 = hop(8, held.at[2, top], near_in.at[1, top], to_y)
    x1 = hop(9, held.at[1, low], near_in.at[0, low], to_x)

    def begin():
        enter((to_x, to_y, to_c))
        for give, take in zip(gives, takes):
            give.start()
            take.start()

    def chip_sum(k):
        takes[k].wait()
        gives[k].wait_recv()
        add_rows(held.at[k], (held.at[k], chip_in.at[k]), 0, rows, held.dtype)

    def diagonal():
        chip_sum(0)
        d0.start()
        d1.start()

    def along_x():
        chip_sum(1)
        x0.start()

    def along_y():
        chip_sum(2)
        y1.start()

    def own():
        chip_sum(3)

    def fold():
        d0.wait_recv()
        add_rows(held.at[2], (held.at[2], far_in.at[0]), 0, part, held.dtype)
        y0.start()
        d1.wait_recv()
        add_rows(held.at[1], (held.at[1], far_in.at[1]), part, part, held.dtype)
        x1.start()

    def finish():
        x0.wait_recv()
        y0.wait_recv()
        add_rows(sum_ref, (held.at[3], near_in.at[0], near_in.at[1]), 0, part, sum_ref.dtype)
        y1.wait_recv()
        x1.wait_recv()
        add_rows(sum_ref, (held.at[3], near_in.at[0], near_in.at[1]), part, part, sum_ref.dtype)
        for copy in gives + [d0, d1, x0, y1, y0, x1]:
            copy.wait_send()

    return begin, diagonal, along_x, along_y, own, fold, finish


def scatter_kernel(*refs):
    for stage in scatter_stages(*refs):
        stage()


def scatter_scratch(rows, width, kind):
    return [
        pltpu.VMEM((4, rows, width), kind),
        pltpu.VMEM((4, rows, width), kind),
        pltpu.VMEM((2, rows, width), kind),
        pltpu.VMEM((2, rows, width), kind),
        pltpu.SemaphoreType.DMA((4,)),
        pltpu.SemaphoreType.DMA((10,)),
        pltpu.SemaphoreType.DMA((10,)),
    ]


def scatter_plane(partial, ident):
    plane = lax.axis_size("tp") * lax.axis_size("seq")
    rows, width = partial.shape[0] // plane, partial.shape[1]
    kind = partial.dtype
    size = rows * width * 2
    return pl.pallas_call(
        scatter_kernel,
        out_shape=jax.ShapeDtypeStruct((rows, width), F32),
        in_specs=[pl.BlockSpec(memory_space=pltpu.HBM)],
        out_specs=pl.BlockSpec(memory_space=pltpu.VMEM),
        scratch_shapes=scatter_scratch(rows, width, kind),
        cost_estimate=pl.CostEstimate(
            flops=0, transcendentals=0, bytes_accessed=plane * size * 14
        ),
        compiler_params=pltpu.CompilerParams(
            collective_id=ident, has_side_effects=True, vmem_limit_bytes=60 << 20
        ),
        name="scatter_plane",
    )(partial.reshape(plane, rows, width))


def fill_bias(bias, starts_ref, t, blocks):
    for b in range(blocks):
        span = min(2, blocks - b) * PIC
        k_at = lax.broadcasted_iota(jnp.int32, (span, PIC), 0) + b * PIC
        q_at = lax.broadcasted_iota(jnp.int32, (span, PIC), 1) + b * PIC
        high, below = jnp.maximum(k_at, q_at), jnp.minimum(k_at, q_at)
        allowed = k_at <= q_at
        for j in range(NPIC):
            start = starts_ref[t, j]
            allowed = allowed | ((below >= start) & (high < start + PIC))
        bias[b, :span, :] = jnp.where(allowed, 0.0, -jnp.inf)


def masked(scores, bias, b):
    late = scores[b * PIC :] + bias[b, : scores.shape[0] - b * PIC, :]
    return jnp.concatenate([scores[: b * PIC], late], axis=0) if b else late


def attn_front_kernel(
    starts_ref,
    norm_hbm,
    weight_hbm,
    cos_ref,
    sin_ref,
    own_ref,
    qkv_ref,
    mixed_ref,
    log_ref,
    out_ref,
    all_ref,
    bias,
    turned,
    norm,
    weight,
    projected,
    stage,
    local,
    *gather,
):
    begin, first, second, *last = gather_stages(own_ref, all_ref, *gather)
    total, dim = cos_ref.shape
    take_weight = pltpu.make_async_copy(weight_hbm, weight, local.at[0])
    take_weight.start()

    def take_norm(t):
        rows = pl.ds(t * total, total)
        return pltpu.make_async_copy(norm_hbm.at[rows], norm.at[t], local.at[1 + t])

    def put_out(t, n):
        rows = pl.ds(t * total + n * (total // 2), total // 2)
        return pltpu.make_async_copy(stage.at[n], out_ref.at[rows], local.at[1 + TP + n])

    for t in range(TP):
        take_norm(t).start()
    begin()
    take_weight.wait()
    heads = mixed_ref.shape[1] // dim
    blocks = total // PIC
    scale = dim ** (-0.5)
    k_cols = slice(heads * dim, (heads + 1) * dim)
    v_cols = slice((heads + 1) * dim, (heads + 2) * dim)

    def turn(rows, at):
        return rows * cos_ref[at, :] + pltpu.roll(rows, dim // 2, 1) * sin_ref[at, :]

    def head_step(i, carry):
        t, h = i // heads, lax.rem(i, heads)
        base = pl.multiple_of(t * total, total)
        cols = pl.ds(pl.multiple_of(h * dim, dim), dim)

        @pl.when(h == 0)
        def _():
            rows = pl.ds(base, total)
            take_norm(t).wait()

            def project(n, carry):
                some = pl.ds(pl.multiple_of(n * PIC, PIC), PIC)
                projected[some, :] = nn(norm[t, some, :], weight[:, : (heads + 2) * dim])
                return carry

            lax.fori_loop(0, blocks, project, 0)
            values = projected[:, v_cols].astype(BF)
            qkv_ref[rows, k_cols] = turn(projected[:, k_cols], pl.ds(0, total)).astype(BF)
            qkv_ref[rows, v_cols] = values
            turned[...] = values.T
            fill_bias(bias, starts_ref, t, blocks)

        for b in range(blocks):
            at = pl.ds(pl.multiple_of(base + b * PIC, PIC), PIC)
            count = min(b + 2, blocks) * PIC
            queries = turn(projected[b * PIC : (b + 1) * PIC, cols], pl.ds(b * PIC, PIC)).astype(BF)
            qkv_ref[at, cols] = queries
            scores = nt(qkv_ref[pl.ds(base, count), k_cols], queries) * scale
            scores = masked(scores, bias, b)
            peak = jnp.max(scores, axis=0, keepdims=True)
            weights = jnp.exp(scores - peak)
            mass = jnp.sum(weights, axis=0, keepdims=True)
            log_ref[i, :, b * PIC : (b + 1) * PIC] = peak + jnp.log(mass)
            probs = (weights * (1.0 / mass)).astype(BF)
            mixed_ref[at, cols] = nn(turned[:, :count], probs).T.astype(BF)
            if b == 0:
                pl.when(i == 1)(first)
                pl.when(i == 3)(second)

        @pl.when(h == heads - 1)
        def _():
            for n in range(2):

                @pl.when(t >= 1)
                def _():
                    put_out(t - 1, n).wait()

                rows = pl.ds(pl.multiple_of(base + n * (total // 2), total // 2), total // 2)
                block = stage.shape[2] // 4

                def out_step(m, carry):
                    some = pl.ds(pl.multiple_of(m * block, block), block)
                    partial = nt(mixed_ref[rows, :], weight[some, (heads + 2) * dim :])
                    stage[n, :, some] = partial.astype(BF)
                    return carry

                lax.fori_loop(0, 4, out_step, 0)
                put_out(t, n).start()

        return carry

    lax.fori_loop(0, log_ref.shape[0], head_step, 0)
    for stage_step in last:
        stage_step()
    for n in range(2):
        put_out(TP - 1, n).wait()


def attn_front_plane(starts, norm, weight, cos, sin, block, ident):
    rows, width = block.shape
    plane = lax.axis_size("tp") * lax.axis_size("seq")
    total, dim = cos.shape
    tokens = norm.shape[0]
    q_part = weight.shape[1] // 2 - dim
    shape = jax.ShapeDtypeStruct
    vmem = pl.BlockSpec(memory_space=pltpu.VMEM)
    smem = pl.BlockSpec(memory_space=pltpu.SMEM)
    hbm = pl.BlockSpec(memory_space=pltpu.HBM)
    return pl.pallas_call(
        attn_front_kernel,
        out_shape=(
            shape((tokens, q_part + 2 * dim), BF),
            shape((tokens, q_part), BF),
            shape((tokens * q_part // dim // total, 1, total), F32),
            shape(norm.shape, BF),
            shape((plane, rows, width), block.dtype),
        ),
        in_specs=[smem, hbm, hbm, vmem, vmem, vmem],
        out_specs=(vmem, vmem, vmem, hbm, hbm),
        scratch_shapes=[
            pltpu.VMEM((total // PIC, 2 * PIC, PIC), F32),
            pltpu.VMEM((dim, total), BF),
            pltpu.VMEM((TP, total, width), BF),
            pltpu.VMEM(weight.shape, BF),
            pltpu.VMEM((total, q_part + 2 * dim), F32),
            pltpu.VMEM((2, total // 2, width), BF),
            pltpu.SemaphoreType.DMA((3 + TP,)),
            *GATHER_SCRATCH,
        ],
        cost_estimate=pl.CostEstimate(
            flops=4 * tokens * total * q_part,
            transcendentals=tokens * total * q_part // dim,
            bytes_accessed=plane * rows * width * 24,
        ),
        compiler_params=pltpu.CompilerParams(
            collective_id=ident, has_side_effects=True, vmem_limit_bytes=40 << 20
        ),
        name="attn_front_plane",
    )(starts, norm, weight, cos, sin, block)


def attn_back_kernel(
    starts_ref,
    qkv_ref,
    g_ref,
    log_ref,
    cos_ref,
    sin_ref,
    part_ref,
    grad_ref,
    sum_ref,
    bias,
    turned,
    keys_sum,
    values_sum,
    *scatter,
):
    begin, diagonal, along_x, along_y, own, fold, finish = scatter_stages(
        part_ref, sum_ref, *scatter
    )
    begin()
    total, dim = cos_ref.shape
    heads = g_ref.shape[1] // dim
    blocks = total // PIC
    scale = dim ** (-0.5)
    k_cols = slice(heads * dim, (heads + 1) * dim)
    v_cols = slice((heads + 1) * dim, (heads + 2) * dim)
    events = {(0, 1): diagonal, (0, 2): along_x, (0, 3): along_y, (1, 0): own, (2, 2): fold}

    def unturn(rows, at):
        return rows * cos_ref[at, :] - pltpu.roll(rows, dim // 2, 1) * sin_ref[at, :]

    def head_step(i, carry):
        t, h = i // heads, lax.rem(i, heads)
        base = pl.multiple_of(t * total, total)
        cols = pl.ds(pl.multiple_of(h * dim, dim), dim)

        @pl.when(h == 0)
        def _():
            turned[...] = qkv_ref[pl.ds(base, total), k_cols].T
            keys_sum[...] = jnp.zeros(keys_sum.shape, F32)
            values_sum[...] = jnp.zeros(values_sum.shape, F32)
            fill_bias(bias, starts_ref, t, blocks)

        for b in range(blocks):
            at = pl.ds(pl.multiple_of(base + b * PIC, PIC), PIC)
            count = min(b + 2, blocks) * PIC
            seen = pl.ds(base, count)
            queries, grads = qkv_ref[at, cols], g_ref[at, cols]
            scores = nt(qkv_ref[seen, k_cols], queries) * scale - log_ref[i, :, b * PIC : (b + 1) * PIC]
            probs = jnp.exp(masked(scores, bias, b))
            prob_grad = nt(qkv_ref[seen, v_cols], grads)
            mean = jnp.sum(probs * prob_grad, axis=0, keepdims=True)
            score_grad = (probs * (prob_grad - mean)).astype(BF)
            values_sum[:count, :] += nn(probs.astype(BF), grads)
            keys_sum[:count, :] += nn(score_grad, queries)
            back = nn(turned[:, :count], score_grad).T * scale
            grad_ref[at, cols] = unturn(back, pl.ds(b * PIC, PIC)).astype(BF)
            for (step, block), stage in events.items():
                if block == b:
                    pl.when(i == step)(stage)

        @pl.when(h == heads - 1)
        def _():
            rows = pl.ds(base, total)
            back = unturn(keys_sum[...] * scale, pl.ds(0, total))
            grad_ref[rows, k_cols] = back.astype(BF)
            grad_ref[rows, v_cols] = values_sum[...].astype(BF)

        return carry

    lax.fori_loop(0, log_ref.shape[0], head_step, 0)
    finish()


def attn_back_plane(starts, qkv, grads, log_total, cos, sin, partial, ident):
    plane = lax.axis_size("tp") * lax.axis_size("seq")
    rows, width = partial.shape[0] // plane, partial.shape[1]
    total, dim = cos.shape
    tokens, q_part = grads.shape
    hbm = pl.BlockSpec(memory_space=pltpu.HBM)
    vmem = pl.BlockSpec(memory_space=pltpu.VMEM)
    smem = pl.BlockSpec(memory_space=pltpu.SMEM)
    return pl.pallas_call(
        attn_back_kernel,
        out_shape=(
            jax.ShapeDtypeStruct((tokens, q_part + 2 * dim), BF),
            jax.ShapeDtypeStruct((rows, width), F32),
        ),
        in_specs=[smem] + [vmem] * 5 + [hbm],
        out_specs=(vmem, vmem),
        scratch_shapes=[
            pltpu.VMEM((total // PIC, 2 * PIC, PIC), F32),
            pltpu.VMEM((dim, total), BF),
            pltpu.VMEM((total, dim), F32),
            pltpu.VMEM((total, dim), F32),
        ]
        + scatter_scratch(rows, width, partial.dtype),
        cost_estimate=pl.CostEstimate(
            flops=10 * tokens * total * q_part,
            transcendentals=tokens * total * q_part // dim,
            bytes_accessed=plane * rows * width * 28,
        ),
        compiler_params=pltpu.CompilerParams(
            collective_id=ident, has_side_effects=True, vmem_limit_bytes=50 << 20
        ),
        name="attn_back_plane",
    )(starts, qkv, grads, log_total, cos, sin, partial.reshape(plane, rows, width))


def exchange_kernel(in_ref, out_ref, stage, local, sends, recvs):
    tp_at, seq_at, _, _, _ = plane_place()
    seq = lax.axis_size("seq")
    plane = lax.axis_size("tp") * seq
    me = tp_at * seq + seq_at
    peers = [lax.rem(me + k, plane) for k in range(1, plane)]
    devices = [at_device(peer // seq, lax.rem(peer, seq)) for peer in peers]
    enter(devices)
    copies = []
    for k, (peer, device) in enumerate(zip(peers, devices)):
        copy = remote(in_ref.at[peer], out_ref.at[me], sends.at[k], recvs.at[k], device)
        copy.start()
        copies.append(copy)
    take = pltpu.make_async_copy(in_ref.at[me], stage, local.at[0])
    take.start()
    take.wait()
    put = pltpu.make_async_copy(stage, out_ref.at[me], local.at[1])
    put.start()
    for copy in copies:
        copy.wait()
    put.wait()


def exchange_plane(blocks, ident):
    plane, rows, width = blocks.shape
    size = plane * rows * width * 2
    return pl.pallas_call(
        exchange_kernel,
        out_shape=jax.ShapeDtypeStruct(blocks.shape, blocks.dtype),
        in_specs=[pl.BlockSpec(memory_space=pltpu.HBM)],
        out_specs=pl.BlockSpec(memory_space=pltpu.HBM),
        scratch_shapes=[
            pltpu.VMEM((rows, width), blocks.dtype),
            pltpu.SemaphoreType.DMA((2,)),
            pltpu.SemaphoreType.DMA((plane - 1,)),
            pltpu.SemaphoreType.DMA((plane - 1,)),
        ],
        cost_estimate=pl.CostEstimate(flops=0, transcendentals=0, bytes_accessed=size * 20),
        compiler_params=pltpu.CompilerParams(collective_id=ident, has_side_effects=True),
        name="exchange_plane",
    )(blocks)


def slopes(wide, narrow, inner, gug):
    ff_part = inner.shape[1]

    def body(i, carry):
        at = pl.ds(i * SUB, SUB)
        gate, upward, grad = wide[at, :ff_part], wide[at, ff_part:], narrow[at, :]
        sigmoid_gate = jax.nn.sigmoid(gate)
        silu_gate = gate * sigmoid_gate
        inner[at, :] = (silu_gate * upward).astype(BF)
        slope = sigmoid_gate * (1.0 + gate * (1.0 - sigmoid_gate))
        gug[at, :ff_part] = (grad * upward * slope).astype(BF)
        gug[at, ff_part:] = (grad * silu_gate).astype(BF)
        return carry

    lax.fori_loop(0, wide.shape[0] // SUB, body, 0)


def weight_step(n, tokens, grads, gug, inner, stage, weight_ref, sems):
    slot = lax.rem(n, 2)
    block, cols = stage.shape[1:]
    ff_part = cols // 3
    count = gug.shape[0] * gug.shape[1]

    def put(m):
        return pltpu.make_async_copy(
            stage.at[lax.rem(m, 2)], weight_ref.at[pl.ds(m * block, block)], sems[0].at[sems[1] + lax.rem(m, 2)]
        )

    @pl.when(n >= 2)
    def _():
        put(n - 2).wait()

    at = pl.ds(pl.multiple_of(n * block, block), block)
    left = tokens[:, :, :, at].reshape(count, block)
    stage[slot, :, : 2 * ff_part] = tn(left, gug[...].reshape(count, 2 * ff_part)).astype(BF)
    left = grads[:, :, :, at].reshape(count, block)
    stage[slot, :, 2 * ff_part :] = tn(left, inner[...].reshape(count, ff_part)).astype(BF)
    put(n).start()
    return put


def ffn_first_kernel(
    own_ref,
    grad_ref,
    weight_hbm,
    all_ref,
    back_ref,
    out_ref,
    grads_out,
    weight,
    tokens,
    grads,
    wide,
    narrow,
    inner,
    gug,
    stage,
    columns_stage,
    sends,
    recvs,
    local,
):
    tp_at, seq_at, far, mate, _ = plane_place()
    seq = lax.axis_size("seq")
    other = 1 - tp_at
    to_x = at_device(tp_at, far)
    to_y = at_device(other, seq_at)
    to_c = at_device(tp_at, mate)
    rows, width = own_ref.shape
    pair = 2 * rows
    half = rows // 2
    block = width // 4
    ff_part = narrow.shape[2]
    gate_up, lower = slice(0, 2 * ff_part), slice(2 * ff_part, 3 * ff_part)
    enter((to_x, to_y, to_c))

    def piece(t, s, h):
        return all_ref.at[t * seq + s, pl.ds(h * half, half)]

    def own(i, h, device):
        return remote(
            own_ref.at[pl.ds(h * half, half)],
            piece(tp_at, seq_at, h),
            sends.at[i],
            recvs.at[i],
            device,
        )

    def relay(i, t, s, h, device):
        return remote(piece(t, s, h), piece(t, s, h), sends.at[i], recvs.at[i], device)

    x0, x1 = own(0, 0, to_x), own(3, 1, to_x)
    y0, y1 = own(1, 0, to_y), own(4, 1, to_y)
    c0, c1 = own(2, 0, to_c), own(5, 1, to_c)
    diag0 = relay(6, tp_at, far, 0, to_y)
    diag1 = relay(7, other, seq_at, 1, to_x)
    rx0, rx1 = relay(8, tp_at, far, 0, to_c), relay(11, tp_at, far, 1, to_c)
    ry0, ry1 = relay(9, other, seq_at, 0, to_c), relay(10, other, seq_at, 1, to_c)
    rd0, rd1 = relay(12, other, far, 0, to_c), relay(13, other, far, 1, to_c)

    def chip_rows(c):
        t = lax.rem(tp_at + c // 2, 2)
        s = lax.rem(seq_at + (seq // 2) * lax.rem(c, 2), seq)
        return pl.ds(t * seq + s - lax.rem(s, 2), 2)

    def take_tokens(c):
        return pltpu.make_async_copy(all_ref.at[chip_rows(c)], tokens.at[c], local.at[c])

    def take_grads(c):
        return pltpu.make_async_copy(grad_ref.at[chip_rows(c)], grads.at[c], local.at[4 + c])

    def put_back(c):
        return pltpu.make_async_copy(stage.at[0], back_ref.at[chip_rows(c)], local.at[8])

    def put_out(c):
        return pltpu.make_async_copy(stage.at[1], out_ref.at[chip_rows(c)], local.at[9])

    take_weight = pltpu.make_async_copy(weight_hbm, weight, local.at[12])
    mine = pltpu.make_async_copy(own_ref, all_ref.at[tp_at * seq + seq_at], local.at[13])
    for copy in (take_weight, x0, y0, c0, x1, y1, c1, mine):
        copy.start()
    for c in range(4):
        take_grads(c).start()
    take_weight.wait()

    def narrow_step(c, carry):
        take_grads(c).wait()
        narrow[c] = nn(grads[c].reshape(pair, width), weight[:, lower])
        return carry

    lax.fori_loop(0, 4, narrow_step, 0)
    mine.wait()
    c0.wait_recv()
    c1.wait_recv()
    take_tokens(0).start()

    def chip_step(c, carry):
        take_tokens(c).wait()
        wide[...] = nn(tokens[c].reshape(pair, width), weight[:, gate_up])

        @pl.when(c == 0)
        def _():
            x0.wait_recv()
            diag0.start()
            rx0.start()
            y0.wait_recv()
            ry0.start()

        @pl.when(c == 1)
        def _():
            ry0.wait_recv()
            ry1.wait_recv()
            take_tokens(2).start()

        @pl.when(c == 2)
        def _():
            diag0.wait_recv()
            rd0.start()
            diag1.wait_recv()
            rd1.start()

        slopes(wide, narrow.at[c], inner.at[c], gug.at[c])

        @pl.when(c >= 1)
        def _():
            put_back(c - 1).wait()
            put_out(c - 1).wait()

        def back_step(n, carry):
            at = pl.ds(pl.multiple_of(n * block, block), block)
            total = nt(gug[c], weight[at, gate_up]).astype(BF)
            stage[0, :, :, at] = total.reshape(2, rows, block)
            total = nt(inner[c], weight[at, lower]).astype(BF)
            stage[1, :, :, at] = total.reshape(2, rows, block)
            return carry

        lax.fori_loop(0, 4, back_step, 0)
        put_back(c).start()
        put_out(c).start()

        @pl.when(c == 0)
        def _():
            y1.wait_recv()
            diag1.start()
            ry1.start()
            x1.wait_recv()
            rx1.start()
            rx0.wait_recv()
            rx1.wait_recv()
            take_tokens(1).start()

        @pl.when(c == 2)
        def _():
            rd0.wait_recv()
            rd1.wait_recv()
            take_tokens(3).start()

        return carry

    lax.fori_loop(0, 4, chip_step, 0)

    def grads_step(n, carry):
        weight_step(n, tokens, grads, gug, inner, columns_stage, grads_out, (local, 10))
        return carry

    lax.fori_loop(0, 4, grads_step, 0)
    for copy in (x0, y0, c0, x1, y1, c1, diag0, diag1, rx0, ry0, ry1, rx1, rd0, rd1):
        copy.wait_send()
    put_back(3).wait()
    put_out(3).wait()
    for n in (2, 3):
        pltpu.make_async_copy(
            columns_stage.at[n - 2], grads_out.at[pl.ds(n * block, block)], local.at[8 + n]
        ).wait()


def ffn_second_kernel(
    all_ref,
    grad_ref,
    weight_hbm,
    back_ref,
    first_ref,
    out_ref,
    grads_out,
    sum_ref,
    weight,
    tokens,
    grads,
    wide,
    narrow,
    inner,
    gug,
    part,
    chip_in,
    far_in,
    near_in,
    stage,
    columns_stage,
    sends,
    recvs,
    local,
):
    tp_at, seq_at, far, mate, _ = plane_place()
    seq = lax.axis_size("seq")
    kind = lax.rem(seq_at, 2)
    to_x = at_device(tp_at, far)
    to_y = at_device(1 - tp_at, seq_at)
    to_c = at_device(tp_at, mate)
    rows, width = sum_ref.shape
    pair = 2 * rows
    half = rows // 2
    block = width // 4
    ff_part = narrow.shape[1]
    gate_up, lower = slice(0, 2 * ff_part), slice(2 * ff_part, 3 * ff_part)
    top, low = pl.ds(0, half), pl.ds(half, half)
    enter((to_x, to_y, to_c))

    def chip_rows(k):
        t = lax.rem(tp_at + 1 - lax.rem(k, 2), 2)
        s = lax.rem(seq_at + (seq // 2) * (1 - k // 2), seq)
        return pl.ds(t * seq + s - lax.rem(s, 2), 2)

    def take(ref, target, sem):
        return lambda k: pltpu.make_async_copy(ref.at[chip_rows(k)], target.at[k], local.at[sem + k])

    take_tokens, take_grads, take_back = (
        take(all_ref, tokens, 0),
        take(grad_ref, grads, 4),
        take(back_ref, part, 8),
    )

    def take_first(k):
        slot = lax.rem(k, 2)
        return pltpu.make_async_copy(first_ref.at[chip_rows(k)], stage.at[slot], local.at[12 + slot])

    def put_out(k):
        slot = lax.rem(k, 2)
        return pltpu.make_async_copy(stage.at[slot], out_ref.at[chip_rows(k)], local.at[14 + slot])

    def give(k):
        return remote(part.at[k, 1 - kind], chip_in.at[k], sends.at[k], recvs.at[k], to_c)

    def held(k):
        return part.at[k, kind]

    def hop(i, src, dst, device):
        return remote(src, dst, sends.at[i], recvs.at[i], device)

    d0 = hop(4, part.at[0, kind, top], far_in.at[0, top], to_x)
    d1 = hop(5, part.at[0, kind, low], far_in.at[1, low], to_y)
    x0 = hop(6, part.at[1, kind, top], near_in.at[0, top], to_x)
    y1 = hop(7, part.at[2, kind, low], near_in.at[1, low], to_y)
    y0 = hop(8, part.at[2, kind, top], near_in.at[1, top], to_y)
    x1 = hop(9, part.at[1, kind, low], near_in.at[0, low], to_x)

    def chip_sum(k):
        give(k).wait_recv()
        add_rows(held(k), (held(k), chip_in.at[k]), 0, rows, part.dtype)

    take_weight = pltpu.make_async_copy(weight_hbm, weight, local.at[18])
    take_weight.start()
    for k in range(4):
        take_grads(k).start()
        take_tokens(k).start()
        take_back(k).start()
    take_first(0).start()
    take_weight.wait()

    def chip_step(k, carry):
        slot = lax.rem(k, 2)
        take_grads(k).wait()
        narrow[...] = nn(grads[k].reshape(pair, width), weight[:, lower])

        @pl.when(k == 1)
        def _():
            chip_sum(0)
            d0.start()
            d1.start()

        @pl.when(k == 2)
        def _():
            chip_sum(1)
            x0.start()

        @pl.when(k == 3)
        def _():
            chip_sum(2)
            y1.start()
            d0.wait_recv()
            add_rows(held(2), (held(2), far_in.at[0]), 0, half, part.dtype)
            y0.start()
            d1.wait_recv()
            add_rows(held(1), (held(1), far_in.at[1]), half, half, part.dtype)
            x1.start()

        take_tokens(k).wait()
        wide[...] = nn(tokens[k].reshape(pair, width), weight[:, gate_up])
        slopes(wide, narrow, inner.at[k], gug.at[k])
        take_back(k).wait()

        def back_step(n, carry):
            at = pl.ds(pl.multiple_of(n * block, block), block)
            total = nt(gug[k], weight[at, gate_up]).reshape(2, rows, block)
            part[k, :, :, at] = (part[k, :, :, at].astype(F32) + total).astype(part.dtype)
            return carry

        lax.fori_loop(0, 4, back_step, 0)
        give(k).start()
        take_first(k).wait()

        @pl.when(k >= 1)
        def _():
            put_out(k - 1).wait()

        @pl.when(k < 3)
        def _():
            take_first(k + 1).start()

        def out_step(n, carry):
            at = pl.ds(pl.multiple_of(n * block, block), block)
            total = nt(inner[k], weight[at, lower]).reshape(2, rows, block)
            stage[slot, :, :, at] = (stage[slot, :, :, at].astype(F32) + total).astype(stage.dtype)
            return carry

        lax.fori_loop(0, 4, out_step, 0)
        put_out(k).start()
        return carry

    lax.fori_loop(0, 4, chip_step, 0)

    def grads_step(n, carry):
        weight_step(n, tokens, grads, gug, inner, columns_stage, grads_out, (local, 16))

        @pl.when(n == 0)
        def _():
            chip_sum(3)

        return carry

    lax.fori_loop(0, 4, grads_step, 0)
    x0.wait_recv()
    y0.wait_recv()
    add_rows(sum_ref, (held(3), near_in.at[0], near_in.at[1]), 0, half, sum_ref.dtype)
    y1.wait_recv()
    x1.wait_recv()
    add_rows(sum_ref, (held(3), near_in.at[0], near_in.at[1]), half, half, sum_ref.dtype)
    for k in range(4):
        give(k).wait_send()
    for copy in (d0, d1, x0, y1, y0, x1):
        copy.wait_send()
    put_out(3).wait()
    for n in (2, 3):
        pltpu.make_async_copy(
            columns_stage.at[n - 2], grads_out.at[pl.ds(n * block, block)], local.at[14 + n]
        ).wait()


def ffn_first_plane(block, grads, weight, ident):
    rows, width = block.shape
    plane = lax.axis_size("tp") * lax.axis_size("seq")
    cols = weight.shape[1]
    ff_part = cols // 3
    shape = jax.ShapeDtypeStruct
    hbm = pl.BlockSpec(memory_space=pltpu.HBM)
    vmem = pl.BlockSpec(memory_space=pltpu.VMEM)
    tokens = plane * rows
    return pl.pallas_call(
        ffn_first_kernel,
        out_shape=(
            shape((plane, rows, width), BF),
            shape((plane, rows, width), BF),
            shape((plane, rows, width), BF),
            shape((width, cols), BF),
        ),
        in_specs=[vmem, hbm, hbm],
        out_specs=(hbm, hbm, hbm, hbm),
        scratch_shapes=[
            pltpu.VMEM(weight.shape, BF),
            pltpu.VMEM((4, 2, rows, width), BF),
            pltpu.VMEM((4, 2, rows, width), BF),
            pltpu.VMEM((2 * rows, 2 * ff_part), F32),
            pltpu.VMEM((4, 2 * rows, ff_part), F32),
            pltpu.VMEM((4, 2 * rows, ff_part), BF),
            pltpu.VMEM((4, 2 * rows, 2 * ff_part), BF),
            pltpu.VMEM((2, 2, rows, width), BF),
            pltpu.VMEM((2, width // 4, cols), BF),
            pltpu.SemaphoreType.DMA((14,)),
            pltpu.SemaphoreType.DMA((14,)),
            pltpu.SemaphoreType.DMA((14,)),
        ],
        cost_estimate=pl.CostEstimate(
            flops=18 * tokens * width * ff_part,
            transcendentals=tokens * ff_part,
            bytes_accessed=22 * tokens * width,
        ),
        compiler_params=pltpu.CompilerParams(
            collective_id=ident, has_side_effects=True, vmem_limit_bytes=60 << 20
        ),
        name="ffn_first_plane",
    )(block, grads, weight)


def ffn_second_plane(block, grads, weight, back, first, ident):
    plane, rows, width = block.shape
    cols = weight.shape[1]
    ff_part = cols // 3
    shape = jax.ShapeDtypeStruct
    hbm = pl.BlockSpec(memory_space=pltpu.HBM)
    vmem = pl.BlockSpec(memory_space=pltpu.VMEM)
    tokens = plane * rows
    return pl.pallas_call(
        ffn_second_kernel,
        out_shape=(
            shape((plane, rows, width), BF),
            shape((width, cols), BF),
            shape((rows, width), F32),
        ),
        in_specs=[hbm] * 5,
        out_specs=(hbm, hbm, vmem),
        scratch_shapes=[
            pltpu.VMEM(weight.shape, BF),
            pltpu.VMEM((4, 2, rows, width), BF),
            pltpu.VMEM((4, 2, rows, width), BF),
            pltpu.VMEM((2 * rows, 2 * ff_part), F32),
            pltpu.VMEM((2 * rows, ff_part), F32),
            pltpu.VMEM((4, 2 * rows, ff_part), BF),
            pltpu.VMEM((4, 2 * rows, 2 * ff_part), BF),
            pltpu.VMEM((4, 2, rows, width), BF),
            pltpu.VMEM((4, rows, width), BF),
            pltpu.VMEM((2, rows, width), BF),
            pltpu.VMEM((2, rows, width), BF),
            pltpu.VMEM((2, 2, rows, width), BF),
            pltpu.VMEM((2, width // 4, cols), BF),
            pltpu.SemaphoreType.DMA((10,)),
            pltpu.SemaphoreType.DMA((10,)),
            pltpu.SemaphoreType.DMA((19,)),
        ],
        cost_estimate=pl.CostEstimate(
            flops=18 * tokens * width * ff_part,
            transcendentals=tokens * ff_part,
            bytes_accessed=22 * tokens * width,
        ),
        compiler_params=pltpu.CompilerParams(
            collective_id=ident, has_side_effects=True, vmem_limit_bytes=63 << 20
        ),
        name="ffn_second_plane",
    )(block, grads, weight, back, first)


def exchange_all_kernel(*refs):
    *blocks, local, sends, recvs = refs
    count = len(blocks) // 2
    tp_at, seq_at, _, _, _ = plane_place()
    seq = lax.axis_size("seq")
    plane = lax.axis_size("tp") * seq
    me = tp_at * seq + seq_at
    peers = [lax.rem(me + k, plane) for k in range(1, plane)]
    devices = [at_device(peer // seq, lax.rem(peer, seq)) for peer in peers]
    enter(devices)
    groups = []
    for n, (ref, into) in enumerate(zip(blocks[:count], blocks[count:])):
        copies = [pltpu.make_async_copy(ref.at[me], into.at[me], local.at[n])]
        for k, (peer, device) in enumerate(zip(peers, devices)):
            i = n * (plane - 1) + k
            copies.append(remote(ref.at[peer], into.at[me], sends.at[i], recvs.at[i], device))
        for copy in copies:
            copy.start()
        groups.append(copies)

    for copies in groups:
        for copy in copies:
            copy.wait()


def exchange_all_plane(blocks, ident):
    plane, count = blocks[0].shape[0], len(blocks)
    hbm = pl.BlockSpec(memory_space=pltpu.HBM)
    vmem = pl.BlockSpec(memory_space=pltpu.VMEM)
    size = sum(block.size for block in blocks) * 2
    return pl.pallas_call(
        exchange_all_kernel,
        out_shape=tuple(jax.ShapeDtypeStruct(b.shape, b.dtype) for b in blocks),
        in_specs=[hbm] * count,
        out_specs=(vmem,) * count,
        scratch_shapes=[
            pltpu.SemaphoreType.DMA((count,)),
            pltpu.SemaphoreType.DMA((count * (plane - 1),)),
            pltpu.SemaphoreType.DMA((count * (plane - 1),)),
        ],
        cost_estimate=pl.CostEstimate(flops=0, transcendentals=0, bytes_accessed=size * 20),
        compiler_params=pltpu.CompilerParams(collective_id=ident, has_side_effects=True),
        name="exchange_all_plane",
    )(*blocks)


def attn_grads_kernel(
    norm_hbm,
    grad_ref,
    columns_ref,
    weight_hbm,
    move_ref,
    grads_out,
    back_out,
    move_out,
    norm,
    weight,
    stage,
    back,
    kept,
    local,
    sends,
    recvs,
):
    tp_at, seq_at, _, _, _ = plane_place()
    seq = lax.axis_size("seq")
    plane = lax.axis_size("tp") * seq
    me = tp_at * seq + seq_at
    tokens, width = norm.shape
    cols = grad_ref.shape[1]
    block, some = width // 4, tokens // 4
    peers = [lax.rem(me + k, plane) for k in range(1, plane)]
    devices = [at_device(peer // seq, lax.rem(peer, seq)) for peer in peers]

    def at(n):
        return pl.ds(pl.multiple_of(n * block, block), block)

    def take(n):
        return pltpu.make_async_copy(norm_hbm.at[:, at(n)], norm.at[:, at(n)], local.at[n])

    def put(n):
        slot = lax.rem(n, 2)
        return pltpu.make_async_copy(stage.at[slot], grads_out.at[at(n)], local.at[4 + slot])

    def put_back(n):
        slot = lax.rem(n, 2)
        rows = pl.ds(pl.multiple_of(n * some, some), some)
        return pltpu.make_async_copy(back.at[slot], back_out.at[rows], local.at[6 + slot])

    for n in range(4):
        take(n).start()
    take_weight = pltpu.make_async_copy(weight_hbm, weight, local.at[8])
    take_weight.start()
    take_kept = pltpu.make_async_copy(move_ref.at[me], kept, local.at[9])
    put_kept = pltpu.make_async_copy(kept, move_out.at[me], local.at[10])
    take_kept.start()
    enter(devices)
    moves = [
        remote(move_ref.at[peer], move_out.at[me], sends.at[k], recvs.at[k], device)
        for k, (peer, device) in enumerate(zip(peers, devices))
    ]
    for move in moves:
        move.start()

    def grads_step(n, carry):
        @pl.when(n >= 2)
        def _():
            put(n - 2).wait()

        slot = lax.rem(n, 2)
        take(n).wait()
        stage[slot, :, :cols] = tn(norm[:, at(n)], grad_ref[...]).astype(BF)
        stage[slot, :, cols:] = columns_ref[at(n), :]
        put(n).start()
        return carry

    lax.fori_loop(0, 4, grads_step, 0)
    take_kept.wait()
    put_kept.start()
    take_weight.wait()

    def back_step(n, carry):
        @pl.when(n >= 2)
        def _():
            put_back(n - 2).wait()

        slot = lax.rem(n, 2)
        left = grad_ref[pl.ds(pl.multiple_of(n * some, some), some), :]

        def back_block(m, carry):
            back[slot, :, at(m)] = nt(left, weight[at(m), :cols]).astype(BF)
            return carry

        lax.fori_loop(0, 4, back_block, 0)
        put_back(n).start()
        return carry

    lax.fori_loop(0, 4, back_step, 0)
    for n in (2, 3):
        put(n).wait()
        put_back(n).wait()
    for move in moves:
        move.wait()
    put_kept.wait()


def attn_grads_plane(norm, grads, columns, weight, blocks, ident):
    tokens, width = norm.shape
    plane = blocks.shape[0]
    shape = jax.ShapeDtypeStruct
    hbm = pl.BlockSpec(memory_space=pltpu.HBM)
    vmem = pl.BlockSpec(memory_space=pltpu.VMEM)
    return pl.pallas_call(
        attn_grads_kernel,
        out_shape=(
            shape(weight.shape, BF),
            shape((tokens, width), BF),
            shape(blocks.shape, blocks.dtype),
        ),
        in_specs=[hbm, vmem, vmem, hbm, hbm],
        out_specs=(hbm,) * 3,
        scratch_shapes=[
            pltpu.VMEM(norm.shape, BF),
            pltpu.VMEM(weight.shape, BF),
            pltpu.VMEM((2, width // 4, weight.shape[1]), BF),
            pltpu.VMEM((2, tokens // 4, width), BF),
            pltpu.VMEM(blocks.shape[1:], blocks.dtype),
            pltpu.SemaphoreType.DMA((11,)),
            pltpu.SemaphoreType.DMA((plane - 1,)),
            pltpu.SemaphoreType.DMA((plane - 1,)),
        ],
        cost_estimate=pl.CostEstimate(
            flops=4 * tokens * width * grads.shape[1],
            transcendentals=0,
            bytes_accessed=12 * tokens * width,
        ),
        compiler_params=pltpu.CompilerParams(
            collective_id=ident, has_side_effects=True, vmem_limit_bytes=48 << 20
        ),
        name="attn_grads_plane",
    )(norm, grads, columns, weight, blocks)


def finish_kernel(
    first_in,
    second_in,
    attn_in,
    gate_weight,
    up_weight,
    query_weight,
    key_weight,
    value_weight,
    gain2_ref,
    gain1_ref,
    gate_out,
    up_out,
    down_out,
    gain2_out,
    query_out,
    key_out,
    value_out,
    out_out,
    gain1_out,
):
    plane = first_in.shape[0]
    gain = gain2_ref[...]
    sizes = [ref.shape[2] // 3 for ref in (first_in, second_in)]
    total = jnp.zeros(gain.shape, F32)
    for n, ref in enumerate((first_in, second_in)):
        size = sizes[n]
        for j in range(plane):
            start = j * sum(sizes) + n * sizes[0]
            at = slice(start, start + size)
            for k, (out, weight) in enumerate(((gate_out, gate_weight), (up_out, up_weight))):
                own = ref[j, :, k * size : (k + 1) * size].astype(F32)
                out[:, at] = own * gain
                total = total + jnp.sum(own * weight[:, at].astype(F32), axis=1, keepdims=True)
            down_out[:, at] = ref[j, :, 2 * size :].astype(F32)
    gain2_out[...] = total

    gain = gain1_ref[...]
    q_part = query_out.shape[1] // plane
    share = plane // KV
    total = jnp.zeros(gain.shape, F32)
    for j in range(plane):
        at = slice(j * q_part, (j + 1) * q_part)
        own = attn_in[j, :, :q_part].astype(F32)
        query_out[:, at] = own * gain
        total = total + jnp.sum(own * query_weight[:, at].astype(F32), axis=1, keepdims=True)
        out_out[:, at] = attn_in[j, :, q_part + 2 * DH :].astype(F32)
    for j in range(KV):
        at = slice(j * DH, (j + 1) * DH)
        for k, (out, weight) in enumerate(((key_out, key_weight), (value_out, value_weight))):
            cols = slice(q_part + k * DH, q_part + (k + 1) * DH)
            own = attn_in[j * share, :, cols].astype(F32)
            for i in range(1, share):
                own = own + attn_in[j * share + i, :, cols].astype(F32)
            out[:, at] = own * gain
            total = total + jnp.sum(own * weight[:, at].astype(F32), axis=1, keepdims=True)
    gain1_out[...] = total


def finish(first, second, attn, weights, gain2, gain1):
    rows = first.shape[1]
    shape = jax.ShapeDtypeStruct
    vmem = pl.BlockSpec(memory_space=pltpu.VMEM)
    gate, up, query, key, value = (shape(w.shape, F32) for w in weights)
    column = shape((rows, 1), F32)
    return pl.pallas_call(
        finish_kernel,
        out_shape=(gate, up, gate, column, query, key, value, query, column),
        in_specs=[vmem] * 10,
        out_specs=(vmem,) * 9,
        cost_estimate=pl.CostEstimate(
            flops=4 * gate.size, transcendentals=0, bytes_accessed=16 * gate.size
        ),
        compiler_params=pltpu.CompilerParams(vmem_limit_bytes=40 << 20),
        name="finish",
    )(first, second, attn, *weights, gain2, gain1)


def columns(matrix, parts):
    rows, cols = matrix.shape
    return jnp.transpose(matrix.reshape(rows, parts, cols // parts), (1, 0, 2))


def uncolumns(blocks):
    parts, rows, cols = blocks.shape
    return jnp.transpose(blocks, (1, 0, 2)).reshape(rows, parts * cols)


def after(value, *earlier):
    return lax.optimization_barrier((value,) + earlier)[0]


def per_device(
    layer_input,
    pic_starts,
    skip_mask,
    gain_attn,
    w_query,
    w_key,
    w_value,
    w_out,
    gain_ffn,
    w_gate,
    w_up,
    w_down,
    cotangent,
):
    _, local_len, width = layer_input.shape
    seq = lax.axis_size("seq")
    plane = lax.axis_size("tp") * seq
    total_len = local_len * seq
    heads = H // plane
    share = plane // KV
    ff_part = w_gate.shape[1] // plane
    q_part = heads * DH

    gain1 = gain_attn[:, None]
    gain2 = gain_ffn[:, None]
    wq32, wk32, wv32 = w_query.astype(F32), w_key.astype(F32), w_value.astype(F32)
    wg32, wu32 = w_gate.astype(F32), w_up.astype(F32)
    attn_pack = jnp.concatenate(
        [
            columns((wq32 * gain1).astype(BF), plane),
            jnp.repeat(columns((wk32 * gain1).astype(BF), KV), share, axis=0),
            jnp.repeat(columns((wv32 * gain1).astype(BF), KV), share, axis=0),
            columns(w_out.T, plane),
        ],
        axis=2,
    )
    attn_rows = exchange_plane(attn_pack, 0)
    attn_rows = attn_rows.reshape(-1, attn_rows.shape[2])
    attn_weight = lax.all_gather(attn_rows, "rep", axis=0, tiled=True)
    qkv_weight = attn_weight[:, : q_part + 2 * DH]
    out_weight = attn_weight[:, q_part + 2 * DH :]

    tokens = layer_input.reshape(local_len, width).astype(F32)
    keep = (1 - skip_mask).astype(F32).reshape(local_len, 1)
    upstream = cotangent.reshape(local_len, width).astype(F32)
    scale1 = rms_scale(tokens)
    norm1 = tokens * scale1

    first_part = (ff_part // 2 + DH - 1) // DH * DH
    split = ((0, first_part), (first_part, ff_part))
    ffn_parts = (
        columns((wg32 * gain2).astype(BF), plane),
        columns((wu32 * gain2).astype(BF), plane),
        columns(w_down.T, plane),
    )
    first_pack, second_pack = (
        jnp.concatenate([m[:, :, a:b] for m in ffn_parts], axis=2) for a, b in split
    )
    first_rows = exchange_plane(after(first_pack, attn_rows), 2)
    norm1_all, second_rows = spread_plane(after(norm1.astype(BF), first_rows), second_pack, 1)
    first_rows = first_rows.reshape(-1, first_rows.shape[2])
    second_rows = second_rows.reshape(-1, second_rows.shape[2])
    first_weight = lax.all_gather(first_rows, "rep", axis=0, tiled=True)
    second_weight = lax.all_gather(second_rows, "rep", axis=0, tiled=True)
    norm1_all = norm1_all.reshape(-1, width)

    other_starts = lax.ppermute(pic_starts, "tp", [(0, 1), (1, 0)])
    starts = jnp.where(
        lax.axis_index("tp") == 0,
        jnp.concatenate([pic_starts, other_starts], axis=0),
        jnp.concatenate([other_starts, pic_starts], axis=0),
    )
    positions = jnp.arange(total_len, dtype=jnp.int32)
    cos_table, sin_table = rotary_tables(positions, DH)
    cos = jnp.concatenate([cos_table, cos_table], axis=1)
    sin = jnp.concatenate([-sin_table, sin_table], axis=1)
    qkv, mixed, log_total, branch_partial, ffn_grad = attn_front_plane(
        starts, norm1_all, attn_weight, cos, sin, (keep * upstream).astype(BF), 3
    )
    branch = scatter_plane(branch_partial, 4)
    hidden = tokens + keep * branch

    scale2 = rms_scale(hidden)
    norm2 = hidden * scale2
    norm2_all, back_first, out_first, first_partial = ffn_first_plane(
        norm2.astype(BF), ffn_grad, first_weight, 5
    )
    first_sums = lax.psum_scatter(first_partial, "rep", scatter_dimension=0, tiled=True)
    out_partial, second_partial, scaled2 = ffn_second_plane(
        norm2_all, ffn_grad, second_weight, back_first, out_first, 6
    )
    second_sums = lax.psum_scatter(second_partial, "rep", scatter_dimension=0, tiled=True)
    hidden_grad = upstream + scale2 * (
        scaled2 - norm2 * jnp.mean(scaled2 * norm2, axis=-1, keepdims=True)
    )

    _, mixed_grad, out_columns = gather_mix_plane(
        (keep * hidden_grad).astype(BF), mixed, out_weight, 7
    )
    qkv_grad, ffn_out = attn_back_plane(
        starts,
        qkv,
        after(mixed_grad, first_sums),
        log_total,
        cos,
        sin,
        out_partial.reshape(-1, width),
        9,
    )
    attn_partial, scaled1_partial, first_own = attn_grads_plane(
        norm1_all,
        qkv_grad,
        out_columns,
        attn_weight,
        first_sums.reshape(plane, -1, first_sums.shape[1]),
        11,
    )
    attn_sums = lax.psum_scatter(attn_partial, "rep", scatter_dimension=0, tiled=True)
    scaled1 = scatter_plane(after(scaled1_partial, second_sums), 8)
    input_grad = hidden_grad + scale1 * (
        scaled1 - norm1 * jnp.mean(scaled1 * norm1, axis=-1, keepdims=True)
    )
    out_hidden = (hidden + keep * ffn_out).astype(BF)

    (second_own,) = exchange_all_plane(
        (after(second_sums, scaled1).reshape(plane, -1, second_sums.shape[1]),), 10
    )
    (attn_own,) = exchange_all_plane(
        (after(attn_sums, second_own, input_grad, out_hidden).reshape(plane, -1, attn_sums.shape[1]),),
        12,
    )
    weights = (w_gate, w_up, w_query, w_key, w_value)
    gate_grad, up_grad, down_grad, gain2_grad, *attn_grads = finish(
        first_own, second_own, attn_own, weights, gain2, gain1
    )
    query_grad, key_grad, value_grad, out_grad, gain1_grad = attn_grads
    return (
        out_hidden[None],
        input_grad[None],
        gain1_grad[:, 0],
        query_grad,
        key_grad,
        value_grad,
        out_grad.T,
        gain2_grad[:, 0],
        gate_grad,
        up_grad,
        down_grad.T,
    )


def solution(mesh):
    devices = mesh.devices
    dp, seq = devices.shape
    inner = Mesh(devices.reshape(dp // TP, TP, seq), ("rep", "tp", "seq"))
    dps = ("rep", "tp")
    every = ("rep", "tp", "seq")
    token = P(dps, "seq", None)
    row = P(every, None)
    col = P(None, every)
    return jax.shard_map(
        per_device,
        mesh=inner,
        in_specs=(
            token,
            P(dps, None),
            P(dps, "seq"),
            P(every),
            row,
            row,
            row,
            col,
            P(every),
            row,
            row,
            col,
            token,
        ),
        out_specs=(token, token, P(every), row, row, row, col, P(every), row, row, col),
        check_vma=False,
    )
```

```python
import jax
import jax.numpy as jnp
import numpy as np
from jax import lax
from jax.experimental import pallas as pl
from jax.experimental.pallas import tpu as pltpu
from jax.sharding import Mesh
from jax.sharding import PartitionSpec as P

H = 16
KV = 4
DH = 128
PIC = 256
NPIC = 2
EPS = 1e-05
TP = 2
BF = jnp.bfloat16
F32 = jnp.float32


def rotary_tables(total, head_dim):
    half = np.arange(head_dim // 2, dtype=np.float32)
    inverse = np.float32(10000.0) ** (half * np.float32(-2.0 / head_dim))
    angles = np.arange(total, dtype=np.float32)[:, None] * inverse[None, :]
    cos, sin = np.cos(angles), np.sin(angles)
    return np.concatenate([cos, cos], axis=1), np.concatenate([-sin, sin], axis=1)


def rms_scale(rows):
    return lax.rsqrt(jnp.mean(rows * rows, axis=-1, keepdims=True) + EPS)


def dot(left, right, contract):
    return lax.dot_general(
        left, right, ((contract[:1], contract[1:]), ((), ())), preferred_element_type=F32
    )


def nn(left, right):
    return dot(left, right, (1, 0))


def nt(left, right):
    return dot(left, right, (1, 1))


def tn(left, right):
    return dot(left, right, (0, 0))


MESH_ID = pl.DeviceIdType.MESH
SUB = 32


def plane_place():
    tp_at = lax.axis_index("tp")
    seq_at = lax.axis_index("seq")
    seq = lax.axis_size("seq")
    half = seq // 2
    far = lax.rem(seq_at + half, seq)
    mate = seq_at + 1 - 2 * lax.rem(seq_at, 2)
    far_mate = far + 1 - 2 * lax.rem(far, 2)
    return tp_at, seq_at, far, mate, far_mate


def at_device(tp_at, seq_at):
    return (lax.axis_index("rep"), tp_at, seq_at)


def enter(devices):
    barrier = pltpu.get_barrier_semaphore()
    for device in devices:
        pl.semaphore_signal(barrier, inc=1, device_id=device, device_id_type=MESH_ID)
    pl.semaphore_wait(barrier, len(devices))


def remote(src, dst, send, recv, device):
    return pltpu.make_async_remote_copy(
        src_ref=src,
        dst_ref=dst,
        send_sem=send,
        recv_sem=recv,
        device_id=device,
        device_id_type=MESH_ID,
    )


def gather_stages(own_ref, all_ref, sends, recvs, local):
    tp_at, seq_at, far, mate, _ = plane_place()
    seq = lax.axis_size("seq")
    other = 1 - tp_at
    to_x = at_device(tp_at, far)
    to_y = at_device(other, seq_at)
    to_c = at_device(tp_at, mate)
    rows = own_ref.shape[0]
    part = rows // 2

    def piece(t, s, h):
        return all_ref.at[t * seq + s, pl.ds(h * part, part)]

    def relay(i, t, s, h, device):
        return remote(piece(t, s, h), piece(t, s, h), sends.at[i], recvs.at[i], device)

    def own(i, h, device):
        return remote(
            own_ref.at[pl.ds(h * part, part)],
            piece(tp_at, seq_at, h),
            sends.at[i],
            recvs.at[i],
            device,
        )

    x0, x1 = own(0, 0, to_x), own(3, 1, to_x)
    y0, y1 = own(1, 0, to_y), own(4, 1, to_y)
    c0, c1 = own(2, 0, to_c), own(5, 1, to_c)
    diag0 = relay(6, tp_at, far, 0, to_y)
    diag1 = relay(7, other, seq_at, 1, to_x)
    rx0, rx1 = relay(8, tp_at, far, 0, to_c), relay(11, tp_at, far, 1, to_c)
    ry0, ry1 = relay(9, other, seq_at, 0, to_c), relay(10, other, seq_at, 1, to_c)
    rd0, rd1 = relay(12, other, far, 0, to_c), relay(13, other, far, 1, to_c)
    mine = pltpu.make_async_copy(own_ref, all_ref.at[tp_at * seq + seq_at], local)

    def begin(peers=(to_x, to_y, to_c)):
        enter(peers)
        for copy in (x0, y0, c0, x1, y1, c1, mine):
            copy.start()

    def first():
        x0.wait_recv()
        diag0.start()
        rx0.start()
        y0.wait_recv()
        ry0.start()

    def second():
        y1.wait_recv()
        diag1.start()
        ry1.start()
        x1.wait_recv()
        rx1.start()

    def far_start():
        diag0.wait_recv()
        rd0.start()
        diag1.wait_recv()
        rd1.start()

    def near_arrive():
        mine.wait()
        for copy in (c0, c1, rx0, ry0, ry1, rx1):
            copy.wait_recv()

    def far_arrive():
        rd0.wait_recv()
        rd1.wait_recv()
        for copy in (x0, y0, c0, x1, y1, c1, diag0, diag1, rx0, ry0, ry1, rx1, rd0, rd1):
            copy.wait_send()

    return begin, first, second, near_arrive, far_start, far_arrive


GATHER_SCRATCH = (
    pltpu.SemaphoreType.DMA((14,)),
    pltpu.SemaphoreType.DMA((14,)),
    pltpu.SemaphoreType.DMA,
)


def gather_mix_kernel(
    own_ref, mixed_ref, weight_ref, all_ref, grad_ref, columns_ref, tokens, total, local, *gather
):
    begin, first, second, near_arrive, far_start, far_arrive = gather_stages(
        own_ref, all_ref, *gather
    )
    tp_at, seq_at, _, _, _ = plane_place()
    seq = lax.axis_size("seq")
    rows, width = own_ref.shape
    pair = 2 * rows
    block = width // 4
    begin()

    def chip_rows(c):
        t = lax.rem(tp_at + c // 2, 2)
        s = lax.rem(seq_at + (seq // 2) * lax.rem(c, 2), seq)
        return t * seq + s - lax.rem(s, 2)

    def take(c):
        return pltpu.make_async_copy(
            all_ref.at[pl.ds(chip_rows(c), 2)], tokens.at[c], local.at[c]
        )

    total[...] = jnp.zeros(total.shape, F32)

    def chip_step(c, carry):
        take(c).wait()
        at = pl.ds(pl.multiple_of(chip_rows(c) * rows, pair), pair)
        chip = nn(tokens[c].reshape(pair, width), weight_ref[...])
        grad_ref[at, :] = chip.astype(BF)

        def grads_step(n, carry):
            some = pl.ds(pl.multiple_of(n * block, block), block)
            total[some, :] += tn(tokens[c, :, :, some].reshape(pair, block), mixed_ref[at, :])
            return carry

        lax.fori_loop(0, 4, grads_step, 0)
        return carry

    first()
    second()
    near_arrive()
    for c in range(3):
        take(c).start()
    lax.fori_loop(0, 3, chip_step, 0)
    far_start()
    far_arrive()
    take(3).start()
    chip_step(3, 0)
    columns_ref[...] = total[...].astype(BF)


def gather_mix_plane(block, mixed, weight, ident):
    rows, width = block.shape
    plane = lax.axis_size("tp") * lax.axis_size("seq")
    tokens, q_part = mixed.shape
    shape = jax.ShapeDtypeStruct
    hbm = pl.BlockSpec(memory_space=pltpu.HBM)
    vmem = pl.BlockSpec(memory_space=pltpu.VMEM)
    return pl.pallas_call(
        gather_mix_kernel,
        out_shape=(
            shape((plane, rows, width), BF),
            shape((tokens, q_part), BF),
            shape((width, q_part), BF),
        ),
        in_specs=[vmem] * 3,
        out_specs=(hbm, vmem, vmem),
        scratch_shapes=[
            pltpu.VMEM((4, 2, rows, width), BF),
            pltpu.VMEM((width, q_part), F32),
            pltpu.SemaphoreType.DMA((4,)),
            *GATHER_SCRATCH,
        ],
        cost_estimate=pl.CostEstimate(
            flops=4 * tokens * width * q_part,
            transcendentals=0,
            bytes_accessed=plane * rows * width * 24,
        ),
        compiler_params=pltpu.CompilerParams(
            collective_id=ident, has_side_effects=True, vmem_limit_bytes=40 << 20
        ),
        name="gather_mix_plane",
    )(block, mixed, weight)


def spread_kernel(
    own_ref, move_ref, all_ref, move_out, kept, copies, *gather
):
    begin, first, second, *last = gather_stages(own_ref, all_ref, *gather)
    tp_at, seq_at, _, _, _ = plane_place()
    seq = lax.axis_size("seq")
    plane = lax.axis_size("tp") * seq
    me = tp_at * seq + seq_at
    peers = [lax.rem(me + k, plane) for k in range(1, plane)]
    devices = [at_device(peer // seq, lax.rem(peer, seq)) for peer in peers]
    sends, recvs, local = copies.at[0], copies.at[1], copies.at[2]
    begin(devices)
    moves = [
        remote(move_ref.at[peer], move_out.at[me], sends.at[k], recvs.at[k], device)
        for k, (peer, device) in enumerate(zip(peers, devices))
    ]
    for move in moves:
        move.start()
    take = pltpu.make_async_copy(move_ref.at[me], kept, local.at[0])
    put = pltpu.make_async_copy(kept, move_out.at[me], local.at[1])
    take.start()
    take.wait()
    put.start()
    first()
    second()
    for move in moves:
        move.wait()
    put.wait()
    for stage in last:
        stage()


def spread_plane(block, blocks, ident):
    rows, width = block.shape
    plane = lax.axis_size("tp") * lax.axis_size("seq")
    hbm = pl.BlockSpec(memory_space=pltpu.HBM)
    vmem = pl.BlockSpec(memory_space=pltpu.VMEM)
    size = plane * rows * width * 2
    return pl.pallas_call(
        spread_kernel,
        out_shape=(
            jax.ShapeDtypeStruct((plane, rows, width), block.dtype),
            jax.ShapeDtypeStruct(blocks.shape, blocks.dtype),
        ),
        in_specs=[vmem, hbm],
        out_specs=(hbm, hbm),
        scratch_shapes=[
            pltpu.VMEM(blocks.shape[1:], blocks.dtype),
            pltpu.SemaphoreType.DMA((3, plane)),
            *GATHER_SCRATCH,
        ],
        cost_estimate=pl.CostEstimate(flops=0, transcendentals=0, bytes_accessed=size * 16),
        compiler_params=pltpu.CompilerParams(collective_id=ident, has_side_effects=True),
        name="spread_plane",
    )(block, blocks)


def add_rows(target, sources, start, count, kind):
    step = min(SUB, count)

    def body(i, carry):
        at = pl.ds(start + i * step, step)
        total = sources[0][at, :].astype(F32)
        for source in sources[1:]:
            total = total + source[at, :].astype(F32)
        target[at, :] = total.astype(kind)
        return carry

    lax.fori_loop(0, count // step, body, 0)


def scatter_stages(part_ref, sum_ref, held, chip_in, far_in, near_in, loads, sends, recvs):
    tp_at, seq_at, far, mate, far_mate = plane_place()
    seq = lax.axis_size("seq")
    other = 1 - tp_at
    to_x = at_device(tp_at, far)
    to_y = at_device(other, seq_at)
    to_c = at_device(tp_at, mate)
    rows = sum_ref.shape[0]
    part = rows // 2
    top, low = pl.ds(0, part), pl.ds(part, part)
    chips = ((other, far, far_mate), (tp_at, far, far_mate), (other, seq_at, mate), (tp_at, seq_at, mate))
    gives = [
        remote(part_ref.at[t * seq + m], chip_in.at[k], sends.at[k], recvs.at[k], to_c)
        for k, (t, s, m) in enumerate(chips)
    ]
    takes = [
        pltpu.make_async_copy(part_ref.at[t * seq + s], held.at[k], loads.at[k])
        for k, (t, s, m) in enumerate(chips)
    ]

    def hop(i, src, dst, device):
        return remote(src, dst, sends.at[i], recvs.at[i], device)

    d0 = hop(4, held.at[0, top], far_in.at[0, top], to_x)
    d1 = hop(5, held.at[0, low], far_in.at[1, low], to_y)
    x0 = hop(6, held.at[1, top], near_in.at[0, top], to_x)
    y1 = hop(7, held.at[2, low], near_in.at[1, low], to_y)
    y0 = hop(8, held.at[2, top], near_in.at[1, top], to_y)
    x1 = hop(9, held.at[1, low], near_in.at[0, low], to_x)

    def begin():
        enter((to_x, to_y, to_c))
        for give, take in zip(gives, takes):
            give.start()
            take.start()

    def chip_sum(k):
        takes[k].wait()
        gives[k].wait_recv()
        add_rows(held.at[k], (held.at[k], chip_in.at[k]), 0, rows, held.dtype)

    def diagonal():
        chip_sum(0)
        d0.start()
        d1.start()

    def along_x():
        chip_sum(1)
        x0.start()

    def along_y():
        chip_sum(2)
        y1.start()

    def own():
        chip_sum(3)

    def fold():
        d0.wait_recv()
        add_rows(held.at[2], (held.at[2], far_in.at[0]), 0, part, held.dtype)
        y0.start()
        d1.wait_recv()
        add_rows(held.at[1], (held.at[1], far_in.at[1]), part, part, held.dtype)
        x1.start()

    def finish():
        x0.wait_recv()
        y0.wait_recv()
        add_rows(sum_ref, (held.at[3], near_in.at[0], near_in.at[1]), 0, part, sum_ref.dtype)
        y1.wait_recv()
        x1.wait_recv()
        add_rows(sum_ref, (held.at[3], near_in.at[0], near_in.at[1]), part, part, sum_ref.dtype)
        for copy in gives + [d0, d1, x0, y1, y0, x1]:
            copy.wait_send()

    return begin, diagonal, along_x, along_y, own, fold, finish


def scatter_kernel(*refs):
    for stage in scatter_stages(*refs):
        stage()


def scatter_scratch(rows, width, kind):
    return [
        pltpu.VMEM((4, rows, width), kind),
        pltpu.VMEM((4, rows, width), kind),
        pltpu.VMEM((2, rows, width), kind),
        pltpu.VMEM((2, rows, width), kind),
        pltpu.SemaphoreType.DMA((4,)),
        pltpu.SemaphoreType.DMA((10,)),
        pltpu.SemaphoreType.DMA((10,)),
    ]


def scatter_plane(partial, ident):
    plane = lax.axis_size("tp") * lax.axis_size("seq")
    rows, width = partial.shape[0] // plane, partial.shape[1]
    kind = partial.dtype
    size = rows * width * 2
    return pl.pallas_call(
        scatter_kernel,
        out_shape=jax.ShapeDtypeStruct((rows, width), F32),
        in_specs=[pl.BlockSpec(memory_space=pltpu.HBM)],
        out_specs=pl.BlockSpec(memory_space=pltpu.VMEM),
        scratch_shapes=scatter_scratch(rows, width, kind),
        cost_estimate=pl.CostEstimate(
            flops=0, transcendentals=0, bytes_accessed=plane * size * 14
        ),
        compiler_params=pltpu.CompilerParams(
            collective_id=ident, has_side_effects=True, vmem_limit_bytes=60 << 20
        ),
        name="scatter_plane",
    )(partial.reshape(plane, rows, width))


def fill_bias(bias, starts_ref, t, blocks):
    for b in range(blocks):
        span = min(2, blocks - b) * PIC
        k_at = lax.broadcasted_iota(jnp.int32, (span, PIC), 0) + b * PIC
        q_at = lax.broadcasted_iota(jnp.int32, (span, PIC), 1) + b * PIC
        high, below = jnp.maximum(k_at, q_at), jnp.minimum(k_at, q_at)
        allowed = k_at <= q_at
        for j in range(NPIC):
            start = starts_ref[t, j]
            allowed = allowed | ((below >= start) & (high < start + PIC))
        bias[b, :span, :] = jnp.where(allowed, 0.0, -jnp.inf)


def masked(scores, bias, b):
    late = scores[b * PIC :] + bias[b, : scores.shape[0] - b * PIC, :]
    return jnp.concatenate([scores[: b * PIC], late], axis=0) if b else late


def attn_front_kernel(
    starts_ref,
    norm_hbm,
    weight_hbm,
    cos_ref,
    sin_ref,
    own_ref,
    qkv_ref,
    mixed_ref,
    log_ref,
    out_ref,
    all_ref,
    bias,
    turned,
    norm,
    weight,
    projected,
    stage,
    local,
    *gather,
):
    begin, first, second, *last = gather_stages(own_ref, all_ref, *gather)
    total, dim = cos_ref.shape
    take_weight = pltpu.make_async_copy(weight_hbm, weight, local.at[0])
    take_weight.start()

    def take_norm(t):
        rows = pl.ds(t * total, total)
        return pltpu.make_async_copy(norm_hbm.at[rows], norm.at[t], local.at[1 + t])

    def put_out(t, n):
        rows = pl.ds(t * total + n * (total // 2), total // 2)
        return pltpu.make_async_copy(stage.at[n], out_ref.at[rows], local.at[1 + TP + n])

    for t in range(TP):
        take_norm(t).start()
    begin()
    take_weight.wait()
    heads = mixed_ref.shape[1] // dim
    blocks = total // PIC
    scale = dim ** (-0.5)
    k_cols = slice(heads * dim, (heads + 1) * dim)
    v_cols = slice((heads + 1) * dim, (heads + 2) * dim)

    def turn(rows, at):
        return rows * cos_ref[at, :] + pltpu.roll(rows, dim // 2, 1) * sin_ref[at, :]

    def head_step(i, carry):
        t, h = i // heads, lax.rem(i, heads)
        base = pl.multiple_of(t * total, total)
        cols = pl.ds(pl.multiple_of(h * dim, dim), dim)

        @pl.when(h == 0)
        def _():
            rows = pl.ds(base, total)
            take_norm(t).wait()

            def project(n, carry):
                some = pl.ds(pl.multiple_of(n * PIC, PIC), PIC)
                projected[some, :] = nn(norm[t, some, :], weight[:, : (heads + 2) * dim])
                return carry

            lax.fori_loop(0, blocks, project, 0)
            values = projected[:, v_cols].astype(BF)
            qkv_ref[rows, k_cols] = turn(projected[:, k_cols], pl.ds(0, total)).astype(BF)
            qkv_ref[rows, v_cols] = values
            turned[...] = values.T
            fill_bias(bias, starts_ref, t, blocks)

        for b in range(blocks):
            at = pl.ds(pl.multiple_of(base + b * PIC, PIC), PIC)
            count = min(b + 2, blocks) * PIC
            queries = turn(projected[b * PIC : (b + 1) * PIC, cols], pl.ds(b * PIC, PIC)).astype(BF)
            qkv_ref[at, cols] = queries
            scores = nt(qkv_ref[pl.ds(base, count), k_cols], queries) * scale
            scores = masked(scores, bias, b)
            peak = jnp.max(scores, axis=0, keepdims=True)
            weights = jnp.exp(scores - peak)
            mass = jnp.sum(weights, axis=0, keepdims=True)
            log_ref[i, :, b * PIC : (b + 1) * PIC] = peak + jnp.log(mass)
            probs = (weights * (1.0 / mass)).astype(BF)
            mixed_ref[at, cols] = nn(turned[:, :count], probs).T.astype(BF)
            if b == 0:
                pl.when(i == 1)(first)
                pl.when(i == 3)(second)

        @pl.when(h == heads - 1)
        def _():
            for n in range(2):

                @pl.when(t >= 1)
                def _():
                    put_out(t - 1, n).wait()

                rows = pl.ds(pl.multiple_of(base + n * (total // 2), total // 2), total // 2)
                block = stage.shape[2] // 4

                def out_step(m, carry):
                    some = pl.ds(pl.multiple_of(m * block, block), block)
                    partial = nt(mixed_ref[rows, :], weight[some, (heads + 2) * dim :])
                    stage[n, :, some] = partial.astype(BF)
                    return carry

                lax.fori_loop(0, 4, out_step, 0)
                put_out(t, n).start()

        return carry

    lax.fori_loop(0, log_ref.shape[0], head_step, 0)
    for stage_step in last:
        stage_step()
    for n in range(2):
        put_out(TP - 1, n).wait()


def attn_front_plane(starts, norm, weight, cos, sin, block, ident):
    rows, width = block.shape
    plane = lax.axis_size("tp") * lax.axis_size("seq")
    total, dim = cos.shape
    tokens = norm.shape[0]
    q_part = weight.shape[1] // 2 - dim
    shape = jax.ShapeDtypeStruct
    vmem = pl.BlockSpec(memory_space=pltpu.VMEM)
    smem = pl.BlockSpec(memory_space=pltpu.SMEM)
    hbm = pl.BlockSpec(memory_space=pltpu.HBM)
    return pl.pallas_call(
        attn_front_kernel,
        out_shape=(
            shape((tokens, q_part + 2 * dim), BF),
            shape((tokens, q_part), BF),
            shape((tokens * q_part // dim // total, 1, total), F32),
            shape(norm.shape, BF),
            shape((plane, rows, width), block.dtype),
        ),
        in_specs=[smem, hbm, hbm, vmem, vmem, vmem],
        out_specs=(vmem, vmem, vmem, hbm, hbm),
        scratch_shapes=[
            pltpu.VMEM((total // PIC, 2 * PIC, PIC), F32),
            pltpu.VMEM((dim, total), BF),
            pltpu.VMEM((TP, total, width), BF),
            pltpu.VMEM(weight.shape, BF),
            pltpu.VMEM((total, q_part + 2 * dim), F32),
            pltpu.VMEM((2, total // 2, width), BF),
            pltpu.SemaphoreType.DMA((3 + TP,)),
            *GATHER_SCRATCH,
        ],
        cost_estimate=pl.CostEstimate(
            flops=4 * tokens * total * q_part,
            transcendentals=tokens * total * q_part // dim,
            bytes_accessed=plane * rows * width * 24,
        ),
        compiler_params=pltpu.CompilerParams(
            collective_id=ident, has_side_effects=True, vmem_limit_bytes=40 << 20
        ),
        name="attn_front_plane",
    )(starts, norm, weight, cos, sin, block)


def attn_back_kernel(
    starts_ref,
    qkv_ref,
    g_ref,
    log_ref,
    cos_ref,
    sin_ref,
    part_ref,
    grad_ref,
    sum_ref,
    bias,
    turned,
    keys_sum,
    values_sum,
    *scatter,
):
    begin, diagonal, along_x, along_y, own, fold, finish = scatter_stages(
        part_ref, sum_ref, *scatter
    )
    begin()
    total, dim = cos_ref.shape
    heads = g_ref.shape[1] // dim
    blocks = total // PIC
    scale = dim ** (-0.5)
    k_cols = slice(heads * dim, (heads + 1) * dim)
    v_cols = slice((heads + 1) * dim, (heads + 2) * dim)
    events = {(0, 1): diagonal, (0, 2): along_x, (0, 3): along_y, (1, 0): own, (2, 2): fold}

    def unturn(rows, at):
        return rows * cos_ref[at, :] - pltpu.roll(rows, dim // 2, 1) * sin_ref[at, :]

    def head_step(i, carry):
        t, h = i // heads, lax.rem(i, heads)
        base = pl.multiple_of(t * total, total)
        cols = pl.ds(pl.multiple_of(h * dim, dim), dim)

        @pl.when(h == 0)
        def _():
            turned[...] = qkv_ref[pl.ds(base, total), k_cols].T
            keys_sum[...] = jnp.zeros(keys_sum.shape, F32)
            values_sum[...] = jnp.zeros(values_sum.shape, F32)
            fill_bias(bias, starts_ref, t, blocks)

        for b in range(blocks):
            at = pl.ds(pl.multiple_of(base + b * PIC, PIC), PIC)
            count = min(b + 2, blocks) * PIC
            seen = pl.ds(base, count)
            queries, grads = qkv_ref[at, cols], g_ref[at, cols]
            scores = nt(qkv_ref[seen, k_cols], queries) * scale - log_ref[i, :, b * PIC : (b + 1) * PIC]
            probs = jnp.exp(masked(scores, bias, b))
            prob_grad = nt(qkv_ref[seen, v_cols], grads)
            mean = jnp.sum(probs * prob_grad, axis=0, keepdims=True)
            score_grad = (probs * (prob_grad - mean)).astype(BF)
            values_sum[:count, :] += nn(probs.astype(BF), grads)
            keys_sum[:count, :] += nn(score_grad, queries)
            back = nn(turned[:, :count], score_grad).T * scale
            grad_ref[at, cols] = unturn(back, pl.ds(b * PIC, PIC)).astype(BF)
            for (step, block), stage in events.items():
                if block == b:
                    pl.when(i == step)(stage)

        @pl.when(h == heads - 1)
        def _():
            rows = pl.ds(base, total)
            back = unturn(keys_sum[...] * scale, pl.ds(0, total))
            grad_ref[rows, k_cols] = back.astype(BF)
            grad_ref[rows, v_cols] = values_sum[...].astype(BF)

        return carry

    lax.fori_loop(0, log_ref.shape[0], head_step, 0)
    finish()


def attn_back_plane(starts, qkv, grads, log_total, cos, sin, partial, ident):
    plane = lax.axis_size("tp") * lax.axis_size("seq")
    rows, width = partial.shape[0] // plane, partial.shape[1]
    total, dim = cos.shape
    tokens, q_part = grads.shape
    hbm = pl.BlockSpec(memory_space=pltpu.HBM)
    vmem = pl.BlockSpec(memory_space=pltpu.VMEM)
    smem = pl.BlockSpec(memory_space=pltpu.SMEM)
    return pl.pallas_call(
        attn_back_kernel,
        out_shape=(
            jax.ShapeDtypeStruct((tokens, q_part + 2 * dim), BF),
            jax.ShapeDtypeStruct((rows, width), F32),
        ),
        in_specs=[smem] + [vmem] * 5 + [hbm],
        out_specs=(vmem, vmem),
        scratch_shapes=[
            pltpu.VMEM((total // PIC, 2 * PIC, PIC), F32),
            pltpu.VMEM((dim, total), BF),
            pltpu.VMEM((total, dim), F32),
            pltpu.VMEM((total, dim), F32),
        ]
        + scatter_scratch(rows, width, partial.dtype),
        cost_estimate=pl.CostEstimate(
            flops=10 * tokens * total * q_part,
            transcendentals=tokens * total * q_part // dim,
            bytes_accessed=plane * rows * width * 28,
        ),
        compiler_params=pltpu.CompilerParams(
            collective_id=ident, has_side_effects=True, vmem_limit_bytes=50 << 20
        ),
        name="attn_back_plane",
    )(starts, qkv, grads, log_total, cos, sin, partial.reshape(plane, rows, width))


def exchange_kernel(in_ref, out_ref, stage, local, sends, recvs):
    tp_at, seq_at, _, _, _ = plane_place()
    seq = lax.axis_size("seq")
    plane = lax.axis_size("tp") * seq
    me = tp_at * seq + seq_at
    peers = [lax.rem(me + k, plane) for k in range(1, plane)]
    devices = [at_device(peer // seq, lax.rem(peer, seq)) for peer in peers]
    enter(devices)
    copies = []
    for k, (peer, device) in enumerate(zip(peers, devices)):
        copy = remote(in_ref.at[peer], out_ref.at[me], sends.at[k], recvs.at[k], device)
        copy.start()
        copies.append(copy)
    take = pltpu.make_async_copy(in_ref.at[me], stage, local.at[0])
    take.start()
    take.wait()
    put = pltpu.make_async_copy(stage, out_ref.at[me], local.at[1])
    put.start()
    for copy in copies:
        copy.wait()
    put.wait()


def exchange_plane(blocks, ident):
    plane, rows, width = blocks.shape
    size = plane * rows * width * 2
    return pl.pallas_call(
        exchange_kernel,
        out_shape=jax.ShapeDtypeStruct(blocks.shape, blocks.dtype),
        in_specs=[pl.BlockSpec(memory_space=pltpu.HBM)],
        out_specs=pl.BlockSpec(memory_space=pltpu.HBM),
        scratch_shapes=[
            pltpu.VMEM((rows, width), blocks.dtype),
            pltpu.SemaphoreType.DMA((2,)),
            pltpu.SemaphoreType.DMA((plane - 1,)),
            pltpu.SemaphoreType.DMA((plane - 1,)),
        ],
        cost_estimate=pl.CostEstimate(flops=0, transcendentals=0, bytes_accessed=size * 20),
        compiler_params=pltpu.CompilerParams(collective_id=ident, has_side_effects=True),
        name="exchange_plane",
    )(blocks)


def slopes(wide, narrow, inner, gug):
    ff_part = inner.shape[1]

    def body(i, carry):
        at = pl.ds(i * SUB, SUB)
        gate, upward, grad = wide[at, :ff_part], wide[at, ff_part:], narrow[at, :]
        sigmoid_gate = jax.nn.sigmoid(gate)
        silu_gate = gate * sigmoid_gate
        inner[at, :] = (silu_gate * upward).astype(BF)
        slope = sigmoid_gate * (1.0 + gate * (1.0 - sigmoid_gate))
        gug[at, :ff_part] = (grad * upward * slope).astype(BF)
        gug[at, ff_part:] = (grad * silu_gate).astype(BF)
        return carry

    lax.fori_loop(0, wide.shape[0] // SUB, body, 0)


def weight_step(n, tokens, grads, gug, inner, stage, weight_ref, sems):
    slot = lax.rem(n, 2)
    block, cols = stage.shape[1:]
    ff_part = cols // 3
    count = gug.shape[0] * gug.shape[1]

    def put(m):
        return pltpu.make_async_copy(
            stage.at[lax.rem(m, 2)], weight_ref.at[pl.ds(m * block, block)], sems[0].at[sems[1] + lax.rem(m, 2)]
        )

    @pl.when(n >= 2)
    def _():
        put(n - 2).wait()

    at = pl.ds(pl.multiple_of(n * block, block), block)
    left = tokens[:, :, :, at].reshape(count, block)
    stage[slot, :, : 2 * ff_part] = tn(left, gug[...].reshape(count, 2 * ff_part)).astype(BF)
    left = grads[:, :, :, at].reshape(count, block)
    stage[slot, :, 2 * ff_part :] = tn(left, inner[...].reshape(count, ff_part)).astype(BF)
    put(n).start()
    return put


def ffn_first_kernel(
    own_ref,
    grad_ref,
    weight_hbm,
    all_ref,
    back_ref,
    out_ref,
    grads_out,
    weight,
    tokens,
    grads,
    wide,
    narrow,
    inner,
    gug,
    stage,
    columns_stage,
    sends,
    recvs,
    local,
):
    tp_at, seq_at, far, mate, _ = plane_place()
    seq = lax.axis_size("seq")
    other = 1 - tp_at
    to_x = at_device(tp_at, far)
    to_y = at_device(other, seq_at)
    to_c = at_device(tp_at, mate)
    rows, width = own_ref.shape
    pair = 2 * rows
    half = rows // 2
    block = width // 4
    ff_part = narrow.shape[2]
    gate_up, lower = slice(0, 2 * ff_part), slice(2 * ff_part, 3 * ff_part)
    enter((to_x, to_y, to_c))

    def piece(t, s, h):
        return all_ref.at[t * seq + s, pl.ds(h * half, half)]

    def own(i, h, device):
        return remote(
            own_ref.at[pl.ds(h * half, half)],
            piece(tp_at, seq_at, h),
            sends.at[i],
            recvs.at[i],
            device,
        )

    def relay(i, t, s, h, device):
        return remote(piece(t, s, h), piece(t, s, h), sends.at[i], recvs.at[i], device)

    x0, x1 = own(0, 0, to_x), own(3, 1, to_x)
    y0, y1 = own(1, 0, to_y), own(4, 1, to_y)
    c0, c1 = own(2, 0, to_c), own(5, 1, to_c)
    diag0 = relay(6, tp_at, far, 0, to_y)
    diag1 = relay(7, other, seq_at, 1, to_x)
    rx0, rx1 = relay(8, tp_at, far, 0, to_c), relay(11, tp_at, far, 1, to_c)
    ry0, ry1 = relay(9, other, seq_at, 0, to_c), relay(10, other, seq_at, 1, to_c)
    rd0, rd1 = relay(12, other, far, 0, to_c), relay(13, other, far, 1, to_c)

    def chip_rows(c):
        t = lax.rem(tp_at + c // 2, 2)
        s = lax.rem(seq_at + (seq // 2) * lax.rem(c, 2), seq)
        return pl.ds(t * seq + s - lax.rem(s, 2), 2)

    def take_tokens(c):
        return pltpu.make_async_copy(all_ref.at[chip_rows(c)], tokens.at[c], local.at[c])

    def take_grads(c):
        return pltpu.make_async_copy(grad_ref.at[chip_rows(c)], grads.at[c], local.at[4 + c])

    def put_back(c):
        return pltpu.make_async_copy(stage.at[0], back_ref.at[chip_rows(c)], local.at[8])

    def put_out(c):
        return pltpu.make_async_copy(stage.at[1], out_ref.at[chip_rows(c)], local.at[9])

    take_weight = pltpu.make_async_copy(weight_hbm, weight, local.at[12])
    mine = pltpu.make_async_copy(own_ref, all_ref.at[tp_at * seq + seq_at], local.at[13])
    for copy in (take_weight, x0, y0, c0, x1, y1, c1, mine):
        copy.start()
    for c in range(4):
        take_grads(c).start()
    take_weight.wait()

    def narrow_step(c, carry):
        take_grads(c).wait()
        narrow[c] = nn(grads[c].reshape(pair, width), weight[:, lower])
        return carry

    lax.fori_loop(0, 4, narrow_step, 0)
    mine.wait()
    c0.wait_recv()
    c1.wait_recv()
    take_tokens(0).start()

    def chip_step(c, carry):
        take_tokens(c).wait()
        wide[...] = nn(tokens[c].reshape(pair, width), weight[:, gate_up])

        @pl.when(c == 0)
        def _():
            x0.wait_recv()
            diag0.start()
            rx0.start()
            y0.wait_recv()
            ry0.start()

        @pl.when(c == 1)
        def _():
            ry0.wait_recv()
            ry1.wait_recv()
            take_tokens(2).start()

        @pl.when(c == 2)
        def _():
            diag0.wait_recv()
            rd0.start()
            diag1.wait_recv()
            rd1.start()

        slopes(wide, narrow.at[c], inner.at[c], gug.at[c])

        @pl.when(c >= 1)
        def _():
            put_back(c - 1).wait()
            put_out(c - 1).wait()

        def back_step(n, carry):
            at = pl.ds(pl.multiple_of(n * block, block), block)
            total = nt(gug[c], weight[at, gate_up]).astype(BF)
            stage[0, :, :, at] = total.reshape(2, rows, block)
            total = nt(inner[c], weight[at, lower]).astype(BF)
            stage[1, :, :, at] = total.reshape(2, rows, block)
            return carry

        lax.fori_loop(0, 4, back_step, 0)
        put_back(c).start()
        put_out(c).start()

        @pl.when(c == 0)
        def _():
            y1.wait_recv()
            diag1.start()
            ry1.start()
            x1.wait_recv()
            rx1.start()
            rx0.wait_recv()
            rx1.wait_recv()
            take_tokens(1).start()

        @pl.when(c == 2)
        def _():
            rd0.wait_recv()
            rd1.wait_recv()
            take_tokens(3).start()

        return carry

    lax.fori_loop(0, 4, chip_step, 0)

    def grads_step(n, carry):
        weight_step(n, tokens, grads, gug, inner, columns_stage, grads_out, (local, 10))
        return carry

    lax.fori_loop(0, 4, grads_step, 0)
    for copy in (x0, y0, c0, x1, y1, c1, diag0, diag1, rx0, ry0, ry1, rx1, rd0, rd1):
        copy.wait_send()
    put_back(3).wait()
    put_out(3).wait()
    for n in (2, 3):
        pltpu.make_async_copy(
            columns_stage.at[n - 2], grads_out.at[pl.ds(n * block, block)], local.at[8 + n]
        ).wait()


def ffn_second_kernel(
    all_ref,
    grad_ref,
    weight_hbm,
    back_ref,
    first_ref,
    out_ref,
    grads_out,
    sum_ref,
    weight,
    tokens,
    grads,
    wide,
    narrow,
    inner,
    gug,
    part,
    chip_in,
    far_in,
    near_in,
    stage,
    columns_stage,
    sends,
    recvs,
    local,
):
    tp_at, seq_at, far, mate, _ = plane_place()
    seq = lax.axis_size("seq")
    kind = lax.rem(seq_at, 2)
    to_x = at_device(tp_at, far)
    to_y = at_device(1 - tp_at, seq_at)
    to_c = at_device(tp_at, mate)
    rows, width = sum_ref.shape
    pair = 2 * rows
    half = rows // 2
    block = width // 4
    ff_part = narrow.shape[1]
    gate_up, lower = slice(0, 2 * ff_part), slice(2 * ff_part, 3 * ff_part)
    top, low = pl.ds(0, half), pl.ds(half, half)
    enter((to_x, to_y, to_c))

    def chip_rows(k):
        t = lax.rem(tp_at + 1 - lax.rem(k, 2), 2)
        s = lax.rem(seq_at + (seq // 2) * (1 - k // 2), seq)
        return pl.ds(t * seq + s - lax.rem(s, 2), 2)

    def take(ref, target, sem):
        return lambda k: pltpu.make_async_copy(ref.at[chip_rows(k)], target.at[k], local.at[sem + k])

    take_tokens, take_grads, take_back = (
        take(all_ref, tokens, 0),
        take(grad_ref, grads, 4),
        take(back_ref, part, 8),
    )

    def take_first(k):
        slot = lax.rem(k, 2)
        return pltpu.make_async_copy(first_ref.at[chip_rows(k)], stage.at[slot], local.at[12 + slot])

    def put_out(k):
        slot = lax.rem(k, 2)
        return pltpu.make_async_copy(stage.at[slot], out_ref.at[chip_rows(k)], local.at[14 + slot])

    def give(k):
        return remote(part.at[k, 1 - kind], chip_in.at[k], sends.at[k], recvs.at[k], to_c)

    def held(k):
        return part.at[k, kind]

    def hop(i, src, dst, device):
        return remote(src, dst, sends.at[i], recvs.at[i], device)

    d0 = hop(4, part.at[0, kind, top], far_in.at[0, top], to_x)
    d1 = hop(5, part.at[0, kind, low], far_in.at[1, low], to_y)
    x0 = hop(6, part.at[1, kind, top], near_in.at[0, top], to_x)
    y1 = hop(7, part.at[2, kind, low], near_in.at[1, low], to_y)
    y0 = hop(8, part.at[2, kind, top], near_in.at[1, top], to_y)
    x1 = hop(9, part.at[1, kind, low], near_in.at[0, low], to_x)

    def chip_sum(k):
        give(k).wait_recv()
        add_rows(held(k), (held(k), chip_in.at[k]), 0, rows, part.dtype)

    take_weight = pltpu.make_async_copy(weight_hbm, weight, local.at[18])
    take_weight.start()
    for k in range(4):
        take_grads(k).start()
        take_tokens(k).start()
        take_back(k).start()
    take_first(0).start()
    take_weight.wait()

    def chip_step(k, carry):
        slot = lax.rem(k, 2)
        take_grads(k).wait()
        narrow[...] = nn(grads[k].reshape(pair, width), weight[:, lower])

        @pl.when(k == 1)
        def _():
            chip_sum(0)
            d0.start()
            d1.start()

        @pl.when(k == 2)
        def _():
            chip_sum(1)
            x0.start()

        @pl.when(k == 3)
        def _():
            chip_sum(2)
            y1.start()
            d0.wait_recv()
            add_rows(held(2), (held(2), far_in.at[0]), 0, half, part.dtype)
            y0.start()
            d1.wait_recv()
            add_rows(held(1), (held(1), far_in.at[1]), half, half, part.dtype)
            x1.start()

        take_tokens(k).wait()
        wide[...] = nn(tokens[k].reshape(pair, width), weight[:, gate_up])
        slopes(wide, narrow, inner.at[k], gug.at[k])
        take_back(k).wait()

        def back_step(n, carry):
            at = pl.ds(pl.multiple_of(n * block, block), block)
            total = nt(gug[k], weight[at, gate_up]).reshape(2, rows, block)
            part[k, :, :, at] = (part[k, :, :, at].astype(F32) + total).astype(part.dtype)
            return carry

        lax.fori_loop(0, 4, back_step, 0)
        give(k).start()
        take_first(k).wait()

        @pl.when(k >= 1)
        def _():
            put_out(k - 1).wait()

        @pl.when(k < 3)
        def _():
            take_first(k + 1).start()

        def out_step(n, carry):
            at = pl.ds(pl.multiple_of(n * block, block), block)
            total = nt(inner[k], weight[at, lower]).reshape(2, rows, block)
            stage[slot, :, :, at] = (stage[slot, :, :, at].astype(F32) + total).astype(stage.dtype)
            return carry

        lax.fori_loop(0, 4, out_step, 0)
        put_out(k).start()
        return carry

    lax.fori_loop(0, 4, chip_step, 0)

    def grads_step(n, carry):
        weight_step(n, tokens, grads, gug, inner, columns_stage, grads_out, (local, 16))

        @pl.when(n == 0)
        def _():
            chip_sum(3)

        return carry

    lax.fori_loop(0, 4, grads_step, 0)
    x0.wait_recv()
    y0.wait_recv()
    add_rows(sum_ref, (held(3), near_in.at[0], near_in.at[1]), 0, half, sum_ref.dtype)
    y1.wait_recv()
    x1.wait_recv()
    add_rows(sum_ref, (held(3), near_in.at[0], near_in.at[1]), half, half, sum_ref.dtype)
    for k in range(4):
        give(k).wait_send()
    for copy in (d0, d1, x0, y1, y0, x1):
        copy.wait_send()
    put_out(3).wait()
    for n in (2, 3):
        pltpu.make_async_copy(
            columns_stage.at[n - 2], grads_out.at[pl.ds(n * block, block)], local.at[14 + n]
        ).wait()


def ffn_first_plane(block, grads, weight, ident):
    rows, width = block.shape
    plane = lax.axis_size("tp") * lax.axis_size("seq")
    cols = weight.shape[1]
    ff_part = cols // 3
    shape = jax.ShapeDtypeStruct
    hbm = pl.BlockSpec(memory_space=pltpu.HBM)
    vmem = pl.BlockSpec(memory_space=pltpu.VMEM)
    tokens = plane * rows
    return pl.pallas_call(
        ffn_first_kernel,
        out_shape=(
            shape((plane, rows, width), BF),
            shape((plane, rows, width), BF),
            shape((plane, rows, width), BF),
            shape((width, cols), BF),
        ),
        in_specs=[vmem, hbm, hbm],
        out_specs=(hbm, hbm, hbm, hbm),
        scratch_shapes=[
            pltpu.VMEM(weight.shape, BF),
            pltpu.VMEM((4, 2, rows, width), BF),
            pltpu.VMEM((4, 2, rows, width), BF),
            pltpu.VMEM((2 * rows, 2 * ff_part), F32),
            pltpu.VMEM((4, 2 * rows, ff_part), F32),
            pltpu.VMEM((4, 2 * rows, ff_part), BF),
            pltpu.VMEM((4, 2 * rows, 2 * ff_part), BF),
            pltpu.VMEM((2, 2, rows, width), BF),
            pltpu.VMEM((2, width // 4, cols), BF),
            pltpu.SemaphoreType.DMA((14,)),
            pltpu.SemaphoreType.DMA((14,)),
            pltpu.SemaphoreType.DMA((14,)),
        ],
        cost_estimate=pl.CostEstimate(
            flops=18 * tokens * width * ff_part,
            transcendentals=tokens * ff_part,
            bytes_accessed=22 * tokens * width,
        ),
        compiler_params=pltpu.CompilerParams(
            collective_id=ident, has_side_effects=True, vmem_limit_bytes=60 << 20
        ),
        name="ffn_first_plane",
    )(block, grads, weight)


def ffn_second_plane(block, grads, weight, back, first, ident):
    plane, rows, width = block.shape
    cols = weight.shape[1]
    ff_part = cols // 3
    shape = jax.ShapeDtypeStruct
    hbm = pl.BlockSpec(memory_space=pltpu.HBM)
    vmem = pl.BlockSpec(memory_space=pltpu.VMEM)
    tokens = plane * rows
    return pl.pallas_call(
        ffn_second_kernel,
        out_shape=(
            shape((plane, rows, width), BF),
            shape((width, cols), BF),
            shape((rows, width), F32),
        ),
        in_specs=[hbm] * 5,
        out_specs=(hbm, hbm, vmem),
        scratch_shapes=[
            pltpu.VMEM(weight.shape, BF),
            pltpu.VMEM((4, 2, rows, width), BF),
            pltpu.VMEM((4, 2, rows, width), BF),
            pltpu.VMEM((2 * rows, 2 * ff_part), F32),
            pltpu.VMEM((2 * rows, ff_part), F32),
            pltpu.VMEM((4, 2 * rows, ff_part), BF),
            pltpu.VMEM((4, 2 * rows, 2 * ff_part), BF),
            pltpu.VMEM((4, 2, rows, width), BF),
            pltpu.VMEM((4, rows, width), BF),
            pltpu.VMEM((2, rows, width), BF),
            pltpu.VMEM((2, rows, width), BF),
            pltpu.VMEM((2, 2, rows, width), BF),
            pltpu.VMEM((2, width // 4, cols), BF),
            pltpu.SemaphoreType.DMA((10,)),
            pltpu.SemaphoreType.DMA((10,)),
            pltpu.SemaphoreType.DMA((19,)),
        ],
        cost_estimate=pl.CostEstimate(
            flops=18 * tokens * width * ff_part,
            transcendentals=tokens * ff_part,
            bytes_accessed=22 * tokens * width,
        ),
        compiler_params=pltpu.CompilerParams(
            collective_id=ident, has_side_effects=True, vmem_limit_bytes=63 << 20
        ),
        name="ffn_second_plane",
    )(block, grads, weight, back, first)


def exchange_all_kernel(*refs):
    *blocks, local, sends, recvs = refs
    count = len(blocks) // 2
    tp_at, seq_at, _, _, _ = plane_place()
    seq = lax.axis_size("seq")
    plane = lax.axis_size("tp") * seq
    me = tp_at * seq + seq_at
    peers = [lax.rem(me + k, plane) for k in range(1, plane)]
    devices = [at_device(peer // seq, lax.rem(peer, seq)) for peer in peers]
    enter(devices)
    groups = []
    for n, (ref, into) in enumerate(zip(blocks[:count], blocks[count:])):
        copies = [pltpu.make_async_copy(ref.at[me], into.at[me], local.at[n])]
        for k, (peer, device) in enumerate(zip(peers, devices)):
            i = n * (plane - 1) + k
            copies.append(remote(ref.at[peer], into.at[me], sends.at[i], recvs.at[i], device))
        for copy in copies:
            copy.start()
        groups.append(copies)

    for copies in groups:
        for copy in copies:
            copy.wait()


def exchange_all_plane(blocks, ident):
    plane, count = blocks[0].shape[0], len(blocks)
    hbm = pl.BlockSpec(memory_space=pltpu.HBM)
    vmem = pl.BlockSpec(memory_space=pltpu.VMEM)
    size = sum(block.size for block in blocks) * 2
    return pl.pallas_call(
        exchange_all_kernel,
        out_shape=tuple(jax.ShapeDtypeStruct(b.shape, b.dtype) for b in blocks),
        in_specs=[hbm] * count,
        out_specs=(vmem,) * count,
        scratch_shapes=[
            pltpu.SemaphoreType.DMA((count,)),
            pltpu.SemaphoreType.DMA((count * (plane - 1),)),
            pltpu.SemaphoreType.DMA((count * (plane - 1),)),
        ],
        cost_estimate=pl.CostEstimate(flops=0, transcendentals=0, bytes_accessed=size * 20),
        compiler_params=pltpu.CompilerParams(collective_id=ident, has_side_effects=True),
        name="exchange_all_plane",
    )(*blocks)


def attn_grads_kernel(
    norm_hbm,
    grad_ref,
    columns_ref,
    weight_hbm,
    move_ref,
    grads_out,
    back_out,
    move_out,
    norm,
    weight,
    stage,
    back,
    kept,
    local,
    sends,
    recvs,
):
    tp_at, seq_at, _, _, _ = plane_place()
    seq = lax.axis_size("seq")
    plane = lax.axis_size("tp") * seq
    me = tp_at * seq + seq_at
    tokens, width = norm.shape
    cols = grad_ref.shape[1]
    block, some = width // 4, tokens // 4
    peers = [lax.rem(me + k, plane) for k in range(1, plane)]
    devices = [at_device(peer // seq, lax.rem(peer, seq)) for peer in peers]

    def at(n):
        return pl.ds(pl.multiple_of(n * block, block), block)

    def take(n):
        return pltpu.make_async_copy(norm_hbm.at[:, at(n)], norm.at[:, at(n)], local.at[n])

    def put(n):
        slot = lax.rem(n, 2)
        return pltpu.make_async_copy(stage.at[slot], grads_out.at[at(n)], local.at[4 + slot])

    def put_back(n):
        slot = lax.rem(n, 2)
        rows = pl.ds(pl.multiple_of(n * some, some), some)
        return pltpu.make_async_copy(back.at[slot], back_out.at[rows], local.at[6 + slot])

    for n in range(4):
        take(n).start()
    take_weight = pltpu.make_async_copy(weight_hbm, weight, local.at[8])
    take_weight.start()
    take_kept = pltpu.make_async_copy(move_ref.at[me], kept, local.at[9])
    put_kept = pltpu.make_async_copy(kept, move_out.at[me], local.at[10])
    take_kept.start()
    enter(devices)
    moves = [
        remote(move_ref.at[peer], move_out.at[me], sends.at[k], recvs.at[k], device)
        for k, (peer, device) in enumerate(zip(peers, devices))
    ]
    for move in moves:
        move.start()

    def grads_step(n, carry):
        @pl.when(n >= 2)
        def _():
            put(n - 2).wait()

        slot = lax.rem(n, 2)
        take(n).wait()
        stage[slot, :, :cols] = tn(norm[:, at(n)], grad_ref[...]).astype(BF)
        stage[slot, :, cols:] = columns_ref[at(n), :]
        put(n).start()
        return carry

    lax.fori_loop(0, 4, grads_step, 0)
    take_kept.wait()
    put_kept.start()
    take_weight.wait()

    def back_step(n, carry):
        @pl.when(n >= 2)
        def _():
            put_back(n - 2).wait()

        slot = lax.rem(n, 2)
        left = grad_ref[pl.ds(pl.multiple_of(n * some, some), some), :]

        def back_block(m, carry):
            back[slot, :, at(m)] = nt(left, weight[at(m), :cols]).astype(BF)
            return carry

        lax.fori_loop(0, 4, back_block, 0)
        put_back(n).start()
        return carry

    lax.fori_loop(0, 4, back_step, 0)
    for n in (2, 3):
        put(n).wait()
        put_back(n).wait()
    for move in moves:
        move.wait()
    put_kept.wait()


def attn_grads_plane(norm, grads, columns, weight, blocks, ident):
    tokens, width = norm.shape
    plane = blocks.shape[0]
    shape = jax.ShapeDtypeStruct
    hbm = pl.BlockSpec(memory_space=pltpu.HBM)
    vmem = pl.BlockSpec(memory_space=pltpu.VMEM)
    return pl.pallas_call(
        attn_grads_kernel,
        out_shape=(
            shape(weight.shape, BF),
            shape((tokens, width), BF),
            shape(blocks.shape, blocks.dtype),
        ),
        in_specs=[hbm, vmem, vmem, hbm, hbm],
        out_specs=(hbm,) * 3,
        scratch_shapes=[
            pltpu.VMEM(norm.shape, BF),
            pltpu.VMEM(weight.shape, BF),
            pltpu.VMEM((2, width // 4, weight.shape[1]), BF),
            pltpu.VMEM((2, tokens // 4, width), BF),
            pltpu.VMEM(blocks.shape[1:], blocks.dtype),
            pltpu.SemaphoreType.DMA((11,)),
            pltpu.SemaphoreType.DMA((plane - 1,)),
            pltpu.SemaphoreType.DMA((plane - 1,)),
        ],
        cost_estimate=pl.CostEstimate(
            flops=4 * tokens * width * grads.shape[1],
            transcendentals=0,
            bytes_accessed=12 * tokens * width,
        ),
        compiler_params=pltpu.CompilerParams(
            collective_id=ident, has_side_effects=True, vmem_limit_bytes=48 << 20
        ),
        name="attn_grads_plane",
    )(norm, grads, columns, weight, blocks)


def finish_kernel(
    first_in,
    second_in,
    attn_in,
    gate_weight,
    up_weight,
    query_weight,
    key_weight,
    value_weight,
    gain2_ref,
    gain1_ref,
    gate_out,
    up_out,
    down_out,
    gain2_out,
    query_out,
    key_out,
    value_out,
    out_out,
    gain1_out,
):
    plane = first_in.shape[0]
    gain = gain2_ref[...]
    sizes = [ref.shape[2] // 3 for ref in (first_in, second_in)]
    total = jnp.zeros(gain.shape, F32)
    for n, ref in enumerate((first_in, second_in)):
        size = sizes[n]
        for j in range(plane):
            start = j * sum(sizes) + n * sizes[0]
            at = slice(start, start + size)
            for k, (out, weight) in enumerate(((gate_out, gate_weight), (up_out, up_weight))):
                own = ref[j, :, k * size : (k + 1) * size].astype(F32)
                out[:, at] = own * gain
                total = total + jnp.sum(own * weight[:, at].astype(F32), axis=1, keepdims=True)
            down_out[:, at] = ref[j, :, 2 * size :].astype(F32)
    gain2_out[...] = total

    gain = gain1_ref[...]
    q_part = query_out.shape[1] // plane
    share = plane // KV
    total = jnp.zeros(gain.shape, F32)
    for j in range(plane):
        at = slice(j * q_part, (j + 1) * q_part)
        own = attn_in[j, :, :q_part].astype(F32)
        query_out[:, at] = own * gain
        total = total + jnp.sum(own * query_weight[:, at].astype(F32), axis=1, keepdims=True)
        out_out[:, at] = attn_in[j, :, q_part + 2 * DH :].astype(F32)
    for j in range(KV):
        at = slice(j * DH, (j + 1) * DH)
        for k, (out, weight) in enumerate(((key_out, key_weight), (value_out, value_weight))):
            cols = slice(q_part + k * DH, q_part + (k + 1) * DH)
            own = attn_in[j * share, :, cols].astype(F32)
            for i in range(1, share):
                own = own + attn_in[j * share + i, :, cols].astype(F32)
            out[:, at] = own * gain
            total = total + jnp.sum(own * weight[:, at].astype(F32), axis=1, keepdims=True)
    gain1_out[...] = total


def finish(first, second, attn, weights, gain2, gain1):
    rows = first.shape[1]
    shape = jax.ShapeDtypeStruct
    vmem = pl.BlockSpec(memory_space=pltpu.VMEM)
    gate, up, query, key, value = (shape(w.shape, F32) for w in weights)
    column = shape((rows, 1), F32)
    return pl.pallas_call(
        finish_kernel,
        out_shape=(gate, up, gate, column, query, key, value, query, column),
        in_specs=[vmem] * 10,
        out_specs=(vmem,) * 9,
        cost_estimate=pl.CostEstimate(
            flops=4 * gate.size, transcendentals=0, bytes_accessed=16 * gate.size
        ),
        compiler_params=pltpu.CompilerParams(vmem_limit_bytes=40 << 20),
        name="finish",
    )(first, second, attn, *weights, gain2, gain1)


def columns(matrix, parts):
    rows, cols = matrix.shape
    return jnp.transpose(matrix.reshape(rows, parts, cols // parts), (1, 0, 2))


def uncolumns(blocks):
    parts, rows, cols = blocks.shape
    return jnp.transpose(blocks, (1, 0, 2)).reshape(rows, parts * cols)


def after(value, *earlier):
    return lax.optimization_barrier((value,) + earlier)[0]


def per_device(
    layer_input,
    pic_starts,
    skip_mask,
    gain_attn,
    w_query,
    w_key,
    w_value,
    w_out,
    gain_ffn,
    w_gate,
    w_up,
    w_down,
    cotangent,
):
    _, local_len, width = layer_input.shape
    seq = lax.axis_size("seq")
    plane = lax.axis_size("tp") * seq
    total_len = local_len * seq
    heads = H // plane
    share = plane // KV
    ff_part = w_gate.shape[1] // plane
    q_part = heads * DH

    gain1 = gain_attn[:, None]
    gain2 = gain_ffn[:, None]
    wq32, wk32, wv32 = w_query.astype(F32), w_key.astype(F32), w_value.astype(F32)
    wg32, wu32 = w_gate.astype(F32), w_up.astype(F32)
    attn_pack = jnp.concatenate(
        [
            columns((wq32 * gain1).astype(BF), plane),
            jnp.repeat(columns((wk32 * gain1).astype(BF), KV), share, axis=0),
            jnp.repeat(columns((wv32 * gain1).astype(BF), KV), share, axis=0),
            columns(w_out.T, plane),
        ],
        axis=2,
    )
    attn_rows = exchange_plane(attn_pack, 0)
    attn_rows = attn_rows.reshape(-1, attn_rows.shape[2])
    attn_weight = lax.all_gather(attn_rows, "rep", axis=0, tiled=True)
    qkv_weight = attn_weight[:, : q_part + 2 * DH]
    out_weight = attn_weight[:, q_part + 2 * DH :]

    tokens = layer_input.reshape(local_len, width).astype(F32)
    keep = (1 - skip_mask).astype(F32).reshape(local_len, 1)
    upstream = cotangent.reshape(local_len, width).astype(F32)
    scale1 = rms_scale(tokens)
    norm1 = tokens * scale1

    first_part = (ff_part // 2 + DH - 1) // DH * DH
    split = ((0, first_part), (first_part, ff_part))
    ffn_parts = (
        columns((wg32 * gain2).astype(BF), plane),
        columns((wu32 * gain2).astype(BF), plane),
        columns(w_down.T, plane),
    )
    first_pack, second_pack = (
        jnp.concatenate([m[:, :, a:b] for m in ffn_parts], axis=2) for a, b in split
    )
    first_rows = exchange_plane(after(first_pack, attn_rows), 2)
    norm1_all, second_rows = spread_plane(after(norm1.astype(BF), first_rows), second_pack, 1)
    first_rows = first_rows.reshape(-1, first_rows.shape[2])
    second_rows = second_rows.reshape(-1, second_rows.shape[2])
    first_weight = lax.all_gather(first_rows, "rep", axis=0, tiled=True)
    second_weight = lax.all_gather(second_rows, "rep", axis=0, tiled=True)
    norm1_all = norm1_all.reshape(-1, width)

    other_starts = lax.ppermute(pic_starts, "tp", [(0, 1), (1, 0)])
    starts = jnp.where(
        lax.axis_index("tp") == 0,
        jnp.concatenate([pic_starts, other_starts], axis=0),
        jnp.concatenate([other_starts, pic_starts], axis=0),
    )
    cos, sin = rotary_tables(total_len, DH)
    qkv, mixed, log_total, branch_partial, ffn_grad = attn_front_plane(
        starts, norm1_all, attn_weight, cos, sin, (keep * upstream).astype(BF), 3
    )
    branch = scatter_plane(branch_partial, 4)
    hidden = tokens + keep * branch

    scale2 = rms_scale(hidden)
    norm2 = hidden * scale2
    norm2_all, back_first, out_first, first_partial = ffn_first_plane(
        norm2.astype(BF), ffn_grad, first_weight, 5
    )
    first_sums = lax.psum_scatter(first_partial, "rep", scatter_dimension=0, tiled=True)
    out_partial, second_partial, scaled2 = ffn_second_plane(
        norm2_all, ffn_grad, second_weight, back_first, out_first, 6
    )
    second_sums = lax.psum_scatter(second_partial, "rep", scatter_dimension=0, tiled=True)
    hidden_grad = upstream + scale2 * (
        scaled2 - norm2 * jnp.mean(scaled2 * norm2, axis=-1, keepdims=True)
    )

    _, mixed_grad, out_columns = gather_mix_plane(
        (keep * hidden_grad).astype(BF), mixed, out_weight, 7
    )
    qkv_grad, ffn_out = attn_back_plane(
        starts,
        qkv,
        after(mixed_grad, first_sums),
        log_total,
        cos,
        sin,
        out_partial.reshape(-1, width),
        9,
    )
    attn_partial, scaled1_partial, first_own = attn_grads_plane(
        norm1_all,
        qkv_grad,
        out_columns,
        attn_weight,
        first_sums.reshape(plane, -1, first_sums.shape[1]),
        11,
    )
    attn_sums = lax.psum_scatter(attn_partial, "rep", scatter_dimension=0, tiled=True)
    scaled1 = scatter_plane(after(scaled1_partial, second_sums), 8)
    input_grad = hidden_grad + scale1 * (
        scaled1 - norm1 * jnp.mean(scaled1 * norm1, axis=-1, keepdims=True)
    )
    out_hidden = (hidden + keep * ffn_out).astype(BF)

    (second_own,) = exchange_all_plane(
        (after(second_sums, scaled1).reshape(plane, -1, second_sums.shape[1]),), 10
    )
    (attn_own,) = exchange_all_plane(
        (after(attn_sums, second_own, input_grad, out_hidden).reshape(plane, -1, attn_sums.shape[1]),),
        12,
    )
    weights = (w_gate, w_up, w_query, w_key, w_value)
    gate_grad, up_grad, down_grad, gain2_grad, *attn_grads = finish(
        first_own, second_own, attn_own, weights, gain2, gain1
    )
    query_grad, key_grad, value_grad, out_grad, gain1_grad = attn_grads
    return (
        out_hidden[None],
        input_grad[None],
        gain1_grad[:, 0],
        query_grad,
        key_grad,
        value_grad,
        out_grad.T,
        gain2_grad[:, 0],
        gate_grad,
        up_grad,
        down_grad.T,
    )


def solution(mesh):
    devices = mesh.devices
    dp, seq = devices.shape
    inner = Mesh(devices.reshape(dp // TP, TP, seq), ("rep", "tp", "seq"))
    dps = ("rep", "tp")
    every = ("rep", "tp", "seq")
    token = P(dps, "seq", None)
    row = P(every, None)
    col = P(None, every)
    return jax.shard_map(
        per_device,
        mesh=inner,
        in_specs=(
            token,
            P(dps, None),
            P(dps, "seq"),
            P(every),
            row,
            row,
            row,
            col,
            P(every),
            row,
            row,
            col,
            token,
        ),
        out_specs=(token, token, P(every), row, row, row, col, P(every), row, row, col),
        check_vma=False,
    )
```
